32 devices in a mesh: wide: 8 (over z, y), narrow: 4 (over x, core).
Axes of the slice: x: 2, y: 2, z: 4, core: 2. Of those that a mesh axis runs over, the one named last changes fastest.
Arguments:
- layer_inputs_matrix: bfloat16 [32768, 768], P(('wide', 'narrow')), may hold values from -6 to 6
- assignment_indices: int32 [32768, 1], P(('wide', 'narrow')), may hold values from 0 to 7
- admitted_counts_matrix: int32 [8], replicated, may hold values from 24 to 48, as said below
- mixer_scaling1_factor: bfloat16 [768], P(('wide', 'narrow')), may hold values from 0.5 to 1.5
- triple_linear_matrix: bfloat16 [768, 2304], P(('wide', 'narrow')), may hold values from -0.21875 to 0.21875
- mixer_exit_matrix: bfloat16 [768, 768], P(('wide', 'narrow')), may hold values from -0.875 to 0.875
- specialist_scaling2_factor: bfloat16 [768], P(('wide', 'narrow')), may hold values from 0.5 to 1.5
- cluster_mean_columns: bfloat16 [768, 8], P(('wide', 'narrow')), may hold values from -0.21875 to 0.21875
- first_linear_matrix: bfloat16 [8, 768, 3072], P('wide', None, 'narrow'), may hold values from -0.21875 to 0.21875
- second_linear_matrix: bfloat16 [8, 768, 3072], P('wide', None, 'narrow'), may hold values from -0.109375 to 0.109375
- incoming_gradient: bfloat16 [32768, 768], P(('wide', 'narrow')), may hold values from -6 to 6
Outputs:
- mixed: bfloat16 [32768, 768], P(('wide', 'narrow'))
- tokens_grad: float32 [32768, 768], P(('wide', 'narrow'))
- norm1_gain_grad: float32 [768], P(('wide', 'narrow'))
- qkv_grad: float32 [768, 2304], P(('wide', 'narrow'))
- out_grad: float32 [768, 768], P(('wide', 'narrow'))
- norm2_gain_grad: float32 [768], P(('wide', 'narrow'))
- centroid_grad: float32 [768, 8], P(('wide', 'narrow'))
- up_grad: float32 [8, 768, 3072], P('wide', None, 'narrow')
- down_grad: float32 [8, 768, 3072], P('wide', None, 'narrow')
The draws below stay inside these ranges and needn't reach their ends.
Inputs may be any that keep to these rules, and one draw needn't show every extreme that they name: `admitted_counts_matrix`: so a device sends at most 48 tokens to one expert.
All inputs are finite; a program needn't handle non-finite values.
Results may differ from the reference program's by a relative error of at most 0.014.
Values may be sent and summed in bfloat16 or wider, within the bound.
A program may use at most 320 MiB of HBM per device.

```python
import jax
import jax.numpy as jnp
from jax import lax

D = 768
HEADS = 12
HD = 64
FF = 3072
SEQ = 1024
SLOT = 48
TOK_DEV = 1024
EXPERTS = 8
TOKENS = 32768


def common_hot(key):
    return jax.random.randint(jax.random.fold_in(key, 11), (), 0, EXPERTS)


def draw_assignment_indices(key, part):
    hot_one = common_hot(key)
    picker = jax.random.randint(jax.random.fold_in(key, 12), (TOKENS, 1), 0, EXPERTS)
    others = jax.random.randint(jax.random.fold_in(key, 13), (TOKENS, 1), 0, EXPERTS)
    return jnp.where(picker < 3, hot_one, others).astype(jnp.int32)


def draw_admitted_counts_matrix(key, part):
    hot_one = common_hot(key)
    spread = jax.random.randint(jax.random.fold_in(key, 14), (EXPERTS,), SLOT // 2, SLOT + 1)
    return jnp.where(jnp.arange(EXPERTS) == hot_one, SLOT, spread).astype(jnp.int32)


def block_scale(stream_key, dims, split, smallest, top_value):
    gain, own = 1.0, jax.random.fold_in(stream_key, 6)
    for dim, parts in split:
        heights = jnp.exp(jax.random.uniform(jax.random.fold_in(own, dim), (parts,), jnp.float32, smallest / len(split), top_value / len(split)))
        gain = gain * jnp.repeat(heights, dims[dim] // parts).reshape([-1 if axis == dim else 1 for axis in range(len(dims))])
    return gain


def bell_draw(stream_key, shape, deviation, most, split=(), kind=jnp.bfloat16):
    entries = deviation * jax.random.normal(stream_key, shape, jnp.float32)
    if split:
        entries = entries * block_scale(stream_key, shape, split, -0.22, 0.18)
    return jnp.clip(entries, -most, most).astype(kind)


def setup_inputs(seed: int = 0) -> dict:
    seeds = jax.random.split(jax.random.key(seed), 12)
    return {
        "layer_inputs_matrix": bell_draw(seeds[0], (TOKENS, D), 1.0, 6.0, ((0, 32),)),
        "assignment_indices": draw_assignment_indices(jax.random.fold_in(seeds[11], 71), 0),
        "admitted_counts_matrix": draw_admitted_counts_matrix(jax.random.fold_in(seeds[11], 71), 0),
        "mixer_scaling1_factor": jnp.clip(1.0 + 0.1 * jax.random.normal(seeds[3], (D,), jnp.float32), 0.5, 1.5).astype(jnp.bfloat16),
        "triple_linear_matrix": bell_draw(seeds[4], (D, 3 * D), D ** -0.5, 0.21875, ((0, 32),)),
        "mixer_exit_matrix": bell_draw(seeds[5], (D, D), (D // 16) ** -0.5, 0.875, ((0, 32),)),
        "specialist_scaling2_factor": jnp.clip(1.0 + 0.1 * jax.random.normal(seeds[6], (D,), jnp.float32), 0.5, 1.5).astype(jnp.bfloat16),
        "cluster_mean_columns": bell_draw(seeds[7], (D, EXPERTS), D ** -0.5, 0.21875, ((0, 32),)),
        "first_linear_matrix": bell_draw(seeds[8], (EXPERTS, D, FF), D ** -0.5, 0.21875, ((0, 8), (2, 4))),
        "second_linear_matrix": bell_draw(seeds[9], (EXPERTS, D, FF), FF ** -0.5, 0.109375, ((0, 8), (2, 4))),
        "incoming_gradient": bell_draw(seeds[10], (TOKENS, D), 1.0, 6.0, ((0, 32),)),
    }


@jax.custom_vjp
def low(v):
    return lax.optimization_barrier(v.astype(jnp.bfloat16)).astype(jnp.float32)

@jax.custom_vjp
def low_back(v):
    return v

def low_keep(v):
    return (low(v), None)

def low_pass(kept, grad):
    return (grad,)

def back_keep(v):
    return (v, None)

def back_low(kept, grad):
    return (low(grad),)
low.defvjp(low_keep, low_pass)
low_back.defvjp(back_keep, back_low)
precise = lax.Precision.HIGHEST

def layer_norm(tensor, gain_vec):
    centered = tensor - lax.optimization_barrier(jnp.mean(tensor, -1, keepdims=True))
    spread = lax.optimization_barrier(jnp.mean(centered * centered, -1, keepdims=True))
    return centered * lax.rsqrt(spread + 1e-05) * gain_vec

def attend(packed):
    queries = packed[:, :D].reshape(SEQ, HEADS, HD)
    key_rows = packed[:, D:2 * D].reshape(SEQ, HEADS, HD)
    value_rows = packed[:, 2 * D:].reshape(SEQ, HEADS, HD)
    raw_scores = jnp.einsum('qhd,khd->hqk', queries, key_rows, precision=precise) * HD ** (-0.5)
    scores = low_back(raw_scores)
    places = jnp.arange(SEQ)
    causal = places[:, None] >= places[None, :]
    attn_probs = low(jax.nn.softmax(jnp.where(causal[None], scores, -1e+30), axis=-1))
    attended = jnp.einsum('hqk,khd->qhd', attn_probs, value_rows, precision=precise)
    return attended.reshape(SEQ, D)

def frozen_assignment_grid(dispatched_items, admitted_counts_matrix):
    blocks = TOKENS // TOK_DEV
    sorted_per_specialist = dispatched_items.reshape(blocks, TOK_DEV)
    specialist_indicator = (sorted_per_specialist[:, :, None] == jnp.arange(EXPERTS, dtype=jnp.int32)[None, None, :]).astype(jnp.int32)
    before = jnp.cumsum(specialist_indicator, axis=1) - specialist_indicator
    ranked = lax.optimization_barrier(jnp.sum(before * specialist_indicator, axis=2))
    position_ceilings = admitted_counts_matrix[sorted_per_specialist]
    retained_couple_filter = ranked < position_ceilings
    starts = jnp.arange(blocks, dtype=jnp.int32)[:, None] * SLOT
    column = jnp.where(retained_couple_filter, starts + ranked, blocks * SLOT).reshape(TOKENS).astype(jnp.int32)
    token_ids = jnp.arange(TOKENS, dtype=jnp.int32)
    specialist_position_grid = jnp.full((EXPERTS, blocks * SLOT), TOKENS, jnp.int32).at[dispatched_items, column].set(token_ids, mode='drop')
    return (specialist_position_grid, retained_couple_filter.reshape(TOKENS))

def expert_sum(inputs_rows, specialist_position_grid, up_mat, down_mat):
    padded = jnp.concatenate([inputs_rows, jnp.zeros((1, D), jnp.float32)], 0)

    def per_expert(member):
        row_ids, up_one, down_one = member
        row_block = padded[row_ids]
        pre_act = low_back(jnp.dot(row_block, up_one, precision=precise))
        hidden = low(jax.nn.gelu(pre_act, approximate=False))
        return lax.dot_general(hidden, down_one, (((1,), (1,)), ((), ())), precision=precise)
    outputs = lax.map(jax.checkpoint(per_expert), (specialist_position_grid, up_mat, down_mat))
    summed = jnp.zeros((TOKENS + 1, D), jnp.float32).at[specialist_position_grid.reshape(-1)].add(outputs.reshape(-1, D))
    return summed[:TOKENS]

def reference(layer_inputs_matrix, assignment_indices, admitted_counts_matrix, mixer_scaling1_factor, triple_linear_matrix, mixer_exit_matrix, specialist_scaling2_factor, cluster_mean_columns, first_linear_matrix, second_linear_matrix, incoming_gradient):
    dispatched_items = assignment_indices[:, 0].astype(jnp.int32)
    specialist_position_grid, retained_couple_filter = frozen_assignment_grid(dispatched_items, admitted_counts_matrix)
    kept_rows = retained_couple_filter.astype(jnp.float32)

    def forward(token_rows, gain_one, qkv_mat, out_mat, gain_two, centers, up_mat, down_mat):
        normed = low(layer_norm(token_rows, gain_one))
        qkv_rows = low_back(low(jnp.dot(normed, qkv_mat, precision=precise)))
        attended = lax.map(jax.checkpoint(attend), qkv_rows.reshape(TOKENS // SEQ, SEQ, 3 * D)).reshape(TOKENS, D)
        attended = low_back(low(attended))
        residual = token_rows + low_back(jnp.dot(attended, out_mat, precision=precise))
        normed_two = layer_norm(residual, gain_two)
        sent_rows = low_back(low(normed_two))
        expert_out = low_back(low(expert_sum(sent_rows, specialist_position_grid, up_mat, down_mat)))
        logits = lax.optimization_barrier(jnp.sum(normed_two * centers.T[dispatched_items], -1))
        gating = jax.nn.sigmoid(logits) * kept_rows
        return residual + gating[:, None] * expert_out
    inputs_all = (layer_inputs_matrix.astype(jnp.float32), mixer_scaling1_factor.astype(jnp.float32), triple_linear_matrix.astype(jnp.float32), mixer_exit_matrix.astype(jnp.float32), specialist_scaling2_factor.astype(jnp.float32), cluster_mean_columns.astype(jnp.float32), first_linear_matrix.astype(jnp.float32), second_linear_matrix.astype(jnp.float32))
    result, pullback = jax.vjp(forward, *inputs_all)
    gradients = pullback(incoming_gradient.astype(jnp.float32))
    return (result.astype(jnp.bfloat16), gradients[0], gradients[1], gradients[2], gradients[3], gradients[4], gradients[5], gradients[6], gradients[7])
```

```python
import functools

import jax
import jax.numpy as jnp
from jax import lax
from jax.experimental import pallas as pl
from jax.experimental.pallas import tpu as pltpu
from jax.sharding import PartitionSpec as P

HD = 64
SEQ = 1024
SLOT = 48
PAIR = 2 * HD
QB = 256
LANES = 128
GAIN1 = 126
GAIN2 = 127
NEG = -1e30
VMEM_CAP = 62 << 20

MESH = pl.DeviceIdType.MESH
NN_ = (((1,), (0,)), ((), ()))
NT_ = (((1,), (1,)), ((), ()))
TN_ = (((0,), (0,)), ((), ()))
f32 = jnp.float32
bf16 = jnp.bfloat16


def mm(a, b, dims=NN_):
    return lax.dot_general(a, b, dims, preferred_element_type=f32)


def wait_bytes(ref, sem):
    pltpu.make_async_copy(ref, ref, sem).wait()


def push(src, dst, send, recv, **where):
    pltpu.make_async_remote_copy(
        src_ref=src, dst_ref=dst, send_sem=send, recv_sem=recv,
        device_id=where, device_id_type=MESH,
    ).start()


def half_mask(rows):
    return lax.broadcasted_iota(jnp.int32, (rows, PAIR), 1) < HD


def pick(mask, h, value):
    zero = jnp.zeros_like(value)
    return jnp.where(mask, value, zero) if h == 0 else jnp.where(mask, zero, value)


def layer_stats(x):
    centered = x - jnp.mean(x, 1, keepdims=True)
    r = lax.rsqrt(jnp.mean(centered * centered, 1, keepdims=True) + 1e-05)
    return centered * r, r


def attend_rows(qkv, seq, i, put_out, put_lse):
    length = (i + 1) * QB
    rows = pl.ds(i * QB, QB)
    mask = half_mask(QB)
    causal = lax.broadcasted_iota(jnp.int32, (QB, QB), 0) <= lax.broadcasted_iota(
        jnp.int32, (QB, QB), 1
    )
    q = qkv[rows, 0:PAIR] * bf16(HD**-0.5)
    k = qkv[pl.ds(0, length), PAIR : 2 * PAIR]
    v = qkv[pl.ds(0, length), 2 * PAIR : 3 * PAIR]
    outs, sums = [], []
    for h in range(2):
        s = mm(k, pick(mask, h, q), NT_)
        last = jnp.where(causal, s[length - QB :], NEG)
        top = jnp.max(last, 0, keepdims=True)
        if i:
            top = jnp.maximum(top, jnp.max(s[: length - QB], 0, keepdims=True))
        p = jnp.exp(last - top)
        total = jnp.sum(p, 0, keepdims=True)
        p = p.astype(bf16)
        if i:
            head = jnp.exp(s[: length - QB] - top)
            total = total + jnp.sum(head, 0, keepdims=True)
            p = jnp.concatenate([head.astype(bf16), p], 0)
        put_lse(h, rows, top + jnp.log(total))
        outs.append(mm(p, v, TN_))
        sums.append(total)
    inv = jnp.transpose(1.0 / jnp.concatenate(sums + [jnp.ones((6, QB), f32)], 0))
    put_out(rows, jnp.where(mask, outs[0] * inv[:, 0:1], outs[1] * inv[:, 1:2]).astype(bf16))


def attend_rows_back(qkv, att, datt, lse, i, first, prod, dk, dv, put_dq):
    length = (i + 1) * QB
    rows = pl.ds(i * QB, QB)
    mask = half_mask(QB)
    mask_all = half_mask(length)
    causal = lax.broadcasted_iota(jnp.int32, (QB, QB), 0) <= lax.broadcasted_iota(
        jnp.int32, (QB, QB), 1
    )
    q = qkv[rows, 0:PAIR] * bf16(HD**-0.5)
    k = qkv[pl.ds(0, length), PAIR : 2 * PAIR]
    v = qkv[pl.ds(0, length), 2 * PAIR : 3 * PAIR]
    do = datt[rows, :]
    dq = None
    for h in range(2):
        qh, dh = pick(mask, h, q), pick(mask, h, do)
        s = mm(k, qh, NT_)
        row = lse[h : h + 1, rows]
        p = jnp.exp(jnp.where(causal, s[length - QB :], NEG) - row)
        if i:
            p = jnp.concatenate([jnp.exp(s[: length - QB] - row), p], 0)
        dp = mm(v, dh, NT_)
        ds = (p * (dp - prod[h : h + 1, rows])).astype(bf16)
        a, b = mm(p.astype(bf16), dh), mm(ds, qh)
        if first and h == 0:
            dv[pl.ds(0, length), :] = a
            dk[pl.ds(0, length), :] = b
        else:
            dv[pl.ds(0, length), :] += a
            dk[pl.ds(0, length), :] += b
        part = mm(ds, pick(mask_all, h, k), TN_)
        dq = part if dq is None else dq + part
    put_dq(rows, (dq * HD**-0.5).astype(bf16))


class Sizes:
    def __init__(self, mesh, tokens, d, slab, ff, experts):
        self.NW, self.NN = mesh.shape["wide"], mesh.shape["narrow"]
        self.A, self.X = self.NW // 2, self.NN // 2
        self.T, self.D, self.slab, self.F, self.E = tokens, d, slab, ff, experts
        self.CW = 3 * PAIR
        self.G = d // PAIR
        self.J = self.G + d // self.CW
        self.R = self.NN * SLOT
        self.S = experts * SLOT
        self.EP = max(8, experts)
        rows = self.NW * self.R
        self.moe = rows * (5 * d + 3 * ff) * 2 < (24 << 20)
        self.fits = (
            self.moe and slab % 8 == 0 and tokens == SEQ and self.NW % 2 == 0 and self.NN % 2 == 0
            and self.NW > 2 and self.NN > 2 and experts == self.NW
        )


def place(c):
    w, n = lax.axis_index("wide"), lax.axis_index("narrow")
    return w, n, w // 2, lax.rem(w, 2), n // 2, lax.rem(n, 2)


def greet(c, w, n):
    bar = pltpu.get_barrier_semaphore()
    x, cc = n // 2, lax.rem(n, 2)

    def wide(i, _):
        pl.semaphore_signal(bar, inc=1, device_id={"wide": lax.rem(w + i, c.NW)}, device_id_type=MESH)
        return 0

    lax.fori_loop(1, c.NW, wide, 0)
    for k in range(1, c.X):
        pl.semaphore_signal(bar, inc=1, device_id={"narrow": lax.rem(x + k, c.X) * 2 + cc}, device_id_type=MESH)
    pl.semaphore_signal(bar, inc=1, device_id={"narrow": x * 2 + 1 - cc}, device_id_type=MESH)
    return lambda: pl.semaphore_wait(bar, c.NW - 1 + c.X)


def forward_kernel(c, *refs):
    (v_hbm, dy_hbm, idx_ref, cap_ref, wq_hbm, wo_hbm, misc_hbm, up_hbm, down_hbm) = refs[:9]
    (wall, mall, qkv_out, lse_out, att_out, resid_out, sent_out, meta_out, mrow_out) = refs[9:18]
    (ret_out, outp_out, ug_out, dg_out, cent_out) = refs[18:23]
    scratch = refs[23:]
    (v, dy, nrm, normed, oh, wbuf, wmat, misc, mrow, qkv, lse, att, sent, sendx, senddy,
     lsem, in_sem, out_sem, ld_sem, s1s, s1r, s2s, s2r, s3s, s3r, s4s, s4r) = scratch[:27]
    A, X, NW, NN, T, D, CW, G, J = c.A, c.X, c.NW, c.NN, c.T, c.D, c.CW, c.G, c.J
    w, n, a, b, x, cc = place(c)
    own = (a, b, x, cc)

    def cols(j):
        dst = wall.at[(j, *own)]
        if j < G:
            return [(wq_hbm.at[:, pl.ds(p * D + j * PAIR, PAIR)], dst.at[:, pl.ds(p * PAIR, PAIR)]) for p in range(3)]
        return [(wo_hbm.at[:, pl.ds((j - G) * CW, CW)], dst)]

    pltpu.make_async_copy(misc_hbm, mall.at[own], lsem.at[J]).start()
    for j in range(J):
        for s, d in cols(j):
            pltpu.make_async_copy(s, d, lsem.at[j]).start()
    loads = [(dy_hbm, dy), (v_hbm, v)]
    if c.moe:
        (up, down, xin, dyin, hid, dpre, dexp, outp, part, lc, lx, stage, cent,
         ds_, dr, xs_, xr, cs_, cr, fs, fr, gs, gr, ks, kr, rs_, rr, ws_, wr) = scratch[27:]
        loads += [(up_hbm.at[0], up), (down_hbm.at[0], down)]
    for i, (s, d) in enumerate(loads):
        pltpu.make_async_copy(s, d, in_sem.at[i]).start()

    def load_wait(i):
        wait_bytes(loads[i][1], in_sem.at[i])

    met = greet(c, w, n)

    one = lax.broadcasted_iota(jnp.int32, (c.EP, T), 0) == idx_ref[...]
    hot = one.astype(f32)
    lane = lax.broadcasted_iota(jnp.int32, (c.EP, T), 1)
    count = hot
    shift = 1
    while shift < T:
        count = count + jnp.where(lane >= shift, pltpu.roll(count, shift, 1), 0.0)
        shift *= 2
    rank = jnp.sum((count - hot) * hot, 0, keepdims=True)
    ceiling = jnp.sum(hot * cap_ref[:, 0:1].astype(f32), 0, keepdims=True)
    kept = rank < ceiling
    slot = jnp.where(kept, idx_ref[...].astype(f32) * SLOT + rank, -1.0)
    meta_out_rows = [slot]

    met()

    def buf(j):
        return mall if j is J else wall.at[j]

    def s1(j):
        wait_bytes(buf(j).at[own], lsem.at[j])
        for k in range(1, A):
            push(buf(j).at[own], buf(j).at[own], s1s.at[j], s1r.at[j], wide=lax.rem(a + k, A) * 2 + b)

    def s2(j):
        wait_bytes(buf(j).at[pl.ds(0, A - 1), b, x, cc], s1r.at[j])
        for k in range(1, X):
            part_ = buf(j).at[:, b, x, cc]
            push(part_, part_, s2s.at[j], s2r.at[j], narrow=lax.rem(x + k, X) * 2 + cc)

    def s3(j):
        wait_bytes(buf(j).at[:, b, pl.ds(0, X - 1), cc], s2r.at[j])
        part_ = buf(j).at[:, b, :, cc]
        push(part_, part_, s3s.at[j], s3r.at[j], wide=a * 2 + 1 - b)

    def s4(j):
        wait_bytes(buf(j).at[:, b, :, cc], s3r.at[j])
        part_ = buf(j).at[:, :, :, cc]
        push(part_, part_, s4s.at[j], s4r.at[j], narrow=x * 2 + 1 - cc)

    def ld(j):
        wait_bytes(buf(j).at[:, :, :, cc], s4r.at[j])
        if j is J:
            pltpu.make_async_copy(mall, misc, ld_sem.at[J]).start()
        else:
            pltpu.make_async_copy(wall.at[j], wbuf.at[lax.rem(j, 2)], ld_sem.at[j]).start()

    def loaded(j, at):
        slot_ = lax.rem(j, 2)
        wait_bytes(wbuf.at[slot_], ld_sem.at[j])
        wmat[at] = wbuf[slot_].reshape(D, CW)

    s1(J)
    for j in range(J):
        s1(j)

    ohv = (lax.broadcasted_iota(jnp.int32, (c.S, T), 0).astype(f32) == slot).astype(bf16)
    oh[...] = ohv
    load_wait(0)
    senddy[...] = mm(oh[...], dy[...]).astype(bf16)
    s2(J)
    s2(0)

    if c.moe:
        for k in range(1, NW):
            to = lax.rem(w + k, NW)
            push(senddy.at[pl.ds(to * SLOT, SLOT)], dyin.at[w, x, cc], ds_, dr, wide=to)
        dyin[w, x, cc] = senddy[pl.ds(w * SLOT, SLOT), :]
    else:
        pltpu.make_async_copy(senddy, senddy_out, out_sem.at[7]).start()
    s3(J)
    s3(0)
    s2(1)

    load_wait(1)

    def norm1(i, _):
        rows = pl.ds(i * 128, 128)
        nrm[rows, :] = layer_stats(v[rows, :].astype(f32))[0]
        return 0

    lax.fori_loop(0, T // 128, norm1, 0)
    s4(J)
    s4(0)
    s3(1)
    s2(2)
    ld(J)
    wait_bytes(misc, ld_sem.at[J])
    mrow[...] = jnp.transpose(misc[...].reshape(D, LANES).astype(f32))
    gain1 = mrow[GAIN1 : GAIN1 + 1, :]
    gain2 = mrow[GAIN2 : GAIN2 + 1, :]
    pltpu.make_async_copy(mrow, mrow_out, out_sem.at[0]).start()

    def norm1b(i, _):
        rows = pl.ds(i * 128, 128)
        normed[rows, :] = (nrm[rows, :] * gain1).astype(bf16)
        return 0

    lax.fori_loop(0, T // 128, norm1b, 0)
    ld(0)

    def pair(g, _):
        loaded(g, 0)

        def project(i, _):
            rows = pl.ds(i * QB, QB)
            qkv[g, rows, :] = mm(normed[rows, :], wmat[0]).astype(bf16)
            return 0

        lax.fori_loop(0, T // QB, project, 0)
        pltpu.make_async_copy(qkv.at[g], qkv_out.at[g], out_sem.at[1]).start()
        s3(g + 2)

        @pl.when(g + 3 < J)
        def _():
            s2(g + 3)

        def put_out(rows, val):
            att[rows, pl.ds(pl.multiple_of(g * PAIR, PAIR), PAIR)] = val

        def put_lse(h, rows, val):
            lse[g, h : h + 1, rows] = val

        for i in range(T // QB):
            if i == T // QB - 1:
                s4(g + 1)
                if c.moe:
                    @pl.when(g == 4)
                    def _():
                        wait_bytes(dyin.at[pl.ds(0, NW - 1), x, cc], dr)
                        for k in range(1, X):
                            push(dyin.at[:, x, cc], dyin.at[:, x, cc], xs_, xr, narrow=lax.rem(x + k, X) * 2 + cc)
            attend_rows(qkv.at[g], T, i, put_out, put_lse)
        ld(g + 1)
        return 0

    lax.fori_loop(0, G, pair, 0)
    pltpu.make_async_copy(lse, lse_out, out_sem.at[2]).start()
    pltpu.make_async_copy(att, att_out, out_sem.at[3]).start()
    for j in range(G + 1, J):
        s4(j)
        ld(j)
    if c.moe:
        wait_bytes(dyin.at[:, pl.ds(0, X - 1), cc], xr)
        push(dyin.at[:, :, cc], dyin.at[:, :, cc], cs_, cr, narrow=x * 2 + 1 - cc)
    for j in range(G, J):
        loaded(j, 1 + j - G)

    def tail(i, _):
        rows = pl.ds(i * QB, QB)
        left = att[rows, :]
        prod = jnp.concatenate([mm(left, wmat[1 + j - G]) for j in range(G, J)], 1)
        resid = v[rows, :].astype(f32) + prod
        nrm[rows, :] = resid
        sent[rows, :] = (layer_stats(resid)[0] * gain2).astype(bf16)
        return 0

    lax.fori_loop(0, T // QB, tail, 0)
    pltpu.make_async_copy(nrm, resid_out, out_sem.at[4]).start()
    sendx[...] = mm(oh[...], sent[...]).astype(bf16)
    if c.moe:
        for k in range(1, NW):
            to = lax.rem(w + k, NW)
            push(sendx.at[pl.ds(to * SLOT, SLOT)], xin.at[w, x, cc], fs.at[k], fr.at[k], wide=to)
        xin[w, x, cc] = sendx[pl.ds(w * SLOT, SLOT), :]
    else:
        pltpu.make_async_copy(sendx, sendx_out, out_sem.at[8]).start()
    pltpu.make_async_copy(sent, sent_out, out_sem.at[5]).start()
    logits = mm(mrow[0 : c.EP, :].astype(bf16), sent[...], NT_)
    logit = jnp.sum(logits * hot, 0, keepdims=True)
    gate = jax.nn.sigmoid(logit) * kept.astype(f32)
    meta_out[...] = jnp.concatenate([slot, gate, jnp.zeros((6, T), f32)], 0)

    if c.moe:
        load_wait(2)
        load_wait(3)
        wait_bytes(dyin.at[:, :, cc], cr)
        cent[...] = jnp.zeros_like(cent)
        crow = mrow[pl.ds(w, 1), :]

        def source(i):
            return lax.rem(w - i + NW, NW)

        def fwd_x(i):
            src = source(i)

            @pl.when(i > 0)
            def _():
                wait_bytes(xin.at[src, x, cc], fr.at[i])

            for k in range(1, X):
                push(xin.at[src, x, cc], xin.at[src, x, cc], gs.at[i], gr.at[i], narrow=lax.rem(x + k, X) * 2 + cc)

        def fwd_c(i):
            src = source(i)
            wait_bytes(xin.at[src, pl.ds(0, X - 1), cc], gr.at[i])
            push(xin.at[src, :, cc], xin.at[src, :, cc], ks.at[i], kr.at[i], narrow=x * 2 + 1 - cc)

        def expert(i):
            src = source(i)
            wait_bytes(xin.at[src, :, cc], kr.at[i])
            xb = xin[src].reshape(c.R, D)
            db = dyin[src].reshape(c.R, D)
            xf, df = xb.astype(f32), db.astype(f32)
            s = jax.nn.sigmoid(jnp.sum(xf * crow, 1, keepdims=True))
            de = (df * s).astype(bf16)
            pre = mm(xb, up[...])
            cdf = 0.5 * (1.0 + lax.erf(pre * 0.7071067811865476))
            hb = (pre * cdf).astype(bf16)
            slope = cdf + pre * (jnp.exp(-0.5 * pre * pre) * 0.3989422804014327)
            dpb = (mm(de, down[...]) * slope).astype(bf16)
            out = mm(hb, down[...], NT_)
            dl = jnp.sum(df * out, 1, keepdims=True) * (s * (1.0 - s))
            dn = mm(dpb, up[...], NT_) + dl * crow
            part[src] = dn.astype(bf16).reshape(X, 2, SLOT, D)
            outp[src] = out.astype(bf16).reshape(X, 2, SLOT, D)
            cent[...] += jnp.broadcast_to(jnp.sum(dl * xf, 0, keepdims=True), cent.shape)
            rows = pl.ds(pl.multiple_of(src * c.R, SLOT), c.R)
            hid[rows, :] = hb
            dpre[rows, :] = dpb
            dexp[rows, :] = de

        def ret_c(i):
            src = source(i)
            push(part.at[src, :, 1 - cc], lc.at[src], rs_.at[0, i], rr.at[0, i], narrow=x * 2 + 1 - cc)

        def ret_x(i):
            src = source(i)
            wait_bytes(lc.at[src], rr.at[0, i])
            part[src, :, cc] = (part[src, :, cc].astype(f32) + lc[src].astype(f32)).astype(bf16)
            for k in range(1, X):
                x2 = lax.rem(x + k, X)
                push(part.at[src, x2, cc], lx.at[src, x], rs_.at[1, i], rr.at[1, i], narrow=x2 * 2 + cc)

        def ret_w(i):
            src = source(i)
            wait_bytes(lx.at[src, pl.ds(0, X - 1)], rr.at[1, i])
            total = part[src, x, cc].astype(f32)
            for k in range(1, X):
                total = total + lx[src, lax.rem(x + k, X)].astype(f32)
            part[src, x, cc] = total.astype(bf16)

            @pl.when(i > 0)
            def _():
                push(part.at[src, x, cc], ret_out.at[w], ws_.at[i], wr.at[i], wide=src)

            @pl.when(i == 0)
            def _():
                pltpu.make_async_copy(part.at[src, x, cc], ret_out.at[w], ws_.at[0]).start()

        fwd_x(0)
        fwd_c(0)
        fwd_x(1)

        def block(i, _):
            @pl.when(i + 1 < NW)
            def _():
                fwd_c(i + 1)

            @pl.when(i + 2 < NW)
            def _():
                fwd_x(i + 2)

            expert(i)
            ret_c(i)

            @pl.when(i >= 1)
            def _():
                ret_x(i - 1)

            @pl.when(i >= 2)
            def _():
                ret_w(i - 2)

            return 0

        lax.fori_loop(0, NW, block, 0)
        ret_x(NW - 1)
        ret_w(NW - 2)
        pltpu.make_async_copy(outp, outp_out, out_sem.at[6]).start()
        cent_out[...] = cent[...]

        def grads(lhs, rhs, out, base, flush):
            def one_block(i, _):
                at = pl.ds(pl.multiple_of(i * QB, QB), QB)
                lhs_block = lhs(at)
                stage[base + i] = mm(lhs_block, rhs[...], TN_)
                pltpu.make_async_copy(stage.at[base + i], out.at[0, at], in_sem.at[4 + base + i]).start()
                return 0

            lax.fori_loop(0, D // QB, one_block, 0)

        grads(lambda at: dexp[:, at], hid, dg_out, 0, None)
        ret_w(NW - 1)
        grads(lambda at: xin[:, :, :, :, at].reshape(NW * c.R, QB), dpre, ug_out, D // QB, None)

    for q, (s, ref) in enumerate([(mrow, None), (qkv, None), (lse, None), (att, None), (nrm, None), (sent, None)]):
        wait_bytes(s, out_sem.at[q])
    for j in [J] + list(range(J)):
        wait_bytes(buf(j).at[pl.ds(0, A - 1), b, x, cc], s1s.at[j])
        wait_bytes(buf(j).at[:, b, pl.ds(0, X - 1), cc], s2s.at[j])
        wait_bytes(buf(j).at[:, b, :, cc], s3s.at[j])
        wait_bytes(buf(j).at[:, :, :, cc], s4s.at[j])
    if c.moe:
        wait_bytes(dyin.at[pl.ds(0, NW - 1), x, cc], ds_)
        wait_bytes(dyin.at[:, pl.ds(0, X - 1), cc], xs_)
        wait_bytes(dyin.at[:, :, cc], cs_)
        wait_bytes(outp, out_sem.at[6])

        def drain(i, _):
            src = source(i)
            wait_bytes(xin.at[src, pl.ds(0, X - 1), cc], gs.at[i])
            wait_bytes(xin.at[src, :, cc], ks.at[i])
            wait_bytes(lc.at[src], rs_.at[0, i])
            wait_bytes(lx.at[src, pl.ds(0, X - 1)], rs_.at[1, i])
            wait_bytes(xin.at[src, x, cc], ws_.at[i])

            @pl.when(i > 0)
            def _():
                wait_bytes(xin.at[src, x, cc], fs.at[i])
                wait_bytes(xin.at[src, x, cc], wr.at[i])

            return 0

        lax.fori_loop(0, NW, drain, 0)
        for i in range(2 * (D // QB)):
            wait_bytes(stage.at[i], in_sem.at[4 + i])
    else:
        wait_bytes(senddy, out_sem.at[7])
        wait_bytes(sendx, out_sem.at[8])


def forward_call(c, v, dy, idx, cap, wq, wo, misc, up, down):
    T, D, CW, G, J, NW, NN, A, X = c.T, c.D, c.CW, c.G, c.J, c.NW, c.NN, c.A, c.X
    any_ = pl.BlockSpec(memory_space=pl.ANY)
    vm = pl.BlockSpec(memory_space=pltpu.VMEM)
    sds = jax.ShapeDtypeStruct
    F = c.F
    outs = [
        (sds((J, A, 2, X, 2, c.slab, CW), bf16), any_),
        (sds((A, 2, X, 2, c.slab, LANES), bf16), any_),
        (sds((G, T, CW), bf16), any_),
        (sds((G, 8, T), f32), any_),
        (sds((T, D), bf16), any_),
        (sds((T, D), f32), any_),
        (sds((T, D), bf16), any_),
        (sds((8, T), f32), vm),
        (sds((LANES, D), f32), any_),
    ]
    dma, V = pltpu.SemaphoreType.DMA, pltpu.VMEM
    scratch = [
        V((T, D), bf16), V((T, D), bf16), V((T, D), f32), V((T, D), bf16), V((c.S, T), bf16),
        V((2, A, 2, X, 2, c.slab, CW), bf16), V((1 + J - G, D, CW), bf16),
        V((A, 2, X, 2, c.slab, LANES), bf16), V((LANES, D), f32), V((G, T, CW), bf16), V((G, 8, T), f32),
        V((T, D), bf16), V((T, D), bf16), V((c.S, D), bf16), V((c.S, D), bf16),
        dma((J + 1,)), dma((4 + 2 * (D // QB),)), dma((9,)), dma((J + 1,)),
    ] + [dma((J + 1,))] * 8
    if c.moe:
        outs += [
            (sds((NW, SLOT, D), bf16), any_),
            (sds((NW, X, 2, SLOT, D), bf16), any_),
            (sds((1, D, F), f32), any_),
            (sds((1, D, F), f32), any_),
            (sds((8, D), f32), vm),
        ]
        rows = NW * c.R
        scratch += [
            V((D, F), bf16), V((D, F), bf16), V((NW, X, 2, SLOT, D), bf16), V((NW, X, 2, SLOT, D), bf16),
            V((rows, F), bf16), V((rows, F), bf16), V((rows, D), bf16), V((NW, X, 2, SLOT, D), bf16),
            V((NW, X, 2, SLOT, D), bf16), V((NW, X, SLOT, D), bf16), V((NW, X, SLOT, D), bf16),
            V((2 * (D // QB), QB, F), f32), V((8, D), f32),
            dma(()), dma(()), dma(()), dma(()), dma(()), dma(()),
            dma((NW,)), dma((NW,)), dma((NW,)), dma((NW,)), dma((NW,)), dma((NW,)),
            dma((2, NW)), dma((2, NW)), dma((NW,)), dma((NW,)),
        ]
    else:
        outs += [(sds((c.S, D), bf16), any_), (sds((c.S, D), bf16), any_)]
    return pl.pallas_call(
        functools.partial(forward_kernel, c),
        out_shape=tuple(o[0] for o in outs),
        in_specs=[any_, any_, vm, vm, any_, any_, any_, any_, any_],
        out_specs=tuple(o[1] for o in outs),
        scratch_shapes=scratch,
        compiler_params=pltpu.CompilerParams(
            collective_id=0, has_side_effects=True, vmem_limit_bytes=VMEM_CAP
        ),
        name="forward",
    )(v, dy, idx, cap, wq, wo, misc, up, down)


def attend_back_kernel(c, qkv, att, datt, lse, dqkv, dk, dv, prod):
    full = jnp.transpose(datt[...].astype(f32) * att[...].astype(f32))
    prod[0:1, :] = jnp.sum(full[0:HD], 0, keepdims=True)
    prod[1:2, :] = jnp.sum(full[HD:], 0, keepdims=True)

    def put_dq(rows, val):
        dqkv[0, rows, 0:PAIR] = val

    blocks = c.T // QB
    for i in reversed(range(blocks)):
        attend_rows_back(qkv.at[0], att, datt, lse.at[0], i, i == blocks - 1, prod, dk, dv, put_dq)
    dqkv[0, :, PAIR : 2 * PAIR] = dk[...].astype(bf16)
    dqkv[0, :, 2 * PAIR :] = dv[...].astype(bf16)


def attend_back_call(c, qkv, att, datt, lse):
    T = c.T
    return pl.pallas_call(
        functools.partial(attend_back_kernel, c),
        grid=(c.G,),
        out_shape=jax.ShapeDtypeStruct((c.G, T, c.CW), bf16),
        in_specs=[
            pl.BlockSpec((1, T, c.CW), lambda g: (g, 0, 0)),
            pl.BlockSpec((T, PAIR), lambda g: (0, g)),
            pl.BlockSpec((T, PAIR), lambda g: (0, g)),
            pl.BlockSpec((1, 8, T), lambda g: (g, 0, 0)),
        ],
        out_specs=pl.BlockSpec((1, T, c.CW), lambda g: (g, 0, 0)),
        scratch_shapes=[pltpu.VMEM((T, PAIR), f32), pltpu.VMEM((T, PAIR), f32), pltpu.VMEM((8, T), f32)],
        compiler_params=pltpu.CompilerParams(vmem_limit_bytes=VMEM_CAP),
        name="attend_back",
    )(qkv, att, datt, lse)


precise = lax.Precision.HIGHEST
over_rows = (((0,), (0,)), ((), ()))
over_cols = (((1,), (1,)), ((), ()))


def layer_norm(tensor, gain_vec):
    centered = tensor - jnp.mean(tensor, -1, keepdims=True)
    spread = jnp.mean(centered * centered, -1, keepdims=True)
    return centered * lax.rsqrt(spread + 1e-05) * gain_vec


def gelu_exact(tensor):
    return jax.nn.gelu(tensor, approximate=False)


def split_heads(packed):
    seq_len = packed.shape[0]
    model_width = packed.shape[1] // 3
    head_count = model_width // HD
    queries = packed[:, :model_width].reshape(seq_len, head_count, HD)
    key_rows = packed[:, model_width : 2 * model_width].reshape(seq_len, head_count, HD)
    value_rows = packed[:, 2 * model_width :].reshape(seq_len, head_count, HD)
    raw_scores = jnp.einsum(
        "qhd,khd->hqk", queries, key_rows, preferred_element_type=jnp.float32
    ) * HD ** (-0.5)
    places = jnp.arange(seq_len)
    causal = places[:, None] >= places[None, :]
    masked = jnp.where(causal[None], raw_scores, -1e30)
    return (queries, key_rows, value_rows, masked)


def attend_forward(packed):
    queries, key_rows, value_rows, masked = split_heads(packed)
    maxima = jnp.max(masked, -1, keepdims=True)
    powers = jnp.exp(masked - maxima)
    totals = jnp.sum(powers, -1, keepdims=True)
    attn_probs = (powers / totals).astype(jnp.bfloat16)
    attended = jnp.einsum(
        "hqk,khd->qhd", attn_probs, value_rows, preferred_element_type=jnp.float32
    )
    return (attended.reshape(packed.shape[0], -1).astype(jnp.bfloat16), maxima + jnp.log(totals))


def attend_backward(member):
    packed, upstream, log_totals = member
    queries, key_rows, value_rows, masked = split_heads(packed)
    attn_probs = jnp.exp(masked - log_totals)
    probs_low = attn_probs.astype(jnp.bfloat16)
    grad_out = upstream.reshape(queries.shape)
    grad_probs = jnp.einsum(
        "qhd,khd->hqk", grad_out, value_rows, preferred_element_type=jnp.float32
    )
    grad_values = jnp.einsum(
        "hqk,qhd->khd", probs_low, grad_out, preferred_element_type=jnp.float32
    )
    grad_scores = (
        attn_probs * (grad_probs - jnp.sum(grad_probs * attn_probs, -1, keepdims=True))
    ).astype(jnp.bfloat16)
    factor = HD ** (-0.5)
    grad_queries = (
        jnp.einsum("hqk,khd->qhd", grad_scores, key_rows, preferred_element_type=jnp.float32)
        * factor
    )
    grad_keys = (
        jnp.einsum("hqk,qhd->khd", grad_scores, queries, preferred_element_type=jnp.float32)
        * factor
    )
    seq_len = packed.shape[0]
    joined = jnp.concatenate(
        [
            grad_queries.reshape(seq_len, -1),
            grad_keys.reshape(seq_len, -1),
            grad_values.reshape(seq_len, -1),
        ],
        1,
    )
    return joined.astype(jnp.bfloat16)


def expert_rows(row_block, up_mat, down_mat):
    pre_act = jnp.dot(row_block, up_mat, preferred_element_type=jnp.float32)
    hidden = gelu_exact(pre_act).astype(jnp.bfloat16)
    return lax.dot_general(hidden, down_mat, over_cols, preferred_element_type=jnp.float32)


def expert_grads(row_block, grad_block, up_mat, down_mat):
    pre_act = jnp.dot(row_block, up_mat, preferred_element_type=jnp.float32)
    hidden, gelu_back = jax.vjp(gelu_exact, pre_act)
    hidden_low = hidden.astype(jnp.bfloat16)
    down_part = lax.dot_general(
        grad_block, hidden_low, over_rows, preferred_element_type=jnp.float32
    )
    grad_hidden = jnp.dot(grad_block, down_mat, preferred_element_type=jnp.float32)
    grad_pre = gelu_back(grad_hidden)[0].astype(jnp.bfloat16)
    up_part = lax.dot_general(row_block, grad_pre, over_rows, preferred_element_type=jnp.float32)
    return (grad_pre, up_part, down_part)


def fill_slots(row_vals, target, slot_count):
    buffer = jnp.zeros((slot_count + 1, row_vals.shape[1]), row_vals.dtype).at[target].set(row_vals)
    return buffer[:slot_count]


def read_slots(buffer, target):
    padded = jnp.concatenate([buffer, jnp.zeros((1, buffer.shape[1]), buffer.dtype)], 0)
    return padded[target]


def plain_shards(
    layer_inputs_matrix,
    assignment_indices,
    admitted_counts_matrix,
    mixer_scaling1_factor,
    triple_linear_matrix,
    mixer_exit_matrix,
    specialist_scaling2_factor,
    cluster_mean_columns,
    first_linear_matrix,
    second_linear_matrix,
    incoming_gradient,
):
    gain_one, qkv_mat, out_mat, gain_two, centers = (
        lax.all_gather(mixer_scaling1_factor, ("wide", "narrow"), axis=0, tiled=True),
        lax.all_gather(triple_linear_matrix, ("wide", "narrow"), axis=0, tiled=True),
        lax.all_gather(mixer_exit_matrix, ("wide", "narrow"), axis=0, tiled=True),
        lax.all_gather(specialist_scaling2_factor, ("wide", "narrow"), axis=0, tiled=True),
        lax.all_gather(cluster_mean_columns, ("wide", "narrow"), axis=0, tiled=True),
    )
    gain_one = gain_one.astype(jnp.float32)
    gain_two = gain_two.astype(jnp.float32)
    centers = centers.astype(jnp.float32)
    token_rows = layer_inputs_matrix.astype(jnp.float32)
    tok_count, model_width = layer_inputs_matrix.shape
    seq_count = tok_count // SEQ
    normed, norm1_back = jax.vjp(layer_norm, token_rows, gain_one)
    normed_low = normed.astype(jnp.bfloat16)
    qkv_rows = jnp.dot(normed_low, qkv_mat, preferred_element_type=jnp.float32).astype(jnp.bfloat16)
    packed_seqs = qkv_rows.reshape(seq_count, SEQ, 3 * model_width)
    attended, log_totals = lax.map(attend_forward, packed_seqs)
    attended = attended.reshape(tok_count, model_width)
    residual = token_rows + jnp.dot(attended, out_mat, preferred_element_type=jnp.float32)
    normed_two, norm2_back = jax.vjp(layer_norm, residual, gain_two)
    sent_rows = normed_two.astype(jnp.bfloat16)
    dispatched_items = assignment_indices[:, 0]
    specialist_overall_sum = admitted_counts_matrix.shape[0]
    slot_count = specialist_overall_sum * SLOT
    specialist_indicator = (
        dispatched_items[:, None] == jnp.arange(specialist_overall_sum, dtype=jnp.int32)[None, :]
    ).astype(jnp.int32)
    before = jnp.cumsum(specialist_indicator, 0) - specialist_indicator
    ranked = jnp.sum(before * specialist_indicator, 1)
    position_ceilings = jnp.sum(specialist_indicator * admitted_counts_matrix[None, :], 1)
    retained_couple_filter = ranked < position_ceilings
    target = jnp.where(retained_couple_filter, dispatched_items * SLOT + ranked, slot_count)
    kept_rows = retained_couple_filter.astype(jnp.float32)
    choose = specialist_indicator.astype(jnp.float32)
    send_buf = fill_slots(sent_rows, target, slot_count).reshape(
        specialist_overall_sum, SLOT, model_width
    )
    local_rows = lax.all_to_all(send_buf, "wide", split_axis=0, concat_axis=0, tiled=True).reshape(
        slot_count, model_width
    )
    gathered = lax.all_gather(local_rows, "narrow", axis=0, tiled=True)
    expert_local = lax.psum_scatter(
        expert_rows(gathered, first_linear_matrix[0], second_linear_matrix[0]).astype(jnp.bfloat16),
        "narrow",
        scatter_dimension=0,
        tiled=True,
    )
    returned = lax.all_to_all(
        expert_local.reshape(specialist_overall_sum, SLOT, model_width),
        "wide",
        split_axis=0,
        concat_axis=0,
        tiled=True,
    )
    expert_tok = read_slots(returned.reshape(slot_count, model_width), target).astype(jnp.float32)
    center_rows = lax.dot_general(choose, centers, over_cols, precision=precise)
    logits = jnp.sum(normed_two * center_rows, 1)
    sigma = jax.nn.sigmoid(logits)
    gating = sigma * kept_rows
    mixed = (residual + gating[:, None] * expert_tok).astype(jnp.bfloat16)
    grad_y = incoming_gradient.astype(jnp.float32)
    grad_logit = jnp.sum(grad_y * expert_tok, 1) * sigma * (1.0 - sigma) * kept_rows
    grad_normed = grad_logit[:, None] * center_rows
    centroid_part = lax.dot_general(
        normed_two, choose * grad_logit[:, None], over_rows, precision=precise
    )
    grad_expert = (grad_y * gating[:, None]).astype(jnp.bfloat16)
    grad_buf = fill_slots(grad_expert, target, slot_count).reshape(
        specialist_overall_sum, SLOT, model_width
    )
    grad_local = lax.all_to_all(grad_buf, "wide", split_axis=0, concat_axis=0, tiled=True).reshape(
        slot_count, model_width
    )
    grad_gathered = lax.all_gather(grad_local, "narrow", axis=0, tiled=True)
    grad_pre, up_part, down_part = expert_grads(
        gathered, grad_gathered, first_linear_matrix[0], second_linear_matrix[0]
    )
    input_back = lax.psum_scatter(
        lax.dot_general(
            grad_pre, first_linear_matrix[0], over_cols, preferred_element_type=jnp.float32
        ).astype(jnp.bfloat16),
        "narrow",
        scatter_dimension=0,
        tiled=True,
    )
    up_grad = up_part[None]
    down_grad = down_part[None]
    back_rows = lax.all_to_all(
        input_back.reshape(specialist_overall_sum, SLOT, model_width),
        "wide",
        split_axis=0,
        concat_axis=0,
        tiled=True,
    )
    grad_normed = grad_normed + read_slots(
        back_rows.reshape(slot_count, model_width), target
    ).astype(jnp.float32)
    grad_resid_norm, gain_two_part = norm2_back(grad_normed)
    grad_resid = grad_y + grad_resid_norm
    grad_branch = grad_resid.astype(jnp.bfloat16)
    out_part = lax.dot_general(attended, grad_branch, over_rows, preferred_element_type=jnp.float32)
    grad_attended = lax.dot_general(
        grad_branch, out_mat, over_cols, preferred_element_type=jnp.float32
    ).astype(jnp.bfloat16)
    grad_packed = lax.map(
        attend_backward,
        (packed_seqs, grad_attended.reshape(seq_count, SEQ, model_width), log_totals),
    )
    grad_packed = grad_packed.reshape(tok_count, 3 * model_width)
    qkv_part = lax.dot_general(
        normed_low, grad_packed, over_rows, preferred_element_type=jnp.float32
    )
    grad_normed_one = lax.dot_general(
        grad_packed, qkv_mat, over_cols, preferred_element_type=jnp.float32
    )
    grad_token_norm, gain_one_part = norm1_back(grad_normed_one)
    tokens_grad = grad_resid + grad_token_norm
    gain_one_grad, qkv_grad, out_grad, gain_two_grad, centroid_grad = (
        lax.psum_scatter(gain_one_part, ("wide", "narrow"), scatter_dimension=0, tiled=True),
        lax.psum_scatter(qkv_part, ("wide", "narrow"), scatter_dimension=0, tiled=True),
        lax.psum_scatter(out_part, ("wide", "narrow"), scatter_dimension=0, tiled=True),
        lax.psum_scatter(gain_two_part, ("wide", "narrow"), scatter_dimension=0, tiled=True),
        lax.psum_scatter(centroid_part, ("wide", "narrow"), scatter_dimension=0, tiled=True),
    )
    return (
        mixed,
        tokens_grad,
        gain_one_grad,
        qkv_grad,
        out_grad,
        gain_two_grad,
        centroid_grad,
        up_grad,
        down_grad,
    )


def shards(mesh, v, idx, caps, g1, wq, wo, g2, centers, up, down, dy):
    T, D = v.shape
    E = caps.shape[0]
    c = Sizes(mesh, T, D, wq.shape[0], up.shape[2], E)
    if not c.fits:
        return plain_shards(v, idx, caps, g1, wq, wo, g2, centers, up, down, dy)
    w = lax.axis_index("wide")
    misc = jnp.concatenate(
        [centers, jnp.zeros((c.slab, GAIN1 - E), bf16), g1[:, None], g2[:, None]], 1
    )
    cap = jnp.broadcast_to(jnp.pad(caps, (0, c.EP - E))[:, None], (c.EP, LANES))
    res = forward_call(c, v, dy, idx.reshape(1, T), cap, wq, wo, misc, up, down)
    wall, mall, qkv, lse, att, resid, sent, meta, mrow = res[:9]
    ret, outp, ug, dg, cent = res[9:]
    cent = cent[0:1]
    outs = lax.psum_scatter(
        outp.reshape(c.NW, c.NN, SLOT, D).transpose(1, 0, 2, 3).reshape(c.NN * c.S, D),
        "narrow", scatter_dimension=0, tiled=True,
    )
    outs = lax.all_to_all(outs.reshape(c.NW, SLOT, D), "wide", split_axis=0, concat_axis=0, tiled=True)
    slot, gate = meta[0:1], meta[1:2]
    onehot = (jnp.arange(c.S, dtype=f32)[:, None] == slot).astype(bf16)
    expert_tok = mm(onehot, outs.reshape(c.S, D), TN_)
    mixed = (resid + gate.reshape(T, 1) * expert_tok).astype(bf16)
    dn2 = mm(onehot, ret.reshape(c.S, D), TN_)
    gain1, gain2 = mrow[GAIN1 : GAIN1 + 1], mrow[GAIN2 : GAIN2 + 1]
    n2, r2 = layer_stats(resid)
    gain2_part = jnp.sum(dn2 * n2, 0)
    dn = dn2 * gain2
    dres = dy.astype(f32) + r2 * (dn - jnp.mean(dn, 1, keepdims=True) - n2 * jnp.mean(dn * n2, 1, keepdims=True))
    dbr = dres.astype(bf16)
    out_part = mm(att, dbr, TN_)
    wmat = wall.reshape(c.J, D, c.CW)
    womat = jnp.concatenate([wmat[j] for j in range(c.G, c.J)], 1)
    datt = mm(dbr, womat, NT_).astype(bf16)
    dqkv = attend_back_call(c, qkv, att, datt, lse)
    n1, r1 = layer_stats(v.astype(f32))
    normed = (n1 * gain1).astype(bf16)

    def flat(t):
        return t.reshape(c.G, T, 3, PAIR).transpose(1, 2, 0, 3).reshape(T, 3 * D)

    dq = flat(dqkv)
    wqm = wmat[: c.G].reshape(c.G, D, 3, PAIR).transpose(1, 2, 0, 3).reshape(D, 3 * D)
    qkv_part = mm(normed, dq, TN_)
    dnm = mm(dq, wqm, NT_)
    gain1_part = jnp.sum(dnm * n1, 0)
    dm = dnm * gain1
    tokens_grad = dres + r1 * (dm - jnp.mean(dm, 1, keepdims=True) - n1 * jnp.mean(dm * n1, 1, keepdims=True))
    cent_part = jnp.where(jnp.arange(E)[None, :] == w, cent.reshape(D, 1), 0.0)
    axes = ("wide", "narrow")
    joined = jnp.concatenate([qkv_part, out_part], 1).astype(bf16)
    joined = lax.psum_scatter(joined, axes, scatter_dimension=0, tiled=True).astype(f32)
    small = jnp.concatenate([gain1_part[:, None], gain2_part[:, None], cent_part], 1)
    small = lax.psum_scatter(small, axes, scatter_dimension=0, tiled=True)
    return (
        mixed, tokens_grad, small[:, 0], joined[:, : 3 * D], joined[:, 3 * D :],
        small[:, 1], small[:, 2:], ug, dg,
    )


def solution(mesh):
    both = ("wide", "narrow")
    in_specs = (
        P(both, None), P(both, None), P(), P(both), P(both, None), P(both, None), P(both), P(both, None),
        P("wide", None, "narrow"), P("wide", None, "narrow"), P(both, None),
    )
    out_specs = (
        P(both, None), P(both, None), P(both), P(both, None), P(both, None), P(both), P(both, None),
        P("wide", None, "narrow"), P("wide", None, "narrow"),
    )
    return jax.shard_map(
        functools.partial(shards, mesh), mesh=mesh, in_specs=in_specs, out_specs=out_specs, check_vma=False
    )
```

```python
import functools

import jax
import jax.numpy as jnp
from jax import lax
from jax.experimental import pallas as pl
from jax.experimental.pallas import tpu as pltpu
from jax.sharding import PartitionSpec as P

HD = 64
SEQ = 1024
SLOT = 48
PAIR = 2 * HD
QB = 256
LANES = 128
GAIN1 = 126
GAIN2 = 127
NEG = -1e30
VMEM_CAP = 62 << 20

MESH = pl.DeviceIdType.MESH
NN_ = (((1,), (0,)), ((), ()))
NT_ = (((1,), (1,)), ((), ()))
TN_ = (((0,), (0,)), ((), ()))
f32 = jnp.float32
bf16 = jnp.bfloat16


def mm(a, b, dims=NN_):
    return lax.dot_general(a, b, dims, preferred_element_type=f32)


def wait_bytes(ref, sem):
    pltpu.make_async_copy(ref, ref, sem).wait()


def push(src, dst, send, recv, **where):
    pltpu.make_async_remote_copy(
        src_ref=src, dst_ref=dst, send_sem=send, recv_sem=recv,
        device_id=where, device_id_type=MESH,
    ).start()


def half_mask(rows):
    return lax.broadcasted_iota(jnp.int32, (rows, PAIR), 1) < HD


def pick(mask, h, value):
    zero = jnp.zeros_like(value)
    return jnp.where(mask, value, zero) if h == 0 else jnp.where(mask, zero, value)


def layer_stats(x):
    centered = x - jnp.mean(x, 1, keepdims=True)
    r = lax.rsqrt(jnp.mean(centered * centered, 1, keepdims=True) + 1e-05)
    return centered * r, r


def attend_rows(qkv, seq, i, put_out, put_lse):
    length = (i + 1) * QB
    rows = pl.ds(i * QB, QB)
    mask = half_mask(QB)
    causal = lax.broadcasted_iota(jnp.int32, (QB, QB), 0) <= lax.broadcasted_iota(
        jnp.int32, (QB, QB), 1
    )
    q = qkv[rows, 0:PAIR] * bf16(HD**-0.5)
    k = qkv[pl.ds(0, length), PAIR : 2 * PAIR]
    v = qkv[pl.ds(0, length), 2 * PAIR : 3 * PAIR]
    outs, sums = [], []
    for h in range(2):
        s = mm(k, pick(mask, h, q), NT_)
        last = jnp.where(causal, s[length - QB :], NEG)
        top = jnp.max(last, 0, keepdims=True)
        if i:
            top = jnp.maximum(top, jnp.max(s[: length - QB], 0, keepdims=True))
        p = jnp.exp(last - top)
        total = jnp.sum(p, 0, keepdims=True)
        p = p.astype(bf16)
        if i:
            head = jnp.exp(s[: length - QB] - top)
            total = total + jnp.sum(head, 0, keepdims=True)
            p = jnp.concatenate([head.astype(bf16), p], 0)
        put_lse(h, rows, top + jnp.log(total))
        outs.append(mm(p, v, TN_))
        sums.append(total)
    inv = jnp.transpose(1.0 / jnp.concatenate(sums + [jnp.ones((6, QB), f32)], 0))
    put_out(rows, jnp.where(mask, outs[0] * inv[:, 0:1], outs[1] * inv[:, 1:2]).astype(bf16))


def attend_rows_back(qkv, att, datt, lse, i, first, prod, dk, dv, put_dq):
    length = (i + 1) * QB
    rows = pl.ds(i * QB, QB)
    mask = half_mask(QB)
    mask_all = half_mask(length)
    causal = lax.broadcasted_iota(jnp.int32, (QB, QB), 0) <= lax.broadcasted_iota(
        jnp.int32, (QB, QB), 1
    )
    q = qkv[rows, 0:PAIR] * bf16(HD**-0.5)
    k = qkv[pl.ds(0, length), PAIR : 2 * PAIR]
    v = qkv[pl.ds(0, length), 2 * PAIR : 3 * PAIR]
    do = datt[rows, :]
    dq = None
    for h in range(2):
        qh, dh = pick(mask, h, q), pick(mask, h, do)
        s = mm(k, qh, NT_)
        row = lse[h : h + 1, rows]
        p = jnp.exp(jnp.where(causal, s[length - QB :], NEG) - row)
        if i:
            p = jnp.concatenate([jnp.exp(s[: length - QB] - row), p], 0)
        dp = mm(v, dh, NT_)
        ds = (p * (dp - prod[h : h + 1, rows])).astype(bf16)
        a, b = mm(p.astype(bf16), dh), mm(ds, qh)
        if first and h == 0:
            dv[pl.ds(0, length), :] = a
            dk[pl.ds(0, length), :] = b
        else:
            dv[pl.ds(0, length), :] += a
            dk[pl.ds(0, length), :] += b
        part = mm(ds, pick(mask_all, h, k), TN_)
        dq = part if dq is None else dq + part
    put_dq(rows, (dq * HD**-0.5).astype(bf16))


class Sizes:
    def __init__(self, mesh, tokens, d, slab, ff, experts):
        self.NW, self.NN = mesh.shape["wide"], mesh.shape["narrow"]
        self.A, self.X = self.NW // 2, self.NN // 2
        self.T, self.D, self.slab, self.F, self.E = tokens, d, slab, ff, experts
        self.CW = 3 * PAIR
        self.G = d // PAIR
        self.J = self.G + d // self.CW
        self.R = self.NN * SLOT
        self.S = experts * SLOT
        self.EP = max(8, experts)
        rows = self.NW * self.R
        self.moe = rows * (5 * d + 3 * ff) * 2 < (24 << 20)
        self.fits = (
            self.moe and slab % 8 == 0 and tokens == SEQ and self.NW % 2 == 0 and self.NN % 2 == 0
            and self.NW > 2 and self.NN > 2 and experts == self.NW
        )


def place(c):
    w, n = lax.axis_index("wide"), lax.axis_index("narrow")
    return w, n, w // 2, lax.rem(w, 2), n // 2, lax.rem(n, 2)


def greet(c, w, n):
    bar = pltpu.get_barrier_semaphore()
    x, cc = n // 2, lax.rem(n, 2)

    def wide(i, _):
        pl.semaphore_signal(bar, inc=1, device_id={"wide": lax.rem(w + i, c.NW)}, device_id_type=MESH)
        return 0

    lax.fori_loop(1, c.NW, wide, 0)
    for k in range(1, c.X):
        pl.semaphore_signal(bar, inc=1, device_id={"narrow": lax.rem(x + k, c.X) * 2 + cc}, device_id_type=MESH)
    pl.semaphore_signal(bar, inc=1, device_id={"narrow": x * 2 + 1 - cc}, device_id_type=MESH)
    return lambda: pl.semaphore_wait(bar, c.NW - 1 + c.X)


def forward_kernel(c, *refs):
    (v_hbm, dy_hbm, idx_ref, cap_ref, wq_hbm, wo_hbm, misc_hbm, up_hbm, down_hbm) = refs[:9]
    (wall, mall, qkv_out, lse_out, att_out, resid_out, sent_out, meta_out, mrow_out) = refs[9:18]
    (ret_out, outp_out, ug_out, dg_out, cent_out) = refs[18:23]
    scratch = refs[23:]
    (v, dy, nrm, normed, oh, wbuf, wmat, misc, mrow, qkv, lse, att, sent, sendx, senddy,
     lsem, in_sem, out_sem, ld_sem, s1s, s1r, s2s, s2r, s3s, s3r, s4s, s4r) = scratch[:27]
    A, X, NW, NN, T, D, CW, G, J = c.A, c.X, c.NW, c.NN, c.T, c.D, c.CW, c.G, c.J
    w, n, a, b, x, cc = place(c)
    own = (a, b, x, cc)

    def cols(j):
        dst = wall.at[(j, *own)]
        if j < G:
            return [(wq_hbm.at[:, pl.ds(p * D + j * PAIR, PAIR)], dst.at[:, pl.ds(p * PAIR, PAIR)]) for p in range(3)]
        return [(wo_hbm.at[:, pl.ds((j - G) * CW, CW)], dst)]

    pltpu.make_async_copy(misc_hbm, mall.at[own], lsem.at[J]).start()
    for j in range(J):
        for s, d in cols(j):
            pltpu.make_async_copy(s, d, lsem.at[j]).start()
    loads = [(dy_hbm, dy), (v_hbm, v)]
    if c.moe:
        (up, down, xin, dyin, hid, dpre, dexp, outp, part, lc, lx, stage, cent,
         ds_, dr, xs_, xr, cs_, cr, fs, fr, gs, gr, ks, kr, rs_, rr, ws_, wr) = scratch[27:]
        loads += [(up_hbm.at[0], up), (down_hbm.at[0], down)]
    for i, (s, d) in enumerate(loads):
        pltpu.make_async_copy(s, d, in_sem.at[i]).start()

    def load_wait(i):
        wait_bytes(loads[i][1], in_sem.at[i])

    met = greet(c, w, n)

    one = lax.broadcasted_iota(jnp.int32, (c.EP, T), 0) == idx_ref[...]
    hot = one.astype(f32)
    lane = lax.broadcasted_iota(jnp.int32, (c.EP, T), 1)
    count = hot
    shift = 1
    while shift < T:
        count = count + jnp.where(lane >= shift, pltpu.roll(count, shift, 1), 0.0)
        shift *= 2
    rank = jnp.sum((count - hot) * hot, 0, keepdims=True)
    ceiling = jnp.sum(hot * cap_ref[:, 0:1].astype(f32), 0, keepdims=True)
    kept = rank < ceiling
    slot = jnp.where(kept, idx_ref[...].astype(f32) * SLOT + rank, -1.0)
    meta_out_rows = [slot]

    met()

    def buf(j):
        return mall if j is J else wall.at[j]

    def s1(j):
        wait_bytes(buf(j).at[own], lsem.at[j])
        for k in range(1, A):
            push(buf(j).at[own], buf(j).at[own], s1s.at[j], s1r.at[j], wide=lax.rem(a + k, A) * 2 + b)

    def s2(j):
        wait_bytes(buf(j).at[pl.ds(0, A - 1), b, x, cc], s1r.at[j])
        for k in range(1, X):
            part_ = buf(j).at[:, b, x, cc]
            push(part_, part_, s2s.at[j], s2r.at[j], narrow=lax.rem(x + k, X) * 2 + cc)

    def s3(j):
        wait_bytes(buf(j).at[:, b, pl.ds(0, X - 1), cc], s2r.at[j])
        part_ = buf(j).at[:, b, :, cc]
        push(part_, part_, s3s.at[j], s3r.at[j], wide=a * 2 + 1 - b)

    def s4(j):
        wait_bytes(buf(j).at[:, b, :, cc], s3r.at[j])
        part_ = buf(j).at[:, :, :, cc]
        push(part_, part_, s4s.at[j], s4r.at[j], narrow=x * 2 + 1 - cc)

    def ld(j):
        wait_bytes(buf(j).at[:, :, :, cc], s4r.at[j])
        if j is J:
            pltpu.make_async_copy(mall, misc, ld_sem.at[J]).start()
        else:
            pltpu.make_async_copy(wall.at[j], wbuf.at[lax.rem(j, 2)], ld_sem.at[j]).start()

    def loaded(j, at):
        slot_ = lax.rem(j, 2)
        wait_bytes(wbuf.at[slot_], ld_sem.at[j])
        wmat[at] = wbuf[slot_].reshape(D, CW)

    s1(J)
    for j in range(J):
        s1(j)

    ohv = (lax.broadcasted_iota(jnp.int32, (c.S, T), 0).astype(f32) == slot).astype(bf16)
    oh[...] = ohv
    load_wait(0)
    senddy[...] = mm(oh[...], dy[...]).astype(bf16)
    s2(J)
    s2(0)

    if c.moe:
        for k in range(1, NW):
            to = lax.rem(w + k, NW)
            push(senddy.at[pl.ds(to * SLOT, SLOT)], dyin.at[w, x, cc], ds_, dr, wide=to)
        dyin[w, x, cc] = senddy[pl.ds(w * SLOT, SLOT), :]
    else:
        pltpu.make_async_copy(senddy, senddy_out, out_sem.at[7]).start()
    s3(J)
    s3(0)
    s2(1)

    load_wait(1)

    def norm1(i, _):
        rows = pl.ds(i * 128, 128)
        nrm[rows, :] = layer_stats(v[rows, :].astype(f32))[0]
        return 0

    lax.fori_loop(0, T // 128, norm1, 0)
    s4(J)
    s4(0)
    s3(1)
    s2(2)
    ld(J)
    wait_bytes(misc, ld_sem.at[J])
    mrow[...] = jnp.transpose(misc[...].reshape(D, LANES).astype(f32))
    gain1 = mrow[GAIN1 : GAIN1 + 1, :]
    gain2 = mrow[GAIN2 : GAIN2 + 1, :]
    pltpu.make_async_copy(mrow, mrow_out, out_sem.at[0]).start()

    def norm1b(i, _):
        rows = pl.ds(i * 128, 128)
        normed[rows, :] = (nrm[rows, :] * gain1).astype(bf16)
        return 0

    lax.fori_loop(0, T // 128, norm1b, 0)
    ld(0)

    def pair(g, _):
        loaded(g, 0)

        def project(i, _):
            rows = pl.ds(i * QB, QB)
            qkv[g, rows, :] = mm(normed[rows, :], wmat[0]).astype(bf16)
            return 0

        lax.fori_loop(0, T // QB, project, 0)
        pltpu.make_async_copy(qkv.at[g], qkv_out.at[g], out_sem.at[1]).start()
        s3(g + 2)

        @pl.when(g + 3 < J)
        def _():
            s2(g + 3)

        def put_out(rows, val):
            att[rows, pl.ds(pl.multiple_of(g * PAIR, PAIR), PAIR)] = val

        def put_lse(h, rows, val):
            lse[g, h : h + 1, rows] = val

        for i in range(T // QB):
            if i == T // QB - 1:
                s4(g + 1)
                if c.moe:
                    @pl.when(g == 4)
                    def _():
                        wait_bytes(dyin.at[pl.ds(0, NW - 1), x, cc], dr)
                        for k in range(1, X):
                            push(dyin.at[:, x, cc], dyin.at[:, x, cc], xs_, xr, narrow=lax.rem(x + k, X) * 2 + cc)
            attend_rows(qkv.at[g], T, i, put_out, put_lse)
        ld(g + 1)
        return 0

    lax.fori_loop(0, G, pair, 0)
    pltpu.make_async_copy(lse, lse_out, out_sem.at[2]).start()
    pltpu.make_async_copy(att, att_out, out_sem.at[3]).start()
    for j in range(G + 1, J):
        s4(j)
        ld(j)
    if c.moe:
        wait_bytes(dyin.at[:, pl.ds(0, X - 1), cc], xr)
        push(dyin.at[:, :, cc], dyin.at[:, :, cc], cs_, cr, narrow=x * 2 + 1 - cc)
    for j in range(G, J):
        loaded(j, 1 + j - G)

    def tail(i, _):
        rows = pl.ds(i * QB, QB)
        left = att[rows, :]
        prod = jnp.concatenate([mm(left, wmat[1 + j - G]) for j in range(G, J)], 1)
        resid = v[rows, :].astype(f32) + prod
        nrm[rows, :] = resid
        sent[rows, :] = (layer_stats(resid)[0] * gain2).astype(bf16)
        return 0

    lax.fori_loop(0, T // QB, tail, 0)
    pltpu.make_async_copy(nrm, resid_out, out_sem.at[4]).start()
    sendx[...] = mm(oh[...], sent[...]).astype(bf16)
    if c.moe:
        for k in range(1, NW):
            to = lax.rem(w + k, NW)
            push(sendx.at[pl.ds(to * SLOT, SLOT)], xin.at[w, x, cc], fs.at[k], fr.at[k], wide=to)
        xin[w, x, cc] = sendx[pl.ds(w * SLOT, SLOT), :]
    else:
        pltpu.make_async_copy(sendx, sendx_out, out_sem.at[8]).start()
    pltpu.make_async_copy(sent, sent_out, out_sem.at[5]).start()
    logits = mm(mrow[0 : c.EP, :].astype(bf16), sent[...], NT_)
    logit = jnp.sum(logits * hot, 0, keepdims=True)
    gate = jax.nn.sigmoid(logit) * kept.astype(f32)
    meta_out[...] = jnp.concatenate([slot, gate, jnp.zeros((6, T), f32)], 0)

    if c.moe:
        load_wait(2)
        load_wait(3)
        wait_bytes(dyin.at[:, :, cc], cr)
        cent[...] = jnp.zeros_like(cent)
        crow = mrow[pl.ds(w, 1), :]

        def source(i):
            return lax.rem(w - i + NW, NW)

        def fwd_x(i):
            src = source(i)

            @pl.when(i > 0)
            def _():
                wait_bytes(xin.at[src, x, cc], fr.at[i])

            for k in range(1, X):
                push(xin.at[src, x, cc], xin.at[src, x, cc], gs.at[i], gr.at[i], narrow=lax.rem(x + k, X) * 2 + cc)

        def fwd_c(i):
            src = source(i)
            wait_bytes(xin.at[src, pl.ds(0, X - 1), cc], gr.at[i])
            push(xin.at[src, :, cc], xin.at[src, :, cc], ks.at[i], kr.at[i], narrow=x * 2 + 1 - cc)

        def expert(i):
            src = source(i)
            wait_bytes(xin.at[src, :, cc], kr.at[i])
            xb = xin[src].reshape(c.R, D)
            db = dyin[src].reshape(c.R, D)
            xf, df = xb.astype(f32), db.astype(f32)
            s = jax.nn.sigmoid(jnp.sum(xf * crow, 1, keepdims=True))
            de = (df * s).astype(bf16)
            pre = mm(xb, up[...])
            cdf = 0.5 * (1.0 + lax.erf(pre * 0.7071067811865476))
            hb = (pre * cdf).astype(bf16)
            slope = cdf + pre * (jnp.exp(-0.5 * pre * pre) * 0.3989422804014327)
            dpb = (mm(de, down[...]) * slope).astype(bf16)
            out = mm(hb, down[...], NT_)
            dl = jnp.sum(df * out, 1, keepdims=True) * (s * (1.0 - s))
            dn = mm(dpb, up[...], NT_) + dl * crow
            part[src] = dn.astype(bf16).reshape(X, 2, SLOT, D)
            outp[src] = out.astype(bf16).reshape(X, 2, SLOT, D)
            cent[...] += jnp.broadcast_to(jnp.sum(dl * xf, 0, keepdims=True), cent.shape)
            rows = pl.ds(pl.multiple_of(src * c.R, SLOT), c.R)
            hid[rows, :] = hb
            dpre[rows, :] = dpb
            dexp[rows, :] = de

        def ret_c(i):
            src = source(i)
            push(part.at[src, :, 1 - cc], lc.at[src], rs_.at[0, i], rr.at[0, i], narrow=x * 2 + 1 - cc)

        def ret_x(i):
            src = source(i)
            wait_bytes(lc.at[src], rr.at[0, i])
            part[src, :, cc] = (part[src, :, cc].astype(f32) + lc[src].astype(f32)).astype(bf16)
            for k in range(1, X):
                x2 = lax.rem(x + k, X)
                push(part.at[src, x2, cc], lx.at[src, x], rs_.at[1, i], rr.at[1, i], narrow=x2 * 2 + cc)

        def ret_w(i):
            src = source(i)
            wait_bytes(lx.at[src, pl.ds(0, X - 1)], rr.at[1, i])
            total = part[src, x, cc].astype(f32)
            for k in range(1, X):
                total = total + lx[src, lax.rem(x + k, X)].astype(f32)
            part[src, x, cc] = total.astype(bf16)

            @pl.when(i > 0)
            def _():
                push(part.at[src, x, cc], ret_out.at[w], ws_.at[i], wr.at[i], wide=src)

            @pl.when(i == 0)
            def _():
                pltpu.make_async_copy(part.at[src, x, cc], ret_out.at[w], ws_.at[0]).start()

        fwd_x(0)
        fwd_c(0)
        fwd_x(1)

        def block(i, _):
            @pl.when(i + 1 < NW)
            def _():
                fwd_c(i + 1)

            @pl.when(i + 2 < NW)
            def _():
                fwd_x(i + 2)

            expert(i)
            ret_c(i)

            @pl.when(i >= 1)
            def _():
                ret_x(i - 1)

            @pl.when(i >= 2)
            def _():
                ret_w(i - 2)

            return 0

        lax.fori_loop(0, NW, block, 0)
        ret_x(NW - 1)
        ret_w(NW - 2)
        pltpu.make_async_copy(outp, outp_out, out_sem.at[6]).start()
        cent_out[...] = cent[...]

        def grads(lhs, rhs, out, base, flush):
            def one_block(i, _):
                at = pl.ds(pl.multiple_of(i * QB, QB), QB)
                lhs_block = lhs(at)
                stage[base + i] = mm(lhs_block, rhs[...], TN_)
                pltpu.make_async_copy(stage.at[base + i], out.at[0, at], in_sem.at[4 + base + i]).start()
                return 0

            lax.fori_loop(0, D // QB, one_block, 0)

        grads(lambda at: dexp[:, at], hid, dg_out, 0, None)
        ret_w(NW - 1)
        grads(lambda at: xin[:, :, :, :, at].reshape(NW * c.R, QB), dpre, ug_out, D // QB, None)

    for q, (s, ref) in enumerate([(mrow, None), (qkv, None), (lse, None), (att, None), (nrm, None), (sent, None)]):
        wait_bytes(s, out_sem.at[q])
    for j in [J] + list(range(J)):
        wait_bytes(buf(j).at[pl.ds(0, A - 1), b, x, cc], s1s.at[j])
        wait_bytes(buf(j).at[:, b, pl.ds(0, X - 1), cc], s2s.at[j])
        wait_bytes(buf(j).at[:, b, :, cc], s3s.at[j])
        wait_bytes(buf(j).at[:, :, :, cc], s4s.at[j])
    if c.moe:
        wait_bytes(dyin.at[pl.ds(0, NW - 1), x, cc], ds_)
        wait_bytes(dyin.at[:, pl.ds(0, X - 1), cc], xs_)
        wait_bytes(dyin.at[:, :, cc], cs_)
        wait_bytes(outp, out_sem.at[6])

        def drain(i, _):
            src = source(i)
            wait_bytes(xin.at[src, pl.ds(0, X - 1), cc], gs.at[i])
            wait_bytes(xin.at[src, :, cc], ks.at[i])
            wait_bytes(lc.at[src], rs_.at[0, i])
            wait_bytes(lx.at[src, pl.ds(0, X - 1)], rs_.at[1, i])
            wait_bytes(xin.at[src, x, cc], ws_.at[i])

            @pl.when(i > 0)
            def _():
                wait_bytes(xin.at[src, x, cc], fs.at[i])
                wait_bytes(xin.at[src, x, cc], wr.at[i])

            return 0

        lax.fori_loop(0, NW, drain, 0)
        for i in range(2 * (D // QB)):
            wait_bytes(stage.at[i], in_sem.at[4 + i])
    else:
        wait_bytes(senddy, out_sem.at[7])
        wait_bytes(sendx, out_sem.at[8])


def forward_call(c, v, dy, idx, cap, wq, wo, misc, up, down):
    T, D, CW, G, J, NW, NN, A, X = c.T, c.D, c.CW, c.G, c.J, c.NW, c.NN, c.A, c.X
    any_ = pl.BlockSpec(memory_space=pl.ANY)
    vm = pl.BlockSpec(memory_space=pltpu.VMEM)
    sds = jax.ShapeDtypeStruct
    F = c.F
    outs = [
        (sds((J, A, 2, X, 2, c.slab, CW), bf16), any_),
        (sds((A, 2, X, 2, c.slab, LANES), bf16), any_),
        (sds((G, T, CW), bf16), any_),
        (sds((G, 8, T), f32), any_),
        (sds((T, D), bf16), any_),
        (sds((T, D), f32), any_),
        (sds((T, D), bf16), any_),
        (sds((8, T), f32), vm),
        (sds((LANES, D), f32), any_),
    ]
    dma, V = pltpu.SemaphoreType.DMA, pltpu.VMEM
    scratch = [
        V((T, D), bf16), V((T, D), bf16), V((T, D), f32), V((T, D), bf16), V((c.S, T), bf16),
        V((2, A, 2, X, 2, c.slab, CW), bf16), V((1 + J - G, D, CW), bf16),
        V((A, 2, X, 2, c.slab, LANES), bf16), V((LANES, D), f32), V((G, T, CW), bf16), V((G, 8, T), f32),
        V((T, D), bf16), V((T, D), bf16), V((c.S, D), bf16), V((c.S, D), bf16),
        dma((J + 1,)), dma((4 + 2 * (D // QB),)), dma((9,)), dma((J + 1,)),
    ] + [dma((J + 1,))] * 8
    if c.moe:
        outs += [
            (sds((NW, SLOT, D), bf16), any_),
            (sds((NW, X, 2, SLOT, D), bf16), any_),
            (sds((1, D, F), f32), any_),
            (sds((1, D, F), f32), any_),
            (sds((8, D), f32), vm),
        ]
        rows = NW * c.R
        scratch += [
            V((D, F), bf16), V((D, F), bf16), V((NW, X, 2, SLOT, D), bf16), V((NW, X, 2, SLOT, D), bf16),
            V((rows, F), bf16), V((rows, F), bf16), V((rows, D), bf16), V((NW, X, 2, SLOT, D), bf16),
            V((NW, X, 2, SLOT, D), bf16), V((NW, X, SLOT, D), bf16), V((NW, X, SLOT, D), bf16),
            V((2 * (D // QB), QB, F), f32), V((8, D), f32),
            dma(()), dma(()), dma(()), dma(()), dma(()), dma(()),
            dma((NW,)), dma((NW,)), dma((NW,)), dma((NW,)), dma((NW,)), dma((NW,)),
            dma((2, NW)), dma((2, NW)), dma((NW,)), dma((NW,)),
        ]
    else:
        outs += [(sds((c.S, D), bf16), any_), (sds((c.S, D), bf16), any_)]
    return pl.pallas_call(
        functools.partial(forward_kernel, c),
        out_shape=tuple(o[0] for o in outs),
        in_specs=[any_, any_, vm, vm, any_, any_, any_, any_, any_],
        out_specs=tuple(o[1] for o in outs),
        scratch_shapes=scratch,
        compiler_params=pltpu.CompilerParams(
            collective_id=0, has_side_effects=True, vmem_limit_bytes=VMEM_CAP
        ),
        name="forward",
    )(v, dy, idx, cap, wq, wo, misc, up, down)


def backward_kernel(c, *refs):
    (v_hbm, dy_hbm, qkv_hbm, lse_hbm, att_hbm, resid_hbm, wall, ret_hbm, outp_hbm, mrow, meta, cent) = refs[:12]
    (mixed_out, tok_out, qg_out, og_out, small_out) = refs[12:17]
    (v, dy, qkv, lse, att, resid, wbuf, wmat, ret, oh, normt, dbr, datt, dnm, dqkv, dk, dv, prod, rowbuf,
     part, lc, lx, got, mixed,
     gb, la, lb, lxx, lz, sgb, sla, slb, slx, slz,
     in_sem, q_sem, out_sem, os_, orv, ows, owr, rs_, rr, tokacc) = refs[17:]
    A, X, NW, NN, T, D, CW, G, J = c.A, c.X, c.NW, c.NN, c.T, c.D, c.CW, c.G, c.J
    H = J - G
    w, n, a, b, x, cc = place(c)
    blocks = T // QB

    loads = [
        (ret_hbm, ret), (resid_hbm, resid), (dy_hbm, dy), (att_hbm, att), (v_hbm, v), (lse_hbm, lse),
    ]
    for i, (s, d) in enumerate(loads):
        pltpu.make_async_copy(s, d, in_sem.at[i]).start()
    own_part = pltpu.make_async_copy(outp_hbm.at[:, :, cc], part, in_sem.at[6])
    own_part.start()

    def load_wait(i):
        wait_bytes(loads[i][1], in_sem.at[i])

    def fetch_w(j, slot_):
        pltpu.make_async_copy(wall.at[j], wbuf.at[slot_], q_sem.at[0, slot_]).start()

    def take_w(slot_, at):
        wait_bytes(wbuf.at[slot_], q_sem.at[0, slot_])
        wmat[at] = wbuf[slot_].reshape(D, CW)

    def fetch_qkv(g, slot_):
        pltpu.make_async_copy(qkv_hbm.at[g], qkv.at[slot_], q_sem.at[1, slot_]).start()

    for h in range(H):
        fetch_w(G + h, h)
    fetch_qkv(0, 0)
    met = greet(c, w, n)

    slot, gate = meta[0:1, :], meta[1:2, :]
    hits = lax.broadcasted_iota(jnp.int32, (c.S, T), 0).astype(f32) == slot
    oh[...] = hits.astype(bf16)
    gain1, gain2 = mrow[GAIN1 : GAIN1 + 1, :], mrow[GAIN2 : GAIN2 + 1, :]
    load_wait(0)
    dnm[...] = mm(oh[...], ret[...].reshape(c.S, D), TN_)
    oh[...] = jnp.where(hits, gate, 0.0).astype(bf16)
    met()
    push(outp_hbm.at[:, :, 1 - cc], lc, os_.at[0], orv.at[0], narrow=x * 2 + 1 - cc)
    load_wait(1)
    load_wait(2)
    rowbuf[...] = jnp.zeros_like(rowbuf)
    rowbuf[pl.ds(w, 1), :] = cent[0:1, :]

    def norm2_back(i, acc):
        rows = pl.ds(i * QB, QB)
        n2, r2 = layer_stats(resid[rows, :])
        dn2 = dnm[rows, :]
        dn = dn2 * gain2
        step = r2 * (dn - jnp.mean(dn, 1, keepdims=True) - n2 * jnp.mean(dn * n2, 1, keepdims=True))
        dres = dy[rows, :].astype(f32) + step
        dnm[rows, :] = dres
        dbr[rows, :] = dres.astype(bf16)
        return acc + jnp.sum(dn2 * n2, 0, keepdims=True)

    rowbuf[GAIN2 : GAIN2 + 1, :] = lax.fori_loop(0, blocks, norm2_back, jnp.zeros((1, D), f32))
    load_wait(3)

    big = (gb, la, lb, lxx, lz, 0)
    tiny = (sgb, sla, slb, slx, slz, J)

    def add(p, q):
        return (p.astype(f32) + q.astype(f32)).astype(bf16)

    def ra(t, j):
        push(t[0].at[j, :, :, :, 1 - cc], t[1].at[j], rs_.at[0, t[5] + j], rr.at[0, t[5] + j], narrow=x * 2 + 1 - cc)

    def rb(t, j):
        wait_bytes(t[1].at[j], rr.at[0, t[5] + j])
        t[0][j, :, :, :, cc] = add(t[0][j, :, :, :, cc], t[1][j])
        push(t[0].at[j, :, 1 - b, :, cc], t[2].at[j], rs_.at[1, t[5] + j], rr.at[1, t[5] + j], wide=a * 2 + 1 - b)

    def rc(t, j):
        wait_bytes(t[2].at[j], rr.at[1, t[5] + j])
        t[0][j, :, b, :, cc] = add(t[0][j, :, b, :, cc], t[2][j])
        for k in range(1, X):
            x2 = lax.rem(x + k, X)
            push(t[0].at[j, :, b, x2, cc], t[3].at[j, x], rs_.at[2, t[5] + j], rr.at[2, t[5] + j], narrow=x2 * 2 + cc)

    def rd(t, j):
        wait_bytes(t[3].at[j, pl.ds(0, X - 1)], rr.at[2, t[5] + j])
        total = t[0][j, :, b, x, cc].astype(f32)
        for k in range(1, X):
            total = total + t[3][j, lax.rem(x + k, X)].astype(f32)
        t[0][j, :, b, x, cc] = total.astype(bf16)
        for k in range(1, A):
            a2 = lax.rem(a + k, A)
            push(t[0].at[j, a2, b, x, cc], t[4].at[j, a], rs_.at[3, t[5] + j], rr.at[3, t[5] + j], wide=a2 * 2 + b)

    def rf(t, j):
        wait_bytes(t[4].at[j, pl.ds(0, A - 1)], rr.at[3, t[5] + j])
        total = t[0][j, a, b, x, cc].astype(f32)
        for k in range(1, A):
            total = total + t[4][j, lax.rem(a + k, A)].astype(f32)
        return total

    def rf_w(j):
        og_out[:, j * CW : (j + 1) * CW] = rf(big, j)

    def rf_q(g):
        total = rf(big, H + g)
        for p in range(3):
            qg_out[:, pl.ds(pl.multiple_of(p * D + g * PAIR, PAIR), PAIR)] = total[:, p * PAIR : (p + 1) * PAIR]

    for h in range(H):
        gb[h] = mm(att[...], dbr[:, h * CW : (h + 1) * CW], TN_).astype(bf16).reshape(A, 2, X, 2, c.slab, CW)
        ra(big, h)

    for h in range(H):
        take_w(h, h)

    def out_back(i, _):
        rows = pl.ds(i * QB, QB)
        total = mm(dbr[rows, 0:CW], wmat[0], NT_)
        for h in range(1, H):
            total = total + mm(dbr[rows, h * CW : (h + 1) * CW], wmat[h], NT_)
        datt[rows, :] = total.astype(bf16)
        return 0

    lax.fori_loop(0, blocks, out_back, 0)
    fetch_w(0, 0)
    load_wait(4)

    def norm1(i, _):
        rows = pl.ds(i * QB, QB)
        val = (layer_stats(v[rows, :].astype(f32))[0] * gain1).astype(bf16)
        normt[:, pl.ds(pl.multiple_of(i * QB, QB), QB)] = jnp.transpose(val)
        return 0

    lax.fori_loop(0, blocks, norm1, 0)
    for h in range(H):
        rb(big, h)
    load_wait(5)
    own_part.wait()

    def o_x(i):
        for k in range(1, X):
            x2 = lax.rem(x + k, X)
            push(part.at[i, x2], lx.at[i, x], os_.at[1 + i], orv.at[1 + i], narrow=x2 * 2 + cc)

    def o_w(i):
        wait_bytes(lx.at[i, pl.ds(0, X - 1)], orv.at[1 + i])
        total = part[i, x].astype(f32)
        for k in range(1, X):
            total = total + lx[i, lax.rem(x + k, X)].astype(f32)
        part[i, x] = total.astype(bf16)

        @pl.when(i != w)
        def _():
            push(part.at[i, x], got.at[w], ows.at[i], owr.at[lax.rem(w - i + NW, NW)], wide=i)

        @pl.when(i == w)
        def _():
            got[w] = part[w, x]

    wait_bytes(lc, orv.at[0])

    def merge(i, _):
        part[i] = add(part[i], lc[i])
        return 0

    lax.fori_loop(0, NW, merge, 0)
    per = -(-NW // 4)

    def spread(fn, step):
        for k in range(per):
            i = lax.rem(w + step * per + k, NW)

            @pl.when(step * per + k < NW)
            def _():
                fn(i)

    def pair(g, _):
        s_ = lax.rem(g, 2)

        @pl.when(g + 1 < G)
        def _():
            fetch_w(g + 1, 1 - s_)
            fetch_qkv(g + 1, 1 - s_)

        wait_bytes(qkv.at[s_], q_sem.at[1, s_])
        lanes = pl.ds(pl.multiple_of(g * PAIR, PAIR), PAIR)
        att_g, datt_g = att.at[:, lanes], datt.at[:, lanes]
        full = jnp.transpose(datt_g[...].astype(f32) * att_g[...].astype(f32))
        prod[0:1, :] = jnp.sum(full[0:HD], 0, keepdims=True)
        prod[1:2, :] = jnp.sum(full[HD:], 0, keepdims=True)

        def put_dq(rows, val):
            dqkv[rows, 0:PAIR] = val

        for i in reversed(range(blocks)):
            attend_rows_back(qkv.at[s_], att_g, datt_g, lse.at[g], i, i == blocks - 1, prod, dk, dv, put_dq)
            if i == blocks - 1:
                @pl.when(g >= 1)
                def _():
                    rb(big, g + H - 1)

                rc(big, g + H - 2)

                @pl.when(g + H >= 3)
                def _():
                    rd(big, g + H - 3)

                @pl.when(g < 4)
                def _():
                    spread(o_x, g)

                @pl.when(g >= 2)
                def _():
                    spread(o_w, g - 2)

        dqkv[:, PAIR : 2 * PAIR] = dk[...].astype(bf16)
        dqkv[:, 2 * PAIR :] = dv[...].astype(bf16)
        gb[H + g] = mm(normt[...], dqkv[...]).astype(bf16).reshape(A, 2, X, 2, c.slab, CW)
        ra(big, H + g)
        take_w(s_, 0)

        def back(i, _):
            rows = pl.ds(i * QB, QB)
            val = mm(dqkv[rows, :], wmat[0], NT_)

            @pl.when(g == 0)
            def _():
                tokacc[rows, :] = val

            @pl.when(g > 0)
            def _():
                tokacc[rows, :] += val

            return 0

        lax.fori_loop(0, blocks, back, 0)
        return 0

    lax.fori_loop(0, G, pair, 0)

    rb(big, J - 1)
    def norm1_back(i, acc):
        rows = pl.ds(i * QB, QB)
        n1, r1 = layer_stats(v[rows, :].astype(f32))
        dm0 = tokacc[rows, :]
        dm = dm0 * gain1
        step = r1 * (dm - jnp.mean(dm, 1, keepdims=True) - n1 * jnp.mean(dm * n1, 1, keepdims=True))
        dnm[rows, :] = dnm[rows, :] + step
        return acc + jnp.sum(dm0 * n1, 0, keepdims=True)

    rowbuf[GAIN1 : GAIN1 + 1, :] = lax.fori_loop(0, blocks, norm1_back, jnp.zeros((1, D), f32))
    tok_copy = pltpu.make_async_copy(dnm, tok_out, out_sem.at[0])
    tok_copy.start()
    sgb[0] = jnp.transpose(rowbuf[...]).astype(bf16).reshape(A, 2, X, 2, c.slab, LANES)
    ra(tiny, 0)
    rc(big, J - 2)
    rd(big, J - 3)
    rb(tiny, 0)
    rc(big, J - 1)

    def o_wait(k, _):
        wait_bytes(got.at[0], owr.at[k])
        return 0

    lax.fori_loop(1, NW, o_wait, 0)
    rd(big, J - 2)
    rc(tiny, 0)

    def mix(i, _):
        cols = pl.ds(pl.multiple_of(i * QB, QB), QB)
        rows = pl.ds(i * QB, QB)
        mixed[rows, :] = (resid[rows, :] + mm(oh[:, cols], got[...].reshape(c.S, D), TN_)).astype(bf16)
        return 0

    lax.fori_loop(0, blocks, mix, 0)
    mix_copy = pltpu.make_async_copy(mixed, mixed_out, out_sem.at[1])
    mix_copy.start()
    rd(big, J - 1)
    rd(tiny, 0)
    for h in range(H):
        rf_w(h)

    def fin(g, _):
        rf_q(g)
        return 0

    lax.fori_loop(0, G, fin, 0)
    small_out[...] = rf(tiny, 0)

    wait_bytes(lc, os_.at[0])

    def drain(i, _):
        wait_bytes(lx.at[i, pl.ds(0, X - 1)], os_.at[1 + i])

        @pl.when(i != w)
        def _():
            wait_bytes(got.at[0], ows.at[i])

        return 0

    lax.fori_loop(0, NW, drain, 0)

    def drain_sums(t, j):
        for q in range(2):
            wait_bytes(t[1 + q].at[j], rs_.at[q, t[5] + j])
        wait_bytes(t[3].at[j, pl.ds(0, X - 1)], rs_.at[2, t[5] + j])
        wait_bytes(t[4].at[j, pl.ds(0, A - 1)], rs_.at[3, t[5] + j])

    def drain_big(j, _):
        drain_sums(big, j)
        return 0

    lax.fori_loop(0, J, drain_big, 0)
    drain_sums(tiny, 0)
    tok_copy.wait()
    mix_copy.wait()


def backward_call(c, v, dy, qkv, lse, att, resid, wall, ret, outp, mrow, meta, cent):
    T, D, CW, G, J, NW, NN, A, X, L = c.T, c.D, c.CW, c.G, c.J, c.NW, c.NN, c.A, c.X, c.slab
    any_ = pl.BlockSpec(memory_space=pl.ANY)
    vm = pl.BlockSpec(memory_space=pltpu.VMEM)
    sds = jax.ShapeDtypeStruct
    dma, V = pltpu.SemaphoreType.DMA, pltpu.VMEM

    def sums(k, width):
        return [
            V((k, A, 2, X, 2, L, width), bf16), V((k, A, 2, X, L, width), bf16), V((k, A, X, L, width), bf16),
            V((k, X, A, L, width), bf16), V((k, A, L, width), bf16),
        ]

    scratch = [
        V((T, D), bf16), V((T, D), bf16), V((2, T, CW), bf16), V((G, 8, T), f32), V((T, D), bf16), V((T, D), f32),
        V((2, A, 2, X, 2, L, CW), bf16), V((J - G, D, CW), bf16), V((NW, SLOT, D), bf16), V((c.S, T), bf16),
        V((D, T), bf16), V((T, D), bf16), V((T, D), bf16), V((T, D), f32), V((T, CW), bf16),
        V((T, PAIR), f32), V((T, PAIR), f32), V((8, T), f32), V((LANES, D), f32),
        V((NW, X, SLOT, D), bf16), V((NW, X, SLOT, D), bf16), V((NW, X, SLOT, D), bf16), V((NW, SLOT, D), bf16),
        V((T, D), bf16),
    ] + sums(J, CW) + sums(1, LANES) + [
        dma((7,)), dma((2, 2)), dma((2,)), dma((NW + 1,)), dma((NW + 1,)), dma((NW,)), dma((NW,)),
        dma((4, J + 1)), dma((4, J + 1)),
        V((T, D), f32),
    ]
    return pl.pallas_call(
        functools.partial(backward_kernel, c),
        out_shape=(
            sds((T, D), bf16), sds((T, D), f32), sds((L, 3 * D), f32), sds((L, D), f32), sds((L, LANES), f32),
        ),
        in_specs=[any_] * 9 + [vm] * 3,
        out_specs=(any_, any_, vm, vm, vm),
        scratch_shapes=scratch,
        compiler_params=pltpu.CompilerParams(
            collective_id=1, has_side_effects=True, vmem_limit_bytes=VMEM_CAP
        ),
        name="backward",
    )(v, dy, qkv, lse, att, resid, wall, ret, outp, mrow, meta, cent)


precise = lax.Precision.HIGHEST
over_rows = (((0,), (0,)), ((), ()))
over_cols = (((1,), (1,)), ((), ()))


def layer_norm(tensor, gain_vec):
    centered = tensor - jnp.mean(tensor, -1, keepdims=True)
    spread = jnp.mean(centered * centered, -1, keepdims=True)
    return centered * lax.rsqrt(spread + 1e-05) * gain_vec


def gelu_exact(tensor):
    return jax.nn.gelu(tensor, approximate=False)


def split_heads(packed):
    seq_len = packed.shape[0]
    model_width = packed.shape[1] // 3
    head_count = model_width // HD
    queries = packed[:, :model_width].reshape(seq_len, head_count, HD)
    key_rows = packed[:, model_width : 2 * model_width].reshape(seq_len, head_count, HD)
    value_rows = packed[:, 2 * model_width :].reshape(seq_len, head_count, HD)
    raw_scores = jnp.einsum(
        "qhd,khd->hqk", queries, key_rows, preferred_element_type=jnp.float32
    ) * HD ** (-0.5)
    places = jnp.arange(seq_len)
    causal = places[:, None] >= places[None, :]
    masked = jnp.where(causal[None], raw_scores, -1e30)
    return (queries, key_rows, value_rows, masked)


def attend_forward(packed):
    queries, key_rows, value_rows, masked = split_heads(packed)
    maxima = jnp.max(masked, -1, keepdims=True)
    powers = jnp.exp(masked - maxima)
    totals = jnp.sum(powers, -1, keepdims=True)
    attn_probs = (powers / totals).astype(jnp.bfloat16)
    attended = jnp.einsum(
        "hqk,khd->qhd", attn_probs, value_rows, preferred_element_type=jnp.float32
    )
    return (attended.reshape(packed.shape[0], -1).astype(jnp.bfloat16), maxima + jnp.log(totals))


def attend_backward(member):
    packed, upstream, log_totals = member
    queries, key_rows, value_rows, masked = split_heads(packed)
    attn_probs = jnp.exp(masked - log_totals)
    probs_low = attn_probs.astype(jnp.bfloat16)
    grad_out = upstream.reshape(queries.shape)
    grad_probs = jnp.einsum(
        "qhd,khd->hqk", grad_out, value_rows, preferred_element_type=jnp.float32
    )
    grad_values = jnp.einsum(
        "hqk,qhd->khd", probs_low, grad_out, preferred_element_type=jnp.float32
    )
    grad_scores = (
        attn_probs * (grad_probs - jnp.sum(grad_probs * attn_probs, -1, keepdims=True))
    ).astype(jnp.bfloat16)
    factor = HD ** (-0.5)
    grad_queries = (
        jnp.einsum("hqk,khd->qhd", grad_scores, key_rows, preferred_element_type=jnp.float32)
        * factor
    )
    grad_keys = (
        jnp.einsum("hqk,qhd->khd", grad_scores, queries, preferred_element_type=jnp.float32)
        * factor
    )
    seq_len = packed.shape[0]
    joined = jnp.concatenate(
        [
            grad_queries.reshape(seq_len, -1),
            grad_keys.reshape(seq_len, -1),
            grad_values.reshape(seq_len, -1),
        ],
        1,
    )
    return joined.astype(jnp.bfloat16)


def expert_rows(row_block, up_mat, down_mat):
    pre_act = jnp.dot(row_block, up_mat, preferred_element_type=jnp.float32)
    hidden = gelu_exact(pre_act).astype(jnp.bfloat16)
    return lax.dot_general(hidden, down_mat, over_cols, preferred_element_type=jnp.float32)


def expert_grads(row_block, grad_block, up_mat, down_mat):
    pre_act = jnp.dot(row_block, up_mat, preferred_element_type=jnp.float32)
    hidden, gelu_back = jax.vjp(gelu_exact, pre_act)
    hidden_low = hidden.astype(jnp.bfloat16)
    down_part = lax.dot_general(
        grad_block, hidden_low, over_rows, preferred_element_type=jnp.float32
    )
    grad_hidden = jnp.dot(grad_block, down_mat, preferred_element_type=jnp.float32)
    grad_pre = gelu_back(grad_hidden)[0].astype(jnp.bfloat16)
    up_part = lax.dot_general(row_block, grad_pre, over_rows, preferred_element_type=jnp.float32)
    return (grad_pre, up_part, down_part)


def fill_slots(row_vals, target, slot_count):
    buffer = jnp.zeros((slot_count + 1, row_vals.shape[1]), row_vals.dtype).at[target].set(row_vals)
    return buffer[:slot_count]


def read_slots(buffer, target):
    padded = jnp.concatenate([buffer, jnp.zeros((1, buffer.shape[1]), buffer.dtype)], 0)
    return padded[target]


def plain_shards(
    layer_inputs_matrix,
    assignment_indices,
    admitted_counts_matrix,
    mixer_scaling1_factor,
    triple_linear_matrix,
    mixer_exit_matrix,
    specialist_scaling2_factor,
    cluster_mean_columns,
    first_linear_matrix,
    second_linear_matrix,
    incoming_gradient,
):
    gain_one, qkv_mat, out_mat, gain_two, centers = (
        lax.all_gather(mixer_scaling1_factor, ("wide", "narrow"), axis=0, tiled=True),
        lax.all_gather(triple_linear_matrix, ("wide", "narrow"), axis=0, tiled=True),
        lax.all_gather(mixer_exit_matrix, ("wide", "narrow"), axis=0, tiled=True),
        lax.all_gather(specialist_scaling2_factor, ("wide", "narrow"), axis=0, tiled=True),
        lax.all_gather(cluster_mean_columns, ("wide", "narrow"), axis=0, tiled=True),
    )
    gain_one = gain_one.astype(jnp.float32)
    gain_two = gain_two.astype(jnp.float32)
    centers = centers.astype(jnp.float32)
    token_rows = layer_inputs_matrix.astype(jnp.float32)
    tok_count, model_width = layer_inputs_matrix.shape
    seq_count = tok_count // SEQ
    normed, norm1_back = jax.vjp(layer_norm, token_rows, gain_one)
    normed_low = normed.astype(jnp.bfloat16)
    qkv_rows = jnp.dot(normed_low, qkv_mat, preferred_element_type=jnp.float32).astype(jnp.bfloat16)
    packed_seqs = qkv_rows.reshape(seq_count, SEQ, 3 * model_width)
    attended, log_totals = lax.map(attend_forward, packed_seqs)
    attended = attended.reshape(tok_count, model_width)
    residual = token_rows + jnp.dot(attended, out_mat, preferred_element_type=jnp.float32)
    normed_two, norm2_back = jax.vjp(layer_norm, residual, gain_two)
    sent_rows = normed_two.astype(jnp.bfloat16)
    dispatched_items = assignment_indices[:, 0]
    specialist_overall_sum = admitted_counts_matrix.shape[0]
    slot_count = specialist_overall_sum * SLOT
    specialist_indicator = (
        dispatched_items[:, None] == jnp.arange(specialist_overall_sum, dtype=jnp.int32)[None, :]
    ).astype(jnp.int32)
    before = jnp.cumsum(specialist_indicator, 0) - specialist_indicator
    ranked = jnp.sum(before * specialist_indicator, 1)
    position_ceilings = jnp.sum(specialist_indicator * admitted_counts_matrix[None, :], 1)
    retained_couple_filter = ranked < position_ceilings
    target = jnp.where(retained_couple_filter, dispatched_items * SLOT + ranked, slot_count)
    kept_rows = retained_couple_filter.astype(jnp.float32)
    choose = specialist_indicator.astype(jnp.float32)
    send_buf = fill_slots(sent_rows, target, slot_count).reshape(
        specialist_overall_sum, SLOT, model_width
    )
    local_rows = lax.all_to_all(send_buf, "wide", split_axis=0, concat_axis=0, tiled=True).reshape(
        slot_count, model_width
    )
    gathered = lax.all_gather(local_rows, "narrow", axis=0, tiled=True)
    expert_local = lax.psum_scatter(
        expert_rows(gathered, first_linear_matrix[0], second_linear_matrix[0]).astype(jnp.bfloat16),
        "narrow",
        scatter_dimension=0,
        tiled=True,
    )
    returned = lax.all_to_all(
        expert_local.reshape(specialist_overall_sum, SLOT, model_width),
        "wide",
        split_axis=0,
        concat_axis=0,
        tiled=True,
    )
    expert_tok = read_slots(returned.reshape(slot_count, model_width), target).astype(jnp.float32)
    center_rows = lax.dot_general(choose, centers, over_cols, precision=precise)
    logits = jnp.sum(normed_two * center_rows, 1)
    sigma = jax.nn.sigmoid(logits)
    gating = sigma * kept_rows
    mixed = (residual + gating[:, None] * expert_tok).astype(jnp.bfloat16)
    grad_y = incoming_gradient.astype(jnp.float32)
    grad_logit = jnp.sum(grad_y * expert_tok, 1) * sigma * (1.0 - sigma) * kept_rows
    grad_normed = grad_logit[:, None] * center_rows
    centroid_part = lax.dot_general(
        normed_two, choose * grad_logit[:, None], over_rows, precision=precise
    )
    grad_expert = (grad_y * gating[:, None]).astype(jnp.bfloat16)
    grad_buf = fill_slots(grad_expert, target, slot_count).reshape(
        specialist_overall_sum, SLOT, model_width
    )
    grad_local = lax.all_to_all(grad_buf, "wide", split_axis=0, concat_axis=0, tiled=True).reshape(
        slot_count, model_width
    )
    grad_gathered = lax.all_gather(grad_local, "narrow", axis=0, tiled=True)
    grad_pre, up_part, down_part = expert_grads(
        gathered, grad_gathered, first_linear_matrix[0], second_linear_matrix[0]
    )
    input_back = lax.psum_scatter(
        lax.dot_general(
            grad_pre, first_linear_matrix[0], over_cols, preferred_element_type=jnp.float32
        ).astype(jnp.bfloat16),
        "narrow",
        scatter_dimension=0,
        tiled=True,
    )
    up_grad = up_part[None]
    down_grad = down_part[None]
    back_rows = lax.all_to_all(
        input_back.reshape(specialist_overall_sum, SLOT, model_width),
        "wide",
        split_axis=0,
        concat_axis=0,
        tiled=True,
    )
    grad_normed = grad_normed + read_slots(
        back_rows.reshape(slot_count, model_width), target
    ).astype(jnp.float32)
    grad_resid_norm, gain_two_part = norm2_back(grad_normed)
    grad_resid = grad_y + grad_resid_norm
    grad_branch = grad_resid.astype(jnp.bfloat16)
    out_part = lax.dot_general(attended, grad_branch, over_rows, preferred_element_type=jnp.float32)
    grad_attended = lax.dot_general(
        grad_branch, out_mat, over_cols, preferred_element_type=jnp.float32
    ).astype(jnp.bfloat16)
    grad_packed = lax.map(
        attend_backward,
        (packed_seqs, grad_attended.reshape(seq_count, SEQ, model_width), log_totals),
    )
    grad_packed = grad_packed.reshape(tok_count, 3 * model_width)
    qkv_part = lax.dot_general(
        normed_low, grad_packed, over_rows, preferred_element_type=jnp.float32
    )
    grad_normed_one = lax.dot_general(
        grad_packed, qkv_mat, over_cols, preferred_element_type=jnp.float32
    )
    grad_token_norm, gain_one_part = norm1_back(grad_normed_one)
    tokens_grad = grad_resid + grad_token_norm
    gain_one_grad, qkv_grad, out_grad, gain_two_grad, centroid_grad = (
        lax.psum_scatter(gain_one_part, ("wide", "narrow"), scatter_dimension=0, tiled=True),
        lax.psum_scatter(qkv_part, ("wide", "narrow"), scatter_dimension=0, tiled=True),
        lax.psum_scatter(out_part, ("wide", "narrow"), scatter_dimension=0, tiled=True),
        lax.psum_scatter(gain_two_part, ("wide", "narrow"), scatter_dimension=0, tiled=True),
        lax.psum_scatter(centroid_part, ("wide", "narrow"), scatter_dimension=0, tiled=True),
    )
    return (
        mixed,
        tokens_grad,
        gain_one_grad,
        qkv_grad,
        out_grad,
        gain_two_grad,
        centroid_grad,
        up_grad,
        down_grad,
    )


def shards(mesh, v, idx, caps, g1, wq, wo, g2, centers, up, down, dy):
    T, D = v.shape
    E = caps.shape[0]
    c = Sizes(mesh, T, D, wq.shape[0], up.shape[2], E)
    if not c.fits:
        return plain_shards(v, idx, caps, g1, wq, wo, g2, centers, up, down, dy)
    w = lax.axis_index("wide")
    misc = jnp.concatenate(
        [centers, jnp.zeros((c.slab, GAIN1 - E), bf16), g1[:, None], g2[:, None]], 1
    )
    cap = jnp.broadcast_to(jnp.pad(caps, (0, c.EP - E))[:, None], (c.EP, LANES))
    res = forward_call(c, v, dy, idx.reshape(1, T), cap, wq, wo, misc, up, down)
    wall, mall, qkv, lse, att, resid, sent, meta, mrow = res[:9]
    ret, outp, ug, dg, cent = res[9:]
    mixed, tokens_grad, qg, og, small = backward_call(
        c, v, dy, qkv, lse, att, resid, wall, ret, outp, mrow, meta, cent
    )
    return (
        mixed, tokens_grad, small[:, GAIN1], qg, og, small[:, GAIN2], small[:, :E], ug, dg,
    )


def solution(mesh):
    both = ("wide", "narrow")
    in_specs = (
        P(both, None), P(both, None), P(), P(both), P(both, None), P(both, None), P(both), P(both, None),
        P("wide", None, "narrow"), P("wide", None, "narrow"), P(both, None),
    )
    out_specs = (
        P(both, None), P(both, None), P(both), P(both, None), P(both, None), P(both), P(both, None),
        P("wide", None, "narrow"), P("wide", None, "narrow"),
    )
    return jax.shard_map(
        functools.partial(shards, mesh), mesh=mesh, in_specs=in_specs, out_specs=out_specs, check_vma=False
    )
```

```python
import functools

import jax
import jax.numpy as jnp
from jax import lax
from jax.experimental import pallas as pl
from jax.experimental.pallas import tpu as pltpu
from jax.sharding import PartitionSpec as P

HD = 64
SEQ = 1024
SLOT = 48
PAIR = 2 * HD
QB = 256
LANES = 128
GAIN1 = 126
GAIN2 = 127
NEG = -1e30
VMEM_CAP = 62 << 20
CID0 = 0
CID1 = 1
AHEAD_W = 4
AHEAD_X = 2
BEHIND_W = 2

MESH = pl.DeviceIdType.MESH
NN_ = (((1,), (0,)), ((), ()))
NT_ = (((1,), (1,)), ((), ()))
TN_ = (((0,), (0,)), ((), ()))
f32 = jnp.float32
bf16 = jnp.bfloat16


def mm(a, b, dims=NN_):
    return lax.dot_general(a, b, dims, preferred_element_type=f32)


def wait_bytes(ref, sem):
    pltpu.make_async_copy(ref, ref, sem).wait()


arrive = wait_bytes


def push(src, dst, send, recv, **where):
    pltpu.make_async_remote_copy(
        src_ref=src, dst_ref=dst, send_sem=send, recv_sem=recv,
        device_id=where, device_id_type=MESH,
    ).start()


def half_mask(rows):
    return lax.broadcasted_iota(jnp.int32, (rows, PAIR), 1) < HD


def pick(mask, h, value):
    zero = jnp.zeros_like(value)
    return jnp.where(mask, value, zero) if h == 0 else jnp.where(mask, zero, value)


def layer_stats(x):
    centered = x - jnp.mean(x, 1, keepdims=True)
    r = lax.rsqrt(jnp.mean(centered * centered, 1, keepdims=True) + 1e-05)
    return centered * r, r


def attend_rows(qkv, seq, i, put_out, put_lse):
    length = (i + 1) * QB
    rows = pl.ds(i * QB, QB)
    mask = half_mask(QB)
    causal = lax.broadcasted_iota(jnp.int32, (QB, QB), 0) <= lax.broadcasted_iota(
        jnp.int32, (QB, QB), 1
    )
    q = qkv[rows, 0:PAIR] * bf16(HD**-0.5)
    k = qkv[pl.ds(0, length), PAIR : 2 * PAIR]
    v = qkv[pl.ds(0, length), 2 * PAIR : 3 * PAIR]
    outs, sums = [], []
    for h in range(2):
        s = mm(k, pick(mask, h, q), NT_)
        last = jnp.where(causal, s[length - QB :], NEG)
        top = jnp.max(last, 0, keepdims=True)
        if i:
            top = jnp.maximum(top, jnp.max(s[: length - QB], 0, keepdims=True))
        p = jnp.exp(last - top)
        total = jnp.sum(p, 0, keepdims=True)
        p = p.astype(bf16)
        if i:
            head = jnp.exp(s[: length - QB] - top)
            total = total + jnp.sum(head, 0, keepdims=True)
            p = jnp.concatenate([head.astype(bf16), p], 0)
        put_lse(h, rows, top + jnp.log(total))
        outs.append(mm(p, v, TN_))
        sums.append(total)
    inv = jnp.transpose(1.0 / jnp.concatenate(sums + [jnp.ones((6, QB), f32)], 0))
    put_out(rows, jnp.where(mask, outs[0] * inv[:, 0:1], outs[1] * inv[:, 1:2]).astype(bf16))


def attend_rows_back(qkv, att, datt, lse, i, first, prod, dk, dv, put_dq):
    length = (i + 1) * QB
    rows = pl.ds(i * QB, QB)
    mask = half_mask(QB)
    mask_all = half_mask(length)
    causal = lax.broadcasted_iota(jnp.int32, (QB, QB), 0) <= lax.broadcasted_iota(
        jnp.int32, (QB, QB), 1
    )
    q = qkv[rows, 0:PAIR] * bf16(HD**-0.5)
    k = qkv[pl.ds(0, length), PAIR : 2 * PAIR]
    v = qkv[pl.ds(0, length), 2 * PAIR : 3 * PAIR]
    do = datt[rows, :]
    dq = None
    for h in range(2):
        qh, dh = pick(mask, h, q), pick(mask, h, do)
        s = mm(k, qh, NT_)
        row = lse[h : h + 1, rows]
        p = jnp.exp(jnp.where(causal, s[length - QB :], NEG) - row)
        if i:
            p = jnp.concatenate([jnp.exp(s[: length - QB] - row), p], 0)
        dp = mm(v, dh, NT_)
        ds = (p * (dp - prod[h : h + 1, rows])).astype(bf16)
        a, b = mm(p.astype(bf16), dh), mm(ds, qh)
        if first and h == 0:
            dv[pl.ds(0, length), :] = a
            dk[pl.ds(0, length), :] = b
        else:
            dv[pl.ds(0, length), :] += a
            dk[pl.ds(0, length), :] += b
        part = mm(ds, pick(mask_all, h, k), TN_)
        dq = part if dq is None else dq + part
    put_dq(rows, (dq * HD**-0.5).astype(bf16))


class Sizes:
    def __init__(self, mesh, tokens, d, slab, ff, experts):
        self.NW, self.NN = mesh.shape["wide"], mesh.shape["narrow"]
        self.A, self.X = self.NW // 2, self.NN // 2
        self.T, self.D, self.slab, self.F, self.E = tokens, d, slab, ff, experts
        self.CW = 3 * PAIR
        self.G = d // PAIR
        self.J = self.G + d // self.CW
        self.R = self.NN * SLOT
        self.S = experts * SLOT
        self.EP = max(8, experts)
        rows = self.NW * self.R
        self.moe = rows * (5 * d + 3 * ff) * 2 < (24 << 20)
        self.fits = (
            self.moe and slab % 8 == 0 and tokens == SEQ and self.NW % 2 == 0 and self.NN % 2 == 0
            and self.NW > 2 and self.NN > 2 and experts == self.NW
        )


def place(c):
    w, n = lax.axis_index("wide"), lax.axis_index("narrow")
    return w, n, w // 2, lax.rem(w, 2), n // 2, lax.rem(n, 2)


def greet(c, w, n):
    bar = pltpu.get_barrier_semaphore()
    x, cc = n // 2, lax.rem(n, 2)

    def wide(i, _):
        pl.semaphore_signal(bar, inc=1, device_id={"wide": lax.rem(w + i, c.NW)}, device_id_type=MESH)
        return 0

    lax.fori_loop(1, c.NW, wide, 0)
    for k in range(1, c.X):
        to = lax.rem(x + k, c.X) * 2 + cc
        pl.semaphore_signal(bar, inc=1, device_id={"narrow": to}, device_id_type=MESH)
        other = w + 1 - 2 * lax.rem(w, 2)
        pl.semaphore_signal(bar, inc=1, device_id={"wide": other, "narrow": to}, device_id_type=MESH)
    pl.semaphore_signal(bar, inc=1, device_id={"narrow": x * 2 + 1 - cc}, device_id_type=MESH)
    return lambda: pl.semaphore_wait(bar, c.NW - 1 + 2 * c.X - 1)


def forward_kernel(c, *refs):
    (v_hbm, dy_hbm, idx_ref, cap_ref, wq_hbm, wo_hbm, cen_ref, g1_ref, g2_ref, up_hbm, down_hbm) = refs[:11]
    (w_out, normt_out, qkv_out, lse_out, att_out, resid_out, meta_out, mrow_out) = refs[11:19]
    (ret_out, outp_out, ug_out, dg_out, cent_out) = refs[19:24]
    (v, nrm, normed, normt, oh, wbuf, wmat, wtr, misc, mrow, qkv, lse, att, sent, sendx, senddy,
     up, down, xin, dyin, hid, dpre, dexp, outp, part, lc, lx, stage, cent,
     lsem, in_sem, out_sem, w_sem, q_sem, st_sem, s1s, s1r, s2s, s2r, s4s, s4r,
     ds_, dr, xs_, xr, cs_, cr, fs, fr, gs, gr, ks, kr, rs_, rr, ws_, wr) = refs[24:]
    A, X, NW, NN, T, D, CW, G, J = c.A, c.X, c.NW, c.NN, c.T, c.D, c.CW, c.G, c.J
    w, n, a, b, x, cc = place(c)
    own = (a, b, x, cc)
    dy = sent

    for j in range(J):
        dst = wbuf.at[(j, *own)]
        if j < G:
            for p in range(3):
                pltpu.make_async_copy(
                    wq_hbm.at[:, pl.ds(p * D + j * PAIR, PAIR)], dst.at[:, pl.ds(p * PAIR, PAIR)], lsem.at[j]
                ).start()
        else:
            pltpu.make_async_copy(wo_hbm.at[:, pl.ds((j - G) * CW, CW)], dst, lsem.at[j]).start()
    loads = [(dy_hbm, dy), (v_hbm, v), (up_hbm.at[0], up), (down_hbm.at[0], down)]
    for i, (s, d) in enumerate(loads):
        pltpu.make_async_copy(s, d, in_sem.at[i]).start()

    def load_wait(i):
        wait_bytes(loads[i][1], in_sem.at[i])

    met = greet(c, w, n)

    pad = LANES - c.slab
    small = jnp.concatenate(
        [cen_ref[...].astype(f32), jnp.zeros((GAIN1 - c.E, c.slab), f32), g1_ref[...].astype(f32), g2_ref[...].astype(f32)], 0
    )
    small = jnp.concatenate([small, jnp.zeros((LANES, pad), f32)], 1)
    misc[own] = jnp.transpose(small)[0 : c.slab].astype(bf16)

    hot = (lax.broadcasted_iota(jnp.int32, (c.EP, T), 0) == idx_ref[...]).astype(f32)
    lane = lax.broadcasted_iota(jnp.int32, (c.EP, T), 1)
    count = hot
    shift = 1
    while shift < T:
        count = count + jnp.where(lane >= shift, pltpu.roll(count, shift, 1), 0.0)
        shift *= 2
    rank = jnp.sum((count - hot) * hot, 0, keepdims=True)
    ceiling = jnp.zeros((1, T), f32)
    for e in range(c.E):
        ceiling = ceiling + hot[e : e + 1, :] * cap_ref[e].astype(f32)
    kept = rank < ceiling
    slot = jnp.where(kept, idx_ref[...].astype(f32) * SLOT + rank, -1.0)

    met()

    def buf(j):
        return misc if isinstance(j, int) and j == J else wbuf.at[j]

    def s1(j):
        if not (isinstance(j, int) and j == J):
            wait_bytes(buf(j).at[own], lsem.at[j])
        for k in range(1, A):
            push(buf(j).at[own], buf(j).at[own], s1s.at[j], s1r.at[j], wide=lax.rem(a + k, A) * 2 + b)

    plane = [(p, q) for p in range(2) for q in range(X) if p or q]

    def s2(j):
        arrive(buf(j).at[pl.ds(0, A - 1), b, x, cc], s1r.at[j])
        mine = buf(j).at[:, b, x, cc]
        for i, (p, q) in enumerate(plane):
            push(
                mine, mine, s2s.at[j, i], s2r.at[j, i],
                wide=a * 2 + lax.rem(b + p, 2), narrow=lax.rem(x + q, X) * 2 + cc,
            )

    def plane_bytes(j, sem):
        for i in range(len(plane)):
            arrive(buf(j).at[:, b, x, cc], sem.at[j, i])

    def s4(j):
        plane_bytes(j, s2r)
        mine = buf(j).at[:, :, :, cc]
        push(mine, mine, s4s.at[j], s4r.at[j], narrow=x * 2 + 1 - cc)

    def take(j):
        arrive(buf(j).at[:, :, :, cc], s4r.at[j])
        val = wbuf[j].reshape(D, CW)
        wmat[j] = val
        wtr[j] = jnp.transpose(val)
        pltpu.make_async_copy(wtr.at[j], w_out.at[j], w_sem.at[j]).start()

    s1(J)
    s1(0)
    oh[...] = (lax.broadcasted_iota(jnp.int32, (c.S, T), 0).astype(f32) == slot).astype(bf16)
    s1(1)
    s2(J)
    s2(0)
    s1(2)
    load_wait(0)
    senddy[...] = mm(oh[...], dy[...]).astype(bf16)
    s2(1)
    s1(3)

    def dy_w(k):
        to = lax.rem(w + k, NW)
        push(senddy.at[pl.ds(pl.multiple_of(to * SLOT, SLOT), SLOT)], dyin.at[w, x, cc], ds_.at[k], dr.at[k], wide=to)

    def dy_x(k):
        src = lax.rem(w - k + NW, NW)

        @pl.when(k > 0)
        def _():
            arrive(dyin.at[src, x, cc], dr.at[k])

        for q in range(1, X):
            push(dyin.at[src, x, cc], dyin.at[src, x, cc], xs_.at[k], xr.at[k], narrow=lax.rem(x + q, X) * 2 + cc)

    dyin[w, x, cc] = senddy[pl.ds(pl.multiple_of(w * SLOT, SLOT), SLOT), :]
    load_wait(1)

    def norm1(i, _):
        rows = pl.ds(i * 128, 128)
        nrm[rows, :] = layer_stats(v[rows, :].astype(f32))[0]
        return 0

    lax.fori_loop(0, T // 128, norm1, 0)
    s4(J)
    s4(0)
    s2(2)
    s1(4)
    arrive(misc.at[:, :, :, cc], s4r.at[J])
    mrow[...] = jnp.transpose(misc[...].reshape(D, LANES).astype(f32))
    gain1 = mrow[GAIN1 : GAIN1 + 1, :]
    gain2 = mrow[GAIN2 : GAIN2 + 1, :]
    pltpu.make_async_copy(mrow, mrow_out, out_sem.at[0]).start()

    def norm1b(i, _):
        rows = pl.ds(i * 128, 128)
        normed[rows, :] = (nrm[rows, :] * gain1).astype(bf16)
        return 0

    lax.fori_loop(0, T // 128, norm1b, 0)
    per = -(-NW // 4)

    def pair(g, _):
        slot_ = lax.rem(g, 2)
        take(g)

        @pl.when(g >= 2)
        def _():
            wait_bytes(qkv.at[slot_], q_sem.at[slot_])

        qkv[slot_] = mm(normed[...], wmat[g]).astype(bf16)
        pltpu.make_async_copy(qkv.at[slot_], qkv_out.at[g], q_sem.at[slot_]).start()
        s4(g + 1)

        @pl.when(g + 3 < J)
        def _():
            s2(g + 3)

        @pl.when(g + 5 < J)
        def _():
            s1(g + 5)

        def put_out(rows, val):
            att[rows, pl.ds(pl.multiple_of(g * PAIR, PAIR), PAIR)] = val

        def put_lse(h, rows, val):
            lse[g, h : h + 1, rows] = val

        for i in range(T // QB):
            if i == T // QB - 1:
                for q in range(per):
                    k = g * per + q

                    @pl.when((k >= 1) & (k < NW))
                    def _():
                        dy_w(k)

                    @pl.when((g >= 2) & (k - 2 * per < NW))
                    def _():
                        dy_x(k - 2 * per)

            attend_rows(qkv.at[slot_], T, i, put_out, put_lse)
        return 0

    lax.fori_loop(0, G, pair, 0)
    pltpu.make_async_copy(lse, lse_out, out_sem.at[1]).start()
    pltpu.make_async_copy(att, att_out, out_sem.at[2]).start()
    for j in range(G + 1, J):
        s4(j)
    for j in range(G, J):
        take(j)

    for j in range(G, J):
        at = slice((j - G) * CW, (j - G + 1) * CW)
        nrm[:, at] = v[:, at].astype(f32) + mm(att[...], wmat[j])

    def tail(i, _):
        rows = pl.ds(i * QB, QB)
        sent[rows, :] = (layer_stats(nrm[rows, :])[0] * gain2).astype(bf16)
        return 0

    lax.fori_loop(0, T // QB, tail, 0)
    pltpu.make_async_copy(nrm, resid_out, out_sem.at[3]).start()
    sendx[...] = mm(oh[...], sent[...]).astype(bf16)

    def x_w(k):
        to = lax.rem(w + k, NW)
        push(sendx.at[pl.ds(pl.multiple_of(to * SLOT, SLOT), SLOT)], xin.at[w, x, cc], fs.at[k], fr.at[k], wide=to)

    for k in range(1, AHEAD_W):
        x_w(k)
    xin[w, x, cc] = sendx[pl.ds(pl.multiple_of(w * SLOT, SLOT), SLOT), :]

    crow = mrow[pl.ds(w, 1), :]

    def source(i):
        return lax.rem(w - i + NW, NW)

    def fwd_x(i):
        src = source(i)

        @pl.when(i > 0)
        def _():
            arrive(xin.at[src, x, cc], fr.at[i])

        for k in range(1, X):
            push(xin.at[src, x, cc], xin.at[src, x, cc], gs.at[i], gr.at[i], narrow=lax.rem(x + k, X) * 2 + cc)

    def fwd_c(i):
        src = source(i)
        arrive(xin.at[src, pl.ds(0, X - 1), cc], gr.at[i])
        push(xin.at[src, :, cc], xin.at[src, :, cc], ks.at[i], kr.at[i], narrow=x * 2 + 1 - cc)

    def expert(i):
        src = source(i)
        arrive(xin.at[src, :, cc], kr.at[i])
        xb = xin[src].reshape(c.R, D)
        db = dyin[src].reshape(c.R, D)
        xf, df = xb.astype(f32), db.astype(f32)
        s = jax.nn.sigmoid(jnp.sum(xf * crow, 1, keepdims=True))
        de = (df * s).astype(bf16)
        pre = mm(xb, up[...])
        cdf = 0.5 * (1.0 + lax.erf(pre * 0.7071067811865476))
        hb = (pre * cdf).astype(bf16)
        slope = cdf + pre * (jnp.exp(-0.5 * pre * pre) * 0.3989422804014327)
        dpb = (mm(de, down[...]) * slope).astype(bf16)
        out = mm(hb, down[...], NT_)
        dl = jnp.sum(df * out, 1, keepdims=True) * (s * (1.0 - s))
        dn = mm(dpb, up[...], NT_) + dl * crow
        part[src] = dn.astype(bf16).reshape(X, 2, SLOT, D)
        outp[src] = out.astype(bf16).reshape(X, 2, SLOT, D)
        cent[...] += jnp.broadcast_to(jnp.sum(dl * xf, 0, keepdims=True), cent.shape)
        rows = pl.ds(pl.multiple_of(src * c.R, SLOT), c.R)
        hid[rows, :] = hb
        dpre[rows, :] = dpb
        dexp[rows, :] = de

    def ret_c(i):
        src = source(i)
        push(part.at[src, :, 1 - cc], lc.at[src], rs_.at[0, i], rr.at[0, i], narrow=x * 2 + 1 - cc)

    def ret_x(i):
        src = source(i)
        arrive(lc.at[src], rr.at[0, i])
        part[src, :, cc] = (part[src, :, cc].astype(f32) + lc[src].astype(f32)).astype(bf16)
        for k in range(1, X):
            x2 = lax.rem(x + k, X)
            push(part.at[src, x2, cc], lx.at[src, x], rs_.at[1, i], rr.at[1, i], narrow=x2 * 2 + cc)

    def ret_w(i):
        src = source(i)
        arrive(lx.at[src, pl.ds(0, X - 1)], rr.at[1, i])
        total = part[src, x, cc].astype(f32)
        for k in range(1, X):
            total = total + lx[src, lax.rem(x + k, X)].astype(f32)
        part[src, x, cc] = total.astype(bf16)

        @pl.when(i > 0)
        def _():
            push(part.at[src, x, cc], ret_out.at[w], ws_.at[i], wr.at[i], wide=src)

        @pl.when(i == 0)
        def _():
            pltpu.make_async_copy(part.at[src, x, cc], ret_out.at[w], ws_.at[0]).start()

    fwd_x(0)
    normt[...] = jnp.transpose(normed[...])
    pltpu.make_async_copy(normt, normt_out, out_sem.at[5]).start()
    for k in range(per * (G - 2), NW):
        dy_x(k)

    logits = mm(mrow[0 : c.EP, :].astype(bf16), sent[...], NT_)
    gate = jax.nn.sigmoid(jnp.sum(logits * hot, 0, keepdims=True)) * kept.astype(f32)
    meta_out[...] = jnp.concatenate([slot, gate, jnp.zeros((6, T), f32)], 0)
    cent[...] = jnp.zeros_like(cent)

    def dy_all(k, _):
        arrive(dyin.at[w, x, cc], xr.at[k])
        return 0

    for q in range(X - 1):
        lax.fori_loop(0, NW, dy_all, 0)
    push(dyin.at[:, :, cc], dyin.at[:, :, cc], cs_, cr, narrow=x * 2 + 1 - cc)
    fwd_c(0)
    for k in range(1, AHEAD_X):
        fwd_x(k)
    load_wait(2)
    load_wait(3)
    arrive(dyin.at[:, :, cc], cr)

    def block(i, _):
        @pl.when(i + AHEAD_W < NW)
        def _():
            x_w(i + AHEAD_W)

        @pl.when(i + 1 < NW)
        def _():
            fwd_c(i + 1)

        @pl.when(i + AHEAD_X < NW)
        def _():
            fwd_x(i + AHEAD_X)

        expert(i)
        ret_c(i)

        @pl.when(i >= 1)
        def _():
            ret_x(i - 1)

        @pl.when(i >= BEHIND_W)
        def _():
            ret_w(i - BEHIND_W)

        return 0

    lax.fori_loop(0, NW, block, 0)
    ret_x(NW - 1)
    for i in range(NW - BEHIND_W, NW - 1):
        ret_w(i)
    pltpu.make_async_copy(outp, outp_out, out_sem.at[4]).start()
    cent_out[...] = cent[...]
    parts = D // QB

    def grads(lhs, rhs, out, second):
        def one_block(i, _):
            at = pl.ds(pl.multiple_of(i * QB, QB), QB)
            if second:
                wait_bytes(stage.at[i], st_sem.at[i])
            stage[i] = mm(lhs(at), rhs[...], TN_)
            pltpu.make_async_copy(stage.at[i], out.at[0, at], st_sem.at[i]).start()
            return 0

        lax.fori_loop(0, parts, one_block, 0)

    grads(lambda at: dexp[:, at], hid, dg_out, False)
    ret_w(NW - 1)
    grads(lambda at: xin[:, :, :, :, at].reshape(NW * c.R, QB), dpre, ug_out, True)

    for q, ref in enumerate([mrow, lse, att, nrm, outp, normt]):
        wait_bytes(ref, out_sem.at[q])
    for q in range(2):
        wait_bytes(qkv.at[q], q_sem.at[q])
    for j in [J] + list(range(J)):
        if not (isinstance(j, int) and j == J):
            wait_bytes(wtr.at[j], w_sem.at[j])
        arrive(buf(j).at[pl.ds(0, A - 1), b, x, cc], s1s.at[j])
        plane_bytes(j, s2s)
        arrive(buf(j).at[:, :, :, cc], s4s.at[j])
    arrive(dyin.at[:, :, cc], cs_)

    def drain(i, _):
        src = source(i)
        arrive(xin.at[src, pl.ds(0, X - 1), cc], xs_.at[i])
        arrive(xin.at[src, pl.ds(0, X - 1), cc], gs.at[i])
        arrive(xin.at[src, :, cc], ks.at[i])
        arrive(lc.at[src], rs_.at[0, i])
        arrive(lx.at[src, pl.ds(0, X - 1)], rs_.at[1, i])

        @pl.when(i > 0)
        def _():
            arrive(xin.at[src, x, cc], ds_.at[i])
            arrive(xin.at[src, x, cc], fs.at[i])
            arrive(xin.at[src, x, cc], ws_.at[i])
            arrive(xin.at[src, x, cc], wr.at[i])

        return 0

    lax.fori_loop(0, NW, drain, 0)
    wait_bytes(part.at[0, 0, 0], ws_.at[0])
    for i in range(parts):
        wait_bytes(stage.at[i], st_sem.at[i])


def forward_call(c, v, dy, idx, cap, wq, wo, cen, g1, g2, up, down):
    T, D, CW, G, J, NW, NN, A, X, L, F = c.T, c.D, c.CW, c.G, c.J, c.NW, c.NN, c.A, c.X, c.slab, c.F
    any_ = pl.BlockSpec(memory_space=pl.ANY)
    vm = pl.BlockSpec(memory_space=pltpu.VMEM)
    sm = pl.BlockSpec(memory_space=pltpu.SMEM)
    sds = jax.ShapeDtypeStruct
    rows_ = (NW, X, 2, SLOT, D)
    outs = [
        (sds((J, CW, D), bf16), any_),
        (sds((D, T), bf16), any_),
        (sds((G, T, CW), bf16), any_),
        (sds((G, 8, T), f32), any_),
        (sds((T, D), bf16), any_),
        (sds((T, D), f32), any_),
        (sds((8, T), f32), vm),
        (sds((LANES, D), f32), any_),
        (sds((NW, SLOT, D), bf16), any_),
        (sds(rows_, bf16), any_),
        (sds((1, D, F), f32), any_),
        (sds((1, D, F), f32), any_),
        (sds((8, D), f32), vm),
    ]
    dma, V = pltpu.SemaphoreType.DMA, pltpu.VMEM
    rows = NW * c.R
    scratch = [
        V((T, D), bf16), V((T, D), f32), V((T, D), bf16), V((D, T), bf16), V((c.S, T), bf16),
        V((J, A, 2, X, 2, L, CW), bf16), V((J, D, CW), bf16), V((J, CW, D), bf16), V((A, 2, X, 2, L, LANES), bf16), V((LANES, D), f32),
        V((2, T, CW), bf16), V((G, 8, T), f32), V((T, D), bf16), V((T, D), bf16), V((c.S, D), bf16), V((c.S, D), bf16),
        V((D, F), bf16), V((D, F), bf16), V(rows_, bf16), V(rows_, bf16),
        V((rows, F), bf16), V((rows, F), bf16), V((rows, D), bf16), V(rows_, bf16), V(rows_, bf16),
        V((NW, X, SLOT, D), bf16), V((NW, X, SLOT, D), bf16), V((D // QB, QB, F), f32), V((8, D), f32),
        dma((J,)), dma((4,)), dma((6,)), dma((J,)), dma((2,)), dma((D // QB,)),
    ] + [dma((J + 1,))] * 2 + [dma((J + 1, 2 * X - 1))] * 2 + [dma((J + 1,))] * 2 + [dma((NW,))] * 4 + [dma(()), dma(())] + [dma((NW,))] * 6 + [
        dma((2, NW)), dma((2, NW)), dma((NW,)), dma((NW,)),
    ]
    return pl.pallas_call(
        functools.partial(forward_kernel, c),
        out_shape=tuple(o[0] for o in outs),
        in_specs=[any_, any_, vm, sm, any_, any_, vm, vm, vm, any_, any_],
        out_specs=tuple(o[1] for o in outs),
        scratch_shapes=scratch,
        compiler_params=pltpu.CompilerParams(
            collective_id=CID0, has_side_effects=True, vmem_limit_bytes=VMEM_CAP
        ),
        name="forward",
    )(v, dy, idx, cap, wq, wo, cen, g1, g2, up, down)


def backward_kernel(c, *refs):
    (v_hbm, dy_hbm, qkv_hbm, lse_hbm, att_hbm, resid_hbm, wt_hbm, nt_hbm, ret_hbm, outp_hbm, mrow, meta, cent) = refs[:13]
    (mixed_out, tok_out, qg_out, og_out, small_out) = refs[13:18]
    (v, dy, qkv, lse, att, resid, wt, ret, oh, normt, dbr, datt, dnm, dqkv, dk, dv, prod, rowbuf,
     part, lc, lx, got, mixed,
     gb, la, lb, lz, sgb, sla, slb, slz,
     in_sem, q_sem, out_sem, os_, orv, ows, owr, rs_, rr, ps_, pr, tokacc) = refs[18:]
    A, X, NW, NN, T, D, CW, G, J = c.A, c.X, c.NW, c.NN, c.T, c.D, c.CW, c.G, c.J
    H = J - G
    w, n, a, b, x, cc = place(c)
    blocks = T // QB

    loads = [
        (ret_hbm, ret), (resid_hbm, resid), (dy_hbm, dy), (att_hbm, att), (v_hbm, v), (lse_hbm, lse), (nt_hbm, normt),
        (wt_hbm.at[pl.ds(G, H)], wt.at[pl.ds(G, H)]), (wt_hbm.at[pl.ds(0, G)], wt.at[pl.ds(0, G)]),
    ]
    for i, (s, d) in enumerate(loads):
        pltpu.make_async_copy(s, d, in_sem.at[i]).start()
    own_part = pltpu.make_async_copy(outp_hbm.at[:, :, cc], part, in_sem.at[9])
    own_part.start()

    def load_wait(i):
        wait_bytes(loads[i][1], in_sem.at[i])

    def fetch_qkv(g, slot_):
        pltpu.make_async_copy(qkv_hbm.at[g], qkv.at[slot_], q_sem.at[1, slot_]).start()

    fetch_qkv(0, 0)
    met = greet(c, w, n)

    slot, gate = meta[0:1, :], meta[1:2, :]
    hits = lax.broadcasted_iota(jnp.int32, (c.S, T), 0).astype(f32) == slot
    oh[...] = hits.astype(bf16)
    gain1, gain2 = mrow[GAIN1 : GAIN1 + 1, :], mrow[GAIN2 : GAIN2 + 1, :]
    load_wait(0)
    dnm[...] = mm(oh[...], ret[...].reshape(c.S, D), TN_)
    oh[...] = jnp.where(hits, gate, 0.0).astype(bf16)
    met()
    push(outp_hbm.at[:, :, 1 - cc], lc, os_.at[0], orv.at[0], narrow=x * 2 + 1 - cc)
    load_wait(1)
    load_wait(2)
    rowbuf[...] = jnp.zeros_like(rowbuf)
    rowbuf[pl.ds(w, 1), :] = cent[0:1, :]

    def norm2_back(i, acc):
        rows = pl.ds(i * QB, QB)
        n2, r2 = layer_stats(resid[rows, :])
        dn2 = dnm[rows, :]
        dn = dn2 * gain2
        step = r2 * (dn - jnp.mean(dn, 1, keepdims=True) - n2 * jnp.mean(dn * n2, 1, keepdims=True))
        dres = dy[rows, :].astype(f32) + step
        dnm[rows, :] = dres
        dbr[rows, :] = dres.astype(bf16)
        return acc + jnp.sum(dn2 * n2, 0, keepdims=True)

    rowbuf[GAIN2 : GAIN2 + 1, :] = lax.fori_loop(0, blocks, norm2_back, jnp.zeros((1, D), f32))
    load_wait(3)

    big = (gb, la, lb, lz, 0)
    tiny = (sgb, sla, slb, slz, J)

    def add(p, q):
        return (p.astype(f32) + q.astype(f32)).astype(bf16)

    def ra(t, j):
        push(t[0].at[j, :, :, :, 1 - cc], t[1].at[j], rs_.at[0, t[4] + j], rr.at[0, t[4] + j], narrow=x * 2 + 1 - cc)

    plane = [(p, q) for p in range(2) for q in range(X) if p or q]

    def rb(t, j):
        arrive(t[1].at[j], rr.at[0, t[4] + j])
        t[0][j, :, :, :, cc] = add(t[0][j, :, :, :, cc], t[1][j])
        for i, (p, q) in enumerate(plane):
            b2, x2 = lax.rem(b + p, 2), lax.rem(x + q, X)
            push(
                t[0].at[j, :, b2, x2, cc], t[2].at[j, b, x], ps_.at[t[4] + j, i], pr.at[t[4] + j, i],
                wide=a * 2 + b2, narrow=x2 * 2 + cc,
            )

    def plane_bytes(t, j, sem):
        for i in range(len(plane)):
            arrive(t[2].at[j, 0, 0], sem.at[t[4] + j, i])

    def rc(t, j):
        plane_bytes(t, j, pr)
        total = t[0][j, :, b, x, cc].astype(f32)
        for p, q in plane:
            total = total + t[2][j, lax.rem(b + p, 2), lax.rem(x + q, X)].astype(f32)
        t[0][j, :, b, x, cc] = total.astype(bf16)
        for k in range(1, A):
            a2 = lax.rem(a + k, A)
            push(t[0].at[j, a2, b, x, cc], t[3].at[j, a], rs_.at[1, t[4] + j], rr.at[1, t[4] + j], wide=a2 * 2 + b)

    def rf(t, j):
        arrive(t[3].at[j, pl.ds(0, A - 1)], rr.at[1, t[4] + j])
        total = t[0][j, a, b, x, cc].astype(f32)
        for k in range(1, A):
            total = total + t[3][j, lax.rem(a + k, A)].astype(f32)
        return total

    def rf_w(j):
        og_out[:, j * CW : (j + 1) * CW] = rf(big, j)

    def rf_q(g):
        total = rf(big, H + g)
        for p in range(3):
            qg_out[:, pl.ds(pl.multiple_of(p * D + g * PAIR, PAIR), PAIR)] = total[:, p * PAIR : (p + 1) * PAIR]

    for h in range(H):
        gb[h] = mm(att[...], dbr[:, h * CW : (h + 1) * CW], TN_).astype(bf16).reshape(A, 2, X, 2, c.slab, CW)
        ra(big, h)

    load_wait(7)

    def out_back(i, _):
        at = pl.ds(pl.multiple_of(i * QB, QB), QB)
        datt[:, at] = mm(dbr[...], wt[pl.ds(G, H), :, at].reshape(D, QB)).astype(bf16)
        return 0

    lax.fori_loop(0, D // QB, out_back, 0)
    load_wait(4)
    load_wait(6)
    for h in range(H):
        rb(big, h)
    load_wait(5)
    own_part.wait()

    def o_x(i):
        for k in range(1, X):
            x2 = lax.rem(x + k, X)
            push(part.at[i, x2], lx.at[i, x], os_.at[1 + i], orv.at[1 + i], narrow=x2 * 2 + cc)

    def o_w(i):
        arrive(lx.at[i, pl.ds(0, X - 1)], orv.at[1 + i])
        total = part[i, x].astype(f32)
        for k in range(1, X):
            total = total + lx[i, lax.rem(x + k, X)].astype(f32)
        part[i, x] = total.astype(bf16)

        @pl.when(i != w)
        def _():
            push(part.at[i, x], got.at[w], ows.at[i], owr.at[lax.rem(w - i + NW, NW)], wide=i)

        @pl.when(i == w)
        def _():
            got[w] = part[w, x]

    arrive(lc, orv.at[0])

    def merge(i, _):
        part[i] = add(part[i], lc[i])
        return 0

    lax.fori_loop(0, NW, merge, 0)
    per = -(-NW // 4)

    def spread(fn, step):
        for k in range(per):
            i = lax.rem(w + step * per + k, NW)

            @pl.when(step * per + k < NW)
            def _():
                fn(i)

    def pair(g, _):
        s_ = lax.rem(g, 2)

        @pl.when(g + 1 < G)
        def _():
            fetch_qkv(g + 1, 1 - s_)

        wait_bytes(qkv.at[s_], q_sem.at[1, s_])
        lanes = pl.ds(pl.multiple_of(g * PAIR, PAIR), PAIR)
        att_g, datt_g = att.at[:, lanes], datt.at[:, lanes]
        full = jnp.transpose(datt_g[...].astype(f32) * att_g[...].astype(f32))
        prod[0:1, :] = jnp.sum(full[0:HD], 0, keepdims=True)
        prod[1:2, :] = jnp.sum(full[HD:], 0, keepdims=True)

        def put_dq(rows, val):
            dqkv[g, rows, 0:PAIR] = val

        for i in reversed(range(blocks)):
            if i == 0:
                rc(big, g + H - 2)
            attend_rows_back(qkv.at[s_], att_g, datt_g, lse.at[g], i, i == blocks - 1, prod, dk, dv, put_dq)
            if i == blocks - 1:
                @pl.when(g >= 1)
                def _():
                    rb(big, g + H - 1)

                @pl.when(g < 4)
                def _():
                    spread(o_x, g)

                @pl.when(g >= 2)
                def _():
                    spread(o_w, g - 2)

        dqkv[g, :, PAIR : 2 * PAIR] = dk[...].astype(bf16)
        dqkv[g, :, 2 * PAIR :] = dv[...].astype(bf16)
        gb[H + g] = mm(normt[...], dqkv[g]).astype(bf16).reshape(A, 2, X, 2, c.slab, CW)
        ra(big, H + g)
        return 0

    lax.fori_loop(0, G, pair, 0)
    load_wait(8)

    def back(i):
        at = slice(i * QB, (i + 1) * QB)
        total = mm(dqkv[0], wt[0, :, at])
        for g in range(1, G):
            total = total + mm(dqkv[g], wt[g, :, at])
        tokacc[:, at] = total

    back(0)
    rb(big, J - 1)
    rc(big, J - 2)
    for i in range(1, D // QB):
        back(i)
    def norm1_back(i, acc):
        rows = pl.ds(i * QB, QB)
        n1, r1 = layer_stats(v[rows, :].astype(f32))
        dm0 = tokacc[rows, :]
        dm = dm0 * gain1
        step = r1 * (dm - jnp.mean(dm, 1, keepdims=True) - n1 * jnp.mean(dm * n1, 1, keepdims=True))
        dnm[rows, :] = dnm[rows, :] + step
        return acc + jnp.sum(dm0 * n1, 0, keepdims=True)

    rowbuf[GAIN1 : GAIN1 + 1, :] = lax.fori_loop(0, blocks, norm1_back, jnp.zeros((1, D), f32))
    tok_copy = pltpu.make_async_copy(dnm, tok_out, out_sem.at[0])
    tok_copy.start()
    sgb[0] = jnp.transpose(rowbuf[...]).astype(bf16).reshape(A, 2, X, 2, c.slab, LANES)
    ra(tiny, 0)
    rc(big, J - 1)
    rb(tiny, 0)

    def o_wait(k, _):
        arrive(got.at[0], owr.at[k])
        return 0

    lax.fori_loop(1, NW, o_wait, 0)

    def mix(i, _):
        cols = pl.ds(pl.multiple_of(i * QB, QB), QB)
        rows = pl.ds(i * QB, QB)
        mixed[rows, :] = (resid[rows, :] + mm(oh[:, cols], got[...].reshape(c.S, D), TN_)).astype(bf16)
        return 0

    lax.fori_loop(0, blocks, mix, 0)
    mix_copy = pltpu.make_async_copy(mixed, mixed_out, out_sem.at[1])
    mix_copy.start()
    rc(tiny, 0)
    for h in range(H):
        rf_w(h)

    def fin(g, _):
        rf_q(g)
        return 0

    lax.fori_loop(0, G, fin, 0)
    small_out[...] = rf(tiny, 0)

    arrive(lc, os_.at[0])

    def drain(i, _):
        arrive(lx.at[i, pl.ds(0, X - 1)], os_.at[1 + i])

        @pl.when(i != w)
        def _():
            arrive(got.at[0], ows.at[i])

        return 0

    lax.fori_loop(0, NW, drain, 0)

    def drain_sums(t, j):
        arrive(t[1].at[j], rs_.at[0, t[4] + j])
        plane_bytes(t, j, ps_)
        arrive(t[3].at[j, pl.ds(0, A - 1)], rs_.at[1, t[4] + j])

    def drain_big(j, _):
        drain_sums(big, j)
        return 0

    lax.fori_loop(0, J, drain_big, 0)
    drain_sums(tiny, 0)
    tok_copy.wait()
    mix_copy.wait()


def backward_call(c, v, dy, qkv, lse, att, resid, wt, nt, ret, outp, mrow, meta, cent):
    T, D, CW, G, J, NW, NN, A, X, L = c.T, c.D, c.CW, c.G, c.J, c.NW, c.NN, c.A, c.X, c.slab
    any_ = pl.BlockSpec(memory_space=pl.ANY)
    vm = pl.BlockSpec(memory_space=pltpu.VMEM)
    sds = jax.ShapeDtypeStruct
    dma, V = pltpu.SemaphoreType.DMA, pltpu.VMEM

    def sums(k, width):
        return [
            V((k, A, 2, X, 2, L, width), bf16), V((k, A, 2, X, L, width), bf16),
            V((k, 2, X, A, L, width), bf16), V((k, A, L, width), bf16),
        ]

    scratch = [
        V((T, D), bf16), V((T, D), bf16), V((2, T, CW), bf16), V((G, 8, T), f32), V((T, D), bf16), V((T, D), f32),
        V((J, CW, D), bf16), V((NW, SLOT, D), bf16), V((c.S, T), bf16),
        V((D, T), bf16), V((T, D), bf16), V((T, D), bf16), V((T, D), f32), V((G, T, CW), bf16),
        V((T, PAIR), f32), V((T, PAIR), f32), V((8, T), f32), V((LANES, D), f32),
        V((NW, X, SLOT, D), bf16), V((NW, X, SLOT, D), bf16), V((NW, X, SLOT, D), bf16), V((NW, SLOT, D), bf16),
        V((T, D), bf16),
    ] + sums(J, CW) + sums(1, LANES) + [
        dma((10,)), dma((2, 2)), dma((2,)), dma((NW + 1,)), dma((NW + 1,)), dma((NW,)), dma((NW,)),
        dma((2, J + 1)), dma((2, J + 1)), dma((J + 1, 2 * X - 1)), dma((J + 1, 2 * X - 1)),
        V((T, D), f32),
    ]
    return pl.pallas_call(
        functools.partial(backward_kernel, c),
        out_shape=(
            sds((T, D), bf16), sds((T, D), f32), sds((L, 3 * D), f32), sds((L, D), f32), sds((L, LANES), f32),
        ),
        in_specs=[any_] * 10 + [vm] * 3,
        out_specs=(any_, any_, vm, vm, vm),
        scratch_shapes=scratch,
        compiler_params=pltpu.CompilerParams(
            collective_id=CID1, has_side_effects=True, vmem_limit_bytes=VMEM_CAP
        ),
        name="backward",
    )(v, dy, qkv, lse, att, resid, wt, nt, ret, outp, mrow, meta, cent)


precise = lax.Precision.HIGHEST
over_rows = (((0,), (0,)), ((), ()))
over_cols = (((1,), (1,)), ((), ()))


def layer_norm(tensor, gain_vec):
    centered = tensor - jnp.mean(tensor, -1, keepdims=True)
    spread = jnp.mean(centered * centered, -1, keepdims=True)
    return centered * lax.rsqrt(spread + 1e-05) * gain_vec


def gelu_exact(tensor):
    return jax.nn.gelu(tensor, approximate=False)


def split_heads(packed):
    seq_len = packed.shape[0]
    model_width = packed.shape[1] // 3
    head_count = model_width // HD
    queries = packed[:, :model_width].reshape(seq_len, head_count, HD)
    key_rows = packed[:, model_width : 2 * model_width].reshape(seq_len, head_count, HD)
    value_rows = packed[:, 2 * model_width :].reshape(seq_len, head_count, HD)
    raw_scores = jnp.einsum(
        "qhd,khd->hqk", queries, key_rows, preferred_element_type=jnp.float32
    ) * HD ** (-0.5)
    places = jnp.arange(seq_len)
    causal = places[:, None] >= places[None, :]
    masked = jnp.where(causal[None], raw_scores, -1e30)
    return (queries, key_rows, value_rows, masked)


def attend_forward(packed):
    queries, key_rows, value_rows, masked = split_heads(packed)
    maxima = jnp.max(masked, -1, keepdims=True)
    powers = jnp.exp(masked - maxima)
    totals = jnp.sum(powers, -1, keepdims=True)
    attn_probs = (powers / totals).astype(jnp.bfloat16)
    attended = jnp.einsum(
        "hqk,khd->qhd", attn_probs, value_rows, preferred_element_type=jnp.float32
    )
    return (attended.reshape(packed.shape[0], -1).astype(jnp.bfloat16), maxima + jnp.log(totals))


def attend_backward(member):
    packed, upstream, log_totals = member
    queries, key_rows, value_rows, masked = split_heads(packed)
    attn_probs = jnp.exp(masked - log_totals)
    probs_low = attn_probs.astype(jnp.bfloat16)
    grad_out = upstream.reshape(queries.shape)
    grad_probs = jnp.einsum(
        "qhd,khd->hqk", grad_out, value_rows, preferred_element_type=jnp.float32
    )
    grad_values = jnp.einsum(
        "hqk,qhd->khd", probs_low, grad_out, preferred_element_type=jnp.float32
    )
    grad_scores = (
        attn_probs * (grad_probs - jnp.sum(grad_probs * attn_probs, -1, keepdims=True))
    ).astype(jnp.bfloat16)
    factor = HD ** (-0.5)
    grad_queries = (
        jnp.einsum("hqk,khd->qhd", grad_scores, key_rows, preferred_element_type=jnp.float32)
        * factor
    )
    grad_keys = (
        jnp.einsum("hqk,qhd->khd", grad_scores, queries, preferred_element_type=jnp.float32)
        * factor
    )
    seq_len = packed.shape[0]
    joined = jnp.concatenate(
        [
            grad_queries.reshape(seq_len, -1),
            grad_keys.reshape(seq_len, -1),
            grad_values.reshape(seq_len, -1),
        ],
        1,
    )
    return joined.astype(jnp.bfloat16)


def expert_rows(row_block, up_mat, down_mat):
    pre_act = jnp.dot(row_block, up_mat, preferred_element_type=jnp.float32)
    hidden = gelu_exact(pre_act).astype(jnp.bfloat16)
    return lax.dot_general(hidden, down_mat, over_cols, preferred_element_type=jnp.float32)


def expert_grads(row_block, grad_block, up_mat, down_mat):
    pre_act = jnp.dot(row_block, up_mat, preferred_element_type=jnp.float32)
    hidden, gelu_back = jax.vjp(gelu_exact, pre_act)
    hidden_low = hidden.astype(jnp.bfloat16)
    down_part = lax.dot_general(
        grad_block, hidden_low, over_rows, preferred_element_type=jnp.float32
    )
    grad_hidden = jnp.dot(grad_block, down_mat, preferred_element_type=jnp.float32)
    grad_pre = gelu_back(grad_hidden)[0].astype(jnp.bfloat16)
    up_part = lax.dot_general(row_block, grad_pre, over_rows, preferred_element_type=jnp.float32)
    return (grad_pre, up_part, down_part)


def fill_slots(row_vals, target, slot_count):
    buffer = jnp.zeros((slot_count + 1, row_vals.shape[1]), row_vals.dtype).at[target].set(row_vals)
    return buffer[:slot_count]


def read_slots(buffer, target):
    padded = jnp.concatenate([buffer, jnp.zeros((1, buffer.shape[1]), buffer.dtype)], 0)
    return padded[target]


def plain_shards(
    layer_inputs_matrix,
    assignment_indices,
    admitted_counts_matrix,
    mixer_scaling1_factor,
    triple_linear_matrix,
    mixer_exit_matrix,
    specialist_scaling2_factor,
    cluster_mean_columns,
    first_linear_matrix,
    second_linear_matrix,
    incoming_gradient,
):
    gain_one, qkv_mat, out_mat, gain_two, centers = (
        lax.all_gather(mixer_scaling1_factor, ("wide", "narrow"), axis=0, tiled=True),
        lax.all_gather(triple_linear_matrix, ("wide", "narrow"), axis=0, tiled=True),
        lax.all_gather(mixer_exit_matrix, ("wide", "narrow"), axis=0, tiled=True),
        lax.all_gather(specialist_scaling2_factor, ("wide", "narrow"), axis=0, tiled=True),
        lax.all_gather(cluster_mean_columns, ("wide", "narrow"), axis=0, tiled=True),
    )
    gain_one = gain_one.astype(jnp.float32)
    gain_two = gain_two.astype(jnp.float32)
    centers = centers.astype(jnp.float32)
    token_rows = layer_inputs_matrix.astype(jnp.float32)
    tok_count, model_width = layer_inputs_matrix.shape
    seq_count = tok_count // SEQ
    normed, norm1_back = jax.vjp(layer_norm, token_rows, gain_one)
    normed_low = normed.astype(jnp.bfloat16)
    qkv_rows = jnp.dot(normed_low, qkv_mat, preferred_element_type=jnp.float32).astype(jnp.bfloat16)
    packed_seqs = qkv_rows.reshape(seq_count, SEQ, 3 * model_width)
    attended, log_totals = lax.map(attend_forward, packed_seqs)
    attended = attended.reshape(tok_count, model_width)
    residual = token_rows + jnp.dot(attended, out_mat, preferred_element_type=jnp.float32)
    normed_two, norm2_back = jax.vjp(layer_norm, residual, gain_two)
    sent_rows = normed_two.astype(jnp.bfloat16)
    dispatched_items = assignment_indices[:, 0]
    specialist_overall_sum = admitted_counts_matrix.shape[0]
    slot_count = specialist_overall_sum * SLOT
    specialist_indicator = (
        dispatched_items[:, None] == jnp.arange(specialist_overall_sum, dtype=jnp.int32)[None, :]
    ).astype(jnp.int32)
    before = jnp.cumsum(specialist_indicator, 0) - specialist_indicator
    ranked = jnp.sum(before * specialist_indicator, 1)
    position_ceilings = jnp.sum(specialist_indicator * admitted_counts_matrix[None, :], 1)
    retained_couple_filter = ranked < position_ceilings
    target = jnp.where(retained_couple_filter, dispatched_items * SLOT + ranked, slot_count)
    kept_rows = retained_couple_filter.astype(jnp.float32)
    choose = specialist_indicator.astype(jnp.float32)
    send_buf = fill_slots(sent_rows, target, slot_count).reshape(
        specialist_overall_sum, SLOT, model_width
    )
    local_rows = lax.all_to_all(send_buf, "wide", split_axis=0, concat_axis=0, tiled=True).reshape(
        slot_count, model_width
    )
    gathered = lax.all_gather(local_rows, "narrow", axis=0, tiled=True)
    expert_local = lax.psum_scatter(
        expert_rows(gathered, first_linear_matrix[0], second_linear_matrix[0]).astype(jnp.bfloat16),
        "narrow",
        scatter_dimension=0,
        tiled=True,
    )
    returned = lax.all_to_all(
        expert_local.reshape(specialist_overall_sum, SLOT, model_width),
        "wide",
        split_axis=0,
        concat_axis=0,
        tiled=True,
    )
    expert_tok = read_slots(returned.reshape(slot_count, model_width), target).astype(jnp.float32)
    center_rows = lax.dot_general(choose, centers, over_cols, precision=precise)
    logits = jnp.sum(normed_two * center_rows, 1)
    sigma = jax.nn.sigmoid(logits)
    gating = sigma * kept_rows
    mixed = (residual + gating[:, None] * expert_tok).astype(jnp.bfloat16)
    grad_y = incoming_gradient.astype(jnp.float32)
    grad_logit = jnp.sum(grad_y * expert_tok, 1) * sigma * (1.0 - sigma) * kept_rows
    grad_normed = grad_logit[:, None] * center_rows
    centroid_part = lax.dot_general(
        normed_two, choose * grad_logit[:, None], over_rows, precision=precise
    )
    grad_expert = (grad_y * gating[:, None]).astype(jnp.bfloat16)
    grad_buf = fill_slots(grad_expert, target, slot_count).reshape(
        specialist_overall_sum, SLOT, model_width
    )
    grad_local = lax.all_to_all(grad_buf, "wide", split_axis=0, concat_axis=0, tiled=True).reshape(
        slot_count, model_width
    )
    grad_gathered = lax.all_gather(grad_local, "narrow", axis=0, tiled=True)
    grad_pre, up_part, down_part = expert_grads(
        gathered, grad_gathered, first_linear_matrix[0], second_linear_matrix[0]
    )
    input_back = lax.psum_scatter(
        lax.dot_general(
            grad_pre, first_linear_matrix[0], over_cols, preferred_element_type=jnp.float32
        ).astype(jnp.bfloat16),
        "narrow",
        scatter_dimension=0,
        tiled=True,
    )
    up_grad = up_part[None]
    down_grad = down_part[None]
    back_rows = lax.all_to_all(
        input_back.reshape(specialist_overall_sum, SLOT, model_width),
        "wide",
        split_axis=0,
        concat_axis=0,
        tiled=True,
    )
    grad_normed = grad_normed + read_slots(
        back_rows.reshape(slot_count, model_width), target
    ).astype(jnp.float32)
    grad_resid_norm, gain_two_part = norm2_back(grad_normed)
    grad_resid = grad_y + grad_resid_norm
    grad_branch = grad_resid.astype(jnp.bfloat16)
    out_part = lax.dot_general(attended, grad_branch, over_rows, preferred_element_type=jnp.float32)
    grad_attended = lax.dot_general(
        grad_branch, out_mat, over_cols, preferred_element_type=jnp.float32
    ).astype(jnp.bfloat16)
    grad_packed = lax.map(
        attend_backward,
        (packed_seqs, grad_attended.reshape(seq_count, SEQ, model_width), log_totals),
    )
    grad_packed = grad_packed.reshape(tok_count, 3 * model_width)
    qkv_part = lax.dot_general(
        normed_low, grad_packed, over_rows, preferred_element_type=jnp.float32
    )
    grad_normed_one = lax.dot_general(
        grad_packed, qkv_mat, over_cols, preferred_element_type=jnp.float32
    )
    grad_token_norm, gain_one_part = norm1_back(grad_normed_one)
    tokens_grad = grad_resid + grad_token_norm
    gain_one_grad, qkv_grad, out_grad, gain_two_grad, centroid_grad = (
        lax.psum_scatter(gain_one_part, ("wide", "narrow"), scatter_dimension=0, tiled=True),
        lax.psum_scatter(qkv_part, ("wide", "narrow"), scatter_dimension=0, tiled=True),
        lax.psum_scatter(out_part, ("wide", "narrow"), scatter_dimension=0, tiled=True),
        lax.psum_scatter(gain_two_part, ("wide", "narrow"), scatter_dimension=0, tiled=True),
        lax.psum_scatter(centroid_part, ("wide", "narrow"), scatter_dimension=0, tiled=True),
    )
    return (
        mixed,
        tokens_grad,
        gain_one_grad,
        qkv_grad,
        out_grad,
        gain_two_grad,
        centroid_grad,
        up_grad,
        down_grad,
    )


def shards(mesh, v, idx, caps, g1, wq, wo, g2, centers, up, down, dy):
    T, D = v.shape
    E = caps.shape[0]
    c = Sizes(mesh, T, D, wq.shape[0], up.shape[2], E)
    if not c.fits:
        return plain_shards(v, idx, caps, g1, wq, wo, g2, centers, up, down, dy)
    res = forward_call(
        c, v, dy, idx.reshape(1, T), caps, wq, wo, centers.T, g1.reshape(1, -1), g2.reshape(1, -1), up, down
    )
    wt, nt, qkv, lse, att, resid, meta, mrow, ret, outp, ug, dg, cent = res
    mixed, tokens_grad, qg, og, small = backward_call(
        c, v, dy, qkv, lse, att, resid, wt, nt, ret, outp, mrow, meta, cent
    )
    return (
        mixed, tokens_grad, small[:, GAIN1], qg, og, small[:, GAIN2], small[:, :E], ug, dg,
    )


def solution(mesh):
    both = ("wide", "narrow")
    in_specs = (
        P(both, None), P(both, None), P(), P(both), P(both, None), P(both, None), P(both), P(both, None),
        P("wide", None, "narrow"), P("wide", None, "narrow"), P(both, None),
    )
    out_specs = (
        P(both, None), P(both, None), P(both), P(both, None), P(both, None), P(both), P(both, None),
        P("wide", None, "narrow"), P("wide", None, "narrow"),
    )
    return jax.shard_map(
        functools.partial(shards, mesh), mesh=mesh, in_specs=in_specs, out_specs=out_specs, check_vma=False
    )
```

```python
import functools

import jax
import jax.numpy as jnp
from jax import lax
from jax.experimental import pallas as pl
from jax.experimental.pallas import tpu as pltpu
from jax.sharding import PartitionSpec as P

HD = 64
SEQ = 1024
SLOT = 48
PAIR = 2 * HD
QB = 256
LANES = 128
GAIN1 = 126
GAIN2 = 127
NEG = -1e30
VMEM_CAP = 62 << 20
CID0 = 0
CID1 = 1
AHEAD_W = 5
AHEAD_X = 3
BEHIND_W = 3
SHORT = 3

MESH = pl.DeviceIdType.MESH
NN_ = (((1,), (0,)), ((), ()))
NT_ = (((1,), (1,)), ((), ()))
TN_ = (((0,), (0,)), ((), ()))
f32 = jnp.float32
bf16 = jnp.bfloat16


def mm(a, b, dims=NN_):
    return lax.dot_general(a, b, dims, preferred_element_type=f32)


def wait_bytes(ref, sem):
    pltpu.make_async_copy(ref, ref, sem).wait()


arrive = wait_bytes


def push(src, dst, send, recv, **where):
    pltpu.make_async_remote_copy(
        src_ref=src, dst_ref=dst, send_sem=send, recv_sem=recv,
        device_id=where, device_id_type=MESH,
    ).start()


def half_mask(rows):
    return lax.broadcasted_iota(jnp.int32, (rows, PAIR), 1) < HD


def pick(mask, h, value):
    zero = jnp.zeros_like(value)
    return jnp.where(mask, value, zero) if h == 0 else jnp.where(mask, zero, value)


def layer_stats(x):
    centered = x - jnp.mean(x, 1, keepdims=True)
    r = lax.rsqrt(jnp.mean(centered * centered, 1, keepdims=True) + 1e-05)
    return centered * r, r


def attend_rows(qkv, seq, i, put_out, put_lse):
    length = (i + 1) * QB
    rows = pl.ds(i * QB, QB)
    mask = half_mask(QB)
    causal = lax.broadcasted_iota(jnp.int32, (QB, QB), 0) <= lax.broadcasted_iota(
        jnp.int32, (QB, QB), 1
    )
    q = qkv[rows, 0:PAIR] * bf16(HD**-0.5)
    k = qkv[pl.ds(0, length), PAIR : 2 * PAIR]
    v = qkv[pl.ds(0, length), 2 * PAIR : 3 * PAIR]
    outs, sums = [], []
    for h in range(2):
        s = mm(k, pick(mask, h, q), NT_)
        last = jnp.where(causal, s[length - QB :], NEG)
        top = jnp.max(last, 0, keepdims=True)
        if i:
            top = jnp.maximum(top, jnp.max(s[: length - QB], 0, keepdims=True))
        p = jnp.exp(last - top)
        total = jnp.sum(p, 0, keepdims=True)
        p = p.astype(bf16)
        if i:
            head = jnp.exp(s[: length - QB] - top)
            total = total + jnp.sum(head, 0, keepdims=True)
            p = jnp.concatenate([head.astype(bf16), p], 0)
        put_lse(h, rows, top + jnp.log(total))
        outs.append(mm(p, v, TN_))
        sums.append(total)
    inv = jnp.transpose(1.0 / jnp.concatenate(sums + [jnp.ones((6, QB), f32)], 0))
    put_out(rows, jnp.where(mask, outs[0] * inv[:, 0:1], outs[1] * inv[:, 1:2]).astype(bf16))


def attend_rows_back(qkv, att, datt, lse, i, first, prod, dk, dv, put_dq):
    length = (i + 1) * QB
    rows = pl.ds(i * QB, QB)
    mask = half_mask(QB)
    mask_all = half_mask(length)
    causal = lax.broadcasted_iota(jnp.int32, (QB, QB), 0) <= lax.broadcasted_iota(
        jnp.int32, (QB, QB), 1
    )
    q = qkv[rows, 0:PAIR] * bf16(HD**-0.5)
    k = qkv[pl.ds(0, length), PAIR : 2 * PAIR]
    v = qkv[pl.ds(0, length), 2 * PAIR : 3 * PAIR]
    do = datt[rows, :]
    dq = None
    for h in range(2):
        qh, dh = pick(mask, h, q), pick(mask, h, do)
        s = mm(k, qh, NT_)
        row = lse[h : h + 1, rows]
        p = jnp.exp(jnp.where(causal, s[length - QB :], NEG) - row)
        if i:
            p = jnp.concatenate([jnp.exp(s[: length - QB] - row), p], 0)
        dp = mm(v, dh, NT_)
        ds = (p * (dp - prod[h : h + 1, rows])).astype(bf16)
        a, b = mm(p.astype(bf16), dh), mm(ds, qh)
        if first and h == 0:
            dv[pl.ds(0, length), :] = a
            dk[pl.ds(0, length), :] = b
        else:
            dv[pl.ds(0, length), :] += a
            dk[pl.ds(0, length), :] += b
        part = mm(ds, pick(mask_all, h, k), TN_)
        dq = part if dq is None else dq + part
    put_dq(rows, (dq * HD**-0.5).astype(bf16))


class Sizes:
    def __init__(self, mesh, tokens, d, slab, ff, experts):
        self.NW, self.NN = mesh.shape["wide"], mesh.shape["narrow"]
        self.A, self.X = self.NW // 2, self.NN // 2
        self.T, self.D, self.slab, self.F, self.E = tokens, d, slab, ff, experts
        self.CW = 3 * PAIR
        self.G = d // PAIR
        self.J = self.G + d // self.CW
        self.R = self.NN * SLOT
        self.S = experts * SLOT
        self.EP = max(8, experts)
        rows = self.NW * self.R
        self.moe = rows * (5 * d + 3 * ff) * 2 < (24 << 20)
        self.fits = (
            self.moe and slab % 8 == 0 and tokens == SEQ and self.NW % 2 == 0 and self.NN % 2 == 0
            and self.NW > 2 and self.NN > 2 and experts == self.NW
        )


def place(c):
    w, n = lax.axis_index("wide"), lax.axis_index("narrow")
    return w, n, w // 2, lax.rem(w, 2), n // 2, lax.rem(n, 2)


def greet(c, w, n):
    bar = pltpu.get_barrier_semaphore()
    x, cc = n // 2, lax.rem(n, 2)

    def wide(i, _):
        pl.semaphore_signal(bar, inc=1, device_id={"wide": lax.rem(w + i, c.NW)}, device_id_type=MESH)
        return 0

    lax.fori_loop(1, c.NW, wide, 0)
    for k in range(1, c.X):
        to = lax.rem(x + k, c.X) * 2 + cc
        pl.semaphore_signal(bar, inc=1, device_id={"narrow": to}, device_id_type=MESH)
        other = w + 1 - 2 * lax.rem(w, 2)
        pl.semaphore_signal(bar, inc=1, device_id={"wide": other, "narrow": to}, device_id_type=MESH)
    pl.semaphore_signal(bar, inc=1, device_id={"narrow": x * 2 + 1 - cc}, device_id_type=MESH)
    return lambda: pl.semaphore_wait(bar, c.NW - 1 + 2 * c.X - 1)


def forward_kernel(c, *refs):
    (v_hbm, dy_hbm, idx_ref, cap_ref, wq_hbm, wo_hbm, cen_ref, g1_ref, g2_ref, up_hbm, down_hbm) = refs[:11]
    (w_out, normt_out, qkv_out, lse_out, att_out, resid_out, meta_out, mrow_out) = refs[11:19]
    (ret_out, outp_out, ug_out, dg_out, cent_out, mine_out) = refs[19:25]
    (v, nrm, normed, normt, oh, wbuf, wmat, wtr, misc, mrow, qkv, lse, att, sent, sendx, senddy,
     up, down, xin, dyin, hid, dpre, dexp, outp, part, lc, lx, stage, cent,
     lsem, in_sem, out_sem, w_sem, q_sem, st_sem, s1s, s1r, s2s, s2r, s4s, s4r,
     ds_, dr, xs_, xr, cs_, cr, fs, fr, gs, gr, ks, kr, rs_, rr, ws_, wr) = refs[25:]
    A, X, NW, NN, T, D, CW, G, J = c.A, c.X, c.NW, c.NN, c.T, c.D, c.CW, c.G, c.J
    w, n, a, b, x, cc = place(c)
    own = (a, b, x, cc)
    dy = sent

    for j in range(J):
        dst = wbuf.at[(j, *own)]
        if j < G:
            for p in range(3):
                pltpu.make_async_copy(
                    wq_hbm.at[:, pl.ds(p * D + j * PAIR, PAIR)], dst.at[:, pl.ds(p * PAIR, PAIR)], lsem.at[j]
                ).start()
        else:
            pltpu.make_async_copy(wo_hbm.at[:, pl.ds((j - G) * CW, CW)], dst, lsem.at[j]).start()
    loads = [(dy_hbm, dy), (v_hbm, v), (up_hbm.at[0], up), (down_hbm.at[0], down)]
    for i, (s, d) in enumerate(loads):
        pltpu.make_async_copy(s, d, in_sem.at[i]).start()

    def load_wait(i):
        wait_bytes(loads[i][1], in_sem.at[i])

    met = greet(c, w, n)

    pad = LANES - c.slab
    small = jnp.concatenate(
        [cen_ref[...].astype(f32), jnp.zeros((GAIN1 - c.E, c.slab), f32), g1_ref[...].astype(f32), g2_ref[...].astype(f32)], 0
    )
    small = jnp.concatenate([small, jnp.zeros((LANES, pad), f32)], 1)
    small = jnp.transpose(small)[0 : c.slab]
    mine_out[...] = small
    misc[own] = small.astype(bf16)

    hot = (lax.broadcasted_iota(jnp.int32, (c.EP, T), 0) == idx_ref[...]).astype(f32)
    lane = lax.broadcasted_iota(jnp.int32, (c.EP, T), 1)
    count = hot
    shift = 1
    while shift < T:
        count = count + jnp.where(lane >= shift, pltpu.roll(count, shift, 1), 0.0)
        shift *= 2
    rank = jnp.sum((count - hot) * hot, 0, keepdims=True)
    ceiling = jnp.zeros((1, T), f32)
    for e in range(c.E):
        ceiling = ceiling + hot[e : e + 1, :] * cap_ref[e].astype(f32)
    kept = rank < ceiling
    slot = jnp.where(kept, idx_ref[...].astype(f32) * SLOT + rank, -1.0)

    met()

    def buf(j):
        return misc if isinstance(j, int) and j == J else wbuf.at[j]

    def s1(j):
        if not (isinstance(j, int) and j == J):
            wait_bytes(buf(j).at[own], lsem.at[j])
        for k in range(1, A):
            push(buf(j).at[own], buf(j).at[own], s1s.at[j], s1r.at[j], wide=lax.rem(a + k, A) * 2 + b)

    plane = [(p, q) for p in range(2) for q in range(X) if p or q]


    def s2_short(j):
        arrive(buf(j).at[pl.ds(0, A - 1), b, x, cc], s1r.at[j])
        mine = buf(j).at[:, b, x, cc]
        for i, (p, q) in enumerate(plane):
            push(
                mine, mine, s2s.at[j, i], s2r.at[j, i],
                wide=a * 2 + lax.rem(b + p, 2), narrow=lax.rem(x + q, X) * 2 + cc,
            )

    def s2_long(j):
        arrive(buf(j).at[pl.ds(0, A - 1), b, x, cc], s1r.at[j])
        mine = buf(j).at[:, b, x, cc]
        for q in range(1, X):
            push(mine, mine, s2s.at[j, q], s2r.at[j, q], narrow=lax.rem(x + q, X) * 2 + cc)

    def s3_long(j):
        for q in range(1, X):
            arrive(buf(j).at[:, b, x, cc], s2r.at[j, q])
        mine = buf(j).at[:, b, :, cc]
        push(mine, mine, s2s.at[j, 0], s2r.at[j, 0], wide=a * 2 + 1 - b)

    def plane_short(j, sem):
        for i in range(len(plane)):
            arrive(buf(j).at[:, b, x, cc], sem.at[j, i])

    def plane_long(j, sem):
        arrive(buf(j).at[:, b, :, cc], sem.at[j, 0])

    def to_core(j):
        mine = buf(j).at[:, :, :, cc]
        push(mine, mine, s4s.at[j], s4r.at[j], narrow=x * 2 + 1 - cc)

    def s4_short(j):
        plane_short(j, s2r)
        to_core(j)

    def s4_long(j):
        plane_long(j, s2r)
        to_core(j)

    def take(j):
        arrive(buf(j).at[:, :, :, cc], s4r.at[j])
        val = wbuf[j].reshape(D, CW)
        wmat[j] = val
        wtr[j] = jnp.transpose(val)
        pltpu.make_async_copy(wtr.at[j], w_out.at[j], w_sem.at[j]).start()

    s1(J)
    s1(0)
    oh[...] = (lax.broadcasted_iota(jnp.int32, (c.S, T), 0).astype(f32) == slot).astype(bf16)
    s1(1)
    s2_short(J)
    s1(3)
    s2_short(0)
    s1(2)
    s1(4)
    load_wait(0)
    senddy[...] = mm(oh[...], dy[...]).astype(bf16)
    s2_short(1)
    s2_long(3)
    s1(5)

    def dy_w(k):
        to = lax.rem(w + k, NW)
        push(senddy.at[pl.ds(pl.multiple_of(to * SLOT, SLOT), SLOT)], dyin.at[w, x, cc], ds_.at[k], dr.at[k], wide=to)

    def dy_x(k):
        src = lax.rem(w - k + NW, NW)

        @pl.when(k > 0)
        def _():
            arrive(dyin.at[src, x, cc], dr.at[k])

        for q in range(1, X):
            push(dyin.at[src, x, cc], dyin.at[src, x, cc], xs_.at[k], xr.at[k], narrow=lax.rem(x + q, X) * 2 + cc)

    dyin[w, x, cc] = senddy[pl.ds(pl.multiple_of(w * SLOT, SLOT), SLOT), :]
    load_wait(1)

    def norm1(i, _):
        rows = pl.ds(i * 128, 128)
        nrm[rows, :] = layer_stats(v[rows, :].astype(f32))[0]
        return 0

    lax.fori_loop(0, T // 128, norm1, 0)
    s4_short(J)
    s4_short(0)
    s2_short(2)
    s2_long(4)
    s1(6)
    arrive(misc.at[:, :, :, cc], s4r.at[J])
    mrow[...] = jnp.transpose(misc[...].reshape(D, LANES).astype(f32))
    gain1 = mrow[GAIN1 : GAIN1 + 1, :]
    gain2 = mrow[GAIN2 : GAIN2 + 1, :]
    pltpu.make_async_copy(mrow, mrow_out, out_sem.at[0]).start()

    def norm1b(i, _):
        rows = pl.ds(i * 128, 128)
        normed[rows, :] = (nrm[rows, :] * gain1).astype(bf16)
        return 0

    lax.fori_loop(0, T // 128, norm1b, 0)
    per = -(-NW // 4)

    def pair(g, _):
        slot_ = lax.rem(g, 2)
        take(g)

        @pl.when(g >= 2)
        def _():
            wait_bytes(qkv.at[slot_], q_sem.at[slot_])

        qkv[slot_] = mm(normed[...], wmat[g]).astype(bf16)
        pltpu.make_async_copy(qkv.at[slot_], qkv_out.at[g], q_sem.at[slot_]).start()

        @pl.when(g + 1 < SHORT)
        def _():
            s4_short(g + 1)

        @pl.when(g + 1 >= SHORT)
        def _():
            s4_long(g + 1)

        @pl.when(g + SHORT < J)
        def _():
            s3_long(g + SHORT)

        @pl.when(g + SHORT + 2 < J)
        def _():
            s2_long(g + SHORT + 2)

        @pl.when(g + SHORT + 4 < J)
        def _():
            s1(g + SHORT + 4)

        def put_out(rows, val):
            att[rows, pl.ds(pl.multiple_of(g * PAIR, PAIR), PAIR)] = val

        def put_lse(h, rows, val):
            lse[g, h : h + 1, rows] = val

        for i in range(T // QB):
            if i == T // QB - 1:
                for q in range(per):
                    k = g * per + q

                    @pl.when((k >= 1) & (k < NW))
                    def _():
                        dy_w(k)

                    @pl.when((g >= 2) & (k - 2 * per < NW))
                    def _():
                        dy_x(k - 2 * per)

            attend_rows(qkv.at[slot_], T, i, put_out, put_lse)
        return 0

    lax.fori_loop(0, G, pair, 0)
    pltpu.make_async_copy(lse, lse_out, out_sem.at[1]).start()
    pltpu.make_async_copy(att, att_out, out_sem.at[2]).start()
    for j in range(G + 1, J):
        s4_long(j)
    for j in range(G, J):
        take(j)

    for j in range(G, J):
        at = slice((j - G) * CW, (j - G + 1) * CW)
        nrm[:, at] = v[:, at].astype(f32) + mm(att[...], wmat[j])

    def tail(i, _):
        rows = pl.ds(i * QB, QB)
        sent[rows, :] = (layer_stats(nrm[rows, :])[0] * gain2).astype(bf16)
        return 0

    lax.fori_loop(0, T // QB, tail, 0)
    pltpu.make_async_copy(nrm, resid_out, out_sem.at[3]).start()
    sendx[...] = mm(oh[...], sent[...]).astype(bf16)

    def x_w(k):
        to = lax.rem(w + k, NW)
        push(sendx.at[pl.ds(pl.multiple_of(to * SLOT, SLOT), SLOT)], xin.at[w, x, cc], fs.at[k], fr.at[k], wide=to)

    for k in range(1, AHEAD_W):
        x_w(k)
    xin[w, x, cc] = sendx[pl.ds(pl.multiple_of(w * SLOT, SLOT), SLOT), :]

    crow = mrow[pl.ds(w, 1), :]

    def source(i):
        return lax.rem(w - i + NW, NW)

    def fwd_x(i):
        src = source(i)

        @pl.when(i > 0)
        def _():
            arrive(xin.at[src, x, cc], fr.at[i])

        for k in range(1, X):
            push(xin.at[src, x, cc], xin.at[src, x, cc], gs.at[i], gr.at[i], narrow=lax.rem(x + k, X) * 2 + cc)

    def fwd_c(i):
        src = source(i)
        arrive(xin.at[src, pl.ds(0, X - 1), cc], gr.at[i])
        push(xin.at[src, :, cc], xin.at[src, :, cc], ks.at[i], kr.at[i], narrow=x * 2 + 1 - cc)

    def expert(i):
        src = source(i)
        arrive(xin.at[src, :, cc], kr.at[i])
        xb = xin[src].reshape(c.R, D)
        db = dyin[src].reshape(c.R, D)
        xf, df = xb.astype(f32), db.astype(f32)
        s = jax.nn.sigmoid(jnp.sum(xf * crow, 1, keepdims=True))
        de = (df * s).astype(bf16)
        pre = mm(xb, up[...])
        cdf = 0.5 * (1.0 + lax.erf(pre * 0.7071067811865476))
        hb = (pre * cdf).astype(bf16)
        slope = cdf + pre * (jnp.exp(-0.5 * pre * pre) * 0.3989422804014327)
        dpb = (mm(de, down[...]) * slope).astype(bf16)
        out = mm(hb, down[...], NT_)
        dl = jnp.sum(df * out, 1, keepdims=True) * (s * (1.0 - s))
        dn = mm(dpb, up[...], NT_) + dl * crow
        part[src] = dn.astype(bf16).reshape(X, 2, SLOT, D)
        outp[src] = out.astype(bf16).reshape(X, 2, SLOT, D)
        cent[...] += jnp.broadcast_to(jnp.sum(dl * xf, 0, keepdims=True), cent.shape)
        rows = pl.ds(pl.multiple_of(src * c.R, SLOT), c.R)
        hid[rows, :] = hb
        dpre[rows, :] = dpb
        dexp[rows, :] = de

    def ret_c(i):
        src = source(i)
        push(part.at[src, :, 1 - cc], lc.at[src], rs_.at[0, i], rr.at[0, i], narrow=x * 2 + 1 - cc)

    def ret_x(i):
        src = source(i)
        arrive(lc.at[src], rr.at[0, i])
        part[src, :, cc] = (part[src, :, cc].astype(f32) + lc[src].astype(f32)).astype(bf16)
        for k in range(1, X):
            x2 = lax.rem(x + k, X)
            push(part.at[src, x2, cc], lx.at[src, x], rs_.at[1, i], rr.at[1, i], narrow=x2 * 2 + cc)

    def ret_w(i):
        src = source(i)
        arrive(lx.at[src, pl.ds(0, X - 1)], rr.at[1, i])
        total = part[src, x, cc].astype(f32)
        for k in range(1, X):
            total = total + lx[src, lax.rem(x + k, X)].astype(f32)
        part[src, x, cc] = total.astype(bf16)

        @pl.when(i > 0)
        def _():
            push(part.at[src, x, cc], ret_out.at[w], ws_.at[i], wr.at[i], wide=src)

        @pl.when(i == 0)
        def _():
            pltpu.make_async_copy(part.at[src, x, cc], ret_out.at[w], ws_.at[0]).start()

    fwd_x(0)
    normt[...] = jnp.transpose(normed[...])
    pltpu.make_async_copy(normt, normt_out, out_sem.at[5]).start()
    for k in range(per * (G - 2), NW):
        dy_x(k)

    logits = mm(mrow[0 : c.EP, :].astype(bf16), sent[...], NT_)
    gate = jax.nn.sigmoid(jnp.sum(logits * hot, 0, keepdims=True)) * kept.astype(f32)
    meta_out[...] = jnp.concatenate([slot, gate, jnp.zeros((6, T), f32)], 0)
    cent[...] = jnp.zeros_like(cent)

    def dy_all(k, _):
        arrive(dyin.at[w, x, cc], xr.at[k])
        return 0

    for q in range(X - 1):
        lax.fori_loop(0, NW, dy_all, 0)
    push(dyin.at[:, :, cc], dyin.at[:, :, cc], cs_, cr, narrow=x * 2 + 1 - cc)
    fwd_c(0)
    for k in range(1, AHEAD_X):
        fwd_x(k)
    load_wait(2)
    load_wait(3)
    arrive(dyin.at[:, :, cc], cr)

    def block(i, _):
        @pl.when(i + AHEAD_W < NW)
        def _():
            x_w(i + AHEAD_W)

        @pl.when(i + 1 < NW)
        def _():
            fwd_c(i + 1)

        @pl.when(i + AHEAD_X < NW)
        def _():
            fwd_x(i + AHEAD_X)

        expert(i)
        ret_c(i)

        @pl.when(i >= 1)
        def _():
            ret_x(i - 1)

        @pl.when(i >= BEHIND_W)
        def _():
            ret_w(i - BEHIND_W)

        return 0

    lax.fori_loop(0, NW, block, 0)
    ret_x(NW - 1)
    for i in range(NW - BEHIND_W, NW - 1):
        ret_w(i)
    pltpu.make_async_copy(outp, outp_out, out_sem.at[4]).start()
    cent_out[...] = cent[...]
    parts = D // QB

    def grads(lhs, rhs, out, second):
        def one_block(i, _):
            at = pl.ds(pl.multiple_of(i * QB, QB), QB)
            if second:
                wait_bytes(stage.at[i], st_sem.at[i])
            stage[i] = mm(lhs(at), rhs[...], TN_)
            pltpu.make_async_copy(stage.at[i], out.at[0, at], st_sem.at[i]).start()
            return 0

        lax.fori_loop(0, parts, one_block, 0)

    grads(lambda at: dexp[:, at], hid, dg_out, False)
    ret_w(NW - 1)
    grads(lambda at: xin[:, :, :, :, at].reshape(NW * c.R, QB), dpre, ug_out, True)

    for q, ref in enumerate([mrow, lse, att, nrm, outp, normt]):
        wait_bytes(ref, out_sem.at[q])
    for q in range(2):
        wait_bytes(qkv.at[q], q_sem.at[q])
    for j in [J] + list(range(J)):
        if not (isinstance(j, int) and j == J):
            wait_bytes(wtr.at[j], w_sem.at[j])
        arrive(buf(j).at[pl.ds(0, A - 1), b, x, cc], s1s.at[j])
        if j == J or j < SHORT:
            plane_short(j, s2s)
        else:
            plane_long(j, s2s)
            for q in range(1, X):
                arrive(buf(j).at[:, b, x, cc], s2s.at[j, q])
        arrive(buf(j).at[:, :, :, cc], s4s.at[j])
    arrive(dyin.at[:, :, cc], cs_)

    def drain(i, _):
        src = source(i)
        arrive(xin.at[src, pl.ds(0, X - 1), cc], xs_.at[i])
        arrive(xin.at[src, pl.ds(0, X - 1), cc], gs.at[i])
        arrive(xin.at[src, :, cc], ks.at[i])
        arrive(lc.at[src], rs_.at[0, i])
        arrive(lx.at[src, pl.ds(0, X - 1)], rs_.at[1, i])

        @pl.when(i > 0)
        def _():
            arrive(xin.at[src, x, cc], ds_.at[i])
            arrive(xin.at[src, x, cc], fs.at[i])
            arrive(xin.at[src, x, cc], ws_.at[i])
            arrive(xin.at[src, x, cc], wr.at[i])

        return 0

    lax.fori_loop(0, NW, drain, 0)
    wait_bytes(part.at[0, 0, 0], ws_.at[0])
    for i in range(parts):
        wait_bytes(stage.at[i], st_sem.at[i])


def forward_call(c, v, dy, idx, cap, wq, wo, cen, g1, g2, up, down):
    T, D, CW, G, J, NW, NN, A, X, L, F = c.T, c.D, c.CW, c.G, c.J, c.NW, c.NN, c.A, c.X, c.slab, c.F
    any_ = pl.BlockSpec(memory_space=pl.ANY)
    vm = pl.BlockSpec(memory_space=pltpu.VMEM)
    sm = pl.BlockSpec(memory_space=pltpu.SMEM)
    sds = jax.ShapeDtypeStruct
    rows_ = (NW, X, 2, SLOT, D)
    outs = [
        (sds((J, CW, D), bf16), any_),
        (sds((D, T), bf16), any_),
        (sds((G, T, CW), bf16), any_),
        (sds((G, 8, T), f32), any_),
        (sds((T, D), bf16), any_),
        (sds((T, D), f32), any_),
        (sds((8, T), f32), vm),
        (sds((LANES, D), f32), any_),
        (sds((NW, SLOT, D), bf16), any_),
        (sds(rows_, bf16), any_),
        (sds((1, D, F), f32), any_),
        (sds((1, D, F), f32), any_),
        (sds((8, D), f32), vm),
        (sds((L, LANES), f32), vm),
    ]
    dma, V = pltpu.SemaphoreType.DMA, pltpu.VMEM
    rows = NW * c.R
    scratch = [
        V((T, D), bf16), V((T, D), f32), V((T, D), bf16), V((D, T), bf16), V((c.S, T), bf16),
        V((J, A, 2, X, 2, L, CW), bf16), V((J, D, CW), bf16), V((J, CW, D), bf16), V((A, 2, X, 2, L, LANES), bf16), V((LANES, D), f32),
        V((2, T, CW), bf16), V((G, 8, T), f32), V((T, D), bf16), V((T, D), bf16), V((c.S, D), bf16), V((c.S, D), bf16),
        V((D, F), bf16), V((D, F), bf16), V(rows_, bf16), V(rows_, bf16),
        V((rows, F), bf16), V((rows, F), bf16), V((rows, D), bf16), V(rows_, bf16), V(rows_, bf16),
        V((NW, X, SLOT, D), bf16), V((NW, X, SLOT, D), bf16), V((D // QB, QB, F), f32), V((8, D), f32),
        dma((J,)), dma((4,)), dma((6,)), dma((J,)), dma((2,)), dma((D // QB,)),
    ] + [dma((J + 1,))] * 2 + [dma((J + 1, 2 * X - 1))] * 2 + [dma((J + 1,))] * 2 + [dma((NW,))] * 4 + [dma(()), dma(())] + [dma((NW,))] * 6 + [
        dma((2, NW)), dma((2, NW)), dma((NW,)), dma((NW,)),
    ]
    return pl.pallas_call(
        functools.partial(forward_kernel, c),
        out_shape=tuple(o[0] for o in outs),
        in_specs=[any_, any_, vm, sm, any_, any_, vm, vm, vm, any_, any_],
        out_specs=tuple(o[1] for o in outs),
        scratch_shapes=scratch,
        compiler_params=pltpu.CompilerParams(
            collective_id=CID0, has_side_effects=True, vmem_limit_bytes=VMEM_CAP
        ),
        name="forward",
    )(v, dy, idx, cap, wq, wo, cen, g1, g2, up, down)


def backward_kernel(c, *refs):
    (v_hbm, dy_hbm, qkv_hbm, lse_hbm, att_hbm, resid_hbm, wt_hbm, nt_hbm, ret_hbm, outp_hbm, mrow, meta, cent, wq, mine) = refs[:15]
    (mixed_out, tok_out, qg_out, og_out, small_out) = refs[15:20]
    (v, dy, qkv, lse, att, resid, wt, ret, oh, normt, dbr, datt, dnm, dqkv, dk, dv, prod, rowbuf,
     part, lc, lx, got, mixed,
     gb, la, lb, lz, sgb, sla, slb, slz,
     in_sem, q_sem, out_sem, os_, orv, ows, owr, rs_, rr, ps_, pr, tokacc) = refs[20:]
    A, X, NW, NN, T, D, CW, G, J = c.A, c.X, c.NW, c.NN, c.T, c.D, c.CW, c.G, c.J
    H = J - G
    w, n, a, b, x, cc = place(c)
    blocks = T // QB

    loads = [
        (ret_hbm, ret), (resid_hbm, resid), (dy_hbm, dy), (att_hbm, att), (v_hbm, v), (lse_hbm, lse), (nt_hbm, normt),
        (wt_hbm.at[pl.ds(G, H)], wt.at[pl.ds(G, H)]), (wt_hbm.at[pl.ds(0, G)], wt.at[pl.ds(0, G)]),
    ]
    for i, (s, d) in enumerate(loads):
        pltpu.make_async_copy(s, d, in_sem.at[i]).start()
    own_part = pltpu.make_async_copy(outp_hbm.at[:, :, cc], part, in_sem.at[9])
    own_part.start()

    def load_wait(i):
        wait_bytes(loads[i][1], in_sem.at[i])

    def fetch_qkv(g, slot_):
        pltpu.make_async_copy(qkv_hbm.at[g], qkv.at[slot_], q_sem.at[1, slot_]).start()

    fetch_qkv(0, 0)
    met = greet(c, w, n)

    slot, gate = meta[0:1, :], meta[1:2, :]
    hits = lax.broadcasted_iota(jnp.int32, (c.S, T), 0).astype(f32) == slot
    oh[...] = hits.astype(bf16)
    gain1, gain2 = mrow[GAIN1 : GAIN1 + 1, :], mrow[GAIN2 : GAIN2 + 1, :]
    load_wait(0)
    dnm[...] = mm(oh[...], ret[...].reshape(c.S, D), TN_)
    oh[...] = jnp.where(hits, gate, 0.0).astype(bf16)
    met()
    push(outp_hbm.at[:, :, 1 - cc], lc, os_.at[0], orv.at[0], narrow=x * 2 + 1 - cc)
    load_wait(1)
    load_wait(2)
    rowbuf[...] = jnp.zeros_like(rowbuf)
    rowbuf[pl.ds(w, 1), :] = cent[0:1, :]

    def norm2_back(i, acc):
        rows = pl.ds(i * QB, QB)
        n2, r2 = layer_stats(resid[rows, :])
        dn2 = dnm[rows, :]
        dn = dn2 * gain2
        step = r2 * (dn - jnp.mean(dn, 1, keepdims=True) - n2 * jnp.mean(dn * n2, 1, keepdims=True))
        dres = dy[rows, :].astype(f32) + step
        dnm[rows, :] = dres
        dbr[rows, :] = dres.astype(bf16)
        return acc + jnp.sum(dn2 * n2, 0, keepdims=True)

    rowbuf[GAIN2 : GAIN2 + 1, :] = lax.fori_loop(0, blocks, norm2_back, jnp.zeros((1, D), f32))
    load_wait(3)

    big = (gb, la, lb, lz, 0)
    tiny = (sgb, sla, slb, slz, J)

    def add(p, q):
        return (p.astype(f32) + q.astype(f32)).astype(bf16)

    def ra(t, j):
        push(t[0].at[j, :, :, :, 1 - cc], t[1].at[j], rs_.at[0, t[4] + j], rr.at[0, t[4] + j], narrow=x * 2 + 1 - cc)

    plane = [(p, q) for p in range(2) for q in range(X) if p or q]

    def rb(t, j):
        arrive(t[1].at[j], rr.at[0, t[4] + j])
        t[0][j, :, :, :, cc] = add(t[0][j, :, :, :, cc], t[1][j])
        for i, (p, q) in enumerate(plane):
            b2, x2 = lax.rem(b + p, 2), lax.rem(x + q, X)
            push(
                t[0].at[j, :, b2, x2, cc], t[2].at[j, b, x], ps_.at[t[4] + j, i], pr.at[t[4] + j, i],
                wide=a * 2 + b2, narrow=x2 * 2 + cc,
            )

    def plane_bytes(t, j, sem):
        for i in range(len(plane)):
            arrive(t[2].at[j, 0, 0], sem.at[t[4] + j, i])

    def rc(t, j):
        plane_bytes(t, j, pr)
        total = t[0][j, :, b, x, cc].astype(f32)
        for p, q in plane:
            total = total + t[2][j, lax.rem(b + p, 2), lax.rem(x + q, X)].astype(f32)
        t[0][j, :, b, x, cc] = total.astype(bf16)
        for k in range(1, A):
            a2 = lax.rem(a + k, A)
            push(t[0].at[j, a2, b, x, cc], t[3].at[j, a], rs_.at[1, t[4] + j], rr.at[1, t[4] + j], wide=a2 * 2 + b)

    def rf(t, j):
        arrive(t[3].at[j, pl.ds(0, A - 1)], rr.at[1, t[4] + j])
        total = t[0][j, a, b, x, cc].astype(f32)
        for k in range(1, A):
            total = total + t[3][j, lax.rem(a + k, A)].astype(f32)
        return total

    def rf_w(j):
        og_out[:, j * CW : (j + 1) * CW] = rf(big, j)

    def rf_q(g):
        total = rf(big, H + g)
        for p in range(3):
            qg_out[:, pl.ds(pl.multiple_of(p * D + g * PAIR, PAIR), PAIR)] = total[:, p * PAIR : (p + 1) * PAIR]

    sgb[0] = jnp.transpose(rowbuf[...]).astype(bf16).reshape(A, 2, X, 2, c.slab, LANES)
    ra(tiny, 0)
    for h in range(H):
        gb[h] = mm(att[...], dbr[:, h * CW : (h + 1) * CW], TN_).astype(bf16).reshape(A, 2, X, 2, c.slab, CW)
        ra(big, h)

    load_wait(7)

    def out_back(i, _):
        at = pl.ds(pl.multiple_of(i * QB, QB), QB)
        datt[:, at] = mm(dbr[...], wt[pl.ds(G, H), :, at].reshape(D, QB)).astype(bf16)
        return 0

    lax.fori_loop(0, D // QB, out_back, 0)
    load_wait(4)
    load_wait(6)
    rb(tiny, 0)
    for h in range(H):
        rb(big, h)
    load_wait(5)
    own_part.wait()
    rc(tiny, 0)

    def o_x(i):
        for k in range(1, X):
            x2 = lax.rem(x + k, X)
            push(part.at[i, x2], lx.at[i, x], os_.at[1 + i], orv.at[1 + i], narrow=x2 * 2 + cc)

    def o_w(i):
        arrive(lx.at[i, pl.ds(0, X - 1)], orv.at[1 + i])
        total = part[i, x].astype(f32)
        for k in range(1, X):
            total = total + lx[i, lax.rem(x + k, X)].astype(f32)
        part[i, x] = total.astype(bf16)

        @pl.when(i != w)
        def _():
            push(part.at[i, x], got.at[w], ows.at[i], owr.at[lax.rem(w - i + NW, NW)], wide=i)

        @pl.when(i == w)
        def _():
            got[w] = part[w, x]

    arrive(lc, orv.at[0])

    def merge(i, _):
        part[i] = add(part[i], lc[i])
        return 0

    lax.fori_loop(0, NW, merge, 0)
    per = -(-NW // 4)

    def spread(fn, step):
        for k in range(per):
            i = lax.rem(w + step * per + k, NW)

            @pl.when(step * per + k < NW)
            def _():
                fn(i)

    def pair(g, _):
        s_ = lax.rem(g, 2)

        @pl.when(g + 1 < G)
        def _():
            fetch_qkv(g + 1, 1 - s_)

        wait_bytes(qkv.at[s_], q_sem.at[1, s_])
        lanes = pl.ds(pl.multiple_of(g * PAIR, PAIR), PAIR)
        att_g, datt_g = att.at[:, lanes], datt.at[:, lanes]
        full = jnp.transpose(datt_g[...].astype(f32) * att_g[...].astype(f32))
        prod[0:1, :] = jnp.sum(full[0:HD], 0, keepdims=True)
        prod[1:2, :] = jnp.sum(full[HD:], 0, keepdims=True)

        def put_dq(rows, val):
            dqkv[g, rows, 0:PAIR] = val

        for i in reversed(range(blocks)):
            if i == 0:
                rc(big, g + H - 2)
            attend_rows_back(qkv.at[s_], att_g, datt_g, lse.at[g], i, i == blocks - 1, prod, dk, dv, put_dq)
            if i == blocks - 1:
                @pl.when(g >= 1)
                def _():
                    rb(big, g + H - 1)

                @pl.when(g < 4)
                def _():
                    spread(o_x, g)

                @pl.when(g >= 2)
                def _():
                    spread(o_w, g - 2)

        dqkv[g, :, PAIR : 2 * PAIR] = dk[...].astype(bf16)
        dqkv[g, :, 2 * PAIR :] = dv[...].astype(bf16)
        gb[H + g] = mm(normt[...], dqkv[g]).astype(bf16).reshape(A, 2, X, 2, c.slab, CW)
        ra(big, H + g)
        return 0

    lax.fori_loop(0, G, pair, 0)
    load_wait(8)

    def back(i):
        at = slice(i * QB, (i + 1) * QB)
        total = mm(dqkv[0], wt[0, :, at])
        for g in range(1, G):
            total = total + mm(dqkv[g], wt[g, :, at])
        tokacc[:, at] = total

    back(0)
    rb(big, J - 1)
    rc(big, J - 2)
    for i in range(1, D // QB):
        back(i)
    def norm1_back(i, _):
        rows = pl.ds(i * QB, QB)
        n1, r1 = layer_stats(v[rows, :].astype(f32))
        dm = tokacc[rows, :] * gain1
        step = r1 * (dm - jnp.mean(dm, 1, keepdims=True) - n1 * jnp.mean(dm * n1, 1, keepdims=True))
        dnm[rows, :] = dnm[rows, :] + step
        return 0

    lax.fori_loop(0, blocks, norm1_back, 0)
    tok_copy = pltpu.make_async_copy(dnm, tok_out, out_sem.at[0])
    tok_copy.start()
    rc(big, J - 1)

    def o_wait(k, _):
        arrive(got.at[0], owr.at[k])
        return 0

    lax.fori_loop(1, NW, o_wait, 0)

    def mix(i, _):
        cols = pl.ds(pl.multiple_of(i * QB, QB), QB)
        rows = pl.ds(i * QB, QB)
        mixed[rows, :] = (resid[rows, :] + mm(oh[:, cols], got[...].reshape(c.S, D), TN_)).astype(bf16)
        return 0

    lax.fori_loop(0, blocks, mix, 0)
    mix_copy = pltpu.make_async_copy(mixed, mixed_out, out_sem.at[1])
    mix_copy.start()
    for h in range(H):
        rf_w(h)

    def fin(g, _):
        rf_q(g)
        return 0

    lax.fori_loop(0, G, fin, 0)
    sums_ = jnp.sum(qg_out[...] * wq[...].astype(f32), 1, keepdims=True) / mine[:, GAIN1 : GAIN1 + 1]
    at_gain = lax.broadcasted_iota(jnp.int32, (c.slab, LANES), 1) == GAIN1
    small_out[...] = jnp.where(at_gain, sums_, rf(tiny, 0))

    arrive(lc, os_.at[0])

    def drain(i, _):
        arrive(lx.at[i, pl.ds(0, X - 1)], os_.at[1 + i])

        @pl.when(i != w)
        def _():
            arrive(got.at[0], ows.at[i])

        return 0

    lax.fori_loop(0, NW, drain, 0)

    def drain_sums(t, j):
        arrive(t[1].at[j], rs_.at[0, t[4] + j])
        plane_bytes(t, j, ps_)
        arrive(t[3].at[j, pl.ds(0, A - 1)], rs_.at[1, t[4] + j])

    def drain_big(j, _):
        drain_sums(big, j)
        return 0

    lax.fori_loop(0, J, drain_big, 0)
    drain_sums(tiny, 0)
    tok_copy.wait()
    mix_copy.wait()


def backward_call(c, v, dy, qkv, lse, att, resid, wt, nt, ret, outp, mrow, meta, cent, wq, mine):
    T, D, CW, G, J, NW, NN, A, X, L = c.T, c.D, c.CW, c.G, c.J, c.NW, c.NN, c.A, c.X, c.slab
    any_ = pl.BlockSpec(memory_space=pl.ANY)
    vm = pl.BlockSpec(memory_space=pltpu.VMEM)
    sds = jax.ShapeDtypeStruct
    dma, V = pltpu.SemaphoreType.DMA, pltpu.VMEM

    def sums(k, width):
        return [
            V((k, A, 2, X, 2, L, width), bf16), V((k, A, 2, X, L, width), bf16),
            V((k, 2, X, A, L, width), bf16), V((k, A, L, width), bf16),
        ]

    scratch = [
        V((T, D), bf16), V((T, D), bf16), V((2, T, CW), bf16), V((G, 8, T), f32), V((T, D), bf16), V((T, D), f32),
        V((J, CW, D), bf16), V((NW, SLOT, D), bf16), V((c.S, T), bf16),
        V((D, T), bf16), V((T, D), bf16), V((T, D), bf16), V((T, D), f32), V((G, T, CW), bf16),
        V((T, PAIR), f32), V((T, PAIR), f32), V((8, T), f32), V((LANES, D), f32),
        V((NW, X, SLOT, D), bf16), V((NW, X, SLOT, D), bf16), V((NW, X, SLOT, D), bf16), V((NW, SLOT, D), bf16),
        V((T, D), bf16),
    ] + sums(J, CW) + sums(1, LANES) + [
        dma((10,)), dma((2, 2)), dma((2,)), dma((NW + 1,)), dma((NW + 1,)), dma((NW,)), dma((NW,)),
        dma((2, J + 1)), dma((2, J + 1)), dma((J + 1, 2 * X - 1)), dma((J + 1, 2 * X - 1)),
        V((T, D), f32),
    ]
    return pl.pallas_call(
        functools.partial(backward_kernel, c),
        out_shape=(
            sds((T, D), bf16), sds((T, D), f32), sds((L, 3 * D), f32), sds((L, D), f32), sds((L, LANES), f32),
        ),
        in_specs=[any_] * 10 + [vm] * 5,
        out_specs=(any_, any_, vm, vm, vm),
        scratch_shapes=scratch,
        compiler_params=pltpu.CompilerParams(
            collective_id=CID1, has_side_effects=True, vmem_limit_bytes=VMEM_CAP
        ),
        name="backward",
    )(v, dy, qkv, lse, att, resid, wt, nt, ret, outp, mrow, meta, cent, wq, mine)


def finish_kernel(c, *refs):
    big, small = refs[:6], refs[6]
    outs, (cen_out, g1_out, g2_out) = refs[7:13], refs[13:16]
    bufs, (in_sem, out_sem) = refs[16:22], refs[22:]
    cuts = []
    for i, ref in enumerate(big):
        axis = len(ref.shape) - 2
        size = ref.shape[axis]
        step = QB if size % QB == 0 else size
        for at in range(0, size, step):
            where = (0,) * axis + (pl.ds(at, step),)
            cuts.append((big[i].at[where], bufs[i].at[where], outs[i].at[where]))
    for k, (src, mid, _) in enumerate(cuts):
        pltpu.make_async_copy(src, mid, in_sem.at[k]).start()
    wide_small = jnp.concatenate([small[...], jnp.zeros((LANES - c.slab, LANES), f32)], 0)
    rows = jnp.transpose(wide_small)[:, 0 : c.slab]
    cen_out[...] = rows[0 : c.E]
    g1_out[...] = rows[GAIN1 : GAIN1 + 1]
    g2_out[...] = rows[GAIN2 : GAIN2 + 1]
    for k, (src, mid, dst) in enumerate(cuts):
        pltpu.make_async_copy(src, mid, in_sem.at[k]).wait()
        pltpu.make_async_copy(mid, dst, out_sem.at[k]).start()
    for k, (_, mid, dst) in enumerate(cuts):
        pltpu.make_async_copy(mid, dst, out_sem.at[k]).wait()


def finish_call(c, big, small):
    any_ = pl.BlockSpec(memory_space=pl.ANY)
    vm = pl.BlockSpec(memory_space=pltpu.VMEM)
    sds = jax.ShapeDtypeStruct
    copies = sum(t.shape[-2] // QB if t.shape[-2] % QB == 0 else 1 for t in big)
    return pl.pallas_call(
        functools.partial(finish_kernel, c),
        out_shape=tuple(sds(t.shape, t.dtype) for t in big)
        + (sds((c.E, c.slab), f32), sds((1, c.slab), f32), sds((1, c.slab), f32)),
        in_specs=[any_] * 6 + [vm],
        out_specs=(any_,) * 6 + (vm,) * 3,
        scratch_shapes=[pltpu.VMEM(t.shape, t.dtype) for t in big]
        + [pltpu.SemaphoreType.DMA((copies,)), pltpu.SemaphoreType.DMA((copies,))],
        compiler_params=pltpu.CompilerParams(vmem_limit_bytes=VMEM_CAP),
        name="finish",
    )(*big, small)


precise = lax.Precision.HIGHEST
over_rows = (((0,), (0,)), ((), ()))
over_cols = (((1,), (1,)), ((), ()))


def layer_norm(tensor, gain_vec):
    centered = tensor - jnp.mean(tensor, -1, keepdims=True)
    spread = jnp.mean(centered * centered, -1, keepdims=True)
    return centered * lax.rsqrt(spread + 1e-05) * gain_vec


def gelu_exact(tensor):
    return jax.nn.gelu(tensor, approximate=False)


def split_heads(packed):
    seq_len = packed.shape[0]
    model_width = packed.shape[1] // 3
    head_count = model_width // HD
    queries = packed[:, :model_width].reshape(seq_len, head_count, HD)
    key_rows = packed[:, model_width : 2 * model_width].reshape(seq_len, head_count, HD)
    value_rows = packed[:, 2 * model_width :].reshape(seq_len, head_count, HD)
    raw_scores = jnp.einsum(
        "qhd,khd->hqk", queries, key_rows, preferred_element_type=jnp.float32
    ) * HD ** (-0.5)
    places = jnp.arange(seq_len)
    causal = places[:, None] >= places[None, :]
    masked = jnp.where(causal[None], raw_scores, -1e30)
    return (queries, key_rows, value_rows, masked)


def attend_forward(packed):
    queries, key_rows, value_rows, masked = split_heads(packed)
    maxima = jnp.max(masked, -1, keepdims=True)
    powers = jnp.exp(masked - maxima)
    totals = jnp.sum(powers, -1, keepdims=True)
    attn_probs = (powers / totals).astype(jnp.bfloat16)
    attended = jnp.einsum(
        "hqk,khd->qhd", attn_probs, value_rows, preferred_element_type=jnp.float32
    )
    return (attended.reshape(packed.shape[0], -1).astype(jnp.bfloat16), maxima + jnp.log(totals))


def attend_backward(member):
    packed, upstream, log_totals = member
    queries, key_rows, value_rows, masked = split_heads(packed)
    attn_probs = jnp.exp(masked - log_totals)
    probs_low = attn_probs.astype(jnp.bfloat16)
    grad_out = upstream.reshape(queries.shape)
    grad_probs = jnp.einsum(
        "qhd,khd->hqk", grad_out, value_rows, preferred_element_type=jnp.float32
    )
    grad_values = jnp.einsum(
        "hqk,qhd->khd", probs_low, grad_out, preferred_element_type=jnp.float32
    )
    grad_scores = (
        attn_probs * (grad_probs - jnp.sum(grad_probs * attn_probs, -1, keepdims=True))
    ).astype(jnp.bfloat16)
    factor = HD ** (-0.5)
    grad_queries = (
        jnp.einsum("hqk,khd->qhd", grad_scores, key_rows, preferred_element_type=jnp.float32)
        * factor
    )
    grad_keys = (
        jnp.einsum("hqk,qhd->khd", grad_scores, queries, preferred_element_type=jnp.float32)
        * factor
    )
    seq_len = packed.shape[0]
    joined = jnp.concatenate(
        [
            grad_queries.reshape(seq_len, -1),
            grad_keys.reshape(seq_len, -1),
            grad_values.reshape(seq_len, -1),
        ],
        1,
    )
    return joined.astype(jnp.bfloat16)


def expert_rows(row_block, up_mat, down_mat):
    pre_act = jnp.dot(row_block, up_mat, preferred_element_type=jnp.float32)
    hidden = gelu_exact(pre_act).astype(jnp.bfloat16)
    return lax.dot_general(hidden, down_mat, over_cols, preferred_element_type=jnp.float32)


def expert_grads(row_block, grad_block, up_mat, down_mat):
    pre_act = jnp.dot(row_block, up_mat, preferred_element_type=jnp.float32)
    hidden, gelu_back = jax.vjp(gelu_exact, pre_act)
    hidden_low = hidden.astype(jnp.bfloat16)
    down_part = lax.dot_general(
        grad_block, hidden_low, over_rows, preferred_element_type=jnp.float32
    )
    grad_hidden = jnp.dot(grad_block, down_mat, preferred_element_type=jnp.float32)
    grad_pre = gelu_back(grad_hidden)[0].astype(jnp.bfloat16)
    up_part = lax.dot_general(row_block, grad_pre, over_rows, preferred_element_type=jnp.float32)
    return (grad_pre, up_part, down_part)


def fill_slots(row_vals, target, slot_count):
    buffer = jnp.zeros((slot_count + 1, row_vals.shape[1]), row_vals.dtype).at[target].set(row_vals)
    return buffer[:slot_count]


def read_slots(buffer, target):
    padded = jnp.concatenate([buffer, jnp.zeros((1, buffer.shape[1]), buffer.dtype)], 0)
    return padded[target]


def plain_shards(
    layer_inputs_matrix,
    assignment_indices,
    admitted_counts_matrix,
    mixer_scaling1_factor,
    triple_linear_matrix,
    mixer_exit_matrix,
    specialist_scaling2_factor,
    cluster_mean_columns,
    first_linear_matrix,
    second_linear_matrix,
    incoming_gradient,
):
    gain_one, qkv_mat, out_mat, gain_two, centers = (
        lax.all_gather(mixer_scaling1_factor, ("wide", "narrow"), axis=0, tiled=True),
        lax.all_gather(triple_linear_matrix, ("wide", "narrow"), axis=0, tiled=True),
        lax.all_gather(mixer_exit_matrix, ("wide", "narrow"), axis=0, tiled=True),
        lax.all_gather(specialist_scaling2_factor, ("wide", "narrow"), axis=0, tiled=True),
        lax.all_gather(cluster_mean_columns, ("wide", "narrow"), axis=0, tiled=True),
    )
    gain_one = gain_one.astype(jnp.float32)
    gain_two = gain_two.astype(jnp.float32)
    centers = centers.astype(jnp.float32)
    token_rows = layer_inputs_matrix.astype(jnp.float32)
    tok_count, model_width = layer_inputs_matrix.shape
    seq_count = tok_count // SEQ
    normed, norm1_back = jax.vjp(layer_norm, token_rows, gain_one)
    normed_low = normed.astype(jnp.bfloat16)
    qkv_rows = jnp.dot(normed_low, qkv_mat, preferred_element_type=jnp.float32).astype(jnp.bfloat16)
    packed_seqs = qkv_rows.reshape(seq_count, SEQ, 3 * model_width)
    attended, log_totals = lax.map(attend_forward, packed_seqs)
    attended = attended.reshape(tok_count, model_width)
    residual = token_rows + jnp.dot(attended, out_mat, preferred_element_type=jnp.float32)
    normed_two, norm2_back = jax.vjp(layer_norm, residual, gain_two)
    sent_rows = normed_two.astype(jnp.bfloat16)
    dispatched_items = assignment_indices[:, 0]
    specialist_overall_sum = admitted_counts_matrix.shape[0]
    slot_count = specialist_overall_sum * SLOT
    specialist_indicator = (
        dispatched_items[:, None] == jnp.arange(specialist_overall_sum, dtype=jnp.int32)[None, :]
    ).astype(jnp.int32)
    before = jnp.cumsum(specialist_indicator, 0) - specialist_indicator
    ranked = jnp.sum(before * specialist_indicator, 1)
    position_ceilings = jnp.sum(specialist_indicator * admitted_counts_matrix[None, :], 1)
    retained_couple_filter = ranked < position_ceilings
    target = jnp.where(retained_couple_filter, dispatched_items * SLOT + ranked, slot_count)
    kept_rows = retained_couple_filter.astype(jnp.float32)
    choose = specialist_indicator.astype(jnp.float32)
    send_buf = fill_slots(sent_rows, target, slot_count).reshape(
        specialist_overall_sum, SLOT, model_width
    )
    local_rows = lax.all_to_all(send_buf, "wide", split_axis=0, concat_axis=0, tiled=True).reshape(
        slot_count, model_width
    )
    gathered = lax.all_gather(local_rows, "narrow", axis=0, tiled=True)
    expert_local = lax.psum_scatter(
        expert_rows(gathered, first_linear_matrix[0], second_linear_matrix[0]).astype(jnp.bfloat16),
        "narrow",
        scatter_dimension=0,
        tiled=True,
    )
    returned = lax.all_to_all(
        expert_local.reshape(specialist_overall_sum, SLOT, model_width),
        "wide",
        split_axis=0,
        concat_axis=0,
        tiled=True,
    )
    expert_tok = read_slots(returned.reshape(slot_count, model_width), target).astype(jnp.float32)
    center_rows = lax.dot_general(choose, centers, over_cols, precision=precise)
    logits = jnp.sum(normed_two * center_rows, 1)
    sigma = jax.nn.sigmoid(logits)
    gating = sigma * kept_rows
    mixed = (residual + gating[:, None] * expert_tok).astype(jnp.bfloat16)
    grad_y = incoming_gradient.astype(jnp.float32)
    grad_logit = jnp.sum(grad_y * expert_tok, 1) * sigma * (1.0 - sigma) * kept_rows
    grad_normed = grad_logit[:, None] * center_rows
    centroid_part = lax.dot_general(
        normed_two, choose * grad_logit[:, None], over_rows, precision=precise
    )
    grad_expert = (grad_y * gating[:, None]).astype(jnp.bfloat16)
    grad_buf = fill_slots(grad_expert, target, slot_count).reshape(
        specialist_overall_sum, SLOT, model_width
    )
    grad_local = lax.all_to_all(grad_buf, "wide", split_axis=0, concat_axis=0, tiled=True).reshape(
        slot_count, model_width
    )
    grad_gathered = lax.all_gather(grad_local, "narrow", axis=0, tiled=True)
    grad_pre, up_part, down_part = expert_grads(
        gathered, grad_gathered, first_linear_matrix[0], second_linear_matrix[0]
    )
    input_back = lax.psum_scatter(
        lax.dot_general(
            grad_pre, first_linear_matrix[0], over_cols, preferred_element_type=jnp.float32
        ).astype(jnp.bfloat16),
        "narrow",
        scatter_dimension=0,
        tiled=True,
    )
    up_grad = up_part[None]
    down_grad = down_part[None]
    back_rows = lax.all_to_all(
        input_back.reshape(specialist_overall_sum, SLOT, model_width),
        "wide",
        split_axis=0,
        concat_axis=0,
        tiled=True,
    )
    grad_normed = grad_normed + read_slots(
        back_rows.reshape(slot_count, model_width), target
    ).astype(jnp.float32)
    grad_resid_norm, gain_two_part = norm2_back(grad_normed)
    grad_resid = grad_y + grad_resid_norm
    grad_branch = grad_resid.astype(jnp.bfloat16)
    out_part = lax.dot_general(attended, grad_branch, over_rows, preferred_element_type=jnp.float32)
    grad_attended = lax.dot_general(
        grad_branch, out_mat, over_cols, preferred_element_type=jnp.float32
    ).astype(jnp.bfloat16)
    grad_packed = lax.map(
        attend_backward,
        (packed_seqs, grad_attended.reshape(seq_count, SEQ, model_width), log_totals),
    )
    grad_packed = grad_packed.reshape(tok_count, 3 * model_width)
    qkv_part = lax.dot_general(
        normed_low, grad_packed, over_rows, preferred_element_type=jnp.float32
    )
    grad_normed_one = lax.dot_general(
        grad_packed, qkv_mat, over_cols, preferred_element_type=jnp.float32
    )
    grad_token_norm, gain_one_part = norm1_back(grad_normed_one)
    tokens_grad = grad_resid + grad_token_norm
    gain_one_grad, qkv_grad, out_grad, gain_two_grad, centroid_grad = (
        lax.psum_scatter(gain_one_part, ("wide", "narrow"), scatter_dimension=0, tiled=True),
        lax.psum_scatter(qkv_part, ("wide", "narrow"), scatter_dimension=0, tiled=True),
        lax.psum_scatter(out_part, ("wide", "narrow"), scatter_dimension=0, tiled=True),
        lax.psum_scatter(gain_two_part, ("wide", "narrow"), scatter_dimension=0, tiled=True),
        lax.psum_scatter(centroid_part, ("wide", "narrow"), scatter_dimension=0, tiled=True),
    )
    return (
        mixed,
        tokens_grad,
        gain_one_grad,
        qkv_grad,
        out_grad,
        gain_two_grad,
        centroid_grad,
        up_grad,
        down_grad,
    )


def shards(mesh, v, idx, caps, g1, wq, wo, g2, centers, up, down, dy):
    T, D = v.shape
    E = caps.shape[0]
    c = Sizes(mesh, T, D, wq.shape[0], up.shape[2], E)
    if not c.fits:
        return plain_shards(v, idx, caps, g1, wq, wo, g2, centers, up, down, dy)
    res = forward_call(
        c, v, dy, idx.reshape(1, T), caps, wq, wo, centers.T, g1.reshape(1, -1), g2.reshape(1, -1), up, down
    )
    wt, nt, qkv, lse, att, resid, meta, mrow, ret, outp, ug, dg, cent, mine = res
    mixed, tokens_grad, qg, og, small = backward_call(
        c, v, dy, qkv, lse, att, resid, wt, nt, ret, outp, mrow, meta, cent, wq, mine
    )
    mixed, tokens_grad, qg, og, ug, dg, cen, g1_grad, g2_grad = finish_call(
        c, (mixed, tokens_grad, qg, og, ug, dg), small
    )
    return (
        mixed, tokens_grad, g1_grad.reshape(-1), qg, og, g2_grad.reshape(-1), cen.T, ug, dg,
    )


def solution(mesh):
    both = ("wide", "narrow")
    in_specs = (
        P(both, None), P(both, None), P(), P(both), P(both, None), P(both, None), P(both), P(both, None),
        P("wide", None, "narrow"), P("wide", None, "narrow"), P(both, None),
    )
    out_specs = (
        P(both, None), P(both, None), P(both), P(both, None), P(both, None), P(both), P(both, None),
        P("wide", None, "narrow"), P("wide", None, "narrow"),
    )
    return jax.shard_map(
        functools.partial(shards, mesh), mesh=mesh, in_specs=in_specs, out_specs=out_specs, check_vma=False
    )
```

```python
import functools

import jax
import jax.numpy as jnp
from jax import lax
from jax.experimental import pallas as pl
from jax.experimental.pallas import tpu as pltpu
from jax.sharding import PartitionSpec as P

HD = 64
SEQ = 1024
SLOT = 48
PAIR = 2 * HD
QB = 256
LANES = 128
GAIN1 = 126
GAIN2 = 127
NEG = -1e30
VMEM_CAP = 62 << 20
CID0 = 0
CID1 = 1
AHEAD_W = 5
AHEAD_X = 3
BEHIND_W = 3
SHORT = 3
LAST = 2

MESH = pl.DeviceIdType.MESH
NN_ = (((1,), (0,)), ((), ()))
NT_ = (((1,), (1,)), ((), ()))
TN_ = (((0,), (0,)), ((), ()))
f32 = jnp.float32
bf16 = jnp.bfloat16


def mm(a, b, dims=NN_):
    return lax.dot_general(a, b, dims, preferred_element_type=f32)


def wait_bytes(ref, sem):
    pltpu.make_async_copy(ref, ref, sem).wait()


arrive = wait_bytes


def push(src, dst, send, recv, **where):
    pltpu.make_async_remote_copy(
        src_ref=src, dst_ref=dst, send_sem=send, recv_sem=recv,
        device_id=where, device_id_type=MESH,
    ).start()


def half_mask(rows):
    return lax.broadcasted_iota(jnp.int32, (rows, PAIR), 1) < HD


def pick(mask, h, value):
    zero = jnp.zeros_like(value)
    return jnp.where(mask, value, zero) if h == 0 else jnp.where(mask, zero, value)


def layer_stats(x):
    centered = x - jnp.mean(x, 1, keepdims=True)
    r = lax.rsqrt(jnp.mean(centered * centered, 1, keepdims=True) + 1e-05)
    return centered * r, r


def attend_rows(qkv, seq, i, put_out, put_lse):
    length = (i + 1) * QB
    rows = pl.ds(i * QB, QB)
    mask = half_mask(QB)
    causal = lax.broadcasted_iota(jnp.int32, (QB, QB), 0) <= lax.broadcasted_iota(
        jnp.int32, (QB, QB), 1
    )
    q = qkv[rows, 0:PAIR] * bf16(HD**-0.5)
    k = qkv[pl.ds(0, length), PAIR : 2 * PAIR]
    v = qkv[pl.ds(0, length), 2 * PAIR : 3 * PAIR]
    outs, sums = [], []
    for h in range(2):
        s = mm(k, pick(mask, h, q), NT_)
        last = jnp.where(causal, s[length - QB :], NEG)
        top = jnp.max(last, 0, keepdims=True)
        if i:
            top = jnp.maximum(top, jnp.max(s[: length - QB], 0, keepdims=True))
        p = jnp.exp(last - top)
        total = jnp.sum(p, 0, keepdims=True)
        p = p.astype(bf16)
        if i:
            head = jnp.exp(s[: length - QB] - top)
            total = total + jnp.sum(head, 0, keepdims=True)
            p = jnp.concatenate([head.astype(bf16), p], 0)
        put_lse(h, rows, top + jnp.log(total))
        outs.append(mm(p, v, TN_))
        sums.append(total)
    inv = jnp.transpose(1.0 / jnp.concatenate(sums + [jnp.ones((6, QB), f32)], 0))
    put_out(rows, jnp.where(mask, outs[0] * inv[:, 0:1], outs[1] * inv[:, 1:2]).astype(bf16))


def attend_rows_back(qkv, att, datt, lse, i, first, prod, dk, dv, put_dq):
    length = (i + 1) * QB
    rows = pl.ds(i * QB, QB)
    mask = half_mask(QB)
    mask_all = half_mask(length)
    causal = lax.broadcasted_iota(jnp.int32, (QB, QB), 0) <= lax.broadcasted_iota(
        jnp.int32, (QB, QB), 1
    )
    q = qkv[rows, 0:PAIR] * bf16(HD**-0.5)
    k = qkv[pl.ds(0, length), PAIR : 2 * PAIR]
    v = qkv[pl.ds(0, length), 2 * PAIR : 3 * PAIR]
    do = datt[rows, :]
    dq = None
    for h in range(2):
        qh, dh = pick(mask, h, q), pick(mask, h, do)
        s = mm(k, qh, NT_)
        row = lse[h : h + 1, rows]
        p = jnp.exp(jnp.where(causal, s[length - QB :], NEG) - row)
        if i:
            p = jnp.concatenate([jnp.exp(s[: length - QB] - row), p], 0)
        dp = mm(v, dh, NT_)
        ds = (p * (dp - prod[h : h + 1, rows])).astype(bf16)
        a, b = mm(p.astype(bf16), dh), mm(ds, qh)
        if first and h == 0:
            dv[pl.ds(0, length), :] = a
            dk[pl.ds(0, length), :] = b
        else:
            dv[pl.ds(0, length), :] += a
            dk[pl.ds(0, length), :] += b
        part = mm(ds, pick(mask_all, h, k), TN_)
        dq = part if dq is None else dq + part
    put_dq(rows, (dq * HD**-0.5).astype(bf16))


class Sizes:
    def __init__(self, mesh, tokens, d, slab, ff, experts):
        self.NW, self.NN = mesh.shape["wide"], mesh.shape["narrow"]
        self.A, self.X = self.NW // 2, self.NN // 2
        self.T, self.D, self.slab, self.F, self.E = tokens, d, slab, ff, experts
        self.CW = 3 * PAIR
        self.G = d // PAIR
        self.J = self.G + d // self.CW
        self.R = self.NN * SLOT
        self.S = experts * SLOT
        self.EP = max(8, experts)
        rows = self.NW * self.R
        self.moe = rows * (5 * d + 3 * ff) * 2 < (24 << 20)
        self.fits = (
            self.moe and slab % 8 == 0 and tokens == SEQ and self.NW % 2 == 0 and self.NN % 2 == 0
            and self.NW > 2 and self.NN > 2 and experts == self.NW
        )


def place(c):
    w, n = lax.axis_index("wide"), lax.axis_index("narrow")
    return w, n, w // 2, lax.rem(w, 2), n // 2, lax.rem(n, 2)


def greet(c, w, n):
    bar = pltpu.get_barrier_semaphore()
    x, cc = n // 2, lax.rem(n, 2)

    def wide(i, _):
        pl.semaphore_signal(bar, inc=1, device_id={"wide": lax.rem(w + i, c.NW)}, device_id_type=MESH)
        return 0

    lax.fori_loop(1, c.NW, wide, 0)
    for k in range(1, c.X):
        to = lax.rem(x + k, c.X) * 2 + cc
        pl.semaphore_signal(bar, inc=1, device_id={"narrow": to}, device_id_type=MESH)
        other = w + 1 - 2 * lax.rem(w, 2)
        pl.semaphore_signal(bar, inc=1, device_id={"wide": other, "narrow": to}, device_id_type=MESH)
    pl.semaphore_signal(bar, inc=1, device_id={"narrow": x * 2 + 1 - cc}, device_id_type=MESH)
    return lambda: pl.semaphore_wait(bar, c.NW - 1 + 2 * c.X - 1)


def forward_kernel(c, *refs):
    (v_hbm, dy_hbm, idx_ref, cap_ref, wq_hbm, wo_hbm, cen_ref, g1_ref, g2_ref, up_hbm, down_hbm) = refs[:11]
    (w_out, normt_out, qkv_out, lse_out, att_out, resid_out, meta_out, mrow_out) = refs[11:19]
    (ret_out, outp_out, ug_out, dg_out, cent_out, mine_out) = refs[19:25]
    (v, nrm, normed, normt, oh, wbuf, wmat, wtr, misc, mrow, qkv, lse, att, sent, sendx, senddy,
     up, down, xin, dyin, hid, dpre, dexp, outp, part, lc, lx, stage, cent,
     lsem, in_sem, out_sem, w_sem, q_sem, st_sem, s1s, s1r, s2s, s2r, s4s, s4r,
     ds_, dr, xs_, xr, cs_, cr, fs, fr, gs, gr, ks, kr, rs_, rr, ws_, wr) = refs[25:]
    A, X, NW, NN, T, D, CW, G, J = c.A, c.X, c.NW, c.NN, c.T, c.D, c.CW, c.G, c.J
    w, n, a, b, x, cc = place(c)
    own = (a, b, x, cc)
    dy = sent

    for j in range(J):
        dst = wbuf.at[(j, *own)]
        if j < G:
            for p in range(3):
                pltpu.make_async_copy(
                    wq_hbm.at[:, pl.ds(p * D + j * PAIR, PAIR)], dst.at[:, pl.ds(p * PAIR, PAIR)], lsem.at[j]
                ).start()
        else:
            pltpu.make_async_copy(wo_hbm.at[:, pl.ds((j - G) * CW, CW)], dst, lsem.at[j]).start()
    loads = [(dy_hbm, dy), (v_hbm, v), (up_hbm.at[0], up), (down_hbm.at[0], down)]
    for i, (s, d) in enumerate(loads):
        pltpu.make_async_copy(s, d, in_sem.at[i]).start()

    def load_wait(i):
        wait_bytes(loads[i][1], in_sem.at[i])

    met = greet(c, w, n)

    pad = LANES - c.slab
    small = jnp.concatenate(
        [cen_ref[...].astype(f32), jnp.zeros((GAIN1 - c.E, c.slab), f32), g1_ref[...].astype(f32), g2_ref[...].astype(f32)], 0
    )
    small = jnp.concatenate([small, jnp.zeros((LANES, pad), f32)], 1)
    small = jnp.transpose(small)[0 : c.slab]
    mine_out[...] = small
    misc[own] = small.astype(bf16)

    met()

    def buf(j):
        return misc if isinstance(j, int) and j == J else wbuf.at[j]

    def s1(j):
        if not (isinstance(j, int) and j == J):
            wait_bytes(buf(j).at[own], lsem.at[j])
        for k in range(1, A):
            push(buf(j).at[own], buf(j).at[own], s1s.at[j], s1r.at[j], wide=lax.rem(a + k, A) * 2 + b)

    plane = [(p, q) for p in range(2) for q in range(X) if p or q]


    def s2_short(j):
        arrive(buf(j).at[pl.ds(0, A - 1), b, x, cc], s1r.at[j])
        mine = buf(j).at[:, b, x, cc]
        for i, (p, q) in enumerate(plane):
            push(
                mine, mine, s2s.at[j, i], s2r.at[j, i],
                wide=a * 2 + lax.rem(b + p, 2), narrow=lax.rem(x + q, X) * 2 + cc,
            )

    def s2_long(j):
        arrive(buf(j).at[pl.ds(0, A - 1), b, x, cc], s1r.at[j])
        mine = buf(j).at[:, b, x, cc]
        for q in range(1, X):
            push(mine, mine, s2s.at[j, q], s2r.at[j, q], narrow=lax.rem(x + q, X) * 2 + cc)

    def s3_long(j):
        for q in range(1, X):
            arrive(buf(j).at[:, b, x, cc], s2r.at[j, q])
        mine = buf(j).at[:, b, :, cc]
        push(mine, mine, s2s.at[j, 0], s2r.at[j, 0], wide=a * 2 + 1 - b)

    def plane_short(j, sem):
        for i in range(len(plane)):
            arrive(buf(j).at[:, b, x, cc], sem.at[j, i])

    def plane_long(j, sem):
        arrive(buf(j).at[:, b, :, cc], sem.at[j, 0])

    def to_core(j):
        mine = buf(j).at[:, :, :, cc]
        push(mine, mine, s4s.at[j], s4r.at[j], narrow=x * 2 + 1 - cc)

    def s4_short(j):
        plane_short(j, s2r)
        to_core(j)

    def s4_long(j):
        plane_long(j, s2r)
        to_core(j)

    def take(j, turn=True):
        arrive(buf(j).at[:, :, :, cc], s4r.at[j])
        val = wbuf[j].reshape(D, CW)
        wmat[j] = val
        if turn:
            turned(j, val)

    def turned(j, val):
        wtr[j] = jnp.transpose(val)
        pltpu.make_async_copy(wtr.at[j], w_out.at[j], w_sem.at[j]).start()

    def due(t):
        for j in range(J):
            short = j < SHORT
            if t == (j + 4):
                (s4_short if short else s4_long)(j)
            if not short and t == j + 2:
                s3_long(j)
            if t == (j + 2 if short else j):
                (s2_short if short else s2_long)(j)
            if t == (j if short else max(j - 2, 1)):
                s1(j)

    s1(J)
    due(0)
    hot = (lax.broadcasted_iota(jnp.int32, (c.EP, T), 0) == idx_ref[...]).astype(f32)
    lane = lax.broadcasted_iota(jnp.int32, (c.EP, T), 1)
    count = hot
    shift = 1
    while shift < T:
        count = count + jnp.where(lane >= shift, pltpu.roll(count, shift, 1), 0.0)
        shift *= 2
    rank = jnp.sum((count - hot) * hot, 0, keepdims=True)
    ceiling = jnp.zeros((1, T), f32)
    for e in range(c.E):
        ceiling = ceiling + hot[e : e + 1, :] * cap_ref[e].astype(f32)
    kept = rank < ceiling
    slot = jnp.where(kept, idx_ref[...].astype(f32) * SLOT + rank, -1.0)

    due(1)
    s2_short(J)
    oh[...] = (lax.broadcasted_iota(jnp.int32, (c.S, T), 0).astype(f32) == slot).astype(bf16)
    due(2)
    load_wait(0)
    senddy[...] = mm(oh[...], dy[...]).astype(bf16)
    due(3)

    def dy_w(k):
        to = lax.rem(w + k, NW)
        push(senddy.at[pl.ds(pl.multiple_of(to * SLOT, SLOT), SLOT)], dyin.at[w, x, cc], ds_.at[k], dr.at[k], wide=to)

    def dy_x(k):
        src = lax.rem(w - k + NW, NW)

        @pl.when(k > 0)
        def _():
            arrive(dyin.at[src, x, cc], dr.at[k])

        for q in range(1, X):
            push(dyin.at[src, x, cc], dyin.at[src, x, cc], xs_.at[k], xr.at[k], narrow=lax.rem(x + q, X) * 2 + cc)

    dyin[w, x, cc] = senddy[pl.ds(pl.multiple_of(w * SLOT, SLOT), SLOT), :]
    load_wait(1)

    def norm1(i, _):
        rows = pl.ds(i * 128, 128)
        nrm[rows, :] = layer_stats(v[rows, :].astype(f32))[0]
        return 0

    lax.fori_loop(0, T // 128, norm1, 0)
    s4_short(J)
    due(4)
    arrive(misc.at[:, :, :, cc], s4r.at[J])
    mrow[...] = jnp.transpose(misc[...].reshape(D, LANES).astype(f32))
    gain1 = mrow[GAIN1 : GAIN1 + 1, :]
    gain2 = mrow[GAIN2 : GAIN2 + 1, :]
    pltpu.make_async_copy(mrow, mrow_out, out_sem.at[0]).start()

    def norm1b(i, _):
        rows = pl.ds(i * 128, 128)
        normed[rows, :] = (nrm[rows, :] * gain1).astype(bf16)
        return 0

    lax.fori_loop(0, T // 128, norm1b, 0)
    per = -(-NW // 4)

    def pair(g, _):
        slot_ = lax.rem(g, 2)
        take(g)

        @pl.when(g >= 2)
        def _():
            wait_bytes(qkv.at[slot_], q_sem.at[slot_])

        qkv[slot_] = mm(normed[...], wmat[g]).astype(bf16)
        pltpu.make_async_copy(qkv.at[slot_], qkv_out.at[g], q_sem.at[slot_]).start()

        def at_step(fn, j, wanted):
            @pl.when(wanted & (j < J))
            def _():
                fn(j)

        at_step(s4_short, g + 1, g + 1 < SHORT)
        at_step(s4_long, g + 1, g + 1 >= SHORT)
        at_step(s3_long, g + 3, g + 3 >= SHORT)
        at_step(s2_short, g + 3, g + 3 < SHORT)
        at_step(s2_long, g + 5, g + 5 >= SHORT)
        at_step(s1, g + 5, g + 5 < SHORT)
        at_step(s1, g + 7, g + 7 >= SHORT)

        def put_out(rows, val):
            att[rows, pl.ds(pl.multiple_of(g * PAIR, PAIR), PAIR)] = val

        def put_lse(h, rows, val):
            lse[g, h : h + 1, rows] = val

        for i in range(T // QB):
            if i == T // QB - 1:
                @pl.when(g == G - 1)
                def _():
                    for j in range(G + 1, J):
                        (s4_short if j < SHORT else s4_long)(j)

                for q in range(per):
                    k = g * per + q

                    @pl.when((k >= 1) & (k < NW))
                    def _():
                        dy_w(k)

                    @pl.when((g >= 2) & (k - 2 * per < NW))
                    def _():
                        dy_x(k - 2 * per)

            attend_rows(qkv.at[slot_], T, i, put_out, put_lse)
        return 0

    lax.fori_loop(0, G, pair, 0)
    pltpu.make_async_copy(lse, lse_out, out_sem.at[1]).start()
    pltpu.make_async_copy(att, att_out, out_sem.at[2]).start()

    for j in range(G, J):
        take(j, False)
        at = slice((j - G) * CW, (j - G + 1) * CW)
        nrm[:, at] = v[:, at].astype(f32) + mm(att[...], wmat[j])

    def tail(i, _):
        rows = pl.ds(i * QB, QB)
        sent[rows, :] = (layer_stats(nrm[rows, :])[0] * gain2).astype(bf16)
        return 0

    lax.fori_loop(0, T // QB, tail, 0)
    pltpu.make_async_copy(nrm, resid_out, out_sem.at[3]).start()
    sendx[...] = mm(oh[...], sent[...]).astype(bf16)

    def x_w(k):
        to = lax.rem(w + k, NW)
        push(sendx.at[pl.ds(pl.multiple_of(to * SLOT, SLOT), SLOT)], xin.at[w, x, cc], fs.at[k], fr.at[k], wide=to)

    for k in range(1, AHEAD_W):
        x_w(k)
    xin[w, x, cc] = sendx[pl.ds(pl.multiple_of(w * SLOT, SLOT), SLOT), :]

    crow = mrow[pl.ds(w, 1), :]

    def source(i):
        return lax.rem(w - i + NW, NW)

    def fwd_x(i):
        src = source(i)

        @pl.when(i > 0)
        def _():
            arrive(xin.at[src, x, cc], fr.at[i])

        for k in range(1, X):
            push(xin.at[src, x, cc], xin.at[src, x, cc], gs.at[i], gr.at[i], narrow=lax.rem(x + k, X) * 2 + cc)

    def fwd_c(i):
        src = source(i)
        arrive(xin.at[src, pl.ds(0, X - 1), cc], gr.at[i])
        push(xin.at[src, :, cc], xin.at[src, :, cc], ks.at[i], kr.at[i], narrow=x * 2 + 1 - cc)

    def expert(i):
        src = source(i)
        arrive(xin.at[src, :, cc], kr.at[i])
        xb = xin[src].reshape(c.R, D)
        db = dyin[src].reshape(c.R, D)
        xf, df = xb.astype(f32), db.astype(f32)
        s = jax.nn.sigmoid(jnp.sum(xf * crow, 1, keepdims=True))
        de = (df * s).astype(bf16)
        pre = mm(xb, up[...])
        cdf = 0.5 * (1.0 + lax.erf(pre * 0.7071067811865476))
        hb = (pre * cdf).astype(bf16)
        slope = cdf + pre * (jnp.exp(-0.5 * pre * pre) * 0.3989422804014327)
        dpb = (mm(de, down[...]) * slope).astype(bf16)
        out = mm(hb, down[...], NT_)
        dl = jnp.sum(df * out, 1, keepdims=True) * (s * (1.0 - s))
        dn = mm(dpb, up[...], NT_) + dl * crow
        part[src] = dn.astype(bf16).reshape(X, 2, SLOT, D)
        outp[src] = out.astype(bf16).reshape(X, 2, SLOT, D)
        cent[...] += jnp.broadcast_to(jnp.sum(dl * xf, 0, keepdims=True), cent.shape)
        rows = pl.ds(pl.multiple_of(src * c.R, SLOT), c.R)
        hid[rows, :] = hb
        dpre[rows, :] = dpb
        dexp[rows, :] = de

    def ret_c(i):
        src = source(i)
        push(part.at[src, :, 1 - cc], lc.at[src], rs_.at[0, i], rr.at[0, i], narrow=x * 2 + 1 - cc)

    def ret_x(i):
        src = source(i)
        arrive(lc.at[src], rr.at[0, i])
        part[src, :, cc] = (part[src, :, cc].astype(f32) + lc[src].astype(f32)).astype(bf16)
        for k in range(1, X):
            x2 = lax.rem(x + k, X)
            push(part.at[src, x2, cc], lx.at[src, x], rs_.at[1, i], rr.at[1, i], narrow=x2 * 2 + cc)

    def ret_w(i):
        src = source(i)
        arrive(lx.at[src, pl.ds(0, X - 1)], rr.at[1, i])
        total = part[src, x, cc].astype(f32)
        for k in range(1, X):
            total = total + lx[src, lax.rem(x + k, X)].astype(f32)
        part[src, x, cc] = total.astype(bf16)

        @pl.when(i > 0)
        def _():
            push(part.at[src, x, cc], ret_out.at[w], ws_.at[i], wr.at[i], wide=src)

        @pl.when(i == 0)
        def _():
            pltpu.make_async_copy(part.at[src, x, cc], ret_out.at[w], ws_.at[0]).start()

    fwd_x(0)
    for j in range(G, J):
        turned(j, wmat[j])
    normt[...] = jnp.transpose(normed[...])
    pltpu.make_async_copy(normt, normt_out, out_sem.at[5]).start()
    for k in range(per * (G - 2), NW):
        dy_x(k)

    logits = mm(mrow[0 : c.EP, :].astype(bf16), sent[...], NT_)
    gate = jax.nn.sigmoid(jnp.sum(logits * hot, 0, keepdims=True)) * kept.astype(f32)
    meta_out[...] = jnp.concatenate([slot, gate, jnp.zeros((6, T), f32)], 0)
    cent[...] = jnp.zeros_like(cent)

    def dy_all(k, _):
        arrive(dyin.at[w, x, cc], xr.at[k])
        return 0

    for q in range(X - 1):
        lax.fori_loop(0, NW, dy_all, 0)
    push(dyin.at[:, :, cc], dyin.at[:, :, cc], cs_, cr, narrow=x * 2 + 1 - cc)
    fwd_c(0)
    for k in range(1, AHEAD_X):
        fwd_x(k)
    load_wait(2)
    load_wait(3)
    arrive(dyin.at[:, :, cc], cr)

    def block(i, _):
        @pl.when(i + AHEAD_W < NW)
        def _():
            x_w(i + AHEAD_W)

        @pl.when(i + 1 < NW)
        def _():
            fwd_c(i + 1)

        @pl.when(i + AHEAD_X < NW)
        def _():
            fwd_x(i + AHEAD_X)

        expert(i)
        ret_c(i)

        @pl.when(i >= 1)
        def _():
            ret_x(i - 1)

        @pl.when(i >= BEHIND_W)
        def _():
            ret_w(i - BEHIND_W)

        return 0

    lax.fori_loop(0, NW, block, 0)
    ret_x(NW - 1)
    for i in range(NW - BEHIND_W, NW - 1):
        ret_w(i)
    pltpu.make_async_copy(outp, outp_out, out_sem.at[4]).start()
    cent_out[...] = cent[...]
    parts = D // QB

    def grads(lhs, rhs, out, second):
        def one_block(i, _):
            at = pl.ds(pl.multiple_of(i * QB, QB), QB)
            if second:
                wait_bytes(stage.at[i], st_sem.at[i])
            stage[i] = mm(lhs(at), rhs[...], TN_).astype(bf16)
            pltpu.make_async_copy(stage.at[i], out.at[0, at], st_sem.at[i]).start()
            return 0

        lax.fori_loop(0, parts, one_block, 0)

    grads(lambda at: dexp[:, at], hid, dg_out, False)
    ret_w(NW - 1)
    grads(lambda at: xin[:, :, :, :, at].reshape(NW * c.R, QB), dpre, ug_out, True)

    for q, ref in enumerate([mrow, lse, att, nrm, outp, normt]):
        wait_bytes(ref, out_sem.at[q])
    for q in range(2):
        wait_bytes(qkv.at[q], q_sem.at[q])
    for j in [J] + list(range(J)):
        if not (isinstance(j, int) and j == J):
            wait_bytes(wtr.at[j], w_sem.at[j])
        arrive(buf(j).at[pl.ds(0, A - 1), b, x, cc], s1s.at[j])
        if j == J or j < SHORT:
            plane_short(j, s2s)
        else:
            plane_long(j, s2s)
            for q in range(1, X):
                arrive(buf(j).at[:, b, x, cc], s2s.at[j, q])
        arrive(buf(j).at[:, :, :, cc], s4s.at[j])
    arrive(dyin.at[:, :, cc], cs_)

    def drain(i, _):
        src = source(i)
        arrive(xin.at[src, pl.ds(0, X - 1), cc], xs_.at[i])
        arrive(xin.at[src, pl.ds(0, X - 1), cc], gs.at[i])
        arrive(xin.at[src, :, cc], ks.at[i])
        arrive(lc.at[src], rs_.at[0, i])
        arrive(lx.at[src, pl.ds(0, X - 1)], rs_.at[1, i])

        @pl.when(i > 0)
        def _():
            arrive(xin.at[src, x, cc], ds_.at[i])
            arrive(xin.at[src, x, cc], fs.at[i])
            arrive(xin.at[src, x, cc], ws_.at[i])
            arrive(xin.at[src, x, cc], wr.at[i])

        return 0

    lax.fori_loop(0, NW, drain, 0)
    wait_bytes(part.at[0, 0, 0], ws_.at[0])
    for i in range(parts):
        wait_bytes(stage.at[i], st_sem.at[i])


def forward_call(c, v, dy, idx, cap, wq, wo, cen, g1, g2, up, down):
    T, D, CW, G, J, NW, NN, A, X, L, F = c.T, c.D, c.CW, c.G, c.J, c.NW, c.NN, c.A, c.X, c.slab, c.F
    any_ = pl.BlockSpec(memory_space=pl.ANY)
    vm = pl.BlockSpec(memory_space=pltpu.VMEM)
    sm = pl.BlockSpec(memory_space=pltpu.SMEM)
    sds = jax.ShapeDtypeStruct
    rows_ = (NW, X, 2, SLOT, D)
    outs = [
        (sds((J, CW, D), bf16), any_),
        (sds((D, T), bf16), any_),
        (sds((G, T, CW), bf16), any_),
        (sds((G, 8, T), f32), any_),
        (sds((T, D), bf16), any_),
        (sds((T, D), f32), any_),
        (sds((8, T), f32), vm),
        (sds((LANES, D), f32), any_),
        (sds((NW, SLOT, D), bf16), any_),
        (sds(rows_, bf16), any_),
        (sds((1, D, F), bf16), any_),
        (sds((1, D, F), bf16), any_),
        (sds((8, D), f32), vm),
        (sds((L, LANES), f32), vm),
    ]
    dma, V = pltpu.SemaphoreType.DMA, pltpu.VMEM
    rows = NW * c.R
    scratch = [
        V((T, D), bf16), V((T, D), f32), V((T, D), bf16), V((D, T), bf16), V((c.S, T), bf16),
        V((J, A, 2, X, 2, L, CW), bf16), V((J, D, CW), bf16), V((J, CW, D), bf16), V((A, 2, X, 2, L, LANES), bf16), V((LANES, D), f32),
        V((2, T, CW), bf16), V((G, 8, T), f32), V((T, D), bf16), V((T, D), bf16), V((c.S, D), bf16), V((c.S, D), bf16),
        V((D, F), bf16), V((D, F), bf16), V(rows_, bf16), V(rows_, bf16),
        V((rows, F), bf16), V((rows, F), bf16), V((rows, D), bf16), V(rows_, bf16), V(rows_, bf16),
        V((NW, X, SLOT, D), bf16), V((NW, X, SLOT, D), bf16), V((D // QB, QB, F), bf16), V((8, D), f32),
        dma((J,)), dma((4,)), dma((6,)), dma((J,)), dma((2,)), dma((D // QB,)),
    ] + [dma((J + 1,))] * 2 + [dma((J + 1, 2 * X - 1))] * 2 + [dma((J + 1,))] * 2 + [dma((NW,))] * 4 + [dma(()), dma(())] + [dma((NW,))] * 6 + [
        dma((2, NW)), dma((2, NW)), dma((NW,)), dma((NW,)),
    ]
    return pl.pallas_call(
        functools.partial(forward_kernel, c),
        out_shape=tuple(o[0] for o in outs),
        in_specs=[any_, any_, vm, sm, any_, any_, vm, vm, vm, any_, any_],
        out_specs=tuple(o[1] for o in outs),
        scratch_shapes=scratch,
        compiler_params=pltpu.CompilerParams(
            collective_id=CID0, has_side_effects=True, vmem_limit_bytes=VMEM_CAP
        ),
        name="forward",
    )(v, dy, idx, cap, wq, wo, cen, g1, g2, up, down)


def backward_kernel(c, *refs):
    (v_hbm, dy_hbm, qkv_hbm, lse_hbm, att_hbm, resid_hbm, wt_hbm, nt_hbm, ret_hbm, outp_hbm, mrow, meta, cent, wq, mine) = refs[:15]
    (mixed_out, tok_out, qg_out, og_out, small_out) = refs[15:20]
    (v, dy, qkv, lse, att, resid, wt, ret, oh, normt, dbr, datt, dnm, dqkv, dk, dv, prod, rowbuf,
     part, lc, lx, got, mixed,
     gb, la, lb, lz, sgb, sla, slb, slz, lxx,
     in_sem, q_sem, out_sem, os_, orv, ows, owr, rs_, rr, ps_, pr, tokacc) = refs[20:]
    A, X, NW, NN, T, D, CW, G, J = c.A, c.X, c.NW, c.NN, c.T, c.D, c.CW, c.G, c.J
    H = J - G
    w, n, a, b, x, cc = place(c)
    blocks = T // QB

    loads = [
        (ret_hbm, ret), (resid_hbm, resid), (dy_hbm, dy), (att_hbm, att), (v_hbm, v), (lse_hbm, lse), (nt_hbm, normt),
        (wt_hbm.at[pl.ds(G, H)], wt.at[pl.ds(G, H)]), (wt_hbm.at[pl.ds(0, G)], wt.at[pl.ds(0, G)]),
    ]
    for i, (s, d) in enumerate(loads):
        pltpu.make_async_copy(s, d, in_sem.at[i]).start()
    own_part = pltpu.make_async_copy(outp_hbm.at[:, :, cc], part, in_sem.at[9])
    own_part.start()

    def load_wait(i):
        wait_bytes(loads[i][1], in_sem.at[i])

    def fetch_qkv(g, slot_):
        pltpu.make_async_copy(qkv_hbm.at[g], qkv.at[slot_], q_sem.at[1, slot_]).start()

    fetch_qkv(0, 0)
    met = greet(c, w, n)

    slot, gate = meta[0:1, :], meta[1:2, :]
    hits = lax.broadcasted_iota(jnp.int32, (c.S, T), 0).astype(f32) == slot
    oh[...] = hits.astype(bf16)
    gain1, gain2 = mrow[GAIN1 : GAIN1 + 1, :], mrow[GAIN2 : GAIN2 + 1, :]
    load_wait(0)
    dnm[...] = mm(oh[...], ret[...].reshape(c.S, D), TN_)
    oh[...] = jnp.where(hits, gate, 0.0).astype(bf16)
    met()
    push(outp_hbm.at[:, :, 1 - cc], lc, os_.at[0], orv.at[0], narrow=x * 2 + 1 - cc)
    load_wait(1)
    load_wait(2)
    rowbuf[...] = jnp.zeros_like(rowbuf)
    rowbuf[pl.ds(w, 1), :] = cent[0:1, :]

    def norm2_back(i, acc):
        rows = pl.ds(i * QB, QB)
        n2, r2 = layer_stats(resid[rows, :])
        dn2 = dnm[rows, :]
        dn = dn2 * gain2
        step = r2 * (dn - jnp.mean(dn, 1, keepdims=True) - n2 * jnp.mean(dn * n2, 1, keepdims=True))
        dres = dy[rows, :].astype(f32) + step
        dnm[rows, :] = dres
        dbr[rows, :] = dres.astype(bf16)
        return acc + jnp.sum(dn2 * n2, 0, keepdims=True)

    rowbuf[GAIN2 : GAIN2 + 1, :] = lax.fori_loop(0, blocks, norm2_back, jnp.zeros((1, D), f32))
    load_wait(3)

    big = (gb, la, lb, lz, 0, lxx)
    tiny = (sgb, sla, slb, slz, J)

    def add(p, q):
        return (p.astype(f32) + q.astype(f32)).astype(bf16)

    def ra(t, j):
        push(t[0].at[j, :, :, :, 1 - cc], t[1].at[j], rs_.at[0, t[4] + j], rr.at[0, t[4] + j], narrow=x * 2 + 1 - cc)

    plane = [(p, q) for p in range(2) for q in range(X) if p or q]

    plane = [(p, q) for p in range(2) for q in range(X) if p or q]

    def join(t, j):
        arrive(t[1].at[j], rr.at[0, t[4] + j])
        t[0][j, :, :, :, cc] = add(t[0][j, :, :, :, cc], t[1][j])

    def to_plane(t, j, i, src, dst, p, q):
        push(
            src, dst, ps_.at[t[4] + j, i], pr.at[t[4] + j, i],
            wide=a * 2 + lax.rem(b + p, 2), narrow=lax.rem(x + q, X) * 2 + cc,
        )

    def to_outer(t, j, total):
        t[0][j, :, b, x, cc] = total.astype(bf16)
        for k in range(1, A):
            a2 = lax.rem(a + k, A)
            push(t[0].at[j, a2, b, x, cc], t[3].at[j, a], rs_.at[1, t[4] + j], rr.at[1, t[4] + j], wide=a2 * 2 + b)

    def rb_short(t, j):
        join(t, j)
        for i, (p, q) in enumerate(plane):
            to_plane(t, j, i, t[0].at[j, :, lax.rem(b + p, 2), lax.rem(x + q, X), cc], t[2].at[j, b, x], p, q)

    def rc_short(t, j):
        plane_short(t, j, pr)
        total = t[0][j, :, b, x, cc].astype(f32)
        for p, q in plane:
            total = total + t[2][j, lax.rem(b + p, 2), lax.rem(x + q, X)].astype(f32)
        to_outer(t, j, total)

    def plane_short(t, j, sem):
        for i in range(len(plane)):
            arrive(t[2].at[j, 0, 0], sem.at[t[4] + j, i])

    def rb_long(t, j):
        join(t, j)
        for q in range(X):
            t[2][j, b, q] = t[0][j, :, 1 - b, q, cc]
        to_plane(t, j, 0, t[2].at[j, b], t[2].at[j, b], 1, 0)

    def rc_long(t, j):
        arrive(t[2].at[j, 0], pr.at[t[4] + j, 0])
        for q in range(X):
            t[0][j, :, b, q, cc] = add(t[0][j, :, b, q, cc], t[2][j, 1 - b, q])
        for q in range(1, X):
            to_plane(t, j, q, t[0].at[j, :, b, lax.rem(x + q, X), cc], t[5].at[j, x], 0, q)

    def rd_long(t, j):
        for q in range(1, X):
            arrive(t[2].at[j, 0, 0], pr.at[t[4] + j, q])
        total = t[0][j, :, b, x, cc].astype(f32)
        for q in range(1, X):
            total = total + t[5][j, lax.rem(x + q, X)].astype(f32)
        to_outer(t, j, total)

    def plane_long(t, j, sem):
        arrive(t[2].at[j, 0], sem.at[t[4] + j, 0])
        for q in range(1, X):
            arrive(t[2].at[j, 0, 0], sem.at[t[4] + j, q])

    def rf(t, j):
        arrive(t[3].at[j, pl.ds(0, A - 1)], rr.at[1, t[4] + j])
        total = t[0][j, a, b, x, cc].astype(f32)
        for k in range(1, A):
            total = total + t[3][j, lax.rem(a + k, A)].astype(f32)
        return total

    def rf_w(j):
        og_out[:, j * CW : (j + 1) * CW] = rf(big, j)

    def rf_q(g):
        total = rf(big, H + g)
        for p in range(3):
            qg_out[:, pl.ds(pl.multiple_of(p * D + g * PAIR, PAIR), PAIR)] = total[:, p * PAIR : (p + 1) * PAIR]

    sgb[0] = jnp.transpose(rowbuf[...]).astype(bf16).reshape(A, 2, X, 2, c.slab, LANES)
    ra(tiny, 0)
    for h in range(H):
        gb[h] = mm(att[...], dbr[:, h * CW : (h + 1) * CW], TN_).astype(bf16).reshape(A, 2, X, 2, c.slab, CW)
        ra(big, h)

    load_wait(7)

    def out_back(i, _):
        at = pl.ds(pl.multiple_of(i * QB, QB), QB)
        datt[:, at] = mm(dbr[...], wt[pl.ds(G, H), :, at].reshape(D, QB)).astype(bf16)
        return 0

    lax.fori_loop(0, D // QB, out_back, 0)
    load_wait(4)
    load_wait(6)
    rb_short(tiny, 0)
    for h in range(H):
        rb_long(big, h)
    load_wait(5)
    own_part.wait()

    def o_x(i):
        for k in range(1, X):
            x2 = lax.rem(x + k, X)
            push(part.at[i, x2], lx.at[i, x], os_.at[1 + i], orv.at[1 + i], narrow=x2 * 2 + cc)

    def o_w(i):
        arrive(lx.at[i, pl.ds(0, X - 1)], orv.at[1 + i])
        total = part[i, x].astype(f32)
        for k in range(1, X):
            total = total + lx[i, lax.rem(x + k, X)].astype(f32)
        part[i, x] = total.astype(bf16)

        @pl.when(i != w)
        def _():
            push(part.at[i, x], got.at[w], ows.at[i], owr.at[lax.rem(w - i + NW, NW)], wide=i)

        @pl.when(i == w)
        def _():
            got[w] = part[w, x]

    arrive(lc, orv.at[0])

    def merge(i, _):
        part[i] = add(part[i], lc[i])
        return 0

    lax.fori_loop(0, NW, merge, 0)
    per = -(-NW // 4)

    def spread(fn, step):
        for k in range(per):
            i = lax.rem(w + step * per + k, NW)

            @pl.when(step * per + k < NW)
            def _():
                fn(i)

    def pair(g, _):
        s_ = lax.rem(g, 2)

        @pl.when(g + 1 < G)
        def _():
            fetch_qkv(g + 1, 1 - s_)

        wait_bytes(qkv.at[s_], q_sem.at[1, s_])
        lanes = pl.ds(pl.multiple_of(g * PAIR, PAIR), PAIR)
        att_g, datt_g = att.at[:, lanes], datt.at[:, lanes]
        full = jnp.transpose(datt_g[...].astype(f32) * att_g[...].astype(f32))
        prod[0:1, :] = jnp.sum(full[0:HD], 0, keepdims=True)
        prod[1:2, :] = jnp.sum(full[HD:], 0, keepdims=True)

        def put_dq(rows, val):
            dqkv[g, rows, 0:PAIR] = val

        for i in reversed(range(blocks)):
            if i == 0:
                @pl.when(g == 0)
                def _():
                    rc_short(tiny, 0)

                rc_long(big, g)

                @pl.when(g >= 1)
                def _():
                    rd_long(big, g - 1)

            attend_rows_back(qkv.at[s_], att_g, datt_g, lse.at[g], i, i == blocks - 1, prod, dk, dv, put_dq)
            if i == blocks - 1:
                @pl.when((g >= 1) & (g + H - 1 < J - LAST))
                def _():
                    rb_long(big, g + H - 1)

                @pl.when((g >= 1) & (g + H - 1 >= J - LAST))
                def _():
                    rb_short(big, g + H - 1)

                @pl.when(g < 4)
                def _():
                    spread(o_x, g)

                @pl.when(g >= 2)
                def _():
                    spread(o_w, g - 2)

        dqkv[g, :, PAIR : 2 * PAIR] = dk[...].astype(bf16)
        dqkv[g, :, 2 * PAIR :] = dv[...].astype(bf16)
        gb[H + g] = mm(normt[...], dqkv[g]).astype(bf16).reshape(A, 2, X, 2, c.slab, CW)
        ra(big, H + g)
        return 0

    lax.fori_loop(0, G, pair, 0)
    load_wait(8)

    def back(i):
        at = slice(i * QB, (i + 1) * QB)
        total = mm(dqkv[0], wt[0, :, at])
        for g in range(1, G):
            total = total + mm(dqkv[g], wt[g, :, at])
        tokacc[:, at] = total

    back(0)
    rb_short(big, J - 1)
    rd_long(big, J - LAST - 1)
    for j in range(J - LAST, J - 1):
        rc_short(big, j)
    for i in range(1, D // QB):
        back(i)
    def norm1_back(i, _):
        rows = pl.ds(i * QB, QB)
        n1, r1 = layer_stats(v[rows, :].astype(f32))
        dm = tokacc[rows, :] * gain1
        step = r1 * (dm - jnp.mean(dm, 1, keepdims=True) - n1 * jnp.mean(dm * n1, 1, keepdims=True))
        dbr[rows, :] = (dnm[rows, :] + step).astype(bf16)
        return 0

    lax.fori_loop(0, blocks, norm1_back, 0)
    tok_copy = pltpu.make_async_copy(dbr, tok_out, out_sem.at[0])
    tok_copy.start()
    rc_short(big, J - 1)

    def o_wait(k, _):
        arrive(got.at[0], owr.at[k])
        return 0

    lax.fori_loop(1, NW, o_wait, 0)

    def mix(i, _):
        cols = pl.ds(pl.multiple_of(i * QB, QB), QB)
        rows = pl.ds(i * QB, QB)
        mixed[rows, :] = (resid[rows, :] + mm(oh[:, cols], got[...].reshape(c.S, D), TN_)).astype(bf16)
        return 0

    lax.fori_loop(0, blocks, mix, 0)
    mix_copy = pltpu.make_async_copy(mixed, mixed_out, out_sem.at[1])
    mix_copy.start()
    for h in range(H):
        rf_w(h)

    def fin(g, _):
        rf_q(g)
        return 0

    lax.fori_loop(0, G, fin, 0)
    sums_ = jnp.sum(qg_out[...] * wq[...].astype(f32), 1, keepdims=True) / mine[:, GAIN1 : GAIN1 + 1]
    at_gain = lax.broadcasted_iota(jnp.int32, (c.slab, LANES), 1) == GAIN1
    small_out[...] = jnp.where(at_gain, sums_, rf(tiny, 0))

    arrive(lc, os_.at[0])

    def drain(i, _):
        arrive(lx.at[i, pl.ds(0, X - 1)], os_.at[1 + i])

        @pl.when(i != w)
        def _():
            arrive(got.at[0], ows.at[i])

        return 0

    lax.fori_loop(0, NW, drain, 0)

    def drain_sums(t, j, route):
        arrive(t[1].at[j], rs_.at[0, t[4] + j])
        route(t, j, ps_)
        arrive(t[3].at[j, pl.ds(0, A - 1)], rs_.at[1, t[4] + j])

    for j in range(J):
        drain_sums(big, j, plane_long if j < J - LAST else plane_short)
    drain_sums(tiny, 0, plane_short)
    tok_copy.wait()
    mix_copy.wait()


def backward_call(c, v, dy, qkv, lse, att, resid, wt, nt, ret, outp, mrow, meta, cent, wq, mine):
    T, D, CW, G, J, NW, NN, A, X, L = c.T, c.D, c.CW, c.G, c.J, c.NW, c.NN, c.A, c.X, c.slab
    any_ = pl.BlockSpec(memory_space=pl.ANY)
    vm = pl.BlockSpec(memory_space=pltpu.VMEM)
    sds = jax.ShapeDtypeStruct
    dma, V = pltpu.SemaphoreType.DMA, pltpu.VMEM

    def sums(k, width):
        return [
            V((k, A, 2, X, 2, L, width), bf16), V((k, A, 2, X, L, width), bf16),
            V((k, 2, X, A, L, width), bf16), V((k, A, L, width), bf16),
        ]

    scratch = [
        V((T, D), bf16), V((T, D), bf16), V((2, T, CW), bf16), V((G, 8, T), f32), V((T, D), bf16), V((T, D), f32),
        V((J, CW, D), bf16), V((NW, SLOT, D), bf16), V((c.S, T), bf16),
        V((D, T), bf16), V((T, D), bf16), V((T, D), bf16), V((T, D), f32), V((G, T, CW), bf16),
        V((T, PAIR), f32), V((T, PAIR), f32), V((8, T), f32), V((LANES, D), f32),
        V((NW, X, SLOT, D), bf16), V((NW, X, SLOT, D), bf16), V((NW, X, SLOT, D), bf16), V((NW, SLOT, D), bf16),
        V((T, D), bf16),
    ] + sums(J, CW) + sums(1, LANES) + [
        V((J, X, A, L, CW), bf16),
        dma((10,)), dma((2, 2)), dma((2,)), dma((NW + 1,)), dma((NW + 1,)), dma((NW,)), dma((NW,)),
        dma((2, J + 1)), dma((2, J + 1)), dma((J + 1, 2 * X - 1)), dma((J + 1, 2 * X - 1)),
        V((T, D), f32),
    ]
    return pl.pallas_call(
        functools.partial(backward_kernel, c),
        out_shape=(
            sds((T, D), bf16), sds((T, D), bf16), sds((L, 3 * D), f32), sds((L, D), f32), sds((L, LANES), f32),
        ),
        in_specs=[any_] * 10 + [vm] * 5,
        out_specs=(any_, any_, vm, vm, vm),
        scratch_shapes=scratch,
        compiler_params=pltpu.CompilerParams(
            collective_id=CID1, has_side_effects=True, vmem_limit_bytes=VMEM_CAP
        ),
        name="backward",
    )(v, dy, qkv, lse, att, resid, wt, nt, ret, outp, mrow, meta, cent, wq, mine)


def cuts_of(shape):
    axis, size = len(shape) - 2, shape[-2]
    step = QB if size % QB == 0 else size
    return [(0,) * axis + (pl.ds(at, step),) for at in range(0, size, step)]


def finish_kernel(c, *refs):
    big, small = refs[:6], refs[6]
    outs, (cen_out, g1_out, g2_out) = refs[7:13], refs[13:16]
    held, wide, (in_sem, out_sem) = refs[16:22], refs[22:28], refs[28:]
    cuts = [(i, where) for i in range(6) for where in cuts_of(big[i].shape)]
    for k, (i, where) in enumerate(cuts):
        pltpu.make_async_copy(big[i].at[where], held[i].at[where], in_sem.at[k]).start()
    wide_small = jnp.concatenate([small[...], jnp.zeros((LANES - c.slab, LANES), f32)], 0)
    rows = jnp.transpose(wide_small)[:, 0 : c.slab]
    cen_out[...] = rows[0 : c.E]
    g1_out[...] = rows[GAIN1 : GAIN1 + 1]
    g2_out[...] = rows[GAIN2 : GAIN2 + 1]
    for k, (i, where) in enumerate(cuts):
        pltpu.make_async_copy(big[i].at[where], held[i].at[where], in_sem.at[k]).wait()
        src = held[i]
        if held[i].dtype != outs[i].dtype:
            wide[i][where] = held[i][where].astype(f32)
            src = wide[i]
        pltpu.make_async_copy(src.at[where], outs[i].at[where], out_sem.at[k]).start()
    for k, (i, where) in enumerate(cuts):
        src = wide[i] if held[i].dtype != outs[i].dtype else held[i]
        pltpu.make_async_copy(src.at[where], outs[i].at[where], out_sem.at[k]).wait()


def finish_call(c, big, kinds, small):
    any_ = pl.BlockSpec(memory_space=pl.ANY)
    vm = pl.BlockSpec(memory_space=pltpu.VMEM)
    sds, V = jax.ShapeDtypeStruct, pltpu.VMEM
    copies = sum(len(cuts_of(t.shape)) for t in big)
    return pl.pallas_call(
        functools.partial(finish_kernel, c),
        out_shape=tuple(sds(t.shape, k) for t, k in zip(big, kinds))
        + (sds((c.E, c.slab), f32), sds((1, c.slab), f32), sds((1, c.slab), f32)),
        in_specs=[any_] * 6 + [vm],
        out_specs=(any_,) * 6 + (vm,) * 3,
        scratch_shapes=[V(t.shape, t.dtype) for t in big]
        + [V(t.shape if t.dtype != k else (8, LANES), f32) for t, k in zip(big, kinds)]
        + [pltpu.SemaphoreType.DMA((copies,)), pltpu.SemaphoreType.DMA((copies,))],
        compiler_params=pltpu.CompilerParams(vmem_limit_bytes=VMEM_CAP),
        name="finish",
    )(*big, small)


precise = lax.Precision.HIGHEST
over_rows = (((0,), (0,)), ((), ()))
over_cols = (((1,), (1,)), ((), ()))


def layer_norm(tensor, gain_vec):
    centered = tensor - jnp.mean(tensor, -1, keepdims=True)
    spread = jnp.mean(centered * centered, -1, keepdims=True)
    return centered * lax.rsqrt(spread + 1e-05) * gain_vec


def gelu_exact(tensor):
    return jax.nn.gelu(tensor, approximate=False)


def split_heads(packed):
    seq_len = packed.shape[0]
    model_width = packed.shape[1] // 3
    head_count = model_width // HD
    queries = packed[:, :model_width].reshape(seq_len, head_count, HD)
    key_rows = packed[:, model_width : 2 * model_width].reshape(seq_len, head_count, HD)
    value_rows = packed[:, 2 * model_width :].reshape(seq_len, head_count, HD)
    raw_scores = jnp.einsum(
        "qhd,khd->hqk", queries, key_rows, preferred_element_type=jnp.float32
    ) * HD ** (-0.5)
    places = jnp.arange(seq_len)
    causal = places[:, None] >= places[None, :]
    masked = jnp.where(causal[None], raw_scores, -1e30)
    return (queries, key_rows, value_rows, masked)


def attend_forward(packed):
    queries, key_rows, value_rows, masked = split_heads(packed)
    maxima = jnp.max(masked, -1, keepdims=True)
    powers = jnp.exp(masked - maxima)
    totals = jnp.sum(powers, -1, keepdims=True)
    attn_probs = (powers / totals).astype(jnp.bfloat16)
    attended = jnp.einsum(
        "hqk,khd->qhd", attn_probs, value_rows, preferred_element_type=jnp.float32
    )
    return (attended.reshape(packed.shape[0], -1).astype(jnp.bfloat16), maxima + jnp.log(totals))


def attend_backward(member):
    packed, upstream, log_totals = member
    queries, key_rows, value_rows, masked = split_heads(packed)
    attn_probs = jnp.exp(masked - log_totals)
    probs_low = attn_probs.astype(jnp.bfloat16)
    grad_out = upstream.reshape(queries.shape)
    grad_probs = jnp.einsum(
        "qhd,khd->hqk", grad_out, value_rows, preferred_element_type=jnp.float32
    )
    grad_values = jnp.einsum(
        "hqk,qhd->khd", probs_low, grad_out, preferred_element_type=jnp.float32
    )
    grad_scores = (
        attn_probs * (grad_probs - jnp.sum(grad_probs * attn_probs, -1, keepdims=True))
    ).astype(jnp.bfloat16)
    factor = HD ** (-0.5)
    grad_queries = (
        jnp.einsum("hqk,khd->qhd", grad_scores, key_rows, preferred_element_type=jnp.float32)
        * factor
    )
    grad_keys = (
        jnp.einsum("hqk,qhd->khd", grad_scores, queries, preferred_element_type=jnp.float32)
        * factor
    )
    seq_len = packed.shape[0]
    joined = jnp.concatenate(
        [
            grad_queries.reshape(seq_len, -1),
            grad_keys.reshape(seq_len, -1),
            grad_values.reshape(seq_len, -1),
        ],
        1,
    )
    return joined.astype(jnp.bfloat16)


def expert_rows(row_block, up_mat, down_mat):
    pre_act = jnp.dot(row_block, up_mat, preferred_element_type=jnp.float32)
    hidden = gelu_exact(pre_act).astype(jnp.bfloat16)
    return lax.dot_general(hidden, down_mat, over_cols, preferred_element_type=jnp.float32)


def expert_grads(row_block, grad_block, up_mat, down_mat):
    pre_act = jnp.dot(row_block, up_mat, preferred_element_type=jnp.float32)
    hidden, gelu_back = jax.vjp(gelu_exact, pre_act)
    hidden_low = hidden.astype(jnp.bfloat16)
    down_part = lax.dot_general(
        grad_block, hidden_low, over_rows, preferred_element_type=jnp.float32
    )
    grad_hidden = jnp.dot(grad_block, down_mat, preferred_element_type=jnp.float32)
    grad_pre = gelu_back(grad_hidden)[0].astype(jnp.bfloat16)
    up_part = lax.dot_general(row_block, grad_pre, over_rows, preferred_element_type=jnp.float32)
    return (grad_pre, up_part, down_part)


def fill_slots(row_vals, target, slot_count):
    buffer = jnp.zeros((slot_count + 1, row_vals.shape[1]), row_vals.dtype).at[target].set(row_vals)
    return buffer[:slot_count]


def read_slots(buffer, target):
    padded = jnp.concatenate([buffer, jnp.zeros((1, buffer.shape[1]), buffer.dtype)], 0)
    return padded[target]


def plain_shards(
    layer_inputs_matrix,
    assignment_indices,
    admitted_counts_matrix,
    mixer_scaling1_factor,
    triple_linear_matrix,
    mixer_exit_matrix,
    specialist_scaling2_factor,
    cluster_mean_columns,
    first_linear_matrix,
    second_linear_matrix,
    incoming_gradient,
):
    gain_one, qkv_mat, out_mat, gain_two, centers = (
        lax.all_gather(mixer_scaling1_factor, ("wide", "narrow"), axis=0, tiled=True),
        lax.all_gather(triple_linear_matrix, ("wide", "narrow"), axis=0, tiled=True),
        lax.all_gather(mixer_exit_matrix, ("wide", "narrow"), axis=0, tiled=True),
        lax.all_gather(specialist_scaling2_factor, ("wide", "narrow"), axis=0, tiled=True),
        lax.all_gather(cluster_mean_columns, ("wide", "narrow"), axis=0, tiled=True),
    )
    gain_one = gain_one.astype(jnp.float32)
    gain_two = gain_two.astype(jnp.float32)
    centers = centers.astype(jnp.float32)
    token_rows = layer_inputs_matrix.astype(jnp.float32)
    tok_count, model_width = layer_inputs_matrix.shape
    seq_count = tok_count // SEQ
    normed, norm1_back = jax.vjp(layer_norm, token_rows, gain_one)
    normed_low = normed.astype(jnp.bfloat16)
    qkv_rows = jnp.dot(normed_low, qkv_mat, preferred_element_type=jnp.float32).astype(jnp.bfloat16)
    packed_seqs = qkv_rows.reshape(seq_count, SEQ, 3 * model_width)
    attended, log_totals = lax.map(attend_forward, packed_seqs)
    attended = attended.reshape(tok_count, model_width)
    residual = token_rows + jnp.dot(attended, out_mat, preferred_element_type=jnp.float32)
    normed_two, norm2_back = jax.vjp(layer_norm, residual, gain_two)
    sent_rows = normed_two.astype(jnp.bfloat16)
    dispatched_items = assignment_indices[:, 0]
    specialist_overall_sum = admitted_counts_matrix.shape[0]
    slot_count = specialist_overall_sum * SLOT
    specialist_indicator = (
        dispatched_items[:, None] == jnp.arange(specialist_overall_sum, dtype=jnp.int32)[None, :]
    ).astype(jnp.int32)
    before = jnp.cumsum(specialist_indicator, 0) - specialist_indicator
    ranked = jnp.sum(before * specialist_indicator, 1)
    position_ceilings = jnp.sum(specialist_indicator * admitted_counts_matrix[None, :], 1)
    retained_couple_filter = ranked < position_ceilings
    target = jnp.where(retained_couple_filter, dispatched_items * SLOT + ranked, slot_count)
    kept_rows = retained_couple_filter.astype(jnp.float32)
    choose = specialist_indicator.astype(jnp.float32)
    send_buf = fill_slots(sent_rows, target, slot_count).reshape(
        specialist_overall_sum, SLOT, model_width
    )
    local_rows = lax.all_to_all(send_buf, "wide", split_axis=0, concat_axis=0, tiled=True).reshape(
        slot_count, model_width
    )
    gathered = lax.all_gather(local_rows, "narrow", axis=0, tiled=True)
    expert_local = lax.psum_scatter(
        expert_rows(gathered, first_linear_matrix[0], second_linear_matrix[0]).astype(jnp.bfloat16),
        "narrow",
        scatter_dimension=0,
        tiled=True,
    )
    returned = lax.all_to_all(
        expert_local.reshape(specialist_overall_sum, SLOT, model_width),
        "wide",
        split_axis=0,
        concat_axis=0,
        tiled=True,
    )
    expert_tok = read_slots(returned.reshape(slot_count, model_width), target).astype(jnp.float32)
    center_rows = lax.dot_general(choose, centers, over_cols, precision=precise)
    logits = jnp.sum(normed_two * center_rows, 1)
    sigma = jax.nn.sigmoid(logits)
    gating = sigma * kept_rows
    mixed = (residual + gating[:, None] * expert_tok).astype(jnp.bfloat16)
    grad_y = incoming_gradient.astype(jnp.float32)
    grad_logit = jnp.sum(grad_y * expert_tok, 1) * sigma * (1.0 - sigma) * kept_rows
    grad_normed = grad_logit[:, None] * center_rows
    centroid_part = lax.dot_general(
        normed_two, choose * grad_logit[:, None], over_rows, precision=precise
    )
    grad_expert = (grad_y * gating[:, None]).astype(jnp.bfloat16)
    grad_buf = fill_slots(grad_expert, target, slot_count).reshape(
        specialist_overall_sum, SLOT, model_width
    )
    grad_local = lax.all_to_all(grad_buf, "wide", split_axis=0, concat_axis=0, tiled=True).reshape(
        slot_count, model_width
    )
    grad_gathered = lax.all_gather(grad_local, "narrow", axis=0, tiled=True)
    grad_pre, up_part, down_part = expert_grads(
        gathered, grad_gathered, first_linear_matrix[0], second_linear_matrix[0]
    )
    input_back = lax.psum_scatter(
        lax.dot_general(
            grad_pre, first_linear_matrix[0], over_cols, preferred_element_type=jnp.float32
        ).astype(jnp.bfloat16),
        "narrow",
        scatter_dimension=0,
        tiled=True,
    )
    up_grad = up_part[None]
    down_grad = down_part[None]
    back_rows = lax.all_to_all(
        input_back.reshape(specialist_overall_sum, SLOT, model_width),
        "wide",
        split_axis=0,
        concat_axis=0,
        tiled=True,
    )
    grad_normed = grad_normed + read_slots(
        back_rows.reshape(slot_count, model_width), target
    ).astype(jnp.float32)
    grad_resid_norm, gain_two_part = norm2_back(grad_normed)
    grad_resid = grad_y + grad_resid_norm
    grad_branch = grad_resid.astype(jnp.bfloat16)
    out_part = lax.dot_general(attended, grad_branch, over_rows, preferred_element_type=jnp.float32)
    grad_attended = lax.dot_general(
        grad_branch, out_mat, over_cols, preferred_element_type=jnp.float32
    ).astype(jnp.bfloat16)
    grad_packed = lax.map(
        attend_backward,
        (packed_seqs, grad_attended.reshape(seq_count, SEQ, model_width), log_totals),
    )
    grad_packed = grad_packed.reshape(tok_count, 3 * model_width)
    qkv_part = lax.dot_general(
        normed_low, grad_packed, over_rows, preferred_element_type=jnp.float32
    )
    grad_normed_one = lax.dot_general(
        grad_packed, qkv_mat, over_cols, preferred_element_type=jnp.float32
    )
    grad_token_norm, gain_one_part = norm1_back(grad_normed_one)
    tokens_grad = grad_resid + grad_token_norm
    gain_one_grad, qkv_grad, out_grad, gain_two_grad, centroid_grad = (
        lax.psum_scatter(gain_one_part, ("wide", "narrow"), scatter_dimension=0, tiled=True),
        lax.psum_scatter(qkv_part, ("wide", "narrow"), scatter_dimension=0, tiled=True),
        lax.psum_scatter(out_part, ("wide", "narrow"), scatter_dimension=0, tiled=True),
        lax.psum_scatter(gain_two_part, ("wide", "narrow"), scatter_dimension=0, tiled=True),
        lax.psum_scatter(centroid_part, ("wide", "narrow"), scatter_dimension=0, tiled=True),
    )
    return (
        mixed,
        tokens_grad,
        gain_one_grad,
        qkv_grad,
        out_grad,
        gain_two_grad,
        centroid_grad,
        up_grad,
        down_grad,
    )


def shards(mesh, v, idx, caps, g1, wq, wo, g2, centers, up, down, dy):
    T, D = v.shape
    E = caps.shape[0]
    c = Sizes(mesh, T, D, wq.shape[0], up.shape[2], E)
    if not c.fits:
        return plain_shards(v, idx, caps, g1, wq, wo, g2, centers, up, down, dy)
    res = forward_call(
        c, v, dy, idx.reshape(1, T), caps, wq, wo, centers.T, g1.reshape(1, -1), g2.reshape(1, -1), up, down
    )
    wt, nt, qkv, lse, att, resid, meta, mrow, ret, outp, ug, dg, cent, mine = res
    mixed, tokens_grad, qg, og, small = backward_call(
        c, v, dy, qkv, lse, att, resid, wt, nt, ret, outp, mrow, meta, cent, wq, mine
    )
    ug, dg, tokens_grad, mixed, qg, og, cen, g1_grad, g2_grad = finish_call(
        c, (ug, dg, tokens_grad, mixed, qg, og), (f32, f32, f32, bf16, f32, f32), small
    )
    return (
        mixed, tokens_grad, g1_grad.reshape(-1), qg, og, g2_grad.reshape(-1), cen.T, ug, dg,
    )


def solution(mesh):
    both = ("wide", "narrow")
    in_specs = (
        P(both, None), P(both, None), P(), P(both), P(both, None), P(both, None), P(both), P(both, None),
        P("wide", None, "narrow"), P("wide", None, "narrow"), P(both, None),
    )
    out_specs = (
        P(both, None), P(both, None), P(both), P(both, None), P(both, None), P(both), P(both, None),
        P("wide", None, "narrow"), P("wide", None, "narrow"),
    )
    return jax.shard_map(
        functools.partial(shards, mesh), mesh=mesh, in_specs=in_specs, out_specs=out_specs, check_vma=False
    )
```

```python
import functools

import jax
import jax.numpy as jnp
from jax import lax
from jax.experimental import pallas as pl
from jax.experimental.pallas import tpu as pltpu
from jax.sharding import PartitionSpec as P

HD = 64
SEQ = 1024
SLOT = 48
PAIR = 2 * HD
QB = 256
LANES = 128
GAIN1 = 126
GAIN2 = 127
NEG = -1e30
VMEM_CAP = 62 << 20
CID0 = 0
CID1 = 1
AHEAD_W = 5
AHEAD_X = 3
BEHIND_W = 3
SHORT = 3
LAST = 2

MESH = pl.DeviceIdType.MESH
NN_ = (((1,), (0,)), ((), ()))
NT_ = (((1,), (1,)), ((), ()))
TN_ = (((0,), (0,)), ((), ()))
f32 = jnp.float32
bf16 = jnp.bfloat16


def mm(a, b, dims=NN_):
    return lax.dot_general(a, b, dims, preferred_element_type=f32)


def wait_bytes(ref, sem):
    pltpu.make_async_copy(ref, ref, sem).wait()


arrive = wait_bytes


def push(src, dst, send, recv, **where):
    pltpu.make_async_remote_copy(
        src_ref=src, dst_ref=dst, send_sem=send, recv_sem=recv,
        device_id=where, device_id_type=MESH,
    ).start()


def half_mask(rows):
    return lax.broadcasted_iota(jnp.int32, (rows, PAIR), 1) < HD


def pick(mask, h, value):
    zero = jnp.zeros_like(value)
    return jnp.where(mask, value, zero) if h == 0 else jnp.where(mask, zero, value)


def layer_stats(x):
    centered = x - jnp.mean(x, 1, keepdims=True)
    r = lax.rsqrt(jnp.mean(centered * centered, 1, keepdims=True) + 1e-05)
    return centered * r, r


def attend_rows(qkv, seq, i, put_out, put_lse):
    length = (i + 1) * QB
    rows = pl.ds(i * QB, QB)
    mask = half_mask(QB)
    causal = lax.broadcasted_iota(jnp.int32, (QB, QB), 0) <= lax.broadcasted_iota(
        jnp.int32, (QB, QB), 1
    )
    q = qkv[rows, 0:PAIR] * bf16(HD**-0.5)
    k = qkv[pl.ds(0, length), PAIR : 2 * PAIR]
    v = qkv[pl.ds(0, length), 2 * PAIR : 3 * PAIR]
    outs, sums = [], []
    for h in range(2):
        s = mm(k, pick(mask, h, q), NT_)
        last = jnp.where(causal, s[length - QB :], NEG)
        top = jnp.max(last, 0, keepdims=True)
        if i:
            top = jnp.maximum(top, jnp.max(s[: length - QB], 0, keepdims=True))
        p = jnp.exp(last - top)
        total = jnp.sum(p, 0, keepdims=True)
        p = p.astype(bf16)
        if i:
            head = jnp.exp(s[: length - QB] - top)
            total = total + jnp.sum(head, 0, keepdims=True)
            p = jnp.concatenate([head.astype(bf16), p], 0)
        put_lse(h, rows, top + jnp.log(total))
        outs.append(mm(p, v, TN_))
        sums.append(total)
    inv = jnp.transpose(1.0 / jnp.concatenate(sums + [jnp.ones((6, QB), f32)], 0))
    put_out(rows, jnp.where(mask, outs[0] * inv[:, 0:1], outs[1] * inv[:, 1:2]).astype(bf16))


def attend_rows_back(qkv, att, datt, lse, i, first, prod, dk, dv, put_dq):
    length = (i + 1) * QB
    rows = pl.ds(i * QB, QB)
    mask = half_mask(QB)
    mask_all = half_mask(length)
    causal = lax.broadcasted_iota(jnp.int32, (QB, QB), 0) <= lax.broadcasted_iota(
        jnp.int32, (QB, QB), 1
    )
    q = qkv[rows, 0:PAIR] * bf16(HD**-0.5)
    k = qkv[pl.ds(0, length), PAIR : 2 * PAIR]
    v = qkv[pl.ds(0, length), 2 * PAIR : 3 * PAIR]
    do = datt[rows, :]
    dq = None
    for h in range(2):
        qh, dh = pick(mask, h, q), pick(mask, h, do)
        s = mm(k, qh, NT_)
        row = lse[h : h + 1, rows]
        p = jnp.exp(jnp.where(causal, s[length - QB :], NEG) - row)
        if i:
            p = jnp.concatenate([jnp.exp(s[: length - QB] - row), p], 0)
        dp = mm(v, dh, NT_)
        ds = (p * (dp - prod[h : h + 1, rows])).astype(bf16)
        a, b = mm(p.astype(bf16), dh), mm(ds, qh)
        if first and h == 0:
            dv[pl.ds(0, length), :] = a
            dk[pl.ds(0, length), :] = b
        else:
            dv[pl.ds(0, length), :] += a
            dk[pl.ds(0, length), :] += b
        part = mm(ds, pick(mask_all, h, k), TN_)
        dq = part if dq is None else dq + part
    put_dq(rows, (dq * HD**-0.5).astype(bf16))


class Sizes:
    def __init__(self, mesh, tokens, d, slab, ff, experts):
        self.NW, self.NN = mesh.shape["wide"], mesh.shape["narrow"]
        self.A, self.X = self.NW // 2, self.NN // 2
        self.T, self.D, self.slab, self.F, self.E = tokens, d, slab, ff, experts
        self.CW = 3 * PAIR
        self.G = d // PAIR
        self.J = self.G + d // self.CW
        self.R = self.NN * SLOT
        self.S = experts * SLOT
        self.EP = max(8, experts)
        rows = self.NW * self.R
        self.moe = rows * (5 * d + 3 * ff) * 2 < (24 << 20)
        self.fits = (
            self.moe and slab % 8 == 0 and tokens == SEQ and self.NW % 2 == 0 and self.NN % 2 == 0
            and self.NW > 2 and self.NN > 2 and experts == self.NW
        )


def place(c):
    w, n = lax.axis_index("wide"), lax.axis_index("narrow")
    return w, n, w // 2, lax.rem(w, 2), n // 2, lax.rem(n, 2)


def greet(c, w, n):
    bar = pltpu.get_barrier_semaphore()
    x, cc = n // 2, lax.rem(n, 2)

    def wide(i, _):
        pl.semaphore_signal(bar, inc=1, device_id={"wide": lax.rem(w + i, c.NW)}, device_id_type=MESH)
        return 0

    lax.fori_loop(1, c.NW, wide, 0)
    for k in range(1, c.X):
        to = lax.rem(x + k, c.X) * 2 + cc
        pl.semaphore_signal(bar, inc=1, device_id={"narrow": to}, device_id_type=MESH)
        other = w + 1 - 2 * lax.rem(w, 2)
        pl.semaphore_signal(bar, inc=1, device_id={"wide": other, "narrow": to}, device_id_type=MESH)
    pl.semaphore_signal(bar, inc=1, device_id={"narrow": x * 2 + 1 - cc}, device_id_type=MESH)
    return lambda: pl.semaphore_wait(bar, c.NW - 1 + 2 * c.X - 1)


def forward_kernel(c, *refs):
    (v_hbm, dy_hbm, idx_ref, cap_ref, wq_hbm, wo_hbm, cen_ref, g1_ref, g2_ref, up_hbm, down_hbm) = refs[:11]
    (w_out, normt_out, qkv_out, lse_out, att_out, resid_out, meta_out, mrow_out) = refs[11:19]
    (ret_out, outp_out, ug_out, dg_out, cent_out, mine_out) = refs[19:25]
    (v, nrm, normed, normt, oh, wbuf, wmat, wtr, misc, mrow, qkv, lse, att, sent, sendx, senddy,
     up, down, xin, dyin, hid, dpre, dexp, outp, part, lc, lx, stage, cent,
     lsem, in_sem, out_sem, w_sem, q_sem, st_sem, s1s, s1r, s2s, s2r, s4s, s4r,
     ds_, dr, xs_, xr, cs_, cr, fs, fr, gs, gr, ks, kr, rs_, rr, ws_, wr) = refs[25:]
    A, X, NW, NN, T, D, CW, G, J = c.A, c.X, c.NW, c.NN, c.T, c.D, c.CW, c.G, c.J
    w, n, a, b, x, cc = place(c)
    own = (a, b, x, cc)
    dy = sent

    for j in range(J):
        dst = wbuf.at[(j, *own)]
        if j < G:
            for p in range(3):
                pltpu.make_async_copy(
                    wq_hbm.at[:, pl.ds(p * D + j * PAIR, PAIR)], dst.at[:, pl.ds(p * PAIR, PAIR)], lsem.at[j]
                ).start()
        else:
            pltpu.make_async_copy(wo_hbm.at[:, pl.ds((j - G) * CW, CW)], dst, lsem.at[j]).start()
    loads = [(dy_hbm, dy), (v_hbm, v), (up_hbm.at[0], up), (down_hbm.at[0], down)]
    for i, (s, d) in enumerate(loads):
        pltpu.make_async_copy(s, d, in_sem.at[i]).start()

    def load_wait(i):
        wait_bytes(loads[i][1], in_sem.at[i])

    met = greet(c, w, n)

    pad = LANES - c.slab
    small = jnp.concatenate(
        [cen_ref[...].astype(f32), jnp.zeros((GAIN1 - c.E, c.slab), f32), g1_ref[...].astype(f32), g2_ref[...].astype(f32)], 0
    )
    small = jnp.concatenate([small, jnp.zeros((LANES, pad), f32)], 1)
    small = jnp.transpose(small)[0 : c.slab]
    mine_out[...] = small
    misc[own] = small.astype(bf16)

    met()

    def buf(j):
        return misc if isinstance(j, int) and j == J else wbuf.at[j]

    def s1(j):
        if not (isinstance(j, int) and j == J):
            wait_bytes(buf(j).at[own], lsem.at[j])
        for k in range(1, A):
            push(buf(j).at[own], buf(j).at[own], s1s.at[j], s1r.at[j], wide=lax.rem(a + k, A) * 2 + b)

    plane = [(p, q) for p in range(2) for q in range(X) if p or q]


    def s2_short(j):
        arrive(buf(j).at[pl.ds(0, A - 1), b, x, cc], s1r.at[j])
        mine = buf(j).at[:, b, x, cc]
        for i, (p, q) in enumerate(plane):
            push(
                mine, mine, s2s.at[j, i], s2r.at[j, i],
                wide=a * 2 + lax.rem(b + p, 2), narrow=lax.rem(x + q, X) * 2 + cc,
            )

    def s2_long(j):
        arrive(buf(j).at[pl.ds(0, A - 1), b, x, cc], s1r.at[j])
        mine = buf(j).at[:, b, x, cc]
        for q in range(1, X):
            push(mine, mine, s2s.at[j, q], s2r.at[j, q], narrow=lax.rem(x + q, X) * 2 + cc)

    def s3_long(j):
        for q in range(1, X):
            arrive(buf(j).at[:, b, x, cc], s2r.at[j, q])
        mine = buf(j).at[:, b, :, cc]
        push(mine, mine, s2s.at[j, 0], s2r.at[j, 0], wide=a * 2 + 1 - b)

    def plane_short(j, sem):
        for i in range(len(plane)):
            arrive(buf(j).at[:, b, x, cc], sem.at[j, i])

    def plane_long(j, sem):
        arrive(buf(j).at[:, b, :, cc], sem.at[j, 0])

    def to_core(j):
        mine = buf(j).at[:, :, :, cc]
        push(mine, mine, s4s.at[j], s4r.at[j], narrow=x * 2 + 1 - cc)

    def s4_short(j):
        plane_short(j, s2r)
        to_core(j)

    def s4_long(j):
        plane_long(j, s2r)
        to_core(j)

    def take(j, turn=True):
        arrive(buf(j).at[:, :, :, cc], s4r.at[j])
        val = wbuf[j].reshape(D, CW)
        wmat[j] = val
        if turn:
            turned(j, val)

    def turned(j, val):
        wtr[j] = jnp.transpose(val)
        pltpu.make_async_copy(wtr.at[j], w_out.at[j], w_sem.at[j]).start()

    def due(t):
        for j in range(J):
            short = j < SHORT
            if t == (j + 4):
                (s4_short if short else s4_long)(j)
            if not short and t == j + 2:
                s3_long(j)
            if t == (j + 2 if short else j):
                (s2_short if short else s2_long)(j)
            if t == (j if short else max(j - 2, 1)):
                s1(j)

    s1(J)
    due(0)
    hot = (lax.broadcasted_iota(jnp.int32, (c.EP, T), 0) == idx_ref[...]).astype(f32)
    lane = lax.broadcasted_iota(jnp.int32, (c.EP, T), 1)
    count = hot
    shift = 1
    while shift < T:
        count = count + jnp.where(lane >= shift, pltpu.roll(count, shift, 1), 0.0)
        shift *= 2
    rank = jnp.sum((count - hot) * hot, 0, keepdims=True)
    ceiling = jnp.zeros((1, T), f32)
    for e in range(c.E):
        ceiling = ceiling + hot[e : e + 1, :] * cap_ref[e].astype(f32)
    kept = rank < ceiling
    slot = jnp.where(kept, idx_ref[...].astype(f32) * SLOT + rank, -1.0)

    due(1)
    s2_short(J)
    oh[...] = (lax.broadcasted_iota(jnp.int32, (c.S, T), 0).astype(f32) == slot).astype(bf16)
    due(2)
    load_wait(0)
    senddy[...] = mm(oh[...], dy[...]).astype(bf16)
    due(3)

    def dy_w(k):
        to = lax.rem(w + k, NW)
        push(senddy.at[pl.ds(pl.multiple_of(to * SLOT, SLOT), SLOT)], dyin.at[w, x, cc], ds_.at[k], dr.at[k], wide=to)

    def dy_x(k):
        src = lax.rem(w - k + NW, NW)

        @pl.when(k > 0)
        def _():
            arrive(dyin.at[src, x, cc], dr.at[k])

        for q in range(1, X):
            push(dyin.at[src, x, cc], dyin.at[src, x, cc], xs_.at[k], xr.at[k], narrow=lax.rem(x + q, X) * 2 + cc)

    dyin[w, x, cc] = senddy[pl.ds(pl.multiple_of(w * SLOT, SLOT), SLOT), :]
    load_wait(1)

    def norm1(i, _):
        rows = pl.ds(i * 128, 128)
        nrm[rows, :] = layer_stats(v[rows, :].astype(f32))[0]
        return 0

    lax.fori_loop(0, T // 128, norm1, 0)
    s4_short(J)
    due(4)
    arrive(misc.at[:, :, :, cc], s4r.at[J])
    mrow[...] = jnp.transpose(misc[...].reshape(D, LANES).astype(f32))
    gain1 = mrow[GAIN1 : GAIN1 + 1, :]
    gain2 = mrow[GAIN2 : GAIN2 + 1, :]
    pltpu.make_async_copy(mrow, mrow_out, out_sem.at[0]).start()

    def norm1b(i, _):
        rows = pl.ds(i * 128, 128)
        normed[rows, :] = (nrm[rows, :] * gain1).astype(bf16)
        return 0

    lax.fori_loop(0, T // 128, norm1b, 0)
    per = -(-NW // 4)

    def pair(g, _):
        slot_ = lax.rem(g, 2)
        take(g)

        @pl.when(g >= 2)
        def _():
            wait_bytes(qkv.at[slot_], q_sem.at[slot_])

        qkv[slot_] = mm(normed[...], wmat[g]).astype(bf16)
        pltpu.make_async_copy(qkv.at[slot_], qkv_out.at[g], q_sem.at[slot_]).start()

        def at_step(fn, j, wanted):
            @pl.when(wanted & (j < J))
            def _():
                fn(j)

        at_step(s4_short, g + 1, g + 1 < SHORT)
        at_step(s4_long, g + 1, g + 1 >= SHORT)
        at_step(s3_long, g + 3, g + 3 >= SHORT)
        at_step(s2_short, g + 3, g + 3 < SHORT)
        at_step(s2_long, g + 5, g + 5 >= SHORT)
        at_step(s1, g + 5, g + 5 < SHORT)
        at_step(s1, g + 7, g + 7 >= SHORT)

        def put_out(rows, val):
            att[rows, pl.ds(pl.multiple_of(g * PAIR, PAIR), PAIR)] = val

        def put_lse(h, rows, val):
            lse[g, h : h + 1, rows] = val

        for i in range(T // QB):
            if i == T // QB - 1:
                @pl.when(g == G - 1)
                def _():
                    for j in range(G + 1, J):
                        (s4_short if j < SHORT else s4_long)(j)

                for q in range(per):
                    k = g * per + q

                    @pl.when((k >= 1) & (k < NW))
                    def _():
                        dy_w(k)

                    @pl.when((g >= 2) & (k - 2 * per < NW))
                    def _():
                        dy_x(k - 2 * per)

            attend_rows(qkv.at[slot_], T, i, put_out, put_lse)
        return 0

    lax.fori_loop(0, G, pair, 0)
    pltpu.make_async_copy(lse, lse_out, out_sem.at[1]).start()
    pltpu.make_async_copy(att, att_out, out_sem.at[2]).start()

    for j in range(G, J):
        take(j, False)
        at = slice((j - G) * CW, (j - G + 1) * CW)
        nrm[:, at] = v[:, at].astype(f32) + mm(att[...], wmat[j])

    def tail(i, _):
        rows = pl.ds(i * QB, QB)
        sent[rows, :] = (layer_stats(nrm[rows, :])[0] * gain2).astype(bf16)
        return 0

    lax.fori_loop(0, T // QB, tail, 0)
    pltpu.make_async_copy(nrm, resid_out, out_sem.at[3]).start()
    sendx[...] = mm(oh[...], sent[...]).astype(bf16)

    def x_w(k):
        to = lax.rem(w + k, NW)
        push(sendx.at[pl.ds(pl.multiple_of(to * SLOT, SLOT), SLOT)], xin.at[w, x, cc], fs.at[k], fr.at[k], wide=to)

    for k in range(1, AHEAD_W):
        x_w(k)
    xin[w, x, cc] = sendx[pl.ds(pl.multiple_of(w * SLOT, SLOT), SLOT), :]

    crow = mrow[pl.ds(w, 1), :]

    def source(i):
        return lax.rem(w - i + NW, NW)

    def fwd_x(i):
        src = source(i)

        @pl.when(i > 0)
        def _():
            arrive(xin.at[src, x, cc], fr.at[i])

        for k in range(1, X):
            push(xin.at[src, x, cc], xin.at[src, x, cc], gs.at[i], gr.at[i], narrow=lax.rem(x + k, X) * 2 + cc)

    def fwd_c(i):
        src = source(i)
        arrive(xin.at[src, pl.ds(0, X - 1), cc], gr.at[i])
        push(xin.at[src, :, cc], xin.at[src, :, cc], ks.at[i], kr.at[i], narrow=x * 2 + 1 - cc)

    def expert(i):
        src = source(i)
        arrive(xin.at[src, :, cc], kr.at[i])
        xb = xin[src].reshape(c.R, D)
        db = dyin[src].reshape(c.R, D)
        xf, df = xb.astype(f32), db.astype(f32)
        s = jax.nn.sigmoid(jnp.sum(xf * crow, 1, keepdims=True))
        de = (df * s).astype(bf16)
        pre = mm(xb, up[...])
        cdf = 0.5 * (1.0 + lax.erf(pre * 0.7071067811865476))
        hb = (pre * cdf).astype(bf16)
        slope = cdf + pre * (jnp.exp(-0.5 * pre * pre) * 0.3989422804014327)
        dpb = (mm(de, down[...]) * slope).astype(bf16)
        out = mm(hb, down[...], NT_)
        dl = jnp.sum(df * out, 1, keepdims=True) * (s * (1.0 - s))
        dn = mm(dpb, up[...], NT_) + dl * crow
        part[src] = dn.astype(bf16).reshape(X, 2, SLOT, D)
        outp[src] = out.astype(bf16).reshape(X, 2, SLOT, D)
        cent[...] += jnp.broadcast_to(jnp.sum(dl * xf, 0, keepdims=True), cent.shape)
        rows = pl.ds(pl.multiple_of(src * c.R, SLOT), c.R)
        hid[rows, :] = hb
        dpre[rows, :] = dpb
        dexp[rows, :] = de

    def ret_c(i):
        src = source(i)
        push(part.at[src, :, 1 - cc], lc.at[src], rs_.at[0, i], rr.at[0, i], narrow=x * 2 + 1 - cc)

    def ret_x(i):
        src = source(i)
        arrive(lc.at[src], rr.at[0, i])
        part[src, :, cc] = (part[src, :, cc].astype(f32) + lc[src].astype(f32)).astype(bf16)
        for k in range(1, X):
            x2 = lax.rem(x + k, X)
            push(part.at[src, x2, cc], lx.at[src, x], rs_.at[1, i], rr.at[1, i], narrow=x2 * 2 + cc)

    def ret_w(i):
        src = source(i)
        arrive(lx.at[src, pl.ds(0, X - 1)], rr.at[1, i])
        total = part[src, x, cc].astype(f32)
        for k in range(1, X):
            total = total + lx[src, lax.rem(x + k, X)].astype(f32)
        part[src, x, cc] = total.astype(bf16)

        @pl.when(i > 0)
        def _():
            push(part.at[src, x, cc], ret_out.at[w], ws_.at[i], wr.at[i], wide=src)

        @pl.when(i == 0)
        def _():
            pltpu.make_async_copy(part.at[src, x, cc], ret_out.at[w], ws_.at[0]).start()

    fwd_x(0)
    for k in range(per * (G - 2), NW):
        dy_x(k)

    def dy_all(k, _):
        arrive(dyin.at[w, x, cc], xr.at[k])
        return 0

    for q in range(X - 1):
        lax.fori_loop(0, NW, dy_all, 0)
    push(dyin.at[:, :, cc], dyin.at[:, :, cc], cs_, cr, narrow=x * 2 + 1 - cc)
    for j in range(G, J):
        turned(j, wmat[j])
    normt[...] = jnp.transpose(normed[...])
    pltpu.make_async_copy(normt, normt_out, out_sem.at[5]).start()

    logits = mm(mrow[0 : c.EP, :].astype(bf16), sent[...], NT_)
    gate = jax.nn.sigmoid(jnp.sum(logits * hot, 0, keepdims=True)) * kept.astype(f32)
    meta_out[...] = jnp.concatenate([slot, gate, jnp.zeros((6, T), f32)], 0)
    cent[...] = jnp.zeros_like(cent)

    fwd_c(0)
    for k in range(1, AHEAD_X):
        fwd_x(k)
    load_wait(2)
    load_wait(3)
    arrive(dyin.at[:, :, cc], cr)

    def block(i, _):
        @pl.when(i + AHEAD_W < NW)
        def _():
            x_w(i + AHEAD_W)

        @pl.when(i + 1 < NW)
        def _():
            fwd_c(i + 1)

        @pl.when(i + AHEAD_X < NW)
        def _():
            fwd_x(i + AHEAD_X)

        expert(i)
        ret_c(i)

        @pl.when(i >= 1)
        def _():
            ret_x(i - 1)

        @pl.when(i >= BEHIND_W)
        def _():
            ret_w(i - BEHIND_W)

        return 0

    lax.fori_loop(0, NW, block, 0)
    ret_x(NW - 1)
    for i in range(NW - BEHIND_W, NW - 1):
        ret_w(i)
    pltpu.make_async_copy(outp, outp_out, out_sem.at[4]).start()
    cent_out[...] = cent[...]
    parts = D // QB

    def grads(lhs, rhs, out, second):
        def one_block(i, _):
            at = pl.ds(pl.multiple_of(i * QB, QB), QB)
            if second:
                wait_bytes(stage.at[i], st_sem.at[i])
            stage[i] = mm(lhs(at), rhs[...], TN_).astype(bf16)
            pltpu.make_async_copy(stage.at[i], out.at[0, at], st_sem.at[i]).start()
            return 0

        lax.fori_loop(0, parts, one_block, 0)

    grads(lambda at: dexp[:, at], hid, dg_out, False)
    ret_w(NW - 1)
    grads(lambda at: xin[:, :, :, :, at].reshape(NW * c.R, QB), dpre, ug_out, True)

    for q, ref in enumerate([mrow, lse, att, nrm, outp, normt]):
        wait_bytes(ref, out_sem.at[q])
    for q in range(2):
        wait_bytes(qkv.at[q], q_sem.at[q])
    for j in [J] + list(range(J)):
        if not (isinstance(j, int) and j == J):
            wait_bytes(wtr.at[j], w_sem.at[j])
        arrive(buf(j).at[pl.ds(0, A - 1), b, x, cc], s1s.at[j])
        if j == J or j < SHORT:
            plane_short(j, s2s)
        else:
            plane_long(j, s2s)
            for q in range(1, X):
                arrive(buf(j).at[:, b, x, cc], s2s.at[j, q])
        arrive(buf(j).at[:, :, :, cc], s4s.at[j])
    arrive(dyin.at[:, :, cc], cs_)

    def drain(i, _):
        src = source(i)
        arrive(xin.at[src, pl.ds(0, X - 1), cc], xs_.at[i])
        arrive(xin.at[src, pl.ds(0, X - 1), cc], gs.at[i])
        arrive(xin.at[src, :, cc], ks.at[i])
        arrive(lc.at[src], rs_.at[0, i])
        arrive(lx.at[src, pl.ds(0, X - 1)], rs_.at[1, i])

        @pl.when(i > 0)
        def _():
            arrive(xin.at[src, x, cc], ds_.at[i])
            arrive(xin.at[src, x, cc], fs.at[i])
            arrive(xin.at[src, x, cc], ws_.at[i])
            arrive(xin.at[src, x, cc], wr.at[i])

        return 0

    lax.fori_loop(0, NW, drain, 0)
    wait_bytes(part.at[0, 0, 0], ws_.at[0])
    for i in range(parts):
        wait_bytes(stage.at[i], st_sem.at[i])


def forward_call(c, v, dy, idx, cap, wq, wo, cen, g1, g2, up, down):
    T, D, CW, G, J, NW, NN, A, X, L, F = c.T, c.D, c.CW, c.G, c.J, c.NW, c.NN, c.A, c.X, c.slab, c.F
    any_ = pl.BlockSpec(memory_space=pl.ANY)
    vm = pl.BlockSpec(memory_space=pltpu.VMEM)
    sm = pl.BlockSpec(memory_space=pltpu.SMEM)
    sds = jax.ShapeDtypeStruct
    rows_ = (NW, X, 2, SLOT, D)
    outs = [
        (sds((J, CW, D), bf16), any_),
        (sds((D, T), bf16), any_),
        (sds((G, T, CW), bf16), any_),
        (sds((G, 8, T), f32), any_),
        (sds((T, D), bf16), any_),
        (sds((T, D), f32), any_),
        (sds((8, T), f32), vm),
        (sds((LANES, D), f32), any_),
        (sds((NW, SLOT, D), bf16), any_),
        (sds(rows_, bf16), any_),
        (sds((1, D, F), bf16), any_),
        (sds((1, D, F), bf16), any_),
        (sds((8, D), f32), vm),
        (sds((L, LANES), f32), vm),
    ]
    dma, V = pltpu.SemaphoreType.DMA, pltpu.VMEM
    rows = NW * c.R
    scratch = [
        V((T, D), bf16), V((T, D), f32), V((T, D), bf16), V((D, T), bf16), V((c.S, T), bf16),
        V((J, A, 2, X, 2, L, CW), bf16), V((J, D, CW), bf16), V((J, CW, D), bf16), V((A, 2, X, 2, L, LANES), bf16), V((LANES, D), f32),
        V((2, T, CW), bf16), V((G, 8, T), f32), V((T, D), bf16), V((T, D), bf16), V((c.S, D), bf16), V((c.S, D), bf16),
        V((D, F), bf16), V((D, F), bf16), V(rows_, bf16), V(rows_, bf16),
        V((rows, F), bf16), V((rows, F), bf16), V((rows, D), bf16), V(rows_, bf16), V(rows_, bf16),
        V((NW, X, SLOT, D), bf16), V((NW, X, SLOT, D), bf16), V((D // QB, QB, F), bf16), V((8, D), f32),
        dma((J,)), dma((4,)), dma((6,)), dma((J,)), dma((2,)), dma((D // QB,)),
    ] + [dma((J + 1,))] * 2 + [dma((J + 1, 2 * X - 1))] * 2 + [dma((J + 1,))] * 2 + [dma((NW,))] * 4 + [dma(()), dma(())] + [dma((NW,))] * 6 + [
        dma((2, NW)), dma((2, NW)), dma((NW,)), dma((NW,)),
    ]
    return pl.pallas_call(
        functools.partial(forward_kernel, c),
        out_shape=tuple(o[0] for o in outs),
        in_specs=[any_, any_, vm, sm, any_, any_, vm, vm, vm, any_, any_],
        out_specs=tuple(o[1] for o in outs),
        scratch_shapes=scratch,
        compiler_params=pltpu.CompilerParams(
            collective_id=CID0, has_side_effects=True, vmem_limit_bytes=VMEM_CAP
        ),
        name="forward",
    )(v, dy, idx, cap, wq, wo, cen, g1, g2, up, down)


def backward_kernel(c, *refs):
    (v_hbm, dy_hbm, qkv_hbm, lse_hbm, att_hbm, resid_hbm, wt_hbm, nt_hbm, ret_hbm, outp_hbm, mrow, meta, cent, wq, mine) = refs[:15]
    (mixed_out, tok_out, qg_out, og_out, small_out) = refs[15:20]
    (v, dy, qkv, lse, att, resid, wt, ret, oh, normt, dbr, datt, dnm, dqkv, dk, dv, prod, rowbuf,
     part, lc, lx, got, mixed,
     gb, la, lb, lz, sgb, sla, slb, slz, lxx,
     in_sem, q_sem, out_sem, os_, orv, ows, owr, rs_, rr, ps_, pr, tokacc) = refs[20:]
    A, X, NW, NN, T, D, CW, G, J = c.A, c.X, c.NW, c.NN, c.T, c.D, c.CW, c.G, c.J
    H = J - G
    w, n, a, b, x, cc = place(c)
    blocks = T // QB

    loads = [
        (ret_hbm, ret), (resid_hbm, resid), (dy_hbm, dy), (att_hbm, att), (v_hbm, v), (lse_hbm, lse), (nt_hbm, normt),
        (wt_hbm.at[pl.ds(G, H)], wt.at[pl.ds(G, H)]), (wt_hbm.at[pl.ds(0, G)], wt.at[pl.ds(0, G)]),
    ]
    for i, (s, d) in enumerate(loads):
        pltpu.make_async_copy(s, d, in_sem.at[i]).start()
    own_part = pltpu.make_async_copy(outp_hbm.at[:, :, cc], part, in_sem.at[9])
    own_part.start()

    def load_wait(i):
        wait_bytes(loads[i][1], in_sem.at[i])

    def fetch_qkv(g, slot_):
        pltpu.make_async_copy(qkv_hbm.at[g], qkv.at[slot_], q_sem.at[1, slot_]).start()

    fetch_qkv(0, 0)
    met = greet(c, w, n)

    slot, gate = meta[0:1, :], meta[1:2, :]
    hits = lax.broadcasted_iota(jnp.int32, (c.S, T), 0).astype(f32) == slot
    oh[...] = hits.astype(bf16)
    gain1, gain2 = mrow[GAIN1 : GAIN1 + 1, :], mrow[GAIN2 : GAIN2 + 1, :]
    load_wait(0)
    dnm[...] = mm(oh[...], ret[...].reshape(c.S, D), TN_)
    oh[...] = jnp.where(hits, gate, 0.0).astype(bf16)
    load_wait(1)
    load_wait(2)
    rowbuf[...] = jnp.zeros_like(rowbuf)
    rowbuf[pl.ds(w, 1), :] = cent[0:1, :]

    def norm2_back(i, acc):
        rows = pl.ds(i * QB, QB)
        n2, r2 = layer_stats(resid[rows, :])
        dn2 = dnm[rows, :]
        dn = dn2 * gain2
        step = r2 * (dn - jnp.mean(dn, 1, keepdims=True) - n2 * jnp.mean(dn * n2, 1, keepdims=True))
        dres = dy[rows, :].astype(f32) + step
        dnm[rows, :] = dres
        dbr[rows, :] = dres.astype(bf16)
        return acc + jnp.sum(dn2 * n2, 0, keepdims=True)

    rowbuf[GAIN2 : GAIN2 + 1, :] = lax.fori_loop(0, blocks, norm2_back, jnp.zeros((1, D), f32))
    load_wait(3)

    big = (gb, la, lb, lz, 0, lxx)
    tiny = (sgb, sla, slb, slz, J)

    def add(p, q):
        return (p.astype(f32) + q.astype(f32)).astype(bf16)

    def ra(t, j):
        push(t[0].at[j, :, :, :, 1 - cc], t[1].at[j], rs_.at[0, t[4] + j], rr.at[0, t[4] + j], narrow=x * 2 + 1 - cc)

    plane = [(p, q) for p in range(2) for q in range(X) if p or q]

    plane = [(p, q) for p in range(2) for q in range(X) if p or q]

    def join(t, j):
        arrive(t[1].at[j], rr.at[0, t[4] + j])
        t[0][j, :, :, :, cc] = add(t[0][j, :, :, :, cc], t[1][j])

    def to_plane(t, j, i, src, dst, p, q):
        push(
            src, dst, ps_.at[t[4] + j, i], pr.at[t[4] + j, i],
            wide=a * 2 + lax.rem(b + p, 2), narrow=lax.rem(x + q, X) * 2 + cc,
        )

    def to_outer(t, j, total):
        t[0][j, :, b, x, cc] = total.astype(bf16)
        for k in range(1, A):
            a2 = lax.rem(a + k, A)
            push(t[0].at[j, a2, b, x, cc], t[3].at[j, a], rs_.at[1, t[4] + j], rr.at[1, t[4] + j], wide=a2 * 2 + b)

    def rb_short(t, j):
        join(t, j)
        for i, (p, q) in enumerate(plane):
            to_plane(t, j, i, t[0].at[j, :, lax.rem(b + p, 2), lax.rem(x + q, X), cc], t[2].at[j, b, x], p, q)

    def rc_short(t, j):
        plane_short(t, j, pr)
        total = t[0][j, :, b, x, cc].astype(f32)
        for p, q in plane:
            total = total + t[2][j, lax.rem(b + p, 2), lax.rem(x + q, X)].astype(f32)
        to_outer(t, j, total)

    def plane_short(t, j, sem):
        for i in range(len(plane)):
            arrive(t[2].at[j, 0, 0], sem.at[t[4] + j, i])

    def rb_long(t, j):
        join(t, j)
        for q in range(X):
            t[2][j, b, q] = t[0][j, :, 1 - b, q, cc]
        to_plane(t, j, 0, t[2].at[j, b], t[2].at[j, b], 1, 0)

    def rc_long(t, j):
        arrive(t[2].at[j, 0], pr.at[t[4] + j, 0])
        for q in range(X):
            t[0][j, :, b, q, cc] = add(t[0][j, :, b, q, cc], t[2][j, 1 - b, q])
        for q in range(1, X):
            to_plane(t, j, q, t[0].at[j, :, b, lax.rem(x + q, X), cc], t[5].at[j, x], 0, q)

    def rd_long(t, j):
        for q in range(1, X):
            arrive(t[2].at[j, 0, 0], pr.at[t[4] + j, q])
        total = t[0][j, :, b, x, cc].astype(f32)
        for q in range(1, X):
            total = total + t[5][j, lax.rem(x + q, X)].astype(f32)
        to_outer(t, j, total)

    def plane_long(t, j, sem):
        arrive(t[2].at[j, 0], sem.at[t[4] + j, 0])
        for q in range(1, X):
            arrive(t[2].at[j, 0, 0], sem.at[t[4] + j, q])

    def rf(t, j):
        arrive(t[3].at[j, pl.ds(0, A - 1)], rr.at[1, t[4] + j])
        total = t[0][j, a, b, x, cc].astype(f32)
        for k in range(1, A):
            total = total + t[3][j, lax.rem(a + k, A)].astype(f32)
        return total

    def rf_w(j):
        og_out[:, j * CW : (j + 1) * CW] = rf(big, j)

    def rf_q(g):
        total = rf(big, H + g)
        for p in range(3):
            qg_out[:, pl.ds(pl.multiple_of(p * D + g * PAIR, PAIR), PAIR)] = total[:, p * PAIR : (p + 1) * PAIR]

    sgb[0] = jnp.transpose(rowbuf[...]).astype(bf16).reshape(A, 2, X, 2, c.slab, LANES)
    for h in range(H):
        gb[h] = mm(att[...], dbr[:, h * CW : (h + 1) * CW], TN_).astype(bf16).reshape(A, 2, X, 2, c.slab, CW)
        if h == 0:
            met()
            push(outp_hbm.at[:, :, 1 - cc], lc, os_.at[0], orv.at[0], narrow=x * 2 + 1 - cc)
            ra(tiny, 0)
        ra(big, h)

    load_wait(7)

    def out_back(i, _):
        at = pl.ds(pl.multiple_of(i * QB, QB), QB)
        datt[:, at] = mm(dbr[...], wt[pl.ds(G, H), :, at].reshape(D, QB)).astype(bf16)
        return 0

    lax.fori_loop(0, D // QB, out_back, 0)
    load_wait(4)
    load_wait(6)
    rb_short(tiny, 0)
    for h in range(H):
        rb_long(big, h)
    load_wait(5)
    own_part.wait()

    def o_x(i):
        for k in range(1, X):
            x2 = lax.rem(x + k, X)
            push(part.at[i, x2], lx.at[i, x], os_.at[1 + i], orv.at[1 + i], narrow=x2 * 2 + cc)

    def o_w(i):
        arrive(lx.at[i, pl.ds(0, X - 1)], orv.at[1 + i])
        total = part[i, x].astype(f32)
        for k in range(1, X):
            total = total + lx[i, lax.rem(x + k, X)].astype(f32)
        part[i, x] = total.astype(bf16)

        @pl.when(i != w)
        def _():
            push(part.at[i, x], got.at[w], ows.at[i], owr.at[lax.rem(w - i + NW, NW)], wide=i)

        @pl.when(i == w)
        def _():
            got[w] = part[w, x]

    arrive(lc, orv.at[0])

    def merge(i, _):
        part[i] = add(part[i], lc[i])
        return 0

    lax.fori_loop(0, NW, merge, 0)
    per = -(-NW // 4)

    def spread(fn, step):
        for k in range(per):
            i = lax.rem(w + step * per + k, NW)

            @pl.when(step * per + k < NW)
            def _():
                fn(i)

    def pair(g, _):
        s_ = lax.rem(g, 2)

        @pl.when(g + 1 < G)
        def _():
            fetch_qkv(g + 1, 1 - s_)

        wait_bytes(qkv.at[s_], q_sem.at[1, s_])
        lanes = pl.ds(pl.multiple_of(g * PAIR, PAIR), PAIR)
        att_g, datt_g = att.at[:, lanes], datt.at[:, lanes]
        full = jnp.transpose(datt_g[...].astype(f32) * att_g[...].astype(f32))
        prod[0:1, :] = jnp.sum(full[0:HD], 0, keepdims=True)
        prod[1:2, :] = jnp.sum(full[HD:], 0, keepdims=True)

        def put_dq(rows, val):
            dqkv[g, rows, 0:PAIR] = val

        for i in reversed(range(blocks)):
            if i == 0:
                @pl.when(g == 0)
                def _():
                    rc_short(tiny, 0)

                rc_long(big, g)

                @pl.when(g >= 1)
                def _():
                    rd_long(big, g - 1)

            attend_rows_back(qkv.at[s_], att_g, datt_g, lse.at[g], i, i == blocks - 1, prod, dk, dv, put_dq)
            if i == blocks - 2:
                @pl.when((g >= 1) & (g + H - 1 < J - LAST))
                def _():
                    rb_long(big, g + H - 1)

                @pl.when((g >= 1) & (g + H - 1 >= J - LAST))
                def _():
                    rb_short(big, g + H - 1)

                @pl.when(g < 4)
                def _():
                    spread(o_x, g)

                @pl.when(g >= 2)
                def _():
                    spread(o_w, g - 2)

        dqkv[g, :, PAIR : 2 * PAIR] = dk[...].astype(bf16)
        dqkv[g, :, 2 * PAIR :] = dv[...].astype(bf16)
        gb[H + g] = mm(normt[...], dqkv[g]).astype(bf16).reshape(A, 2, X, 2, c.slab, CW)
        ra(big, H + g)
        return 0

    lax.fori_loop(0, G, pair, 0)
    load_wait(8)

    def back(i):
        at = slice(i * QB, (i + 1) * QB)
        total = mm(dqkv[0], wt[0, :, at])
        for g in range(1, G):
            total = total + mm(dqkv[g], wt[g, :, at])
        tokacc[:, at] = total

    back(0)
    rb_short(big, J - 1)
    rd_long(big, J - LAST - 1)
    for j in range(J - LAST, J - 1):
        rc_short(big, j)
    for i in range(1, D // QB):
        back(i)
    def norm1_back(i, _):
        rows = pl.ds(i * QB, QB)
        n1, r1 = layer_stats(v[rows, :].astype(f32))
        dm = tokacc[rows, :] * gain1
        step = r1 * (dm - jnp.mean(dm, 1, keepdims=True) - n1 * jnp.mean(dm * n1, 1, keepdims=True))
        dbr[rows, :] = (dnm[rows, :] + step).astype(bf16)
        return 0

    lax.fori_loop(0, blocks, norm1_back, 0)
    tok_copy = pltpu.make_async_copy(dbr, tok_out, out_sem.at[0])
    tok_copy.start()
    rc_short(big, J - 1)

    def o_wait(k, _):
        arrive(got.at[0], owr.at[k])
        return 0

    lax.fori_loop(1, NW, o_wait, 0)

    def mix(i, _):
        cols = pl.ds(pl.multiple_of(i * QB, QB), QB)
        rows = pl.ds(i * QB, QB)
        mixed[rows, :] = (resid[rows, :] + mm(oh[:, cols], got[...].reshape(c.S, D), TN_)).astype(bf16)
        return 0

    lax.fori_loop(0, blocks, mix, 0)
    mix_copy = pltpu.make_async_copy(mixed, mixed_out, out_sem.at[1])
    mix_copy.start()
    for h in range(H):
        rf_w(h)

    def fin(g, _):
        rf_q(g)
        return 0

    lax.fori_loop(0, G, fin, 0)
    sums_ = jnp.sum(qg_out[...] * wq[...].astype(f32), 1, keepdims=True) / mine[:, GAIN1 : GAIN1 + 1]
    at_gain = lax.broadcasted_iota(jnp.int32, (c.slab, LANES), 1) == GAIN1
    small_out[...] = jnp.where(at_gain, sums_, rf(tiny, 0))

    arrive(lc, os_.at[0])

    def drain(i, _):
        arrive(lx.at[i, pl.ds(0, X - 1)], os_.at[1 + i])

        @pl.when(i != w)
        def _():
            arrive(got.at[0], ows.at[i])

        return 0

    lax.fori_loop(0, NW, drain, 0)

    def drain_sums(t, j, route):
        arrive(t[1].at[j], rs_.at[0, t[4] + j])
        route(t, j, ps_)
        arrive(t[3].at[j, pl.ds(0, A - 1)], rs_.at[1, t[4] + j])

    for j in range(J):
        drain_sums(big, j, plane_long if j < J - LAST else plane_short)
    drain_sums(tiny, 0, plane_short)
    tok_copy.wait()
    mix_copy.wait()


def backward_call(c, v, dy, qkv, lse, att, resid, wt, nt, ret, outp, mrow, meta, cent, wq, mine):
    T, D, CW, G, J, NW, NN, A, X, L = c.T, c.D, c.CW, c.G, c.J, c.NW, c.NN, c.A, c.X, c.slab
    any_ = pl.BlockSpec(memory_space=pl.ANY)
    vm = pl.BlockSpec(memory_space=pltpu.VMEM)
    sds = jax.ShapeDtypeStruct
    dma, V = pltpu.SemaphoreType.DMA, pltpu.VMEM

    def sums(k, width):
        return [
            V((k, A, 2, X, 2, L, width), bf16), V((k, A, 2, X, L, width), bf16),
            V((k, 2, X, A, L, width), bf16), V((k, A, L, width), bf16),
        ]

    scratch = [
        V((T, D), bf16), V((T, D), bf16), V((2, T, CW), bf16), V((G, 8, T), f32), V((T, D), bf16), V((T, D), f32),
        V((J, CW, D), bf16), V((NW, SLOT, D), bf16), V((c.S, T), bf16),
        V((D, T), bf16), V((T, D), bf16), V((T, D), bf16), V((T, D), f32), V((G, T, CW), bf16),
        V((T, PAIR), f32), V((T, PAIR), f32), V((8, T), f32), V((LANES, D), f32),
        V((NW, X, SLOT, D), bf16), V((NW, X, SLOT, D), bf16), V((NW, X, SLOT, D), bf16), V((NW, SLOT, D), bf16),
        V((T, D), bf16),
    ] + sums(J, CW) + sums(1, LANES) + [
        V((J, X, A, L, CW), bf16),
        dma((10,)), dma((2, 2)), dma((2,)), dma((NW + 1,)), dma((NW + 1,)), dma((NW,)), dma((NW,)),
        dma((2, J + 1)), dma((2, J + 1)), dma((J + 1, 2 * X - 1)), dma((J + 1, 2 * X - 1)),
        V((T, D), f32),
    ]
    return pl.pallas_call(
        functools.partial(backward_kernel, c),
        out_shape=(
            sds((T, D), bf16), sds((T, D), bf16), sds((L, 3 * D), f32), sds((L, D), f32), sds((L, LANES), f32),
        ),
        in_specs=[any_] * 10 + [vm] * 5,
        out_specs=(any_, any_, vm, vm, vm),
        scratch_shapes=scratch,
        compiler_params=pltpu.CompilerParams(
            collective_id=CID1, has_side_effects=True, vmem_limit_bytes=VMEM_CAP
        ),
        name="backward",
    )(v, dy, qkv, lse, att, resid, wt, nt, ret, outp, mrow, meta, cent, wq, mine)


def cuts_of(shape):
    axis, size = len(shape) - 2, shape[-2]
    step = QB if size % QB == 0 else size
    return [(0,) * axis + (pl.ds(at, step),) for at in range(0, size, step)]


def finish_kernel(c, *refs):
    big, small = refs[:6], refs[6]
    outs, (cen_out, g1_out, g2_out) = refs[7:13], refs[13:16]
    held, wide, (in_sem, out_sem) = refs[16:22], refs[22:28], refs[28:]
    cuts = [(i, where) for i in range(6) for where in cuts_of(big[i].shape)]
    for k, (i, where) in enumerate(cuts):
        pltpu.make_async_copy(big[i].at[where], held[i].at[where], in_sem.at[k]).start()
    wide_small = jnp.concatenate([small[...], jnp.zeros((LANES - c.slab, LANES), f32)], 0)
    rows = jnp.transpose(wide_small)[:, 0 : c.slab]
    cen_out[...] = rows[0 : c.E]
    g1_out[...] = rows[GAIN1 : GAIN1 + 1]
    g2_out[...] = rows[GAIN2 : GAIN2 + 1]
    for k, (i, where) in enumerate(cuts):
        pltpu.make_async_copy(big[i].at[where], held[i].at[where], in_sem.at[k]).wait()
        src = held[i]
        if held[i].dtype != outs[i].dtype:
            wide[i][where] = held[i][where].astype(f32)
            src = wide[i]
        pltpu.make_async_copy(src.at[where], outs[i].at[where], out_sem.at[k]).start()
    for k, (i, where) in enumerate(cuts):
        src = wide[i] if held[i].dtype != outs[i].dtype else held[i]
        pltpu.make_async_copy(src.at[where], outs[i].at[where], out_sem.at[k]).wait()


def finish_call(c, big, kinds, small):
    any_ = pl.BlockSpec(memory_space=pl.ANY)
    vm = pl.BlockSpec(memory_space=pltpu.VMEM)
    sds, V = jax.ShapeDtypeStruct, pltpu.VMEM
    copies = sum(len(cuts_of(t.shape)) for t in big)
    return pl.pallas_call(
        functools.partial(finish_kernel, c),
        out_shape=tuple(sds(t.shape, k) for t, k in zip(big, kinds))
        + (sds((c.E, c.slab), f32), sds((1, c.slab), f32), sds((1, c.slab), f32)),
        in_specs=[any_] * 6 + [vm],
        out_specs=(any_,) * 6 + (vm,) * 3,
        scratch_shapes=[V(t.shape, t.dtype) for t in big]
        + [V(t.shape if t.dtype != k else (8, LANES), f32) for t, k in zip(big, kinds)]
        + [pltpu.SemaphoreType.DMA((copies,)), pltpu.SemaphoreType.DMA((copies,))],
        compiler_params=pltpu.CompilerParams(vmem_limit_bytes=VMEM_CAP),
        name="finish",
    )(*big, small)


precise = lax.Precision.HIGHEST
over_rows = (((0,), (0,)), ((), ()))
over_cols = (((1,), (1,)), ((), ()))


def layer_norm(tensor, gain_vec):
    centered = tensor - jnp.mean(tensor, -1, keepdims=True)
    spread = jnp.mean(centered * centered, -1, keepdims=True)
    return centered * lax.rsqrt(spread + 1e-05) * gain_vec


def gelu_exact(tensor):
    return jax.nn.gelu(tensor, approximate=False)


def split_heads(packed):
    seq_len = packed.shape[0]
    model_width = packed.shape[1] // 3
    head_count = model_width // HD
    queries = packed[:, :model_width].reshape(seq_len, head_count, HD)
    key_rows = packed[:, model_width : 2 * model_width].reshape(seq_len, head_count, HD)
    value_rows = packed[:, 2 * model_width :].reshape(seq_len, head_count, HD)
    raw_scores = jnp.einsum(
        "qhd,khd->hqk", queries, key_rows, preferred_element_type=jnp.float32
    ) * HD ** (-0.5)
    places = jnp.arange(seq_len)
    causal = places[:, None] >= places[None, :]
    masked = jnp.where(causal[None], raw_scores, -1e30)
    return (queries, key_rows, value_rows, masked)


def attend_forward(packed):
    queries, key_rows, value_rows, masked = split_heads(packed)
    maxima = jnp.max(masked, -1, keepdims=True)
    powers = jnp.exp(masked - maxima)
    totals = jnp.sum(powers, -1, keepdims=True)
    attn_probs = (powers / totals).astype(jnp.bfloat16)
    attended = jnp.einsum(
        "hqk,khd->qhd", attn_probs, value_rows, preferred_element_type=jnp.float32
    )
    return (attended.reshape(packed.shape[0], -1).astype(jnp.bfloat16), maxima + jnp.log(totals))


def attend_backward(member):
    packed, upstream, log_totals = member
    queries, key_rows, value_rows, masked = split_heads(packed)
    attn_probs = jnp.exp(masked - log_totals)
    probs_low = attn_probs.astype(jnp.bfloat16)
    grad_out = upstream.reshape(queries.shape)
    grad_probs = jnp.einsum(
        "qhd,khd->hqk", grad_out, value_rows, preferred_element_type=jnp.float32
    )
    grad_values = jnp.einsum(
        "hqk,qhd->khd", probs_low, grad_out, preferred_element_type=jnp.float32
    )
    grad_scores = (
        attn_probs * (grad_probs - jnp.sum(grad_probs * attn_probs, -1, keepdims=True))
    ).astype(jnp.bfloat16)
    factor = HD ** (-0.5)
    grad_queries = (
        jnp.einsum("hqk,khd->qhd", grad_scores, key_rows, preferred_element_type=jnp.float32)
        * factor
    )
    grad_keys = (
        jnp.einsum("hqk,qhd->khd", grad_scores, queries, preferred_element_type=jnp.float32)
        * factor
    )
    seq_len = packed.shape[0]
    joined = jnp.concatenate(
        [
            grad_queries.reshape(seq_len, -1),
            grad_keys.reshape(seq_len, -1),
            grad_values.reshape(seq_len, -1),
        ],
        1,
    )
    return joined.astype(jnp.bfloat16)


def expert_rows(row_block, up_mat, down_mat):
    pre_act = jnp.dot(row_block, up_mat, preferred_element_type=jnp.float32)
    hidden = gelu_exact(pre_act).astype(jnp.bfloat16)
    return lax.dot_general(hidden, down_mat, over_cols, preferred_element_type=jnp.float32)


def expert_grads(row_block, grad_block, up_mat, down_mat):
    pre_act = jnp.dot(row_block, up_mat, preferred_element_type=jnp.float32)
    hidden, gelu_back = jax.vjp(gelu_exact, pre_act)
    hidden_low = hidden.astype(jnp.bfloat16)
    down_part = lax.dot_general(
        grad_block, hidden_low, over_rows, preferred_element_type=jnp.float32
    )
    grad_hidden = jnp.dot(grad_block, down_mat, preferred_element_type=jnp.float32)
    grad_pre = gelu_back(grad_hidden)[0].astype(jnp.bfloat16)
    up_part = lax.dot_general(row_block, grad_pre, over_rows, preferred_element_type=jnp.float32)
    return (grad_pre, up_part, down_part)


def fill_slots(row_vals, target, slot_count):
    buffer = jnp.zeros((slot_count + 1, row_vals.shape[1]), row_vals.dtype).at[target].set(row_vals)
    return buffer[:slot_count]


def read_slots(buffer, target):
    padded = jnp.concatenate([buffer, jnp.zeros((1, buffer.shape[1]), buffer.dtype)], 0)
    return padded[target]


def plain_shards(
    layer_inputs_matrix,
    assignment_indices,
    admitted_counts_matrix,
    mixer_scaling1_factor,
    triple_linear_matrix,
    mixer_exit_matrix,
    specialist_scaling2_factor,
    cluster_mean_columns,
    first_linear_matrix,
    second_linear_matrix,
    incoming_gradient,
):
    gain_one, qkv_mat, out_mat, gain_two, centers = (
        lax.all_gather(mixer_scaling1_factor, ("wide", "narrow"), axis=0, tiled=True),
        lax.all_gather(triple_linear_matrix, ("wide", "narrow"), axis=0, tiled=True),
        lax.all_gather(mixer_exit_matrix, ("wide", "narrow"), axis=0, tiled=True),
        lax.all_gather(specialist_scaling2_factor, ("wide", "narrow"), axis=0, tiled=True),
        lax.all_gather(cluster_mean_columns, ("wide", "narrow"), axis=0, tiled=True),
    )
    gain_one = gain_one.astype(jnp.float32)
    gain_two = gain_two.astype(jnp.float32)
    centers = centers.astype(jnp.float32)
    token_rows = layer_inputs_matrix.astype(jnp.float32)
    tok_count, model_width = layer_inputs_matrix.shape
    seq_count = tok_count // SEQ
    normed, norm1_back = jax.vjp(layer_norm, token_rows, gain_one)
    normed_low = normed.astype(jnp.bfloat16)
    qkv_rows = jnp.dot(normed_low, qkv_mat, preferred_element_type=jnp.float32).astype(jnp.bfloat16)
    packed_seqs = qkv_rows.reshape(seq_count, SEQ, 3 * model_width)
    attended, log_totals = lax.map(attend_forward, packed_seqs)
    attended = attended.reshape(tok_count, model_width)
    residual = token_rows + jnp.dot(attended, out_mat, preferred_element_type=jnp.float32)
    normed_two, norm2_back = jax.vjp(layer_norm, residual, gain_two)
    sent_rows = normed_two.astype(jnp.bfloat16)
    dispatched_items = assignment_indices[:, 0]
    specialist_overall_sum = admitted_counts_matrix.shape[0]
    slot_count = specialist_overall_sum * SLOT
    specialist_indicator = (
        dispatched_items[:, None] == jnp.arange(specialist_overall_sum, dtype=jnp.int32)[None, :]
    ).astype(jnp.int32)
    before = jnp.cumsum(specialist_indicator, 0) - specialist_indicator
    ranked = jnp.sum(before * specialist_indicator, 1)
    position_ceilings = jnp.sum(specialist_indicator * admitted_counts_matrix[None, :], 1)
    retained_couple_filter = ranked < position_ceilings
    target = jnp.where(retained_couple_filter, dispatched_items * SLOT + ranked, slot_count)
    kept_rows = retained_couple_filter.astype(jnp.float32)
    choose = specialist_indicator.astype(jnp.float32)
    send_buf = fill_slots(sent_rows, target, slot_count).reshape(
        specialist_overall_sum, SLOT, model_width
    )
    local_rows = lax.all_to_all(send_buf, "wide", split_axis=0, concat_axis=0, tiled=True).reshape(
        slot_count, model_width
    )
    gathered = lax.all_gather(local_rows, "narrow", axis=0, tiled=True)
    expert_local = lax.psum_scatter(
        expert_rows(gathered, first_linear_matrix[0], second_linear_matrix[0]).astype(jnp.bfloat16),
        "narrow",
        scatter_dimension=0,
        tiled=True,
    )
    returned = lax.all_to_all(
        expert_local.reshape(specialist_overall_sum, SLOT, model_width),
        "wide",
        split_axis=0,
        concat_axis=0,
        tiled=True,
    )
    expert_tok = read_slots(returned.reshape(slot_count, model_width), target).astype(jnp.float32)
    center_rows = lax.dot_general(choose, centers, over_cols, precision=precise)
    logits = jnp.sum(normed_two * center_rows, 1)
    sigma = jax.nn.sigmoid(logits)
    gating = sigma * kept_rows
    mixed = (residual + gating[:, None] * expert_tok).astype(jnp.bfloat16)
    grad_y = incoming_gradient.astype(jnp.float32)
    grad_logit = jnp.sum(grad_y * expert_tok, 1) * sigma * (1.0 - sigma) * kept_rows
    grad_normed = grad_logit[:, None] * center_rows
    centroid_part = lax.dot_general(
        normed_two, choose * grad_logit[:, None], over_rows, precision=precise
    )
    grad_expert = (grad_y * gating[:, None]).astype(jnp.bfloat16)
    grad_buf = fill_slots(grad_expert, target, slot_count).reshape(
        specialist_overall_sum, SLOT, model_width
    )
    grad_local = lax.all_to_all(grad_buf, "wide", split_axis=0, concat_axis=0, tiled=True).reshape(
        slot_count, model_width
    )
    grad_gathered = lax.all_gather(grad_local, "narrow", axis=0, tiled=True)
    grad_pre, up_part, down_part = expert_grads(
        gathered, grad_gathered, first_linear_matrix[0], second_linear_matrix[0]
    )
    input_back = lax.psum_scatter(
        lax.dot_general(
            grad_pre, first_linear_matrix[0], over_cols, preferred_element_type=jnp.float32
        ).astype(jnp.bfloat16),
        "narrow",
        scatter_dimension=0,
        tiled=True,
    )
    up_grad = up_part[None]
    down_grad = down_part[None]
    back_rows = lax.all_to_all(
        input_back.reshape(specialist_overall_sum, SLOT, model_width),
        "wide",
        split_axis=0,
        concat_axis=0,
        tiled=True,
    )
    grad_normed = grad_normed + read_slots(
        back_rows.reshape(slot_count, model_width), target
    ).astype(jnp.float32)
    grad_resid_norm, gain_two_part = norm2_back(grad_normed)
    grad_resid = grad_y + grad_resid_norm
    grad_branch = grad_resid.astype(jnp.bfloat16)
    out_part = lax.dot_general(attended, grad_branch, over_rows, preferred_element_type=jnp.float32)
    grad_attended = lax.dot_general(
        grad_branch, out_mat, over_cols, preferred_element_type=jnp.float32
    ).astype(jnp.bfloat16)
    grad_packed = lax.map(
        attend_backward,
        (packed_seqs, grad_attended.reshape(seq_count, SEQ, model_width), log_totals),
    )
    grad_packed = grad_packed.reshape(tok_count, 3 * model_width)
    qkv_part = lax.dot_general(
        normed_low, grad_packed, over_rows, preferred_element_type=jnp.float32
    )
    grad_normed_one = lax.dot_general(
        grad_packed, qkv_mat, over_cols, preferred_element_type=jnp.float32
    )
    grad_token_norm, gain_one_part = norm1_back(grad_normed_one)
    tokens_grad = grad_resid + grad_token_norm
    gain_one_grad, qkv_grad, out_grad, gain_two_grad, centroid_grad = (
        lax.psum_scatter(gain_one_part, ("wide", "narrow"), scatter_dimension=0, tiled=True),
        lax.psum_scatter(qkv_part, ("wide", "narrow"), scatter_dimension=0, tiled=True),
        lax.psum_scatter(out_part, ("wide", "narrow"), scatter_dimension=0, tiled=True),
        lax.psum_scatter(gain_two_part, ("wide", "narrow"), scatter_dimension=0, tiled=True),
        lax.psum_scatter(centroid_part, ("wide", "narrow"), scatter_dimension=0, tiled=True),
    )
    return (
        mixed,
        tokens_grad,
        gain_one_grad,
        qkv_grad,
        out_grad,
        gain_two_grad,
        centroid_grad,
        up_grad,
        down_grad,
    )


def shards(mesh, v, idx, caps, g1, wq, wo, g2, centers, up, down, dy):
    T, D = v.shape
    E = caps.shape[0]
    c = Sizes(mesh, T, D, wq.shape[0], up.shape[2], E)
    if not c.fits:
        return plain_shards(v, idx, caps, g1, wq, wo, g2, centers, up, down, dy)
    res = forward_call(
        c, v, dy, idx.reshape(1, T), caps, wq, wo, centers.T, g1.reshape(1, -1), g2.reshape(1, -1), up, down
    )
    wt, nt, qkv, lse, att, resid, meta, mrow, ret, outp, ug, dg, cent, mine = res
    mixed, tokens_grad, qg, og, small = backward_call(
        c, v, dy, qkv, lse, att, resid, wt, nt, ret, outp, mrow, meta, cent, wq, mine
    )
    ug, dg, tokens_grad, mixed, qg, og, cen, g1_grad, g2_grad = finish_call(
        c, (ug, dg, tokens_grad, mixed, qg, og), (f32, f32, f32, bf16, f32, f32), small
    )
    return (
        mixed, tokens_grad, g1_grad.reshape(-1), qg, og, g2_grad.reshape(-1), cen.T, ug, dg,
    )


def solution(mesh):
    both = ("wide", "narrow")
    in_specs = (
        P(both, None), P(both, None), P(), P(both), P(both, None), P(both, None), P(both), P(both, None),
        P("wide", None, "narrow"), P("wide", None, "narrow"), P(both, None),
    )
    out_specs = (
        P(both, None), P(both, None), P(both), P(both, None), P(both, None), P(both), P(both, None),
        P("wide", None, "narrow"), P("wide", None, "narrow"),
    )
    return jax.shard_map(
        functools.partial(shards, mesh), mesh=mesh, in_specs=in_specs, out_specs=out_specs, check_vma=False
    )
```

```python
import functools

import jax
import jax.numpy as jnp
from jax import lax
from jax.experimental import pallas as pl
from jax.experimental.pallas import tpu as pltpu
from jax.sharding import PartitionSpec as P

HD = 64
SEQ = 1024
SLOT = 48
PAIR = 2 * HD
QB = 256
LANES = 128
GAIN1 = 126
GAIN2 = 127
NEG = -1e30
VMEM_CAP = 62 << 20
CID0 = 0
CID1 = 1
AHEAD_W = 5
AHEAD_X = 3
BEHIND_W = 3
SHORT = 3
LAST = 2

MESH = pl.DeviceIdType.MESH
NN_ = (((1,), (0,)), ((), ()))
NT_ = (((1,), (1,)), ((), ()))
TN_ = (((0,), (0,)), ((), ()))
f32 = jnp.float32
bf16 = jnp.bfloat16


def mm(a, b, dims=NN_):
    return lax.dot_general(a, b, dims, preferred_element_type=f32)


def wait_bytes(ref, sem):
    pltpu.make_async_copy(ref, ref, sem).wait()


arrive = wait_bytes


def push(src, dst, send, recv, **where):
    pltpu.make_async_remote_copy(
        src_ref=src, dst_ref=dst, send_sem=send, recv_sem=recv,
        device_id=where, device_id_type=MESH,
    ).start()


def half_mask(rows):
    return lax.broadcasted_iota(jnp.int32, (rows, PAIR), 1) < HD


def pick(mask, h, value):
    zero = jnp.zeros_like(value)
    return jnp.where(mask, value, zero) if h == 0 else jnp.where(mask, zero, value)


def layer_stats(x):
    centered = x - jnp.mean(x, 1, keepdims=True)
    r = lax.rsqrt(jnp.mean(centered * centered, 1, keepdims=True) + 1e-05)
    return centered * r, r


def attend_rows(qkv, seq, i, put_out, put_lse):
    length = (i + 1) * QB
    rows = pl.ds(i * QB, QB)
    mask = half_mask(QB)
    causal = lax.broadcasted_iota(jnp.int32, (QB, QB), 0) <= lax.broadcasted_iota(
        jnp.int32, (QB, QB), 1
    )
    q = qkv[rows, 0:PAIR] * bf16(HD**-0.5)
    k = qkv[pl.ds(0, length), PAIR : 2 * PAIR]
    v = qkv[pl.ds(0, length), 2 * PAIR : 3 * PAIR]
    outs, sums = [], []
    for h in range(2):
        s = mm(k, pick(mask, h, q), NT_)
        last = jnp.where(causal, s[length - QB :], NEG)
        top = jnp.max(last, 0, keepdims=True)
        if i:
            top = jnp.maximum(top, jnp.max(s[: length - QB], 0, keepdims=True))
        p = jnp.exp(last - top)
        total = jnp.sum(p, 0, keepdims=True)
        p = p.astype(bf16)
        if i:
            head = jnp.exp(s[: length - QB] - top)
            total = total + jnp.sum(head, 0, keepdims=True)
            p = jnp.concatenate([head.astype(bf16), p], 0)
        put_lse(h, rows, top + jnp.log(total))
        outs.append(mm(p, v, TN_))
        sums.append(total)
    inv = jnp.transpose(1.0 / jnp.concatenate(sums + [jnp.ones((6, QB), f32)], 0))
    put_out(rows, jnp.where(mask, outs[0] * inv[:, 0:1], outs[1] * inv[:, 1:2]).astype(bf16))


def attend_rows_back(qkv, att, datt, lse, i, first, prod, dk, dv, put_dq):
    length = (i + 1) * QB
    rows = pl.ds(i * QB, QB)
    mask = half_mask(QB)
    mask_all = half_mask(length)
    causal = lax.broadcasted_iota(jnp.int32, (QB, QB), 0) <= lax.broadcasted_iota(
        jnp.int32, (QB, QB), 1
    )
    q = qkv[rows, 0:PAIR] * bf16(HD**-0.5)
    k = qkv[pl.ds(0, length), PAIR : 2 * PAIR]
    v = qkv[pl.ds(0, length), 2 * PAIR : 3 * PAIR]
    do = datt[rows, :]
    dq = None
    for h in range(2):
        qh, dh = pick(mask, h, q), pick(mask, h, do)
        s = mm(k, qh, NT_)
        row = lse[h : h + 1, rows]
        p = jnp.exp(jnp.where(causal, s[length - QB :], NEG) - row)
        if i:
            p = jnp.concatenate([jnp.exp(s[: length - QB] - row), p], 0)
        dp = mm(v, dh, NT_)
        ds = (p * (dp - prod[h : h + 1, rows])).astype(bf16)
        a, b = mm(p.astype(bf16), dh), mm(ds, qh)
        if first and h == 0:
            dv[pl.ds(0, length), :] = a
            dk[pl.ds(0, length), :] = b
        else:
            dv[pl.ds(0, length), :] += a
            dk[pl.ds(0, length), :] += b
        part = mm(ds, pick(mask_all, h, k), TN_)
        dq = part if dq is None else dq + part
    put_dq(rows, (dq * HD**-0.5).astype(bf16))


class Sizes:
    def __init__(self, mesh, tokens, d, slab, ff, experts):
        self.NW, self.NN = mesh.shape["wide"], mesh.shape["narrow"]
        self.A, self.X = self.NW // 2, self.NN // 2
        self.T, self.D, self.slab, self.F, self.E = tokens, d, slab, ff, experts
        self.CW = 3 * PAIR
        self.G = d // PAIR
        self.J = self.G + d // self.CW
        self.R = self.NN * SLOT
        self.S = experts * SLOT
        self.EP = max(8, experts)
        rows = self.NW * self.R
        self.moe = rows * (5 * d + 3 * ff) * 2 < (24 << 20)
        self.fits = (
            self.moe and slab % 8 == 0 and tokens == SEQ and self.NW % 2 == 0 and self.NN % 2 == 0
            and self.NW > 2 and self.NN > 2 and experts == self.NW
        )


def place(c):
    w, n = lax.axis_index("wide"), lax.axis_index("narrow")
    return w, n, w // 2, lax.rem(w, 2), n // 2, lax.rem(n, 2)


def greet(c, w, n):
    bar = pltpu.get_barrier_semaphore()
    x, cc = n // 2, lax.rem(n, 2)

    def wide(i, _):
        pl.semaphore_signal(bar, inc=1, device_id={"wide": lax.rem(w + i, c.NW)}, device_id_type=MESH)
        return 0

    lax.fori_loop(1, c.NW, wide, 0)
    for k in range(1, c.X):
        to = lax.rem(x + k, c.X) * 2 + cc
        pl.semaphore_signal(bar, inc=1, device_id={"narrow": to}, device_id_type=MESH)
        other = w + 1 - 2 * lax.rem(w, 2)
        pl.semaphore_signal(bar, inc=1, device_id={"wide": other, "narrow": to}, device_id_type=MESH)
    pl.semaphore_signal(bar, inc=1, device_id={"narrow": x * 2 + 1 - cc}, device_id_type=MESH)
    return lambda: pl.semaphore_wait(bar, c.NW - 1 + 2 * c.X - 1)


def forward_kernel(c, *refs):
    (v_hbm, dy_hbm, idx_ref, cap_ref, wq_hbm, wo_hbm, cen_ref, g1_ref, g2_ref, up_hbm, down_hbm) = refs[:11]
    (w_out, normt_out, qkv_out, lse_out, att_out, resid_out, meta_out, mrow_out) = refs[11:19]
    (ret_out, outp_out, ug_out, dg_out, cent_out, mine_out) = refs[19:25]
    (v, nrm, normed, normt, oh, wbuf, wmat, wtr, misc, mrow, qkv, lse, att, sent, sendx, senddy,
     up, down, xin, dyin, hid, dpre, dexp, outp, part, lc, lx, stage, cent,
     lsem, in_sem, out_sem, w_sem, q_sem, st_sem, s1s, s1r, s2s, s2r, s4s, s4r,
     ds_, dr, xs_, xr, cs_, cr, fs, fr, gs, gr, ks, kr, rs_, rr, ws_, wr) = refs[25:]
    A, X, NW, NN, T, D, CW, G, J = c.A, c.X, c.NW, c.NN, c.T, c.D, c.CW, c.G, c.J
    w, n, a, b, x, cc = place(c)
    own = (a, b, x, cc)
    dy = sent

    for j in range(J):
        dst = wbuf.at[(j, *own)]
        if j < G:
            for p in range(3):
                pltpu.make_async_copy(
                    wq_hbm.at[:, pl.ds(p * D + j * PAIR, PAIR)], dst.at[:, pl.ds(p * PAIR, PAIR)], lsem.at[j]
                ).start()
        else:
            pltpu.make_async_copy(wo_hbm.at[:, pl.ds((j - G) * CW, CW)], dst, lsem.at[j]).start()
    loads = [(dy_hbm, dy), (v_hbm, v), (up_hbm.at[0], up), (down_hbm.at[0], down)]
    for i, (s, d) in enumerate(loads):
        pltpu.make_async_copy(s, d, in_sem.at[i]).start()

    def load_wait(i):
        wait_bytes(loads[i][1], in_sem.at[i])

    met = greet(c, w, n)

    pad = LANES - c.slab
    small = jnp.concatenate(
        [cen_ref[...].astype(f32), jnp.zeros((GAIN1 - c.E, c.slab), f32), g1_ref[...].astype(f32), g2_ref[...].astype(f32)], 0
    )
    small = jnp.concatenate([small, jnp.zeros((LANES, pad), f32)], 1)
    small = jnp.transpose(small)[0 : c.slab]
    mine_out[...] = small
    misc[own] = small.astype(bf16)

    met()

    def buf(j):
        return misc if isinstance(j, int) and j == J else wbuf.at[j]

    def s1(j):
        if not (isinstance(j, int) and j == J):
            wait_bytes(buf(j).at[own], lsem.at[j])
        for k in range(1, A):
            push(buf(j).at[own], buf(j).at[own], s1s.at[j], s1r.at[j], wide=lax.rem(a + k, A) * 2 + b)

    plane = [(p, q) for p in range(2) for q in range(X) if p or q]


    def s2_short(j):
        arrive(buf(j).at[pl.ds(0, A - 1), b, x, cc], s1r.at[j])
        mine = buf(j).at[:, b, x, cc]
        for i, (p, q) in enumerate(plane):
            push(
                mine, mine, s2s.at[j, i], s2r.at[j, i],
                wide=a * 2 + lax.rem(b + p, 2), narrow=lax.rem(x + q, X) * 2 + cc,
            )

    def s2_long(j):
        arrive(buf(j).at[pl.ds(0, A - 1), b, x, cc], s1r.at[j])
        mine = buf(j).at[:, b, x, cc]
        for q in range(1, X):
            push(mine, mine, s2s.at[j, q], s2r.at[j, q], narrow=lax.rem(x + q, X) * 2 + cc)

    def s3_long(j):
        for q in range(1, X):
            arrive(buf(j).at[:, b, x, cc], s2r.at[j, q])
        mine = buf(j).at[:, b, :, cc]
        push(mine, mine, s2s.at[j, 0], s2r.at[j, 0], wide=a * 2 + 1 - b)

    def plane_short(j, sem):
        for i in range(len(plane)):
            arrive(buf(j).at[:, b, x, cc], sem.at[j, i])

    def plane_long(j, sem):
        arrive(buf(j).at[:, b, :, cc], sem.at[j, 0])

    def to_core(j):
        mine = buf(j).at[:, :, :, cc]
        push(mine, mine, s4s.at[j], s4r.at[j], narrow=x * 2 + 1 - cc)

    def s4_short(j):
        plane_short(j, s2r)
        to_core(j)

    def s4_long(j):
        plane_long(j, s2r)
        to_core(j)

    def take(j, turn=True):
        arrive(buf(j).at[:, :, :, cc], s4r.at[j])
        val = wbuf[j].reshape(D, CW)
        wmat[j] = val
        if turn:
            turned(j, val)

    def turned(j, val):
        wtr[j] = jnp.transpose(val)
        pltpu.make_async_copy(wtr.at[j], w_out.at[j], w_sem.at[j]).start()

    def due(t):
        for j in range(J):
            short = j < SHORT
            if t == (j + 4):
                (s4_short if short else s4_long)(j)
            if not short and t == j + 2:
                s3_long(j)
            if t == (j + 2 if short else j):
                (s2_short if short else s2_long)(j)
            if t == (j if short else max(j - 2, 1)):
                s1(j)

    s1(J)
    due(0)
    hot = (lax.broadcasted_iota(jnp.int32, (c.EP, T), 0) == idx_ref[...]).astype(f32)
    lane = lax.broadcasted_iota(jnp.int32, (c.EP, T), 1)
    count = hot
    shift = 1
    while shift < T:
        count = count + jnp.where(lane >= shift, pltpu.roll(count, shift, 1), 0.0)
        shift *= 2
    rank = jnp.sum((count - hot) * hot, 0, keepdims=True)
    ceiling = jnp.zeros((1, T), f32)
    for e in range(c.E):
        ceiling = ceiling + hot[e : e + 1, :] * cap_ref[e].astype(f32)
    kept = rank < ceiling
    slot = jnp.where(kept, idx_ref[...].astype(f32) * SLOT + rank, -1.0)

    due(1)
    s2_short(J)
    oh[...] = (lax.broadcasted_iota(jnp.int32, (c.S, T), 0).astype(f32) == slot).astype(bf16)
    due(2)
    load_wait(0)
    senddy[...] = mm(oh[...], dy[...]).astype(bf16)
    due(3)

    def dy_w(k):
        to = lax.rem(w + k, NW)
        push(senddy.at[pl.ds(pl.multiple_of(to * SLOT, SLOT), SLOT)], dyin.at[w, x, cc], ds_.at[k], dr.at[k], wide=to)

    def dy_x(k):
        src = lax.rem(w - k + NW, NW)

        @pl.when(k > 0)
        def _():
            arrive(dyin.at[src, x, cc], dr.at[k])

        for q in range(1, X):
            push(dyin.at[src, x, cc], dyin.at[src, x, cc], xs_.at[k], xr.at[k], narrow=lax.rem(x + q, X) * 2 + cc)

    dyin[w, x, cc] = senddy[pl.ds(pl.multiple_of(w * SLOT, SLOT), SLOT), :]
    load_wait(1)

    def norm1(i, _):
        rows = pl.ds(i * 128, 128)
        nrm[rows, :] = layer_stats(v[rows, :].astype(f32))[0]
        return 0

    lax.fori_loop(0, T // 128, norm1, 0)
    s4_short(J)
    due(4)
    arrive(misc.at[:, :, :, cc], s4r.at[J])
    mrow[...] = jnp.transpose(misc[...].reshape(D, LANES).astype(f32))
    gain1 = mrow[GAIN1 : GAIN1 + 1, :]
    gain2 = mrow[GAIN2 : GAIN2 + 1, :]
    mrow_out[...] = mrow[LANES - 8 : LANES, :]

    def norm1b(i, _):
        rows = pl.ds(i * 128, 128)
        normed[rows, :] = (nrm[rows, :] * gain1).astype(bf16)
        return 0

    lax.fori_loop(0, T // 128, norm1b, 0)
    per = -(-NW // 4)

    def pair(g, _):
        slot_ = lax.rem(g, 2)
        take(g)

        @pl.when(g >= 2)
        def _():
            wait_bytes(qkv.at[slot_], q_sem.at[slot_])

        qkv[slot_] = mm(normed[...], wmat[g]).astype(bf16)
        pltpu.make_async_copy(qkv.at[slot_], qkv_out.at[g], q_sem.at[slot_]).start()

        def at_step(fn, j, wanted):
            @pl.when(wanted & (j < J))
            def _():
                fn(j)

        at_step(s4_short, g + 1, g + 1 < SHORT)
        at_step(s4_long, g + 1, g + 1 >= SHORT)
        at_step(s3_long, g + 3, g + 3 >= SHORT)
        at_step(s2_short, g + 3, g + 3 < SHORT)
        at_step(s2_long, g + 5, g + 5 >= SHORT)
        at_step(s1, g + 5, g + 5 < SHORT)
        at_step(s1, g + 7, g + 7 >= SHORT)

        def put_out(rows, val):
            att[rows, pl.ds(pl.multiple_of(g * PAIR, PAIR), PAIR)] = val

        def put_lse(h, rows, val):
            lse[g, h : h + 1, rows] = val

        for i in range(T // QB):
            if i == T // QB - 1:
                @pl.when(g == G - 1)
                def _():
                    for j in range(G + 1, J):
                        (s4_short if j < SHORT else s4_long)(j)

                for q in range(per):
                    k = g * per + q

                    @pl.when((k >= 1) & (k < NW))
                    def _():
                        dy_w(k)

                    @pl.when((g >= 2) & (k - 2 * per < NW))
                    def _():
                        dy_x(k - 2 * per)

            attend_rows(qkv.at[slot_], T, i, put_out, put_lse)
        return 0

    lax.fori_loop(0, G, pair, 0)
    pltpu.make_async_copy(lse, lse_out, out_sem.at[1]).start()
    pltpu.make_async_copy(att, att_out, out_sem.at[2]).start()

    for j in range(G, J):
        take(j, False)
        at = slice((j - G) * CW, (j - G + 1) * CW)
        nrm[:, at] = v[:, at].astype(f32) + mm(att[...], wmat[j])

    def tail(i, _):
        rows = pl.ds(i * QB, QB)
        sent[rows, :] = (layer_stats(nrm[rows, :])[0] * gain2).astype(bf16)
        return 0

    lax.fori_loop(0, T // QB, tail, 0)
    pltpu.make_async_copy(nrm, resid_out, out_sem.at[3]).start()
    sendx[...] = mm(oh[...], sent[...]).astype(bf16)

    def x_w(k):
        to = lax.rem(w + k, NW)
        push(sendx.at[pl.ds(pl.multiple_of(to * SLOT, SLOT), SLOT)], xin.at[w, x, cc], fs.at[k], fr.at[k], wide=to)

    for k in range(1, AHEAD_W):
        x_w(k)
    xin[w, x, cc] = sendx[pl.ds(pl.multiple_of(w * SLOT, SLOT), SLOT), :]

    crow = mrow[pl.ds(w, 1), :]

    def source(i):
        return lax.rem(w - i + NW, NW)

    def fwd_x(i):
        src = source(i)

        @pl.when(i > 0)
        def _():
            arrive(xin.at[src, x, cc], fr.at[i])

        for k in range(1, X):
            push(xin.at[src, x, cc], xin.at[src, x, cc], gs.at[i], gr.at[i], narrow=lax.rem(x + k, X) * 2 + cc)

    def fwd_c(i):
        src = source(i)
        arrive(xin.at[src, pl.ds(0, X - 1), cc], gr.at[i])
        push(xin.at[src, :, cc], xin.at[src, :, cc], ks.at[i], kr.at[i], narrow=x * 2 + 1 - cc)

    def expert(i):
        src = source(i)
        arrive(xin.at[src, :, cc], kr.at[i])
        xb = xin[src].reshape(c.R, D)
        db = dyin[src].reshape(c.R, D)
        xf, df = xb.astype(f32), db.astype(f32)
        s = jax.nn.sigmoid(jnp.sum(xf * crow, 1, keepdims=True))
        de = (df * s).astype(bf16)
        pre = mm(xb, up[...])
        cdf = 0.5 * (1.0 + lax.erf(pre * 0.7071067811865476))
        hb = (pre * cdf).astype(bf16)
        slope = cdf + pre * (jnp.exp(-0.5 * pre * pre) * 0.3989422804014327)
        dpb = (mm(de, down[...]) * slope).astype(bf16)
        out = mm(hb, down[...], NT_)
        dl = jnp.sum(df * out, 1, keepdims=True) * (s * (1.0 - s))
        dn = mm(dpb, up[...], NT_) + dl * crow
        part[src] = dn.astype(bf16).reshape(X, 2, SLOT, D)
        outp[src] = out.astype(bf16).reshape(X, 2, SLOT, D)
        cent[...] += jnp.broadcast_to(jnp.sum(dl * xf, 0, keepdims=True), cent.shape)
        rows = pl.ds(pl.multiple_of(src * c.R, SLOT), c.R)
        hid[rows, :] = hb
        dpre[rows, :] = dpb
        dexp[rows, :] = de

    def ret_c(i):
        src = source(i)
        push(part.at[src, :, 1 - cc], lc.at[src], rs_.at[0, i], rr.at[0, i], narrow=x * 2 + 1 - cc)

    def ret_x(i):
        src = source(i)
        arrive(lc.at[src], rr.at[0, i])
        part[src, :, cc] = (part[src, :, cc].astype(f32) + lc[src].astype(f32)).astype(bf16)
        for k in range(1, X):
            x2 = lax.rem(x + k, X)
            push(part.at[src, x2, cc], lx.at[src, x], rs_.at[1, i], rr.at[1, i], narrow=x2 * 2 + cc)

    def ret_w(i):
        src = source(i)
        arrive(lx.at[src, pl.ds(0, X - 1)], rr.at[1, i])
        total = part[src, x, cc].astype(f32)
        for k in range(1, X):
            total = total + lx[src, lax.rem(x + k, X)].astype(f32)
        part[src, x, cc] = total.astype(bf16)

        @pl.when(i > 0)
        def _():
            push(part.at[src, x, cc], ret_out.at[w], ws_.at[i], wr.at[i], wide=src)

        @pl.when(i == 0)
        def _():
            pltpu.make_async_copy(part.at[src, x, cc], ret_out.at[w], ws_.at[0]).start()

    fwd_x(0)
    for k in range(per * (G - 2), NW):
        dy_x(k)

    def dy_all(k, _):
        arrive(dyin.at[w, x, cc], xr.at[k])
        return 0

    for q in range(X - 1):
        lax.fori_loop(0, NW, dy_all, 0)
    push(dyin.at[:, :, cc], dyin.at[:, :, cc], cs_, cr, narrow=x * 2 + 1 - cc)
    for j in range(G, J):
        turned(j, wmat[j])
    normt[...] = jnp.transpose(normed[...])
    pltpu.make_async_copy(normt, normt_out, out_sem.at[5]).start()

    logits = mm(mrow[0 : c.EP, :].astype(bf16), sent[...], NT_)
    gate = jax.nn.sigmoid(jnp.sum(logits * hot, 0, keepdims=True)) * kept.astype(f32)
    meta_out[...] = jnp.concatenate([slot, gate, jnp.zeros((6, T), f32)], 0)
    cent[...] = jnp.zeros_like(cent)

    fwd_c(0)
    for k in range(1, AHEAD_X):
        fwd_x(k)
    load_wait(2)
    load_wait(3)
    arrive(dyin.at[:, :, cc], cr)

    def block(i, _):
        @pl.when(i + AHEAD_W < NW)
        def _():
            x_w(i + AHEAD_W)

        @pl.when(i + 1 < NW)
        def _():
            fwd_c(i + 1)

        @pl.when(i + AHEAD_X < NW)
        def _():
            fwd_x(i + AHEAD_X)

        expert(i)
        ret_c(i)

        @pl.when(i >= 1)
        def _():
            ret_x(i - 1)

        @pl.when(i >= BEHIND_W)
        def _():
            ret_w(i - BEHIND_W)

        return 0

    lax.fori_loop(0, NW, block, 0)
    ret_x(NW - 1)
    for i in range(NW - BEHIND_W, NW - 1):
        ret_w(i)
    pltpu.make_async_copy(outp, outp_out, out_sem.at[4]).start()
    cent_out[...] = cent[...]
    parts = D // QB

    def grads(lhs, rhs, out, second):
        def one_block(i, _):
            at = pl.ds(pl.multiple_of(i * QB, QB), QB)
            if second:
                wait_bytes(stage.at[i], st_sem.at[i])
            stage[i] = mm(lhs(at), rhs[...], TN_).astype(bf16)
            pltpu.make_async_copy(stage.at[i], out.at[0, at], st_sem.at[i]).start()
            return 0

        lax.fori_loop(0, parts, one_block, 0)

    grads(lambda at: dexp[:, at], hid, dg_out, False)
    ret_w(NW - 1)
    grads(lambda at: xin[:, :, :, :, at].reshape(NW * c.R, QB), dpre, ug_out, True)

    for q, ref in enumerate([lse, att, nrm, outp, normt]):
        wait_bytes(ref, out_sem.at[q + 1])
    for q in range(2):
        wait_bytes(qkv.at[q], q_sem.at[q])
    for j in [J] + list(range(J)):
        if not (isinstance(j, int) and j == J):
            wait_bytes(wtr.at[j], w_sem.at[j])
        arrive(buf(j).at[pl.ds(0, A - 1), b, x, cc], s1s.at[j])
        if j == J or j < SHORT:
            plane_short(j, s2s)
        else:
            plane_long(j, s2s)
            for q in range(1, X):
                arrive(buf(j).at[:, b, x, cc], s2s.at[j, q])
        arrive(buf(j).at[:, :, :, cc], s4s.at[j])
    arrive(dyin.at[:, :, cc], cs_)

    def drain(i, _):
        src = source(i)
        arrive(xin.at[src, pl.ds(0, X - 1), cc], xs_.at[i])
        arrive(xin.at[src, pl.ds(0, X - 1), cc], gs.at[i])
        arrive(xin.at[src, :, cc], ks.at[i])
        arrive(lc.at[src], rs_.at[0, i])
        arrive(lx.at[src, pl.ds(0, X - 1)], rs_.at[1, i])

        @pl.when(i > 0)
        def _():
            arrive(xin.at[src, x, cc], ds_.at[i])
            arrive(xin.at[src, x, cc], fs.at[i])
            arrive(xin.at[src, x, cc], ws_.at[i])
            arrive(xin.at[src, x, cc], wr.at[i])

        return 0

    lax.fori_loop(0, NW, drain, 0)
    wait_bytes(part.at[0, 0, 0], ws_.at[0])
    for i in range(parts):
        wait_bytes(stage.at[i], st_sem.at[i])


def forward_call(c, v, dy, idx, cap, wq, wo, cen, g1, g2, up, down):
    T, D, CW, G, J, NW, NN, A, X, L, F = c.T, c.D, c.CW, c.G, c.J, c.NW, c.NN, c.A, c.X, c.slab, c.F
    any_ = pl.BlockSpec(memory_space=pl.ANY)
    vm = pl.BlockSpec(memory_space=pltpu.VMEM)
    sm = pl.BlockSpec(memory_space=pltpu.SMEM)
    sds = jax.ShapeDtypeStruct
    rows_ = (NW, X, 2, SLOT, D)
    outs = [
        (sds((J, CW, D), bf16), any_),
        (sds((D, T), bf16), any_),
        (sds((G, T, CW), bf16), any_),
        (sds((G, 8, T), f32), any_),
        (sds((T, D), bf16), any_),
        (sds((T, D), f32), any_),
        (sds((8, T), f32), vm),
        (sds((8, D), f32), vm),
        (sds((NW, SLOT, D), bf16), any_),
        (sds(rows_, bf16), any_),
        (sds((1, D, F), bf16), any_),
        (sds((1, D, F), bf16), any_),
        (sds((8, D), f32), vm),
        (sds((L, LANES), f32), vm),
    ]
    dma, V = pltpu.SemaphoreType.DMA, pltpu.VMEM
    rows = NW * c.R
    scratch = [
        V((T, D), bf16), V((T, D), f32), V((T, D), bf16), V((D, T), bf16), V((c.S, T), bf16),
        V((J, A, 2, X, 2, L, CW), bf16), V((J, D, CW), bf16), V((J, CW, D), bf16), V((A, 2, X, 2, L, LANES), bf16), V((LANES, D), f32),
        V((2, T, CW), bf16), V((G, 8, T), f32), V((T, D), bf16), V((T, D), bf16), V((c.S, D), bf16), V((c.S, D), bf16),
        V((D, F), bf16), V((D, F), bf16), V(rows_, bf16), V(rows_, bf16),
        V((rows, F), bf16), V((rows, F), bf16), V((rows, D), bf16), V(rows_, bf16), V(rows_, bf16),
        V((NW, X, SLOT, D), bf16), V((NW, X, SLOT, D), bf16), V((D // QB, QB, F), bf16), V((8, D), f32),
        dma((J,)), dma((4,)), dma((6,)), dma((J,)), dma((2,)), dma((D // QB,)),
    ] + [dma((J + 1,))] * 2 + [dma((J + 1, 2 * X - 1))] * 2 + [dma((J + 1,))] * 2 + [dma((NW,))] * 4 + [dma(()), dma(())] + [dma((NW,))] * 6 + [
        dma((2, NW)), dma((2, NW)), dma((NW,)), dma((NW,)),
    ]
    return pl.pallas_call(
        functools.partial(forward_kernel, c),
        out_shape=tuple(o[0] for o in outs),
        in_specs=[any_, any_, vm, sm, any_, any_, vm, vm, vm, any_, any_],
        out_specs=tuple(o[1] for o in outs),
        scratch_shapes=scratch,
        compiler_params=pltpu.CompilerParams(
            collective_id=CID0, has_side_effects=True, vmem_limit_bytes=VMEM_CAP
        ),
        name="forward",
    )(v, dy, idx, cap, wq, wo, cen, g1, g2, up, down)


def backward_kernel(c, *refs):
    (v_hbm, dy_hbm, qkv_hbm, lse_hbm, att_hbm, resid_hbm, wt_hbm, nt_hbm, ret_hbm, outp_hbm, mrow, meta, cent, wq_hbm, mine) = refs[:15]
    (mixed_out, tok_out, qg_out, og_out, small_out) = refs[15:20]
    (v, dy, qkv, lse, att, resid, wt, ret, oh, normt, dbr, datt, dnm, dqkv, dk, dv, prod, rowbuf,
     part, lc, lx, got, mixed,
     gb, la, lb, lz, sgb, sla, slb, slz, lxx,
     in_sem, q_sem, out_sem, os_, orv, ows, owr, rs_, rr, ps_, pr, tokacc, wq) = refs[20:]
    A, X, NW, NN, T, D, CW, G, J = c.A, c.X, c.NW, c.NN, c.T, c.D, c.CW, c.G, c.J
    H = J - G
    w, n, a, b, x, cc = place(c)
    blocks = T // QB

    loads = [
        (ret_hbm, ret), (resid_hbm, resid), (dy_hbm, dy), (att_hbm, att), (v_hbm, v), (lse_hbm, lse), (nt_hbm, normt),
        (wt_hbm.at[pl.ds(G, H)], wt.at[pl.ds(G, H)]), (wt_hbm.at[pl.ds(0, G)], wt.at[pl.ds(0, G)]), (wq_hbm, wq),
    ]
    for i, (s, d) in enumerate(loads):
        pltpu.make_async_copy(s, d, in_sem.at[i]).start()
    own_part = pltpu.make_async_copy(outp_hbm.at[:, :, cc], part, in_sem.at[10])
    own_part.start()

    def load_wait(i):
        wait_bytes(loads[i][1], in_sem.at[i])

    def fetch_qkv(g, slot_):
        pltpu.make_async_copy(qkv_hbm.at[g], qkv.at[slot_], q_sem.at[1, slot_]).start()

    fetch_qkv(0, 0)
    met = greet(c, w, n)

    slot, gate = meta[0:1, :], meta[1:2, :]
    hits = lax.broadcasted_iota(jnp.int32, (c.S, T), 0).astype(f32) == slot
    oh[...] = hits.astype(bf16)
    gain1, gain2 = mrow[6:7, :], mrow[7:8, :]
    load_wait(0)
    dnm[...] = mm(oh[...], ret[...].reshape(c.S, D), TN_)
    oh[...] = jnp.where(hits, gate, 0.0).astype(bf16)
    load_wait(1)
    load_wait(2)
    rowbuf[...] = jnp.zeros_like(rowbuf)
    rowbuf[pl.ds(w, 1), :] = cent[0:1, :]

    def norm2_back(i, acc):
        rows = pl.ds(i * QB, QB)
        n2, r2 = layer_stats(resid[rows, :])
        dn2 = dnm[rows, :]
        dn = dn2 * gain2
        step = r2 * (dn - jnp.mean(dn, 1, keepdims=True) - n2 * jnp.mean(dn * n2, 1, keepdims=True))
        dres = dy[rows, :].astype(f32) + step
        dnm[rows, :] = dres
        dbr[rows, :] = dres.astype(bf16)
        return acc + jnp.sum(dn2 * n2, 0, keepdims=True)

    rowbuf[GAIN2 : GAIN2 + 1, :] = lax.fori_loop(0, blocks, norm2_back, jnp.zeros((1, D), f32))
    load_wait(3)

    big = (gb, la, lb, lz, 0, lxx)
    tiny = (sgb, sla, slb, slz, J)

    def add(p, q):
        return (p.astype(f32) + q.astype(f32)).astype(bf16)

    def ra(t, j):
        push(t[0].at[j, :, :, :, 1 - cc], t[1].at[j], rs_.at[0, t[4] + j], rr.at[0, t[4] + j], narrow=x * 2 + 1 - cc)

    plane = [(p, q) for p in range(2) for q in range(X) if p or q]

    plane = [(p, q) for p in range(2) for q in range(X) if p or q]

    def join(t, j):
        arrive(t[1].at[j], rr.at[0, t[4] + j])
        t[0][j, :, :, :, cc] = add(t[0][j, :, :, :, cc], t[1][j])

    def to_plane(t, j, i, src, dst, p, q):
        push(
            src, dst, ps_.at[t[4] + j, i], pr.at[t[4] + j, i],
            wide=a * 2 + lax.rem(b + p, 2), narrow=lax.rem(x + q, X) * 2 + cc,
        )

    def to_outer(t, j, total):
        t[0][j, :, b, x, cc] = total.astype(bf16)
        for k in range(1, A):
            a2 = lax.rem(a + k, A)
            push(t[0].at[j, a2, b, x, cc], t[3].at[j, a], rs_.at[1, t[4] + j], rr.at[1, t[4] + j], wide=a2 * 2 + b)

    def rb_short(t, j):
        join(t, j)
        for i, (p, q) in enumerate(plane):
            to_plane(t, j, i, t[0].at[j, :, lax.rem(b + p, 2), lax.rem(x + q, X), cc], t[2].at[j, b, x], p, q)

    def rc_short(t, j):
        plane_short(t, j, pr)
        total = t[0][j, :, b, x, cc].astype(f32)
        for p, q in plane:
            total = total + t[2][j, lax.rem(b + p, 2), lax.rem(x + q, X)].astype(f32)
        to_outer(t, j, total)

    def plane_short(t, j, sem):
        for i in range(len(plane)):
            arrive(t[2].at[j, 0, 0], sem.at[t[4] + j, i])

    def rb_long(t, j):
        join(t, j)
        for q in range(X):
            t[2][j, b, q] = t[0][j, :, 1 - b, q, cc]
        to_plane(t, j, 0, t[2].at[j, b], t[2].at[j, b], 1, 0)

    def rc_long(t, j):
        arrive(t[2].at[j, 0], pr.at[t[4] + j, 0])
        for q in range(X):
            t[0][j, :, b, q, cc] = add(t[0][j, :, b, q, cc], t[2][j, 1 - b, q])
        for q in range(1, X):
            to_plane(t, j, q, t[0].at[j, :, b, lax.rem(x + q, X), cc], t[5].at[j, x], 0, q)

    def rd_long(t, j):
        for q in range(1, X):
            arrive(t[2].at[j, 0, 0], pr.at[t[4] + j, q])
        total = t[0][j, :, b, x, cc].astype(f32)
        for q in range(1, X):
            total = total + t[5][j, lax.rem(x + q, X)].astype(f32)
        to_outer(t, j, total)

    def plane_long(t, j, sem):
        arrive(t[2].at[j, 0], sem.at[t[4] + j, 0])
        for q in range(1, X):
            arrive(t[2].at[j, 0, 0], sem.at[t[4] + j, q])

    def rf(t, j):
        arrive(t[3].at[j, pl.ds(0, A - 1)], rr.at[1, t[4] + j])
        total = t[0][j, a, b, x, cc].astype(f32)
        for k in range(1, A):
            total = total + t[3][j, lax.rem(a + k, A)].astype(f32)
        return total

    def rf_w(j):
        og_out[:, j * CW : (j + 1) * CW] = rf(big, j)

    def rf_q(g):
        total = rf(big, H + g)
        for p in range(3):
            qg_out[:, pl.ds(pl.multiple_of(p * D + g * PAIR, PAIR), PAIR)] = total[:, p * PAIR : (p + 1) * PAIR]

    sgb[0] = jnp.transpose(rowbuf[...]).astype(bf16).reshape(A, 2, X, 2, c.slab, LANES)
    for h in range(H):
        gb[h] = mm(att[...], dbr[:, h * CW : (h + 1) * CW], TN_).astype(bf16).reshape(A, 2, X, 2, c.slab, CW)
        if h == 0:
            met()
            push(outp_hbm.at[:, :, 1 - cc], lc, os_.at[0], orv.at[0], narrow=x * 2 + 1 - cc)
            ra(tiny, 0)
        ra(big, h)

    load_wait(7)

    def out_back(i, _):
        at = pl.ds(pl.multiple_of(i * QB, QB), QB)
        datt[:, at] = mm(dbr[...], wt[pl.ds(G, H), :, at].reshape(D, QB)).astype(bf16)
        return 0

    lax.fori_loop(0, D // QB, out_back, 0)
    load_wait(4)
    load_wait(6)
    rb_short(tiny, 0)
    for h in range(H):
        rb_long(big, h)
    load_wait(5)
    own_part.wait()

    def o_x(i):
        for k in range(1, X):
            x2 = lax.rem(x + k, X)
            push(part.at[i, x2], lx.at[i, x], os_.at[1 + i], orv.at[1 + i], narrow=x2 * 2 + cc)

    def o_w(i):
        arrive(lx.at[i, pl.ds(0, X - 1)], orv.at[1 + i])
        total = part[i, x].astype(f32)
        for k in range(1, X):
            total = total + lx[i, lax.rem(x + k, X)].astype(f32)
        part[i, x] = total.astype(bf16)

        @pl.when(i != w)
        def _():
            push(part.at[i, x], got.at[w], ows.at[i], owr.at[lax.rem(w - i + NW, NW)], wide=i)

        @pl.when(i == w)
        def _():
            got[w] = part[w, x]

    arrive(lc, orv.at[0])

    def merge(i, _):
        part[i] = add(part[i], lc[i])
        return 0

    lax.fori_loop(0, NW, merge, 0)
    per = -(-NW // 4)

    def spread(fn, step):
        for k in range(per):
            i = lax.rem(w + step * per + k, NW)

            @pl.when(step * per + k < NW)
            def _():
                fn(i)

    def pair(g, _):
        s_ = lax.rem(g, 2)

        @pl.when(g + 1 < G)
        def _():
            fetch_qkv(g + 1, 1 - s_)

        wait_bytes(qkv.at[s_], q_sem.at[1, s_])
        lanes = pl.ds(pl.multiple_of(g * PAIR, PAIR), PAIR)
        att_g, datt_g = att.at[:, lanes], datt.at[:, lanes]
        full = jnp.transpose(datt_g[...].astype(f32) * att_g[...].astype(f32))
        prod[0:1, :] = jnp.sum(full[0:HD], 0, keepdims=True)
        prod[1:2, :] = jnp.sum(full[HD:], 0, keepdims=True)

        def put_dq(rows, val):
            dqkv[g, rows, 0:PAIR] = val

        for i in reversed(range(blocks)):
            if i == 0:
                @pl.when(g == 0)
                def _():
                    rc_short(tiny, 0)

                rc_long(big, g)

                @pl.when(g >= 1)
                def _():
                    rd_long(big, g - 1)

            attend_rows_back(qkv.at[s_], att_g, datt_g, lse.at[g], i, i == blocks - 1, prod, dk, dv, put_dq)
            if i == blocks - 2:
                @pl.when((g >= 1) & (g + H - 1 < J - LAST))
                def _():
                    rb_long(big, g + H - 1)

                @pl.when((g >= 1) & (g + H - 1 >= J - LAST))
                def _():
                    rb_short(big, g + H - 1)

                @pl.when(g < 4)
                def _():
                    spread(o_x, g)

                @pl.when(g >= 2)
                def _():
                    spread(o_w, g - 2)

        dqkv[g, :, PAIR : 2 * PAIR] = dk[...].astype(bf16)
        dqkv[g, :, 2 * PAIR :] = dv[...].astype(bf16)
        gb[H + g] = mm(normt[...], dqkv[g]).astype(bf16).reshape(A, 2, X, 2, c.slab, CW)
        ra(big, H + g)
        return 0

    lax.fori_loop(0, G, pair, 0)
    load_wait(8)

    def back(i):
        at = slice(i * QB, (i + 1) * QB)
        total = mm(dqkv[0], wt[0, :, at])
        for g in range(1, G):
            total = total + mm(dqkv[g], wt[g, :, at])
        tokacc[:, at] = total

    back(0)
    rb_short(big, J - 1)
    rd_long(big, J - LAST - 1)
    for j in range(J - LAST, J - 1):
        rc_short(big, j)
    for i in range(1, D // QB):
        back(i)
    def norm1_back(i, _):
        rows = pl.ds(i * QB, QB)
        n1, r1 = layer_stats(v[rows, :].astype(f32))
        dm = tokacc[rows, :] * gain1
        step = r1 * (dm - jnp.mean(dm, 1, keepdims=True) - n1 * jnp.mean(dm * n1, 1, keepdims=True))
        dbr[rows, :] = (dnm[rows, :] + step).astype(bf16)
        return 0

    lax.fori_loop(0, blocks, norm1_back, 0)
    tok_copy = pltpu.make_async_copy(dbr, tok_out, out_sem.at[0])
    tok_copy.start()
    rc_short(big, J - 1)

    def o_wait(k, _):
        arrive(got.at[0], owr.at[k])
        return 0

    lax.fori_loop(1, NW, o_wait, 0)

    def mix(i, _):
        cols = pl.ds(pl.multiple_of(i * QB, QB), QB)
        rows = pl.ds(i * QB, QB)
        mixed[rows, :] = (resid[rows, :] + mm(oh[:, cols], got[...].reshape(c.S, D), TN_)).astype(bf16)
        return 0

    lax.fori_loop(0, blocks, mix, 0)
    mix_copy = pltpu.make_async_copy(mixed, mixed_out, out_sem.at[1])
    mix_copy.start()
    for h in range(H):
        rf_w(h)

    def fin(g, _):
        rf_q(g)
        return 0

    lax.fori_loop(0, G, fin, 0)
    load_wait(9)
    sums_ = jnp.sum(qg_out[...] * wq[...].astype(f32), 1, keepdims=True) / mine[:, GAIN1 : GAIN1 + 1]
    at_gain = lax.broadcasted_iota(jnp.int32, (c.slab, LANES), 1) == GAIN1
    small_out[...] = jnp.where(at_gain, sums_, rf(tiny, 0))

    arrive(lc, os_.at[0])

    def drain(i, _):
        arrive(lx.at[i, pl.ds(0, X - 1)], os_.at[1 + i])

        @pl.when(i != w)
        def _():
            arrive(got.at[0], ows.at[i])

        return 0

    lax.fori_loop(0, NW, drain, 0)

    def drain_sums(t, j, route):
        arrive(t[1].at[j], rs_.at[0, t[4] + j])
        route(t, j, ps_)
        arrive(t[3].at[j, pl.ds(0, A - 1)], rs_.at[1, t[4] + j])

    for j in range(J):
        drain_sums(big, j, plane_long if j < J - LAST else plane_short)
    drain_sums(tiny, 0, plane_short)
    tok_copy.wait()
    mix_copy.wait()


def backward_call(c, v, dy, qkv, lse, att, resid, wt, nt, ret, outp, mrow, meta, cent, wq, mine):
    T, D, CW, G, J, NW, NN, A, X, L = c.T, c.D, c.CW, c.G, c.J, c.NW, c.NN, c.A, c.X, c.slab
    any_ = pl.BlockSpec(memory_space=pl.ANY)
    vm = pl.BlockSpec(memory_space=pltpu.VMEM)
    sds = jax.ShapeDtypeStruct
    dma, V = pltpu.SemaphoreType.DMA, pltpu.VMEM

    def sums(k, width):
        return [
            V((k, A, 2, X, 2, L, width), bf16), V((k, A, 2, X, L, width), bf16),
            V((k, 2, X, A, L, width), bf16), V((k, A, L, width), bf16),
        ]

    scratch = [
        V((T, D), bf16), V((T, D), bf16), V((2, T, CW), bf16), V((G, 8, T), f32), V((T, D), bf16), V((T, D), f32),
        V((J, CW, D), bf16), V((NW, SLOT, D), bf16), V((c.S, T), bf16),
        V((D, T), bf16), V((T, D), bf16), V((T, D), bf16), V((T, D), f32), V((G, T, CW), bf16),
        V((T, PAIR), f32), V((T, PAIR), f32), V((8, T), f32), V((LANES, D), f32),
        V((NW, X, SLOT, D), bf16), V((NW, X, SLOT, D), bf16), V((NW, X, SLOT, D), bf16), V((NW, SLOT, D), bf16),
        V((T, D), bf16),
    ] + sums(J, CW) + sums(1, LANES) + [
        V((J, X, A, L, CW), bf16),
        dma((11,)), dma((2, 2)), dma((2,)), dma((NW + 1,)), dma((NW + 1,)), dma((NW,)), dma((NW,)),
        dma((2, J + 1)), dma((2, J + 1)), dma((J + 1, 2 * X - 1)), dma((J + 1, 2 * X - 1)),
        V((T, D), f32), V((L, 3 * D), bf16),
    ]
    return pl.pallas_call(
        functools.partial(backward_kernel, c),
        out_shape=(
            sds((T, D), bf16), sds((T, D), bf16), sds((L, 3 * D), f32), sds((L, D), f32), sds((L, LANES), f32),
        ),
        in_specs=[any_] * 10 + [vm] * 3 + [any_, vm],
        out_specs=(any_, any_, vm, vm, vm),
        scratch_shapes=scratch,
        compiler_params=pltpu.CompilerParams(
            collective_id=CID1, has_side_effects=True, vmem_limit_bytes=VMEM_CAP
        ),
        name="backward",
    )(v, dy, qkv, lse, att, resid, wt, nt, ret, outp, mrow, meta, cent, wq, mine)


def cuts_of(shape):
    axis, size = len(shape) - 2, shape[-2]
    step = QB if size % QB == 0 else size
    return [(0,) * axis + (pl.ds(at, step),) for at in range(0, size, step)]


def finish_kernel(c, *refs):
    big, small = refs[:6], refs[6]
    outs, (cen_out, g1_out, g2_out) = refs[7:13], refs[13:16]
    held, wide, (in_sem, out_sem) = refs[16:22], refs[22:28], refs[28:]
    cuts = [(i, where) for i in range(6) for where in cuts_of(big[i].shape)]
    for k, (i, where) in enumerate(cuts):
        pltpu.make_async_copy(big[i].at[where], held[i].at[where], in_sem.at[k]).start()
    wide_small = jnp.concatenate([small[...], jnp.zeros((LANES - c.slab, LANES), f32)], 0)
    rows = jnp.transpose(wide_small)[:, 0 : c.slab]
    cen_out[...] = rows[0 : c.E]
    g1_out[...] = rows[GAIN1 : GAIN1 + 1]
    g2_out[...] = rows[GAIN2 : GAIN2 + 1]
    for k, (i, where) in enumerate(cuts):
        pltpu.make_async_copy(big[i].at[where], held[i].at[where], in_sem.at[k]).wait()
        src = held[i]
        if held[i].dtype != outs[i].dtype:
            wide[i][where] = held[i][where].astype(f32)
            src = wide[i]
        pltpu.make_async_copy(src.at[where], outs[i].at[where], out_sem.at[k]).start()
    for k, (i, where) in enumerate(cuts):
        src = wide[i] if held[i].dtype != outs[i].dtype else held[i]
        pltpu.make_async_copy(src.at[where], outs[i].at[where], out_sem.at[k]).wait()


def finish_call(c, big, kinds, small):
    any_ = pl.BlockSpec(memory_space=pl.ANY)
    vm = pl.BlockSpec(memory_space=pltpu.VMEM)
    sds, V = jax.ShapeDtypeStruct, pltpu.VMEM
    copies = sum(len(cuts_of(t.shape)) for t in big)
    return pl.pallas_call(
        functools.partial(finish_kernel, c),
        out_shape=tuple(sds(t.shape, k) for t, k in zip(big, kinds))
        + (sds((c.E, c.slab), f32), sds((1, c.slab), f32), sds((1, c.slab), f32)),
        in_specs=[any_] * 6 + [vm],
        out_specs=(any_,) * 6 + (vm,) * 3,
        scratch_shapes=[V(t.shape, t.dtype) for t in big]
        + [V(t.shape if t.dtype != k else (8, LANES), f32) for t, k in zip(big, kinds)]
        + [pltpu.SemaphoreType.DMA((copies,)), pltpu.SemaphoreType.DMA((copies,))],
        compiler_params=pltpu.CompilerParams(vmem_limit_bytes=VMEM_CAP),
        name="finish",
    )(*big, small)


precise = lax.Precision.HIGHEST
over_rows = (((0,), (0,)), ((), ()))
over_cols = (((1,), (1,)), ((), ()))


def layer_norm(tensor, gain_vec):
    centered = tensor - jnp.mean(tensor, -1, keepdims=True)
    spread = jnp.mean(centered * centered, -1, keepdims=True)
    return centered * lax.rsqrt(spread + 1e-05) * gain_vec


def gelu_exact(tensor):
    return jax.nn.gelu(tensor, approximate=False)


def split_heads(packed):
    seq_len = packed.shape[0]
    model_width = packed.shape[1] // 3
    head_count = model_width // HD
    queries = packed[:, :model_width].reshape(seq_len, head_count, HD)
    key_rows = packed[:, model_width : 2 * model_width].reshape(seq_len, head_count, HD)
    value_rows = packed[:, 2 * model_width :].reshape(seq_len, head_count, HD)
    raw_scores = jnp.einsum(
        "qhd,khd->hqk", queries, key_rows, preferred_element_type=jnp.float32
    ) * HD ** (-0.5)
    places = jnp.arange(seq_len)
    causal = places[:, None] >= places[None, :]
    masked = jnp.where(causal[None], raw_scores, -1e30)
    return (queries, key_rows, value_rows, masked)


def attend_forward(packed):
    queries, key_rows, value_rows, masked = split_heads(packed)
    maxima = jnp.max(masked, -1, keepdims=True)
    powers = jnp.exp(masked - maxima)
    totals = jnp.sum(powers, -1, keepdims=True)
    attn_probs = (powers / totals).astype(jnp.bfloat16)
    attended = jnp.einsum(
        "hqk,khd->qhd", attn_probs, value_rows, preferred_element_type=jnp.float32
    )
    return (attended.reshape(packed.shape[0], -1).astype(jnp.bfloat16), maxima + jnp.log(totals))


def attend_backward(member):
    packed, upstream, log_totals = member
    queries, key_rows, value_rows, masked = split_heads(packed)
    attn_probs = jnp.exp(masked - log_totals)
    probs_low = attn_probs.astype(jnp.bfloat16)
    grad_out = upstream.reshape(queries.shape)
    grad_probs = jnp.einsum(
        "qhd,khd->hqk", grad_out, value_rows, preferred_element_type=jnp.float32
    )
    grad_values = jnp.einsum(
        "hqk,qhd->khd", probs_low, grad_out, preferred_element_type=jnp.float32
    )
    grad_scores = (
        attn_probs * (grad_probs - jnp.sum(grad_probs * attn_probs, -1, keepdims=True))
    ).astype(jnp.bfloat16)
    factor = HD ** (-0.5)
    grad_queries = (
        jnp.einsum("hqk,khd->qhd", grad_scores, key_rows, preferred_element_type=jnp.float32)
        * factor
    )
    grad_keys = (
        jnp.einsum("hqk,qhd->khd", grad_scores, queries, preferred_element_type=jnp.float32)
        * factor
    )
    seq_len = packed.shape[0]
    joined = jnp.concatenate(
        [
            grad_queries.reshape(seq_len, -1),
            grad_keys.reshape(seq_len, -1),
            grad_values.reshape(seq_len, -1),
        ],
        1,
    )
    return joined.astype(jnp.bfloat16)


def expert_rows(row_block, up_mat, down_mat):
    pre_act = jnp.dot(row_block, up_mat, preferred_element_type=jnp.float32)
    hidden = gelu_exact(pre_act).astype(jnp.bfloat16)
    return lax.dot_general(hidden, down_mat, over_cols, preferred_element_type=jnp.float32)


def expert_grads(row_block, grad_block, up_mat, down_mat):
    pre_act = jnp.dot(row_block, up_mat, preferred_element_type=jnp.float32)
    hidden, gelu_back = jax.vjp(gelu_exact, pre_act)
    hidden_low = hidden.astype(jnp.bfloat16)
    down_part = lax.dot_general(
        grad_block, hidden_low, over_rows, preferred_element_type=jnp.float32
    )
    grad_hidden = jnp.dot(grad_block, down_mat, preferred_element_type=jnp.float32)
    grad_pre = gelu_back(grad_hidden)[0].astype(jnp.bfloat16)
    up_part = lax.dot_general(row_block, grad_pre, over_rows, preferred_element_type=jnp.float32)
    return (grad_pre, up_part, down_part)


def fill_slots(row_vals, target, slot_count):
    buffer = jnp.zeros((slot_count + 1, row_vals.shape[1]), row_vals.dtype).at[target].set(row_vals)
    return buffer[:slot_count]


def read_slots(buffer, target):
    padded = jnp.concatenate([buffer, jnp.zeros((1, buffer.shape[1]), buffer.dtype)], 0)
    return padded[target]


def plain_shards(
    layer_inputs_matrix,
    assignment_indices,
    admitted_counts_matrix,
    mixer_scaling1_factor,
    triple_linear_matrix,
    mixer_exit_matrix,
    specialist_scaling2_factor,
    cluster_mean_columns,
    first_linear_matrix,
    second_linear_matrix,
    incoming_gradient,
):
    gain_one, qkv_mat, out_mat, gain_two, centers = (
        lax.all_gather(mixer_scaling1_factor, ("wide", "narrow"), axis=0, tiled=True),
        lax.all_gather(triple_linear_matrix, ("wide", "narrow"), axis=0, tiled=True),
        lax.all_gather(mixer_exit_matrix, ("wide", "narrow"), axis=0, tiled=True),
        lax.all_gather(specialist_scaling2_factor, ("wide", "narrow"), axis=0, tiled=True),
        lax.all_gather(cluster_mean_columns, ("wide", "narrow"), axis=0, tiled=True),
    )
    gain_one = gain_one.astype(jnp.float32)
    gain_two = gain_two.astype(jnp.float32)
    centers = centers.astype(jnp.float32)
    token_rows = layer_inputs_matrix.astype(jnp.float32)
    tok_count, model_width = layer_inputs_matrix.shape
    seq_count = tok_count // SEQ
    normed, norm1_back = jax.vjp(layer_norm, token_rows, gain_one)
    normed_low = normed.astype(jnp.bfloat16)
    qkv_rows = jnp.dot(normed_low, qkv_mat, preferred_element_type=jnp.float32).astype(jnp.bfloat16)
    packed_seqs = qkv_rows.reshape(seq_count, SEQ, 3 * model_width)
    attended, log_totals = lax.map(attend_forward, packed_seqs)
    attended = attended.reshape(tok_count, model_width)
    residual = token_rows + jnp.dot(attended, out_mat, preferred_element_type=jnp.float32)
    normed_two, norm2_back = jax.vjp(layer_norm, residual, gain_two)
    sent_rows = normed_two.astype(jnp.bfloat16)
    dispatched_items = assignment_indices[:, 0]
    specialist_overall_sum = admitted_counts_matrix.shape[0]
    slot_count = specialist_overall_sum * SLOT
    specialist_indicator = (
        dispatched_items[:, None] == jnp.arange(specialist_overall_sum, dtype=jnp.int32)[None, :]
    ).astype(jnp.int32)
    before = jnp.cumsum(specialist_indicator, 0) - specialist_indicator
    ranked = jnp.sum(before * specialist_indicator, 1)
    position_ceilings = jnp.sum(specialist_indicator * admitted_counts_matrix[None, :], 1)
    retained_couple_filter = ranked < position_ceilings
    target = jnp.where(retained_couple_filter, dispatched_items * SLOT + ranked, slot_count)
    kept_rows = retained_couple_filter.astype(jnp.float32)
    choose = specialist_indicator.astype(jnp.float32)
    send_buf = fill_slots(sent_rows, target, slot_count).reshape(
        specialist_overall_sum, SLOT, model_width
    )
    local_rows = lax.all_to_all(send_buf, "wide", split_axis=0, concat_axis=0, tiled=True).reshape(
        slot_count, model_width
    )
    gathered = lax.all_gather(local_rows, "narrow", axis=0, tiled=True)
    expert_local = lax.psum_scatter(
        expert_rows(gathered, first_linear_matrix[0], second_linear_matrix[0]).astype(jnp.bfloat16),
        "narrow",
        scatter_dimension=0,
        tiled=True,
    )
    returned = lax.all_to_all(
        expert_local.reshape(specialist_overall_sum, SLOT, model_width),
        "wide",
        split_axis=0,
        concat_axis=0,
        tiled=True,
    )
    expert_tok = read_slots(returned.reshape(slot_count, model_width), target).astype(jnp.float32)
    center_rows = lax.dot_general(choose, centers, over_cols, precision=precise)
    logits = jnp.sum(normed_two * center_rows, 1)
    sigma = jax.nn.sigmoid(logits)
    gating = sigma * kept_rows
    mixed = (residual + gating[:, None] * expert_tok).astype(jnp.bfloat16)
    grad_y = incoming_gradient.astype(jnp.float32)
    grad_logit = jnp.sum(grad_y * expert_tok, 1) * sigma * (1.0 - sigma) * kept_rows
    grad_normed = grad_logit[:, None] * center_rows
    centroid_part = lax.dot_general(
        normed_two, choose * grad_logit[:, None], over_rows, precision=precise
    )
    grad_expert = (grad_y * gating[:, None]).astype(jnp.bfloat16)
    grad_buf = fill_slots(grad_expert, target, slot_count).reshape(
        specialist_overall_sum, SLOT, model_width
    )
    grad_local = lax.all_to_all(grad_buf, "wide", split_axis=0, concat_axis=0, tiled=True).reshape(
        slot_count, model_width
    )
    grad_gathered = lax.all_gather(grad_local, "narrow", axis=0, tiled=True)
    grad_pre, up_part, down_part = expert_grads(
        gathered, grad_gathered, first_linear_matrix[0], second_linear_matrix[0]
    )
    input_back = lax.psum_scatter(
        lax.dot_general(
            grad_pre, first_linear_matrix[0], over_cols, preferred_element_type=jnp.float32
        ).astype(jnp.bfloat16),
        "narrow",
        scatter_dimension=0,
        tiled=True,
    )
    up_grad = up_part[None]
    down_grad = down_part[None]
    back_rows = lax.all_to_all(
        input_back.reshape(specialist_overall_sum, SLOT, model_width),
        "wide",
        split_axis=0,
        concat_axis=0,
        tiled=True,
    )
    grad_normed = grad_normed + read_slots(
        back_rows.reshape(slot_count, model_width), target
    ).astype(jnp.float32)
    grad_resid_norm, gain_two_part = norm2_back(grad_normed)
    grad_resid = grad_y + grad_resid_norm
    grad_branch = grad_resid.astype(jnp.bfloat16)
    out_part = lax.dot_general(attended, grad_branch, over_rows, preferred_element_type=jnp.float32)
    grad_attended = lax.dot_general(
        grad_branch, out_mat, over_cols, preferred_element_type=jnp.float32
    ).astype(jnp.bfloat16)
    grad_packed = lax.map(
        attend_backward,
        (packed_seqs, grad_attended.reshape(seq_count, SEQ, model_width), log_totals),
    )
    grad_packed = grad_packed.reshape(tok_count, 3 * model_width)
    qkv_part = lax.dot_general(
        normed_low, grad_packed, over_rows, preferred_element_type=jnp.float32
    )
    grad_normed_one = lax.dot_general(
        grad_packed, qkv_mat, over_cols, preferred_element_type=jnp.float32
    )
    grad_token_norm, gain_one_part = norm1_back(grad_normed_one)
    tokens_grad = grad_resid + grad_token_norm
    gain_one_grad, qkv_grad, out_grad, gain_two_grad, centroid_grad = (
        lax.psum_scatter(gain_one_part, ("wide", "narrow"), scatter_dimension=0, tiled=True),
        lax.psum_scatter(qkv_part, ("wide", "narrow"), scatter_dimension=0, tiled=True),
        lax.psum_scatter(out_part, ("wide", "narrow"), scatter_dimension=0, tiled=True),
        lax.psum_scatter(gain_two_part, ("wide", "narrow"), scatter_dimension=0, tiled=True),
        lax.psum_scatter(centroid_part, ("wide", "narrow"), scatter_dimension=0, tiled=True),
    )
    return (
        mixed,
        tokens_grad,
        gain_one_grad,
        qkv_grad,
        out_grad,
        gain_two_grad,
        centroid_grad,
        up_grad,
        down_grad,
    )


def shards(mesh, v, idx, caps, g1, wq, wo, g2, centers, up, down, dy):
    T, D = v.shape
    E = caps.shape[0]
    c = Sizes(mesh, T, D, wq.shape[0], up.shape[2], E)
    if not c.fits:
        return plain_shards(v, idx, caps, g1, wq, wo, g2, centers, up, down, dy)
    res = forward_call(
        c, v, dy, idx.reshape(1, T), caps, wq, wo, centers.T, g1.reshape(1, -1), g2.reshape(1, -1), up, down
    )
    wt, nt, qkv, lse, att, resid, meta, mrow, ret, outp, ug, dg, cent, mine = res
    mixed, tokens_grad, qg, og, small = backward_call(
        c, v, dy, qkv, lse, att, resid, wt, nt, ret, outp, mrow, meta, cent, wq, mine
    )
    ug, dg, tokens_grad, mixed, qg, og, cen, g1_grad, g2_grad = finish_call(
        c, (ug, dg, tokens_grad, mixed, qg, og), (f32, f32, f32, bf16, f32, f32), small
    )
    return (
        mixed, tokens_grad, g1_grad.reshape(-1), qg, og, g2_grad.reshape(-1), cen.T, ug, dg,
    )


def solution(mesh):
    both = ("wide", "narrow")
    in_specs = (
        P(both, None), P(both, None), P(), P(both), P(both, None), P(both, None), P(both), P(both, None),
        P("wide", None, "narrow"), P("wide", None, "narrow"), P(both, None),
    )
    out_specs = (
        P(both, None), P(both, None), P(both), P(both, None), P(both, None), P(both), P(both, None),
        P("wide", None, "narrow"), P("wide", None, "narrow"),
    )
    return jax.shard_map(
        functools.partial(shards, mesh), mesh=mesh, in_specs=in_specs, out_specs=out_specs, check_vma=False
    )
```
